32 devices in a mesh: fsdp: 8 (over y, x, core), tp: 4 (over z).
Axes of the slice: x: 2, y: 2, z: 4, core: 2. Of those that a mesh axis runs over, the one named last changes fastest.
Arguments:
- tokens: bfloat16 [8192, 768], P(('fsdp', 'tp')), may hold values from -6 to 6
- segment_ids: int32 [8, 1024], P('fsdp'), may hold values from 0 to 7, never falling along the last dimension, each value on 1 to 384 neighbouring positions
- patch_pos: int32 [2, 8192], P(None, ('fsdp', 'tp')), may hold values from 0 to 63
- row_table: bfloat16 [64, 768], P(None, ('fsdp', 'tp')), may hold values from -3 to 3
- col_table: bfloat16 [64, 768], P(None, ('fsdp', 'tp')), may hold values from -3 to 3
- ln_gain: bfloat16 [2, 2, 768], P(None, None, ('fsdp', 'tp')), may hold values from 0.5 to 1.5
- ln_bias: bfloat16 [2, 2, 768], P(None, None, ('fsdp', 'tp')), may hold values from -1.796875 to 1.796875
- qkv_bias: bfloat16 [2, 3, 768], P(None, None, ('fsdp', 'tp')), may hold values from -1.796875 to 1.796875
- qk_gain: bfloat16 [2, 2, 768], P(None, None, ('fsdp', 'tp')), may hold values from 0.5 to 1.5
- query_bias: bfloat16 [2, 768], P(None, ('fsdp', 'tp')), may hold values from -3 to 3
- out_bias: bfloat16 [2, 768], P(None, ('fsdp', 'tp')), may hold values from -1.796875 to 1.796875
- fc1_bias: bfloat16 [2, 3072], P(None, ('fsdp', 'tp')), may hold values from -1.796875 to 1.796875
- fc2_bias: bfloat16 [2, 768], P(None, ('fsdp', 'tp')), may hold values from -1.796875 to 1.796875
- w_qkv: bfloat16 [2, 768, 3, 768], P(None, 'fsdp', None, 'tp'), may hold values from -0.21875 to 0.21875
- w_out: bfloat16 [2, 768, 768], P(None, 'tp', 'fsdp'), may hold values from -1.75 to 1.75
- w_fc1: bfloat16 [2, 768, 3072], P(None, 'fsdp', 'tp'), may hold values from -0.21875 to 0.21875
- w_fc2: bfloat16 [2, 3072, 768], P(None, 'tp', 'fsdp'), may hold values from -0.109375 to 0.109375
- cotangent: float32 [8192, 768], P(('fsdp', 'tp')), may hold values from -6 to 6
Outputs:
- activations: float32 [8192, 768], P(('fsdp', 'tp'))
- token_grad: float32 [8192, 768], P(('fsdp', 'tp'))
- row_table_grad: float32 [64, 768], P(None, ('fsdp', 'tp'))
- col_table_grad: float32 [64, 768], P(None, ('fsdp', 'tp'))
- ln_gain_grad: float32 [2, 2, 768], P(None, None, ('fsdp', 'tp'))
- ln_bias_grad: float32 [2, 2, 768], P(None, None, ('fsdp', 'tp'))
- qkv_bias_grad: float32 [2, 3, 768], P(None, None, ('fsdp', 'tp'))
- qk_gain_grad: float32 [2, 2, 768], P(None, None, ('fsdp', 'tp'))
- query_bias_grad: float32 [2, 768], P(None, ('fsdp', 'tp'))
- out_bias_grad: float32 [2, 768], P(None, ('fsdp', 'tp'))
- fc1_bias_grad: float32 [2, 3072], P(None, ('fsdp', 'tp'))
- fc2_bias_grad: float32 [2, 768], P(None, ('fsdp', 'tp'))
- w_qkv_grad: float32 [2, 768, 3, 768], P(None, 'fsdp', None, 'tp')
- w_out_grad: float32 [2, 768, 768], P(None, 'tp', 'fsdp')
- w_fc1_grad: float32 [2, 768, 3072], P(None, 'fsdp', 'tp')
- w_fc2_grad: float32 [2, 3072, 768], P(None, 'tp', 'fsdp')
The draws below stay inside these ranges and needn't reach their ends.
Inputs may be any that keep to these rules, and one draw needn't show every extreme that they name: `segment_ids`: each row is one sequence; ids never fall along it and every id from 0 to 7 appears in one run of 1 to 384 tokens; some image has exactly 384.
All inputs are finite; a program needn't handle non-finite values.
Results may differ from the reference program's by a relative error of at most 0.019.
Values may be sent and summed in bfloat16 or wider, within the bound.
A program may use at most 192 MiB of HBM per device.

```python
import math
import jax
import jax.numpy as jnp
import numpy as np
from jax import lax

D = 768
H = 12
HD = 64
FF = 3072
GRID = 64
LAYERS = 2
SEQ_LEN = 1024
NSEQ = 8
TOKENS = 8192
IMAGES = 8
IMG_MOST = 384


def touch_ends(values, key, low, largest):
    spot = [jax.random.randint(jax.random.fold_in(key, axis), (), 0, length) for axis, length in enumerate(values.shape)]
    longest = values.shape.index(max(values.shape))
    next_to = spot[:longest] + [(spot[longest] + 1) % values.shape[longest]] + spot[longest + 1:]
    return values.at[tuple(spot)].set(low).at[tuple(next_to)].set(largest)


def spiked(array, own_key, source, target, shards_of, factor):
    owner, partner = [(jnp.arange(array.shape[axis_at]) // (array.shape[axis_at] // shards_of)).reshape([-1 if axis == axis_at else 1 for axis in range(array.ndim)]) for axis_at in (source, target)]
    chosen = jax.random.permutation(own_key, shards_of)[partner]
    strong = (owner == chosen) | (owner == (partner + shards_of // 2) % shards_of)
    return jnp.where(strong, factor * array, array)


def steps_of(key, dims, shards, smallest, top_value):
    factor_of = 1.0
    for position, parts in shards:
        steps = jax.random.uniform(jax.random.fold_in(jax.random.fold_in(key, 6), position), (parts,), jnp.float32, smallest / len(shards), top_value / len(shards))
        factor_of = factor_of * jnp.repeat(jnp.exp(steps), dims[position] // parts).reshape((-1,) + (1,) * (len(dims) - 1 - position))
    return factor_of


def profile(amount, total, limit, skew):
    loads = [(1 << 20) // math.isqrt(standing ** skew) + 1 for standing in range(2, amount + 1)]
    spare, given = total - limit - (amount - 1), [1] * (amount - 1)
    while spare > 0:
        candidates = [i for i in range(amount - 1) if given[i] < limit]
        mass, remaining = sum([loads[i] for i in candidates]), spare
        for i in candidates:
            extra = min(limit - given[i], max(1, remaining * loads[i] // mass), spare)
            given[i] = given[i] + extra
            spare = spare - extra
    return np.array([limit] + given)


def ragged(rng, number_of, total, reach, lean):
    if number_of == 2:
        one = jax.random.randint(rng, (), max(1, total - reach), min(reach, total - 1) + 1)
        return jnp.stack([one, total - one])
    sizes = jnp.asarray(profile(number_of, total, reach, lean), jnp.int32)
    twos = (number_of - 1) // 2
    donor, sink = sizes[1:1 + 2 * twos:2], sizes[2:2 + 2 * twos:2]
    room = jnp.minimum(donor - 1, reach - sink)
    passed = jax.random.randint(jax.random.fold_in(rng, 1), (twos,), 0, 1 << 20) % (room + 1)
    sizes = sizes.at[1:1 + 2 * twos:2].set(donor - passed).at[2:2 + 2 * twos:2].set(sink + passed)
    return sizes[jax.random.permutation(jax.random.fold_in(rng, 2), number_of)]


def bell_draw(rng, extent, scale, reach, shards=(), held_as=jnp.bfloat16):
    values = jax.random.normal(rng, extent, jnp.float32) * scale
    if len(shards) > 0:
        values = steps_of(rng, extent, shards, -0.22, 0.18) * values
    return jnp.clip(values, min=-reach, max=reach).astype(held_as)


def heavy_noise(key, extent, scale, limit, cuts, heavy, kind=jnp.bfloat16):
    values = scale * jax.random.normal(key, extent, jnp.float32)
    if cuts:
        values = values * steps_of(key, extent, cuts, -0.22, 0.18)
    return jnp.clip(spiked(values, jax.random.fold_in(key, 3), *heavy), -limit, limit).astype(kind)


def setup_inputs(seed: int = 0) -> dict:
    seeds = jax.random.split(jax.random.key(seed), 19)
    tokens = bell_draw(seeds[0], (TOKENS, D), 1.0, 6.0, ((0, 32),))
    segment_ids = jax.vmap(lambda own: jnp.searchsorted(jnp.cumsum(ragged(own, IMAGES, SEQ_LEN, IMG_MOST, 2)), jnp.arange(SEQ_LEN), side="right"))(jax.random.split(seeds[1], NSEQ)).reshape((NSEQ, SEQ_LEN)).astype(jnp.int32)
    patch_pos = touch_ends(jax.random.randint(seeds[2], (2, TOKENS), 0, GRID), jax.random.fold_in(seeds[2], 1), 0, GRID - 1).astype(jnp.int32)
    row_table = bell_draw(seeds[3], (GRID, D), 0.5, 3.0, ((1, 32),))
    col_table = bell_draw(seeds[4], (GRID, D), 0.5, 3.0, ((1, 32),))
    ln_gain = jnp.clip(1.0 + 0.1 * jax.random.normal(seeds[5], (LAYERS, 2, D), jnp.float32), 0.5, 1.5).astype(jnp.bfloat16)
    ln_bias = bell_draw(seeds[6], (LAYERS, 2, D), 0.3, 1.796875, ((2, 32),))
    qkv_bias = bell_draw(seeds[7], (LAYERS, 3, D), 0.3, 1.796875, ((2, 32),))
    qk_gain = jnp.clip(1.0 + 0.1 * jax.random.normal(seeds[8], (LAYERS, 2, D), jnp.float32), 0.5, 1.5).astype(jnp.bfloat16)
    query_bias = bell_draw(seeds[9], (LAYERS, D), 0.5, 3.0, ((1, 32),))
    out_bias = bell_draw(seeds[10], (LAYERS, D), 0.3, 1.796875, ((1, 32),))
    fc1_bias = bell_draw(seeds[11], (LAYERS, FF), 0.3, 1.796875, ((1, 32),))
    fc2_bias = bell_draw(seeds[12], (LAYERS, D), 0.3, 1.796875, ((1, 32),))
    w_qkv = bell_draw(seeds[13], (LAYERS, D, 3, D), D ** -0.5, 0.21875, ((1, 8), (3, 4)))
    w_out = bell_draw(seeds[14], (LAYERS, D, D), (D // 64) ** -0.5, 1.75, ((1, 4), (2, 8)))
    w_fc1 = bell_draw(seeds[15], (LAYERS, D, FF), D ** -0.5, 0.21875, ((1, 8), (2, 4)))
    w_fc2 = bell_draw(seeds[16], (LAYERS, FF, D), FF ** -0.5, 0.109375, ((1, 4), (2, 8)))
    cotangent = heavy_noise(seeds[17], (TOKENS, D), 1.0, 6.0, ((0, 32),), (0, 1, 32, 2.75), jnp.float32)
    return {"tokens": tokens, "segment_ids": segment_ids, "patch_pos": patch_pos, "row_table": row_table, "col_table": col_table, "ln_gain": ln_gain, "ln_bias": ln_bias, "qkv_bias": qkv_bias, "qk_gain": qk_gain, "query_bias": query_bias, "out_bias": out_bias, "fc1_bias": fc1_bias, "fc2_bias": fc2_bias, "w_qkv": w_qkv, "w_out": w_out, "w_fc1": w_fc1, "w_fc2": w_fc2, "cotangent": cotangent}


epsilon = 1e-06
negative_fill = -1e+30
highest = lax.Precision.HIGHEST

@jax.custom_vjp
def low(v):
    return lax.optimization_barrier(v.astype(jnp.bfloat16)).astype(jnp.float32)

@jax.custom_vjp
def low_back(v):
    return v

def low_keep(v):
    return (low(v), None)

def low_pass(kept, grad):
    return (grad,)

def back_keep(v):
    return (v, None)

def back_low(kept, grad):
    return (low(grad),)
low.defvjp(low_keep, low_pass)
low_back.defvjp(back_keep, back_low)

def norm_rows(value):
    centered = value - lax.optimization_barrier(jnp.mean(value, axis=-1, keepdims=True))
    return centered * lax.rsqrt(lax.optimization_barrier(jnp.mean(centered * centered, axis=-1, keepdims=True)) + epsilon)

def encoder_layer(resid, layer, params, same_image):
    ln_gain, ln_bias, qkv_bias, qk_gain, query_bias, out_bias, fc1_bias, fc2_bias, w_qkv, w_out, w_fc1, w_fc2 = params
    length = resid.shape[0]
    normed = low(norm_rows(resid) * ln_gain[layer, 0] + ln_bias[layer, 0])
    proj = low_back(jnp.einsum('td,dcf->tcf', normed, w_qkv[layer], precision=highest) + qkv_bias[layer][None])
    query = proj[:, 0].reshape(length, H, HD)
    keys = proj[:, 1].reshape(length, H, HD)
    query_n = low(norm_rows(query) * qk_gain[layer, 0].reshape(H, HD) + query_bias[layer].reshape(H, HD))
    keys_n = low(norm_rows(keys) * qk_gain[layer, 1].reshape(H, HD))
    values_n = low(proj[:, 2].reshape(length, H, HD))
    scores = low_back(jnp.einsum('qhd,khd->hqk', query_n, keys_n, precision=highest) * HD ** (-0.5))
    scores = jnp.where(same_image[None], scores, negative_fill)
    top = lax.optimization_barrier(jnp.max(scores, axis=-1, keepdims=True))
    weights = jnp.exp(scores - top)
    probs = low(weights / lax.optimization_barrier(jnp.sum(weights, axis=-1, keepdims=True)))
    mixed = jnp.einsum('hqk,khd->qhd', probs, values_n, precision=highest).reshape(length, D)
    mixed = low(low_back(mixed))
    middle = resid + low_back(jnp.dot(mixed, w_out[layer], precision=highest) + out_bias[layer])
    normed_mid = low(norm_rows(middle) * ln_gain[layer, 1] + ln_bias[layer, 1])
    hidden = low_back(jnp.dot(normed_mid, w_fc1[layer], precision=highest) + fc1_bias[layer])
    activated = low(jax.nn.gelu(hidden, approximate=False))
    return middle + low_back(jnp.dot(activated, w_fc2[layer], precision=highest) + fc2_bias[layer])

def reference(tokens, segment_ids, patch_pos, row_table, col_table, ln_gain, ln_bias, qkv_bias, qk_gain, query_bias, out_bias, fc1_bias, fc2_bias, w_qkv, w_out, w_fc1, w_fc2, cotangent):
    params = tuple((item.astype(jnp.float32) for item in (ln_gain, ln_bias, qkv_bias, qk_gain, query_bias, out_bias, fc1_bias, fc2_bias, w_qkv, w_out, w_fc1, w_fc2)))
    tables = (row_table.astype(jnp.float32), col_table.astype(jnp.float32))
    seq_count = segment_ids.shape[0]
    length = segment_ids.shape[1]
    seq_tokens = tokens.astype(jnp.float32).reshape(seq_count, length, D)
    seq_cots = cotangent.reshape(seq_count, length, D)
    seq_pos = patch_pos.reshape(2, seq_count, length).transpose(1, 0, 2)
    grid_ids = jnp.arange(GRID, dtype=jnp.int32)

    def one_sequence(totals, item):
        start_rows, cot_rows, images, places = item
        same_image = images[:, None] == images[None, :]
        row_hot = (places[0][:, None] == grid_ids[None, :]).astype(jnp.float32)
        col_hot = (places[1][:, None] == grid_ids[None, :]).astype(jnp.float32)

        def forward(start, tabs, weights):
            resid = start + jnp.dot(row_hot, tabs[0], precision=highest) + jnp.dot(col_hot, tabs[1], precision=highest)
            for layer in range(LAYERS):
                resid = encoder_layer(resid, layer, weights, same_image)
            return resid
        result, pull = jax.vjp(forward, start_rows, tables, params)
        grad_start, grad_tabs, grad_params = pull(cot_rows)
        totals = jax.tree.map(lambda left, right: left + right, totals, (grad_tabs, grad_params))
        return (totals, (result, grad_start))
    zeros = jax.tree.map(jnp.zeros_like, (tables, params))
    totals, (results, grad_starts) = lax.scan(one_sequence, zeros, (seq_tokens, seq_cots, segment_ids, seq_pos))
    grad_tabs, grad_params = totals
    g_ln_gain, g_ln_bias, g_qkv_bias, g_qk_gain, g_query_bias, g_out_bias, g_fc1_bias, g_fc2_bias, g_w_qkv, g_w_out, g_w_fc1, g_w_fc2 = grad_params
    return (results.reshape(-1, D), grad_starts.reshape(-1, D), grad_tabs[0], grad_tabs[1], g_ln_gain, g_ln_bias, g_qkv_bias, g_qk_gain, g_query_bias, g_out_bias, g_fc1_bias, g_fc2_bias, g_w_qkv, g_w_out, g_w_fc1, g_w_fc2)
```

```python
import functools

import jax
import jax.numpy as jnp
from jax import lax
from jax.experimental import pallas as pl
from jax.experimental.pallas import tpu as pltpu
from jax.sharding import PartitionSpec as P

HD = 64
PAIR = 128
REACH = 384
EPS = 1e-06
FILL = -1e30
ROOT_HALF = 0.7071067811865476
INV_ROOT_TWO_PI = 0.3989422804014327
HIGHEST = lax.Precision.HIGHEST
F32 = jnp.float32
BF16 = jnp.bfloat16
TILE = 512


def nn(left, right):
    return lax.dot_general(left, right, (((1,), (0,)), ((), ())), preferred_element_type=F32)


def nt(left, right):
    return lax.dot_general(left, right, (((1,), (1,)), ((), ())), preferred_element_type=F32)


def halves(array):
    middle = array.shape[1] // 2
    return array[:, :middle], array[:, middle:]


def row_norm(value):
    centered = value - jnp.mean(value, axis=-1, keepdims=True)
    scale = lax.rsqrt(jnp.mean(centered * centered, axis=-1, keepdims=True) + EPS)
    return centered * scale, scale


def row_norm_back(grad_hat, normed, scale):
    return scale * (
        grad_hat
        - jnp.mean(grad_hat, axis=-1, keepdims=True)
        - normed * jnp.mean(grad_hat * normed, axis=-1, keepdims=True)
    )


def head_mean(value):
    rows = lax.broadcasted_iota(jnp.int32, (PAIR, PAIR), 0) // HD
    cols = lax.broadcasted_iota(jnp.int32, (PAIR, PAIR), 1) // HD
    spread = jnp.where(rows == cols, 1.0 / HD, 0.0).astype(BF16)
    high = value.astype(BF16)
    low = (value - high.astype(F32)).astype(BF16)
    return nn(high, spread) + nn(low, spread)


def head_norm(value):
    centered = value - head_mean(value)
    scale = lax.rsqrt(head_mean(centered * centered) + EPS)
    return centered * scale, scale


def head_norm_back(grad_hat, normed, scale):
    return scale * (grad_hat - head_mean(grad_hat) - normed * head_mean(grad_hat * normed))


def attend_kernel(
    a_ref, own_ref, far_ref, bias_ref, q_gain_ref, k_gain_ref, q_shift_ref, seg_k_ref, seg_q_ref,
    qn_ref, kn_ref, v_ref, q_hat_ref, k_hat_ref, q_scale_ref, k_scale_ref, p_ref, o_ref, mask_ref,
):
    rows = qn_ref.shape[0]

    @pl.when(pl.program_id(0) == 0)
    def _():
        mask_ref[...] = jnp.where(seg_k_ref[...] == seg_q_ref[...], 0.0, FILL)

    near, distant = halves(a_ref[...])
    near_q, distant_q = halves(a_ref[REACH : REACH + rows, :])
    kv = nn(near, own_ref[:, PAIR:]) + nn(distant, far_ref[:, PAIR:]) + bias_ref[:, PAIR:]
    q = nn(near_q, own_ref[:, :PAIR]) + nn(distant_q, far_ref[:, :PAIR]) + bias_ref[:, :PAIR]
    q_hat, q_scale = head_norm(q)
    k_hat, k_scale = head_norm(kv[:, :PAIR])
    qn = (q_hat * q_gain_ref[...] + q_shift_ref[...]).astype(BF16)
    kn = (k_hat * k_gain_ref[...]).astype(BF16)
    v = kv[:, PAIR:].astype(BF16)
    qn_ref[...] = qn
    kn_ref[...] = kn
    v_ref[...] = v
    q_hat_ref[...] = q_hat.astype(BF16)
    k_hat_ref[...] = k_hat.astype(BF16)
    q_scale_ref[...] = q_scale.astype(BF16)
    k_scale_ref[...] = k_scale.astype(BF16)
    head_of = lax.broadcasted_iota(jnp.int32, (1, PAIR), 1) // HD
    v_t = v.T
    mixed = []
    for head in range(PAIR // HD):
        q_head = jnp.where(head_of == head, qn * HD ** (-0.5), 0.0).astype(BF16)
        scores = nt(kn, q_head) + mask_ref[...]
        weights = jnp.exp(scores - jnp.max(scores, axis=0, keepdims=True))
        total = jnp.sum(weights, axis=0, keepdims=True)
        probs = (weights * (1.0 / total)).astype(BF16)
        p_ref[head] = probs
        mixed.append(nn(v_t[head * HD : (head + 1) * HD], probs))
    o_ref[...] = jnp.concatenate(mixed, axis=0).T.astype(BF16)


def attend(a_win, w_own, w_far, bias, q_gain, k_gain, q_shift, seg_k, seg_q, rows):
    window, width = a_win.shape
    half = width // 2
    pairs = width // PAIR
    whole = lambda shape: pl.BlockSpec(shape, lambda p: (0,) * len(shape))
    col = lambda height, wide=PAIR: pl.BlockSpec((height, wide), lambda p: (0, p))
    outs = [
        (rows, width), (window, width), (window, width), (rows, width), (window, width), (rows, width), (window, width),
    ]
    return pl.pallas_call(
        attend_kernel,
        grid=(pairs,),
        in_specs=[
            whole((window, width)), col(half, 3 * PAIR), col(half, 3 * PAIR), col(1, 3 * PAIR), col(1), col(1), col(1),
            whole((window, 1)), whole((1, rows)),
        ],
        out_specs=[col(height) for height, _ in outs]
        + [pl.BlockSpec((2, window, rows), lambda p: (p, 0, 0)), col(rows)],
        out_shape=[jax.ShapeDtypeStruct(shape, BF16) for shape in outs]
        + [jax.ShapeDtypeStruct((2 * pairs, window, rows), BF16), jax.ShapeDtypeStruct((rows, width), BF16)],
        scratch_shapes=[pltpu.VMEM((window, rows), F32)],
        cost_estimate=pl.CostEstimate(
            flops=2 * window * width * width * 2 + 8 * window * rows * width * 4,
            bytes_accessed=20 * window * width,
            transcendentals=2 * pairs * window * rows,
        ),
        name="attend",
    )(a_win, w_own, w_far, bias, q_gain, k_gain, q_shift, seg_k, seg_q)


def mlp_kernel(
    o_ref, x_ref, mix_own_ref, mix_far_ref, out_shift_ref, gain_ref, shift_ref, up_own_ref, up_far_ref, up_shift_ref,
    down_own_ref, down_far_ref, last_shift_ref, next_gain_ref, next_shift_ref,
    mid_ref, m_ref, act_ref, slope_ref, x2_ref, a_ref, acc_ref,
):
    half = mix_own_ref.shape[0]
    step = pl.program_id(0)

    @pl.when(step == 0)
    def _():
        o = o_ref[...]
        mid_ref[:, :half] = x_ref[:, :half] + (nt(o, mix_own_ref[...]) + out_shift_ref[:, :half])
        mid_ref[:, half:] = x_ref[:, half:] + (nt(o, mix_far_ref[...]) + out_shift_ref[:, half:])
        hat, _ = row_norm(mid_ref[...])
        m_ref[...] = (hat * gain_ref[...] + shift_ref[...]).astype(BF16)
        acc_ref[...] = jnp.zeros_like(acc_ref)

    near, distant = halves(m_ref[...])
    hidden = nn(near, up_own_ref[...]) + nn(distant, up_far_ref[...]) + up_shift_ref[...]
    phi = 0.5 * (1.0 + lax.erf(hidden * ROOT_HALF))
    act = (hidden * phi).astype(BF16)
    act_ref[...] = act
    slope_ref[...] = (phi + hidden * jnp.exp(-0.5 * hidden * hidden) * INV_ROOT_TWO_PI).astype(BF16)
    acc_ref[:, :half] += nt(act, down_own_ref[...])
    acc_ref[:, half:] += nt(act, down_far_ref[...])

    @pl.when(step == pl.num_programs(0) - 1)
    def _():
        x2 = mid_ref[...] + (acc_ref[...] + last_shift_ref[...])
        x2_ref[...] = x2
        hat, _ = row_norm(x2)
        a_ref[...] = (hat * next_gain_ref[...] + next_shift_ref[...]).astype(BF16)


def mlp(o, x, attn_own, attn_far, out_shift, gain, shift, mlp_own, mlp_far, up_shift, last_shift, next_gain, next_shift):
    rows, width = x.shape
    half = width // 2
    hidden = up_shift.shape[1]
    steps = hidden // TILE
    whole = lambda shape: pl.BlockSpec(shape, lambda j: (0,) * len(shape))
    mix = pl.BlockSpec((half, width), lambda j: (0, 3))
    up = pl.BlockSpec((half, TILE), lambda j: (0, j))
    down = pl.BlockSpec((half, TILE), lambda j: (0, j + steps))
    row = whole((1, width))
    full = whole((rows, width))
    tall = pl.BlockSpec((rows, TILE), lambda j: (0, j))
    return pl.pallas_call(
        mlp_kernel,
        grid=(steps,),
        in_specs=[
            full, full, mix, mix, row, row, row, up, up, pl.BlockSpec((1, TILE), lambda j: (0, j)), down, down, row, row, row,
        ],
        out_specs=[full, full, tall, tall, full, full],
        out_shape=[
            jax.ShapeDtypeStruct((rows, width), F32),
            jax.ShapeDtypeStruct((rows, width), BF16),
            jax.ShapeDtypeStruct((rows, hidden), BF16),
            jax.ShapeDtypeStruct((rows, hidden), BF16),
            jax.ShapeDtypeStruct((rows, width), F32),
            jax.ShapeDtypeStruct((rows, width), BF16),
        ],
        scratch_shapes=[pltpu.VMEM((rows, width), F32)],
        cost_estimate=pl.CostEstimate(
            flops=2 * rows * width * (width + 2 * hidden),
            bytes_accessed=2 * width * (width + 2 * hidden),
            transcendentals=2 * rows * hidden,
        ),
        name="mlp",
    )(
        o, x, attn_own, attn_far, out_shift, gain, shift, mlp_own, mlp_far, up_shift, mlp_own, mlp_far, last_shift,
        next_gain, next_shift,
    )


def mlp_back_kernel(
    g_ref, down_own_ref, down_far_ref, slope_ref, up_own_ref, up_far_ref, mid_ref, gain_ref, mix_own_ref, mix_far_ref,
    gz_ref, gh_ref, up_shift_grad_ref, g1_ref, gr_ref, go_ref, small_ref, acc_ref,
):
    half = mix_own_ref.shape[0]
    step = pl.program_id(0)

    @pl.when(step == 0)
    def _():
        gz_ref[...] = g_ref[...].astype(BF16)
        acc_ref[...] = jnp.zeros_like(acc_ref)

    near, distant = halves(gz_ref[...])
    gh = ((nn(near, down_own_ref[...]) + nn(distant, down_far_ref[...])) * slope_ref[...].astype(F32)).astype(BF16)
    gh_ref[...] = gh
    up_shift_grad_ref[...] = jnp.sum(gh.astype(F32), axis=0, keepdims=True)
    acc_ref[:, :half] += nt(gh, up_own_ref[...])
    acc_ref[:, half:] += nt(gh, up_far_ref[...])

    @pl.when(step == pl.num_programs(0) - 1)
    def _():
        gm = acc_ref[...]
        hat, scale = row_norm(mid_ref[...])
        g1 = g_ref[...] + row_norm_back(gm * gain_ref[...], hat, scale)
        gr = g1.astype(BF16)
        g1_ref[...] = g1
        gr_ref[...] = gr
        small_ref[...] = jnp.zeros_like(small_ref)
        small_ref[0:1, :] = jnp.sum(gz_ref[...].astype(F32), axis=0, keepdims=True)
        small_ref[1:2, :] = jnp.sum(gr.astype(F32), axis=0, keepdims=True)
        small_ref[2:3, :] = jnp.sum(gm * hat, axis=0, keepdims=True)
        small_ref[3:4, :] = jnp.sum(gm, axis=0, keepdims=True)
        go_ref[...] = (nn(gr[:, :half], mix_own_ref[...]) + nn(gr[:, half:], mix_far_ref[...])).astype(BF16)


def mlp_back(grad, mlp_own, mlp_far, slope, mid, gain, attn_own, attn_far):
    rows, width = grad.shape
    half = width // 2
    hidden = slope.shape[1]
    steps = hidden // TILE
    whole = lambda shape: pl.BlockSpec(shape, lambda j: (0,) * len(shape))
    mix = pl.BlockSpec((half, width), lambda j: (0, 3))
    up = pl.BlockSpec((half, TILE), lambda j: (0, j))
    down = pl.BlockSpec((half, TILE), lambda j: (0, j + steps))
    full = whole((rows, width))
    tall = pl.BlockSpec((rows, TILE), lambda j: (0, j))
    return pl.pallas_call(
        mlp_back_kernel,
        grid=(steps,),
        in_specs=[full, down, down, tall, up, up, full, whole((1, width)), mix, mix],
        out_specs=[full, tall, pl.BlockSpec((1, TILE), lambda j: (0, j)), full, full, full, whole((8, width))],
        out_shape=[
            jax.ShapeDtypeStruct((rows, width), BF16),
            jax.ShapeDtypeStruct((rows, hidden), BF16),
            jax.ShapeDtypeStruct((1, hidden), F32),
            jax.ShapeDtypeStruct((rows, width), F32),
            jax.ShapeDtypeStruct((rows, width), BF16),
            jax.ShapeDtypeStruct((rows, width), BF16),
            jax.ShapeDtypeStruct((8, width), F32),
        ],
        scratch_shapes=[pltpu.VMEM((rows, width), F32)],
        cost_estimate=pl.CostEstimate(
            flops=2 * rows * width * (width + 2 * hidden),
            bytes_accessed=2 * width * (width + 2 * hidden),
            transcendentals=0,
        ),
        name="mlp_back",
    )(grad, mlp_own, mlp_far, slope, mlp_own, mlp_far, mid, gain, attn_own, attn_far)


def attend_back_kernel(
    go_ref, qn_ref, kn_ref, v_ref, q_hat_ref, k_hat_ref, q_scale_ref, k_scale_ref, p_ref, own_ref, far_ref, q_gain_ref,
    k_gain_ref, gq_ref, gkv_ref, mine_ref, left_ref, right_ref, small_ref, acc_ref,
):
    rows = go_ref.shape[0]
    half = own_ref.shape[0]
    step = pl.program_id(0)

    @pl.when(step == 0)
    def _():
        acc_ref[...] = jnp.zeros_like(acc_ref)

    head_of = lax.broadcasted_iota(jnp.int32, (1, PAIR), 1) // HD
    go, qn, kn, v = go_ref[...], qn_ref[...], kn_ref[...], v_ref[...]
    k_t = kn.T
    grad_q, grad_k, grad_v = [], 0.0, 0.0
    for head in range(PAIR // HD):
        go_head = jnp.where(head_of == head, go, 0.0).astype(BF16)
        q_head = jnp.where(head_of == head, qn * HD ** (-0.5), 0.0).astype(BF16)
        stored = p_ref[head]
        probs = stored.astype(F32)
        grad_probs = nt(v, go_head)
        delta = jnp.sum(probs * grad_probs, axis=0, keepdims=True)
        grad_scores = (probs * (grad_probs - delta)).astype(BF16)
        grad_v += nn(stored, go_head)
        grad_k += nn(grad_scores, q_head)
        grad_q.append(nn(k_t[head * HD : (head + 1) * HD], grad_scores))
    grad_q = jnp.concatenate(grad_q, axis=0).T * HD ** (-0.5)
    q_hat = q_hat_ref[...].astype(F32)
    k_hat = k_hat_ref[...].astype(F32)
    gq = head_norm_back(grad_q * q_gain_ref[...], q_hat, q_scale_ref[...].astype(F32)).astype(BF16)
    gk = head_norm_back(grad_k * k_gain_ref[...], k_hat, k_scale_ref[...].astype(F32)).astype(BF16)
    gv = grad_v.astype(BF16)
    gkv = jnp.concatenate([gk, gv], axis=1)
    gq_ref[...] = gq
    gkv_ref[...] = gkv
    small_ref[...] = jnp.zeros_like(small_ref)
    small_ref[0:1, :] = jnp.sum(grad_q * q_hat, axis=0, keepdims=True)
    small_ref[1:2, :] = jnp.sum(grad_k * k_hat, axis=0, keepdims=True)
    small_ref[2:3, :] = jnp.sum(grad_q, axis=0, keepdims=True)
    small_ref[3:4, :] = jnp.sum(gq.astype(F32), axis=0, keepdims=True)
    small_ref[4:5, :] = jnp.sum(gk.astype(F32), axis=0, keepdims=True)
    small_ref[5:6, :] = jnp.sum(gv.astype(F32), axis=0, keepdims=True)
    acc_ref[:, :half] += nt(gkv, own_ref[:, PAIR:])
    acc_ref[:, half:] += nt(gkv, far_ref[:, PAIR:])
    acc_ref[REACH : REACH + rows, :half] += nt(gq, own_ref[:, :PAIR])
    acc_ref[REACH : REACH + rows, half:] += nt(gq, far_ref[:, :PAIR])

    @pl.when(step == pl.num_programs(0) - 1)
    def _():
        left_ref[...] = acc_ref[:REACH, :].astype(BF16)
        mine_ref[...] = acc_ref[REACH : REACH + rows, :]
        right_ref[...] = acc_ref[REACH + rows :, :].astype(BF16)


def attend_back(go, qn, kn, v, q_hat, k_hat, q_scale, k_scale, probs, attn_own, attn_far, q_gain, k_gain):
    rows, width = go.shape
    window = kn.shape[0]
    half = width // 2
    pairs = width // PAIR
    whole = lambda shape: pl.BlockSpec(shape, lambda p: (0,) * len(shape))
    col = lambda height, wide=PAIR: pl.BlockSpec((height, wide), lambda p: (0, p))
    return pl.pallas_call(
        attend_back_kernel,
        grid=(pairs,),
        in_specs=[
            col(rows), col(rows), col(window), col(window), col(rows), col(window), col(rows), col(window),
            pl.BlockSpec((2, window, rows), lambda p: (p, 0, 0)), col(half, 3 * PAIR), col(half, 3 * PAIR), col(1), col(1),
        ],
        out_specs=[
            col(rows), col(window, 2 * PAIR), whole((rows, width)), whole((REACH, width)), whole((REACH, width)), col(8),
        ],
        out_shape=[
            jax.ShapeDtypeStruct((rows, width), BF16),
            jax.ShapeDtypeStruct((window, 2 * width), BF16),
            jax.ShapeDtypeStruct((rows, width), F32),
            jax.ShapeDtypeStruct((REACH, width), BF16),
            jax.ShapeDtypeStruct((REACH, width), BF16),
            jax.ShapeDtypeStruct((8, width), F32),
        ],
        scratch_shapes=[pltpu.VMEM((window, width), F32)],
        cost_estimate=pl.CostEstimate(
            flops=2 * window * width * width * 2 + 20 * window * rows * width * 2,
            bytes_accessed=20 * window * width,
            transcendentals=0,
        ),
        name="attend_back",
    )(go, qn, kn, v, q_hat, k_hat, q_scale, k_scale, probs, attn_own, attn_far, q_gain, k_gain)


def attn_weight_kernel(a_ref, gq_ref, gkv_ref, gr_ref, o_ref, keep_ref, send_ref, a_t_ref, gr_t_ref):
    rows = gq_ref.shape[0]
    half = keep_ref.shape[0]
    step = pl.program_id(0)
    pairs = pl.num_programs(0) - 2

    @pl.when(step == 0)
    def _():
        a_t_ref[...] = a_ref[...].T
        gr_t_ref[...] = gr_ref[...].T

    @pl.when(step < pairs)
    def _():
        for part, ref in ((slice(0, half), keep_ref), (slice(half, 2 * half), send_ref)):
            ref[:, :PAIR] = nn(a_t_ref[part, REACH : REACH + rows], gq_ref[...]).astype(BF16)
            ref[:, PAIR:] = nn(a_t_ref[part, :], gkv_ref[...]).astype(BF16)

    @pl.when(step >= pairs)
    def _():
        for part, ref in ((slice(0, half), keep_ref), (slice(half, 2 * half), send_ref)):
            ref[...] = nn(gr_t_ref[part, :], o_ref[...]).astype(BF16)


def attn_weight_grads(a_win, gq, gkv, gr, o):
    window, width = a_win.shape
    rows = gr.shape[0]
    half = width // 2
    pairs = width // PAIR
    wide = 3 * PAIR
    whole = lambda shape: pl.BlockSpec(shape, lambda p: (0,) * len(shape))
    out = pl.BlockSpec((half, wide), lambda p: (0, p))
    return pl.pallas_call(
        attn_weight_kernel,
        grid=(pairs + 2,),
        in_specs=[
            whole((window, width)),
            pl.BlockSpec((rows, PAIR), lambda p: (0, jnp.minimum(p, pairs - 1))),
            pl.BlockSpec((window, 2 * PAIR), lambda p: (0, jnp.minimum(p, pairs - 1))),
            whole((rows, width)),
            pl.BlockSpec((rows, wide), lambda p: (0, jnp.maximum(p - pairs, 0))),
        ],
        out_specs=[out, out],
        out_shape=[jax.ShapeDtypeStruct((half, 4 * width), BF16)] * 2,
        scratch_shapes=[pltpu.VMEM((width, window), BF16), pltpu.VMEM((width, rows), BF16)],
        cost_estimate=pl.CostEstimate(
            flops=2 * width * width * (2 * window + 2 * rows), bytes_accessed=8 * width * width, transcendentals=0
        ),
        name="attn_weight_grads",
    )(a_win, gq, gkv, gr, o)


def mlp_weight_kernel(m_ref, gh_ref, gz_ref, act_ref, keep_ref, send_ref, m_t_ref, gz_t_ref):
    half = keep_ref.shape[0]
    step = pl.program_id(0)
    steps = pl.num_programs(0) // 2

    @pl.when(step == 0)
    def _():
        m_t_ref[...] = m_ref[...].T
        gz_t_ref[...] = gz_ref[...].T

    @pl.when(step < steps)
    def _():
        keep_ref[...] = nn(m_t_ref[:half, :], gh_ref[...]).astype(BF16)
        send_ref[...] = nn(m_t_ref[half:, :], gh_ref[...]).astype(BF16)

    @pl.when(step >= steps)
    def _():
        keep_ref[...] = nn(gz_t_ref[:half, :], act_ref[...]).astype(BF16)
        send_ref[...] = nn(gz_t_ref[half:, :], act_ref[...]).astype(BF16)


def mlp_weight_grads(m, gh, gz, act):
    rows, width = m.shape
    half = width // 2
    hidden = gh.shape[1]
    steps = hidden // TILE
    whole = lambda shape: pl.BlockSpec(shape, lambda j: (0,) * len(shape))
    out = pl.BlockSpec((half, TILE), lambda j: (0, j))
    return pl.pallas_call(
        mlp_weight_kernel,
        grid=(2 * steps,),
        in_specs=[
            whole((rows, width)),
            pl.BlockSpec((rows, TILE), lambda j: (0, jnp.minimum(j, steps - 1))),
            whole((rows, width)),
            pl.BlockSpec((rows, TILE), lambda j: (0, jnp.maximum(j - steps, 0))),
        ],
        out_specs=[out, out],
        out_shape=[jax.ShapeDtypeStruct((half, 2 * hidden), BF16)] * 2,
        scratch_shapes=[pltpu.VMEM((width, rows), BF16), pltpu.VMEM((width, rows), BF16)],
        cost_estimate=pl.CostEstimate(
            flops=4 * width * hidden * rows, bytes_accessed=4 * width * hidden, transcendentals=0
        ),
        name="mlp_weight_grads",
    )(m, gh, gz, act)


def flip(array, bit, axis="fsdp"):
    size = lax.axis_size(axis)
    return lax.ppermute(array, axis, [(i, i ^ (1 << bit)) for i in range(size)])


def ring(array):
    size = lax.axis_size("tp")
    return lax.ppermute(array, "tp", [(i, (i + 1) % size) for i in range(size)])


def hop(array, distance):
    size = lax.axis_size("tp")
    return lax.ppermute(array, "tp", [(i, i + distance) for i in range(size) if 0 <= i + distance < size])


def bits_of(size):
    return size.bit_length() - 1


def row_bits(first_top):
    count = bits_of(lax.axis_size("fsdp"))
    tops = [count - 1, count - 2] if first_top else [count - 2, count - 1]
    return list(range(1, count - 2)), tops


def over_tp(block):
    pieces = [block]
    for _ in range(lax.axis_size("tp") - 1):
        pieces.append(ring(pieces[-1]))
    return pieces


def over_rows(block, first_top):
    low, tops = row_bits(first_top)
    have = []
    for bit in low + tops:
        axis = sum(other > bit for other in have)
        block = jnp.stack([block, flip(block, bit)], axis=axis)
        have.append(bit)
    return block.reshape((-1, block.shape[-1]))


def add(left, right, kind=BF16):
    return (left.astype(F32) + right.astype(F32)).astype(kind)


def reduce_rows(keep, send, first_top):
    low, tops = row_bits(first_top)
    block = add(keep, flip(send, 0))
    order = tops + low[::-1]
    have = sorted(order, reverse=True)
    block = block.reshape((2,) * len(have) + (-1, block.shape[-1]))
    for bit in order:
        axis = have.index(bit)
        mine = lax.index_in_dim(block, 0, axis, keepdims=False)
        other = lax.index_in_dim(block, 1, axis, keepdims=False)
        block = add(mine, flip(other, bit))
        have.remove(bit)
    return block


def reduce_tp(pieces):
    total = pieces[1]
    for piece in pieces[2:]:
        total = add(ring(total), piece)
    return add(ring(total), pieces[0], F32)


def gather_layer(w_qkv, w_out, w_fc1, w_fc2, first_top):
    chunk, _, head_cols = w_qkv.shape
    size = lax.axis_size("tp")
    pairs = size * head_cols // PAIR
    pieces = over_tp(jnp.concatenate([w_qkv.reshape(chunk, 3 * head_cols), w_out.T], axis=1))
    qkv = jnp.concatenate([piece[:, : 3 * head_cols].reshape(chunk, 3, head_cols) for piece in pieces], axis=2)
    qkv = qkv.reshape(chunk, 3, pairs, PAIR).transpose(0, 2, 1, 3).reshape(chunk, -1)
    attn = jnp.concatenate([qkv] + [piece[:, 3 * head_cols :] for piece in pieces], axis=1)
    attn = over_rows(attn, first_top)
    pieces = over_tp(jnp.concatenate([w_fc1, w_fc2.T], axis=1))
    cols = w_fc1.shape[1]
    mlp_w = jnp.concatenate([piece[:, :cols] for piece in pieces] + [piece[:, cols:] for piece in pieces], axis=1)
    mlp_w = over_rows(mlp_w, not first_top)
    return attn, flip(attn, 0), mlp_w, flip(mlp_w, 0)


def split_tp(array, axis=-1):
    return jnp.split(array, lax.axis_size("tp"), axis=axis)


def reduce_attn(keep, send, first_top):
    block = reduce_rows(keep, send, first_top)
    chunk, total = block.shape
    width = total // 4
    qkv = block[:, : 3 * width].reshape(chunk, width // PAIR, 3, PAIR).transpose(0, 2, 1, 3).reshape(chunk, 3, width)
    pieces = [
        jnp.concatenate([left.reshape(chunk, -1), right], axis=1)
        for left, right in zip(split_tp(qkv), split_tp(block[:, 3 * width :]))
    ]
    total = reduce_tp(pieces)
    cols = total.shape[1] // 4
    return total[:, : 3 * cols].reshape(chunk, 3, cols), total[:, 3 * cols :].T


def reduce_mlp(keep, send, first_top):
    block = reduce_rows(keep, send, first_top)
    hidden = block.shape[1] // 2
    pieces = [
        jnp.concatenate([left, right], axis=1)
        for left, right in zip(split_tp(block[:, :hidden]), split_tp(block[:, hidden:]))
    ]
    total = reduce_tp(pieces)
    cols = total.shape[1] // 2
    return total[:, :cols], total[:, cols:].T


def body(
    tokens, segment_ids, patch_pos, row_table, col_table, ln_gain, ln_bias, qkv_bias, qk_gain, query_bias, out_bias,
    fc1_bias, fc2_bias, w_qkv, w_out, w_fc1, w_fc2, cotangent,
):
    layers = w_qkv.shape[0]
    rows, width = tokens.shape
    fsdp, tp = lax.axis_size("fsdp"), lax.axis_size("tp")
    f_index, t_index = lax.axis_index("fsdp"), lax.axis_index("tp")
    hidden = fc1_bias.shape[1] * fsdp * tp
    grid = row_table.shape[0]
    fine = width // (fsdp * tp)
    parts = hidden // width

    place = jnp.arange(width, dtype=jnp.int32)
    chunk = width // fsdp
    slot = place // chunk
    away = (slot % (fsdp // 2)) * 2 + slot // (fsdp // 2)
    feature_at = (f_index ^ away) * chunk + place % chunk
    head_cols = width // tp
    head_at = ((t_index - place // head_cols) % tp) * head_cols + place % head_cols
    far = place // fine
    arrived_at = ((f_index ^ (far // tp)) * tp + (t_index ^ (far % tp))) * fine + place % fine
    to_feature = (arrived_at[:, None] == feature_at[None, :]).astype(BF16)
    to_head = (arrived_at[:, None] == head_at[None, :]).astype(BF16)
    reorder = (place[:, None] == feature_at[None, :]).astype(BF16)
    device = jnp.arange(fsdp * tp, dtype=jnp.int32)
    device_at = (f_index ^ (device // tp)) * tp + (t_index ^ (device % tp))
    wanted = ((t_index - device // fsdp) % tp) * fsdp + device % fsdp
    to_hidden = (wanted[:, None] == device_at[None, :]).astype(BF16)

    shares = [row_table, col_table] + [
        item.reshape(-1, fine) for item in (ln_gain, ln_bias, out_bias, fc2_bias, qkv_bias, qk_gain, query_bias)
    ]
    small = jnp.concatenate(shares + [fc1_bias.reshape(layers * parts, fine)], axis=0)
    count = small.shape[0]
    flat = small.reshape(1, -1)
    for bit in range(bits_of(tp)):
        flat = jnp.concatenate([flat, flip(flat, bit, "tp")], axis=0)
    for bit in range(bits_of(fsdp)):
        flat = jnp.concatenate([flat, flip(flat, bit)], axis=0)
    gathered = flat.reshape(fsdp * tp, count, fine)
    lined = gathered.transpose(1, 0, 2).reshape(count, width)
    wide = 2 * grid + 6 * layers
    by_feature = jnp.dot(lined[:wide], to_feature, preferred_element_type=F32)
    by_head = jnp.dot(lined[wide : wide + 6 * layers], to_head, preferred_element_type=F32)
    up_shift = jnp.einsum(
        "or,rlsi->losi",
        to_hidden,
        gathered[:, wide + 6 * layers :].reshape(fsdp * tp, layers, parts, fine),
        preferred_element_type=F32,
    ).reshape(layers, 1, hidden)
    rows_full = by_feature[:grid].astype(BF16)
    cols_full = by_feature[grid : 2 * grid].astype(BF16)
    rest = by_feature[2 * grid :]
    gains = rest[: 2 * layers].reshape(layers, 2, 1, width)
    shifts = rest[2 * layers : 4 * layers].reshape(layers, 2, 1, width)
    out_shift = rest[4 * layers : 5 * layers].reshape(layers, 1, width)
    last_shift = rest[5 * layers :].reshape(layers, 1, width)
    pairs = width // PAIR
    proj_shift = by_head[: 3 * layers].reshape(layers, 3, pairs, PAIR).transpose(0, 2, 1, 3).reshape(layers, 1, 3 * width)
    head_gain = by_head[3 * layers : 5 * layers].reshape(layers, 2, 1, width)
    head_shift = by_head[5 * layers :].reshape(layers, 1, width)

    weights = [
        gather_layer(w_qkv[layer], w_out[layer], w_fc1[layer], w_fc2[layer], layer % 2 == 0) for layer in range(layers)
    ]

    grid_ids = jnp.arange(grid, dtype=jnp.int32)
    row_hot = patch_pos[0][:, None] == grid_ids[None, :]
    col_hot = patch_pos[1][:, None] == grid_ids[None, :]
    residual = (
        jnp.dot(tokens, reorder, preferred_element_type=F32)
        + jnp.dot(row_hot.astype(BF16), rows_full, preferred_element_type=F32)
        + jnp.dot(col_hot.astype(BF16), cols_full, preferred_element_type=F32)
    )
    segments = segment_ids[0]
    padded = jnp.pad(segments, (REACH, REACH), constant_values=-1)
    seg_k = lax.dynamic_slice_in_dim(padded, t_index * rows, rows + 2 * REACH).reshape(-1, 1)
    seg_q = lax.dynamic_slice_in_dim(segments, t_index * rows, rows).reshape(1, -1)
    spill = REACH - rows

    hat, _ = row_norm(residual)
    a_own = (hat * gains[0, 0] + shifts[0, 0]).astype(BF16)
    saved = []
    for layer in range(layers):
        attn_own, attn_far, mlp_own, mlp_far = weights[layer]
        a_win = jnp.concatenate(
            [hop(a_own[rows - spill :], 2), hop(a_own, 1), a_own, hop(a_own, -1), hop(a_own[:spill], -2)], axis=0
        )
        qn, kn, v, q_hat, k_hat, q_scale, k_scale, probs, o = attend(
            a_win, attn_own, attn_far, proj_shift[layer], head_gain[layer, 0], head_gain[layer, 1], head_shift[layer],
            seg_k, seg_q, rows,
        )
        after = min(layer + 1, layers - 1)
        mid, m, act, slope, x2, a_next = mlp(
            o, residual, attn_own, attn_far, out_shift[layer], gains[layer, 1], shifts[layer, 1], mlp_own, mlp_far,
            up_shift[layer], last_shift[layer], gains[after, 0], shifts[after, 0],
        )
        saved.append((residual, a_win, qn, kn, v, q_hat, k_hat, q_scale, k_scale, probs, o, mid, m, act, slope))
        residual, a_own = x2, a_next

    restore = functools.partial(
        lax.dot_general, dimension_numbers=(((1,), (1,)), ((), ())), precision=HIGHEST, preferred_element_type=F32
    )
    exact = reorder.astype(F32)
    activations = restore(residual, exact)
    grad = jnp.dot(cotangent, exact, precision=HIGHEST, preferred_element_type=F32)
    kept = [None] * layers
    w_qkv_grad, w_out_grad, w_fc1_grad, w_fc2_grad = ([None] * layers for _ in range(4))
    for layer in reversed(range(layers)):
        attn_own, attn_far, mlp_own, mlp_far = weights[layer]
        x, a_win, qn, kn, v, q_hat, k_hat, q_scale, k_scale, probs, o, mid, m, act, slope = saved[layer]
        gz, gh, up_grad, g1, gr, go, mlp_small = mlp_back(
            grad, mlp_own, mlp_far, slope, mid, gains[layer, 1], attn_own, attn_far
        )
        keep, send = mlp_weight_grads(m, gh, gz, act)
        w_fc1_grad[layer], w_fc2_grad[layer] = reduce_mlp(keep, send, layer % 2 == 0)
        gq, gkv, mine, left, right, attn_small = attend_back(
            go, qn, kn, v, q_hat, k_hat, q_scale, k_scale, probs, attn_own, attn_far, head_gain[layer, 0],
            head_gain[layer, 1],
        )
        keep, send = attn_weight_grads(a_win, gq, gkv, gr, o)
        w_qkv_grad[layer], w_out_grad[layer] = reduce_attn(keep, send, layer % 2 == 1)
        ends = jnp.concatenate([hop(right[rows:], 2), hop(left[:spill], -2)], axis=0).astype(F32)
        attn_grad = mine + hop(right[:rows], 1).astype(F32) + hop(left[spill:], -1).astype(F32) + ends
        hat, scale = row_norm(x)
        grad = g1 + row_norm_back(attn_grad * gains[layer, 0], hat, scale)
        kept[layer] = (
            jnp.sum(attn_grad * hat, axis=0), jnp.sum(attn_grad, axis=0), mlp_small, attn_small,
            up_grad.reshape(parts, width),
        )

    token_grad = restore(grad, exact)
    row_grad = jnp.einsum("tg,td->gd", row_hot.astype(F32), grad, precision=HIGHEST)
    col_grad = jnp.einsum("tg,td->gd", col_hot.astype(F32), grad, precision=HIGHEST)
    featured = [row_grad, col_grad]
    featured.append(jnp.stack([line for a_gain, _, sums, _, _ in kept for line in (a_gain, sums[2])]))
    featured.append(jnp.stack([line for _, a_shift, sums, _, _ in kept for line in (a_shift, sums[3])]))
    featured.append(jnp.stack([sums[1] for _, _, sums, _, _ in kept]))
    featured.append(jnp.stack([sums[0] for _, _, sums, _, _ in kept]))
    headed = jnp.concatenate(
        [sums[3:6] for _, _, _, sums, _ in kept]
        + [sums[0:2] for _, _, _, sums, _ in kept]
        + [sums[2:3] for _, _, _, sums, _ in kept]
    )
    spread = jnp.concatenate(
        [restore(jnp.concatenate(featured), to_feature.astype(F32)), restore(headed, to_head.astype(F32))]
    )
    spread = spread.reshape(-1, fsdp * tp, fine).transpose(1, 0, 2)
    up_all = jnp.stack([item[4] for item in kept]).reshape(layers, fsdp * tp, parts * fine)
    up_all = jnp.einsum("or,lok->rlk", to_hidden.astype(F32), up_all, precision=HIGHEST)
    flat = jnp.concatenate([spread.reshape(fsdp * tp, -1), up_all.reshape(fsdp * tp, -1)], axis=1)
    for bit in reversed(range(bits_of(fsdp))):
        middle = flat.shape[0] // 2
        flat = flat[:middle] + flip(flat[middle:], bit)
    for bit in reversed(range(bits_of(tp))):
        middle = flat.shape[0] // 2
        flat = flat[:middle] + flip(flat[middle:], bit, "tp")
    flat = flat.reshape(-1)
    sizes = [grid, grid, 2 * layers, 2 * layers, layers, layers, 3 * layers, 2 * layers, layers, layers * parts]
    shapes = [
        (grid, fine), (grid, fine), (layers, 2, fine), (layers, 2, fine), (layers, fine), (layers, fine),
        (layers, 3, fine), (layers, 2, fine), (layers, fine), (layers, parts * fine),
    ]
    found = []
    start = 0
    for lines, shape in zip(sizes, shapes):
        found.append(flat[start : start + lines * fine].reshape(shape))
        start += lines * fine
    rows_g, cols_g, gain_g, shift_g, out_g, last_g, proj_g, head_gain_g, head_shift_g, up_g = found
    return (
        activations, token_grad, rows_g, cols_g, gain_g, shift_g, proj_g, head_gain_g, head_shift_g, out_g, up_g, last_g,
        jnp.stack(w_qkv_grad), jnp.stack(w_out_grad), jnp.stack(w_fc1_grad), jnp.stack(w_fc2_grad),
    )


def solution(mesh):
    both = ("fsdp", "tp")
    in_specs = (
        P(both, None), P("fsdp", None), P(None, both), P(None, both), P(None, both), P(None, None, both),
        P(None, None, both), P(None, None, both), P(None, None, both), P(None, both), P(None, both), P(None, both),
        P(None, both), P(None, "fsdp", None, "tp"), P(None, "tp", "fsdp"), P(None, "fsdp", "tp"), P(None, "tp", "fsdp"),
        P(both, None),
    )
    out_specs = (
        P(both, None), P(both, None), P(None, both), P(None, both), P(None, None, both), P(None, None, both),
        P(None, None, both), P(None, None, both), P(None, both), P(None, both), P(None, both), P(None, both),
        P(None, "fsdp", None, "tp"), P(None, "tp", "fsdp"), P(None, "fsdp", "tp"), P(None, "tp", "fsdp"),
    )
    return jax.shard_map(body, mesh=mesh, in_specs=in_specs, out_specs=out_specs, check_vma=False)
```

```python
import functools

import jax
import jax.numpy as jnp
from jax import lax
from jax.experimental import pallas as pl
from jax.experimental.pallas import tpu as pltpu
from jax.sharding import PartitionSpec as P

HD = 64
PAIR = 128
REACH = 384
EPS = 1e-06
FILL = -1e30
ROOT_HALF = 0.7071067811865476
INV_ROOT_TWO_PI = 0.3989422804014327
HIGHEST = lax.Precision.HIGHEST
F32 = jnp.float32
BF16 = jnp.bfloat16
MESH = pl.DeviceIdType.MESH
ANY = pl.BlockSpec(memory_space=pl.ANY)


def nn(left, right):
    return lax.dot_general(left, right, (((1,), (0,)), ((), ())), preferred_element_type=F32)


def nt(left, right):
    return lax.dot_general(left, right, (((1,), (1,)), ((), ())), preferred_element_type=F32)


def halves(array):
    middle = array.shape[1] // 2
    return array[:, :middle], array[:, middle:]


def row_norm(value):
    centered = value - jnp.mean(value, axis=-1, keepdims=True)
    scale = lax.rsqrt(jnp.mean(centered * centered, axis=-1, keepdims=True) + EPS)
    return centered * scale, scale


def row_norm_back(grad_hat, normed, scale):
    return scale * (
        grad_hat
        - jnp.mean(grad_hat, axis=-1, keepdims=True)
        - normed * jnp.mean(grad_hat * normed, axis=-1, keepdims=True)
    )


def head_mean(value, exact=False):
    wide = value.shape[1]
    rows = lax.broadcasted_iota(jnp.int32, (wide, wide), 0) // HD
    cols = lax.broadcasted_iota(jnp.int32, (wide, wide), 1) // HD
    spread = jnp.where(rows == cols, 1.0 / HD, 0.0).astype(BF16)
    high = value.astype(BF16)
    mean = nn(high, spread)
    if exact:
        mean += nn((value - high.astype(F32)).astype(BF16), spread)
    return mean


def head_norm(value):
    centered = value - head_mean(value, exact=True)
    scale = lax.rsqrt(head_mean(centered * centered) + EPS)
    return centered * scale, scale


def head_norm_back(grad_hat, normed, scale):
    return scale * (grad_hat - head_mean(grad_hat) - normed * head_mean(grad_hat * normed))


def only(array, part):
    return jnp.where(lax.broadcasted_iota(jnp.int32, (1, PAIR), 1) // HD == part, array, jnp.zeros_like(array))


def side(*parts):
    return jnp.concatenate(parts, axis=1)


def whole(shape):
    return pl.BlockSpec(shape, lambda step: (0,) * len(shape))


def column(height, wide, every=1, first=0):
    return pl.BlockSpec((height, wide), lambda step: (0, step * every + first))


def shaped(shape, kind=BF16):
    return jax.ShapeDtypeStruct(shape, kind)


class Gather:
    KINDS = 7

    def __init__(self, shard, near, far, send, recv, local):
        self.shard, self.near, self.far, self.send, self.recv, self.local = shard, near, far, send, recv, local
        self.chunk, self.wide = shard.shape
        self.pieces = near.shape[1] // self.wide
        fsdp, tp = lax.axis_index("fsdp"), lax.axis_index("tp")
        size = lax.axis_size("tp")
        self.x, self.y, self.core = ({"fsdp": jnp.bitwise_xor(fsdp, bit)} for bit in (2, 4, 1))
        self.right, self.left = {"tp": lax.rem(tp + 1, size)}, {"tp": lax.rem(tp + size - 1, size)}

    def greet(self):
        barrier = pltpu.get_barrier_semaphore()
        for target in (self.x, self.y, self.core, self.left):
            pl.semaphore_signal(barrier, inc=1, device_id=target, device_id_type=MESH)
        pl.semaphore_wait(barrier, 4)

    def at(self, piece, start, count, half=None):
        first, wide = piece * self.wide, self.wide
        if half is not None:
            wide //= 2
            first += half * wide
        return self.near.at[pl.ds(start * self.chunk, count * self.chunk), pl.ds(first, wide)]

    def copy(self, piece, kind, source, target, device):
        return pltpu.make_async_remote_copy(
            src_ref=source, dst_ref=target, send_sem=self.send.at[piece, kind], recv_sem=self.recv.at[piece, kind],
            device_id=device, device_id_type=MESH,
        )

    def copies(self, piece, stage):
        if stage == "z":
            source = self.shard if piece == 0 else self.at(piece, 0, 1)
            return [self.copy(piece, 0, source, self.at(piece + 1, 0, 1), self.right)]
        if stage == "first":
            half = self.wide // 2
            left = self.shard.at[:, pl.ds(0, half)] if piece == 0 else self.at(piece, 0, 1, 0)
            right = self.shard.at[:, pl.ds(half, half)] if piece == 0 else self.at(piece, 0, 1, 1)
            return [
                self.copy(piece, 1, left, self.at(piece, 1, 1, 0), self.x),
                self.copy(piece, 2, right, self.at(piece, 2, 1, 1), self.y),
            ]
        if stage == "second":
            return [
                self.copy(piece, 3, self.at(piece, 0, 2, 0), self.at(piece, 2, 2, 0), self.y),
                self.copy(piece, 4, self.at(piece, 0, 1, 1), self.at(piece, 1, 1, 1), self.x),
                self.copy(piece, 5, self.at(piece, 2, 1, 1), self.at(piece, 3, 1, 1), self.x),
            ]
        span = pl.ds(piece * self.wide, self.wide)
        return [self.copy(piece, 6, self.near.at[:, span], self.far.at[:, span], self.core)]

    def start(self, piece, stage):
        for copy in self.copies(piece, stage):
            copy.start()

    def arrived(self, piece, stage):
        for copy in self.copies(piece, stage):
            copy.wait_recv()

    def run(self, event):
        name, piece = event
        if name == "begin":
            self.greet()
            own = pltpu.make_async_copy(self.shard, self.at(0, 0, 1), self.local)
            own.start()
            self.start(0, "z")
            self.start(0, "first")
            own.wait()
        elif name == "A":
            self.arrived(piece - 1, "z")
            if piece + 1 < self.pieces:
                self.start(piece, "z")
            self.start(piece, "first")
        elif name == "B":
            self.arrived(piece, "first")
            self.start(piece, "second")
        elif name == "C":
            self.arrived(piece, "second")
            self.start(piece, "core")
        else:
            for piece in range(self.pieces):
                self.arrived(piece, "core")
                for stage in ("z", "first", "second", "core"):
                    if stage != "z" or piece + 1 < self.pieces:
                        for copy in self.copies(piece, stage):
                            copy.wait_send()


def gather_events(pieces):
    order = [("begin", 0)]
    for piece in range(pieces):
        if piece:
            order.append(("A", piece))
        if piece > 1:
            order.append(("C", piece - 2))
        if piece:
            order.append(("B", piece - 1))
    order += [("C", pieces - 2), ("B", pieces - 1), ("C", pieces - 1), ("end", 0)]
    return order


def spaced(events, counts):
    table = []
    for count in counts:
        table.append(events[:count])
        events = events[count:]
    return table + [events]


def gather_specs(shard, pieces, halved):
    chunk, wide = shard.shape
    full = shaped((halved, pieces * wide))
    semaphores = pltpu.SemaphoreType.DMA((pieces, Gather.KINDS))
    return [whole((chunk, wide))], [full, full], [semaphores, semaphores, pltpu.SemaphoreType.DMA]


def gather_kernel(shard_ref, near_ref, far_ref, send, recv, local):
    gather = Gather(shard_ref, near_ref, far_ref, send, recv, local)
    for event in gather_events(gather.pieces):
        gather.run(event)


def params(collective=None):
    if collective is None:
        return pltpu.CompilerParams()
    return pltpu.CompilerParams(collective_id=collective, has_side_effects=True)


def gather_alone(shard, pieces, halved, collective):
    operands, results, scratch = gather_specs(shard, pieces, halved)
    return pl.pallas_call(
        gather_kernel,
        grid=(1,),
        in_specs=operands,
        out_specs=[ANY] * 2,
        out_shape=results,
        scratch_shapes=scratch,
        compiler_params=params(collective),
        name="gather_block",
    )(shard)


def halo_kernel(a_ref, out_ref, send, recv):
    rows = a_ref.shape[0]
    spill = REACH - rows
    place, size = lax.axis_index("tp"), lax.axis_size("tp")
    out_ref[REACH : REACH + rows, :] = a_ref[...]
    moves = [
        (1, pl.ds(0, rows), pl.ds(spill, rows)),
        (-1, pl.ds(0, rows), pl.ds(REACH + rows, rows)),
        (2, pl.ds(rows - spill, spill), pl.ds(0, spill)),
        (-2, pl.ds(0, spill), pl.ds(REACH + 2 * rows, spill)),
    ]
    barrier = pltpu.get_barrier_semaphore()
    inside = lambda other: jnp.logical_and(other >= 0, other < size)
    for distance, _, _ in moves:

        @pl.when(inside(place + distance))
        def _():
            pl.semaphore_signal(barrier, inc=1, device_id={"tp": place + distance}, device_id_type=MESH)

    pl.semaphore_wait(barrier, jnp.minimum(place, 2) + jnp.minimum(size - 1 - place, 2))

    def copy(index):
        distance, source, target = moves[index]
        return pltpu.make_async_remote_copy(
            src_ref=a_ref.at[source, :], dst_ref=out_ref.at[target, :], send_sem=send.at[index], recv_sem=recv.at[index],
            device_id={"tp": place + distance}, device_id_type=MESH,
        )

    for index, (distance, _, _) in enumerate(moves):

        @pl.when(inside(place + distance))
        def _():
            copy(index).start()

        @pl.when(jnp.logical_not(inside(place - distance)))
        def _():
            target = moves[index][2]
            out_ref[target, :] = jnp.zeros((target.size, out_ref.shape[1]), BF16)

    for index, (distance, _, _) in enumerate(moves):

        @pl.when(inside(place + distance))
        def _():
            copy(index).wait_send()

        @pl.when(inside(place - distance))
        def _():
            copy(index).wait_recv()


def halo(a_own, collective):
    rows, width = a_own.shape
    return pl.pallas_call(
        halo_kernel,
        grid=(1,),
        in_specs=[whole((rows, width))],
        out_specs=whole((rows + 2 * REACH, width)),
        out_shape=shaped((rows + 2 * REACH, width)),
        scratch_shapes=[pltpu.SemaphoreType.DMA((4,)), pltpu.SemaphoreType.DMA((4,))],
        compiler_params=params(collective),
        name="halo",
    )(a_own)


class Rows:
    def __init__(self, layers, grid):
        self.layers, self.grid = layers, grid

    def ln_gain(self, layer, which):
        return 2 * self.grid + 2 * layer + which

    def ln_bias(self, layer, which):
        return 2 * self.grid + 2 * self.layers + 2 * layer + which

    def out_bias(self, layer):
        return 2 * self.grid + 4 * self.layers + layer

    def last_bias(self, layer):
        return 2 * self.grid + 5 * self.layers + layer

    def proj_bias(self, layer, which):
        return 3 * layer + which

    def head_gain(self, layer, which):
        return 3 * self.layers + 2 * layer + which

    def head_bias(self, layer):
        return 5 * self.layers + layer


def line(ref, row, start=0, wide=None):
    return ref[row : row + 1, start : start + (wide or ref.shape[1] - start)]


def hooked(gather, table, slots):
    step = pl.program_id(0)

    def at(slot):
        if gather is None:
            return
        for index in range(slot, len(table) - 1, slots):
            if table[index]:

                @pl.when(step == index // slots)
                def _(events=table[index]):
                    for event in events:
                        gather.run(event)

    def after():
        if gather is None:
            return

        @pl.when(step == pl.num_programs(0) - 1)
        def _():
            for event in table[-1]:
                gather.run(event)

    return at, after


def attend_kernel(*refs, rows_of, layer, table):
    a_ref, near_ref, far_ref, heads_ref, feats_ref, x_ref, seg_k_ref, seg_q_ref = refs[:8]
    rest = refs[8:]
    gather = None
    if table:
        gather = Gather(rest[0], *rest[11:13], *rest[-3:])
        rest = rest[1:11] + rest[13:-3]
    q_ref, kv_ref, q_hat_ref, k_hat_ref, q_scale_ref, k_scale_ref, p_ref, o_ref, mid_ref, m_ref = rest[:10]
    mask_ref, acc_ref = rest[10:]
    rows = q_ref.shape[0]
    half = near_ref.shape[0]
    step = pl.program_id(0)
    at, after = hooked(gather, table, 2)
    at(0)

    @pl.when(step == 0)
    def _():
        mask_ref[...] = jnp.where(seg_k_ref[...] == seg_q_ref[...], 0.0, FILL)
        acc_ref[...] = jnp.zeros_like(acc_ref)

    tile = lambda row, which: line(heads_ref, row, which * PAIR, PAIR)
    bias = [rows_of.proj_bias(layer, which) for which in range(3)]
    q_gain, k_gain = (rows_of.head_gain(layer, which) for which in range(2))
    q_shift = rows_of.head_bias(layer)
    near, distant = halves(a_ref[...])
    own, own_far = halves(a_ref[REACH : REACH + rows, :])
    kv = nn(near, near_ref[:, PAIR : 4 * PAIR]) + nn(distant, far_ref[:, PAIR : 4 * PAIR])
    kv += side(tile(bias[1], 0), tile(bias[2], 0), tile(bias[1], 1) + tile(bias[2], 2))
    q = side(
        nn(own, near_ref[:, :PAIR]) + nn(own_far, far_ref[:, :PAIR]),
        nn(own, near_ref[:, 4 * PAIR : 5 * PAIR]) + nn(own_far, far_ref[:, 4 * PAIR : 5 * PAIR]),
    ) + line(heads_ref, bias[0], 0, 2 * PAIR)
    q_hat, q_scale = head_norm(q)
    k_hat, k_scale = head_norm(side(kv[:, :PAIR], kv[:, 2 * PAIR :]))
    qn = (q_hat * line(heads_ref, q_gain, 0, 2 * PAIR) + line(heads_ref, q_shift, 0, 2 * PAIR)).astype(BF16)
    qn = side(qn[:, :PAIR], only(qn[:, PAIR:], 0))
    kn = (k_hat * line(heads_ref, k_gain, 0, 2 * PAIR)).astype(BF16)
    v = kv[:, PAIR:].astype(BF16)
    low = lax.broadcasted_iota(jnp.int32, (1, PAIR), 1) < HD
    first, second = kn[:, :PAIR], jnp.where(low, kn[:, PAIR:], v[:, PAIR:])
    values = v[:, :PAIR]
    q_ref[...] = qn
    kv_ref[...] = side(first, values, second)
    q_hat_ref[...] = q_hat.astype(BF16)
    k_hat_ref[...] = k_hat.astype(BF16)
    q_scale_ref[...] = q_scale.astype(BF16)
    k_scale_ref[...] = k_scale.astype(BF16)
    at(1)
    values_t, second_t = values.T, second.T
    mixed = []
    for head in range(3):
        keys = (first, first, second)[head]
        query = only(qn[:, PAIR * (head // 2) : PAIR * (head // 2 + 1)] * HD ** (-0.5), head % 2).astype(BF16)
        scores = nt(keys, query) + mask_ref[...]
        weights = jnp.exp(scores - jnp.max(scores, axis=0, keepdims=True))
        total = jnp.sum(weights, axis=0, keepdims=True)
        probs = (weights * (1.0 / total)).astype(BF16)
        p_ref[head] = probs
        mixed.append(nn((values_t[:HD], values_t[HD:], second_t[HD:])[head], probs))
    o = jnp.concatenate([jnp.zeros_like(mixed[2]), mixed[2], mixed[0], mixed[1]], axis=0).T.astype(BF16)
    o_ref[...] = o
    acc_ref[:, :half] += nt(o, near_ref[:, 4 * PAIR :])
    acc_ref[:, half:] += nt(o, far_ref[:, 4 * PAIR :])

    @pl.when(step == pl.num_programs(0) - 1)
    def _():
        mid = x_ref[...] + (acc_ref[...] + line(feats_ref, rows_of.out_bias(layer)))
        mid_ref[...] = mid
        hat, _ = row_norm(mid)
        m_ref[...] = (
            hat * line(feats_ref, rows_of.ln_gain(layer, 1)) + line(feats_ref, rows_of.ln_bias(layer, 1))
        ).astype(BF16)

    after()


def attend(a_win, near, far, heads, feats, x, seg_k, seg_q, rows_of, layer, shard=None, collective=None):
    window, width = a_win.shape
    rows = x.shape[0]
    half = width // 2
    pieces = near.shape[1] // (6 * PAIR)
    extra = gather_specs(shard, pieces, half) if shard is not None else ([], [], [])
    table = spaced(gather_events(pieces), [1, 0, 1, 1, 1, 1, 1, 2]) if shard is not None else None
    outs = [(rows, 2 * PAIR), (window, 3 * PAIR), (rows, 2 * PAIR), (window, 2 * PAIR), (rows, 2 * PAIR), (window, 2 * PAIR)]
    return pl.pallas_call(
        functools.partial(attend_kernel, rows_of=rows_of, layer=layer, table=table),
        grid=(pieces,),
        in_specs=[
            whole((window, width)), column(half, 6 * PAIR), column(half, 6 * PAIR), column(heads.shape[0], 3 * PAIR),
            whole(feats.shape), whole((rows, width)), whole((window, 1)), whole((1, rows)), *extra[0],
        ],
        out_specs=[column(*shape) for shape in outs]
        + [pl.BlockSpec((3, window, rows), lambda step: (step, 0, 0)), column(rows, 2 * PAIR)]
        + [whole((rows, width))] * 2 + [ANY] * len(extra[1]),
        out_shape=[shaped((height, pieces * wide)) for height, wide in outs]
        + [shaped((3 * pieces, window, rows)), shaped((rows, pieces * 2 * PAIR)), shaped((rows, width), F32), shaped((rows, width))]
        + extra[1],
        scratch_shapes=[pltpu.VMEM((window, rows), F32), pltpu.VMEM((rows, width), F32), *extra[2]],
        compiler_params=params(collective),
        cost_estimate=pl.CostEstimate(
            flops=2 * window * width * width * 2 + 8 * window * rows * width * 4,
            bytes_accessed=20 * window * width,
            transcendentals=3 * pieces * window * rows,
        ),
        name="attend",
    )(a_win, near, far, heads, feats, x, seg_k, seg_q, *([] if shard is None else [shard]))


def mlp_kernel(*refs, rows_of, layer, table):
    m_ref, mid_ref, up_near_ref, up_far_ref, down_near_ref, down_far_ref, up_shift_ref, feats_ref = refs[:8]
    rest = refs[8:]
    gather = None
    if table:
        gather = Gather(rest[0], *rest[5:7], *rest[-3:])
        rest = rest[1:5] + rest[7:-3]
    act_ref, slope_ref, x2_ref, a_ref, acc_ref = rest
    half = up_near_ref.shape[0]
    step = pl.program_id(0)
    at, after = hooked(gather, table, 2)
    at(0)

    @pl.when(step == 0)
    def _():
        acc_ref[...] = jnp.zeros_like(acc_ref)

    near, distant = halves(m_ref[...])
    hidden = nn(near, up_near_ref[...]) + nn(distant, up_far_ref[...]) + up_shift_ref[...]
    at(1)
    phi = 0.5 * (1.0 + lax.erf(hidden * ROOT_HALF))
    act = (hidden * phi).astype(BF16)
    act_ref[...] = act
    slope_ref[...] = (phi + hidden * jnp.exp(-0.5 * hidden * hidden) * INV_ROOT_TWO_PI).astype(BF16)
    acc_ref[:, :half] += nt(act, down_near_ref[...])
    acc_ref[:, half:] += nt(act, down_far_ref[...])

    @pl.when(step == pl.num_programs(0) - 1)
    def _():
        x2 = mid_ref[...] + (acc_ref[...] + line(feats_ref, rows_of.last_bias(layer)))
        x2_ref[...] = x2
        hat, _ = row_norm(x2)
        after = min(layer + 1, rows_of.layers - 1)
        a_ref[...] = (
            hat * line(feats_ref, rows_of.ln_gain(after, 0)) + line(feats_ref, rows_of.ln_bias(after, 0))
        ).astype(BF16)

    after()


def mlp(m, mid, near, far, up_shift, feats, rows_of, layer, shard=None, collective=None):
    rows, width = mid.shape
    half = width // 2
    hidden = up_shift.shape[1]
    pieces = lax.axis_size("tp")
    wide = hidden // pieces
    extra = gather_specs(shard, pieces, half) if shard is not None else ([], [], [])
    table = spaced(gather_events(pieces), [1, 0, 1, 1, 1, 1, 1, 2]) if shard is not None else None
    full = whole((rows, width))
    return pl.pallas_call(
        functools.partial(mlp_kernel, rows_of=rows_of, layer=layer, table=table),
        grid=(pieces,),
        in_specs=[
            full, full, column(half, wide, 2), column(half, wide, 2), column(half, wide, 2, 1), column(half, wide, 2, 1),
            column(1, wide), whole(feats.shape), *extra[0],
        ],
        out_specs=[column(rows, wide), column(rows, wide), full, full] + [ANY] * len(extra[1]),
        out_shape=[shaped((rows, hidden)), shaped((rows, hidden)), shaped((rows, width), F32), shaped((rows, width))] + extra[1],
        scratch_shapes=[pltpu.VMEM((rows, width), F32), *extra[2]],
        compiler_params=params(collective),
        cost_estimate=pl.CostEstimate(
            flops=4 * rows * width * hidden, bytes_accessed=4 * width * hidden, transcendentals=2 * rows * hidden
        ),
        name="mlp",
    )(m, mid, near, far, near, far, up_shift, feats, *([] if shard is None else [shard]))


def mlp_back_kernel(
    g_ref, down_near_ref, down_far_ref, slope_ref, up_near_ref, up_far_ref, mid_ref, feats_ref,
    gz_ref, gh_ref, up_shift_grad_ref, g1_ref, gr_ref, small_ref, acc_ref, *, gain_row,
):
    half = up_near_ref.shape[0]
    step = pl.program_id(0)

    @pl.when(step == 0)
    def _():
        gz_ref[...] = g_ref[...].astype(BF16)
        acc_ref[...] = jnp.zeros_like(acc_ref)

    near, distant = halves(gz_ref[...])
    gh = ((nn(near, down_near_ref[...]) + nn(distant, down_far_ref[...])) * slope_ref[...].astype(F32)).astype(BF16)
    gh_ref[...] = gh
    up_shift_grad_ref[...] = jnp.sum(gh.astype(F32), axis=0, keepdims=True)
    acc_ref[:, :half] += nt(gh, up_near_ref[...])
    acc_ref[:, half:] += nt(gh, up_far_ref[...])

    @pl.when(step == pl.num_programs(0) - 1)
    def _():
        gm = acc_ref[...]
        hat, scale = row_norm(mid_ref[...])
        g1 = g_ref[...] + row_norm_back(gm * line(feats_ref, gain_row), hat, scale)
        gr = g1.astype(BF16)
        g1_ref[...] = g1
        gr_ref[...] = gr
        small_ref[...] = jnp.zeros_like(small_ref)
        small_ref[0:1, :] = jnp.sum(gz_ref[...].astype(F32), axis=0, keepdims=True)
        small_ref[1:2, :] = jnp.sum(gr.astype(F32), axis=0, keepdims=True)
        small_ref[2:3, :] = jnp.sum(gm * hat, axis=0, keepdims=True)
        small_ref[3:4, :] = jnp.sum(gm, axis=0, keepdims=True)


def mlp_back(grad, near, far, slope, mid, feats, gain_row):
    rows, width = grad.shape
    half = width // 2
    hidden = slope.shape[1]
    pieces = lax.axis_size("tp")
    wide = hidden // pieces
    full = whole((rows, width))
    return pl.pallas_call(
        functools.partial(mlp_back_kernel, gain_row=gain_row),
        grid=(pieces,),
        in_specs=[
            full, column(half, wide, 2, 1), column(half, wide, 2, 1), column(rows, wide), column(half, wide, 2),
            column(half, wide, 2), full, whole(feats.shape),
        ],
        out_specs=[full, column(rows, wide), column(1, wide), full, full, whole((8, width))],
        out_shape=[
            shaped((rows, width)), shaped((rows, hidden)), shaped((1, hidden), F32), shaped((rows, width), F32),
            shaped((rows, width)), shaped((8, width), F32),
        ],
        scratch_shapes=[pltpu.VMEM((rows, width), F32)],
        cost_estimate=pl.CostEstimate(
            flops=4 * rows * width * hidden, bytes_accessed=4 * width * hidden, transcendentals=0
        ),
        name="mlp_back",
    )(grad, near, far, slope, near, far, mid, feats)


def attend_back_kernel(
    gr_ref, q_ref, kv_ref, q_hat_ref, k_hat_ref, q_scale_ref, k_scale_ref, p_ref, near_ref, far_ref, heads_ref,
    gq_ref, gkv_ref, mine_ref, left_ref, right_ref, small_ref, acc_ref, *, rows_of, layer,
):
    rows = gr_ref.shape[0]
    half = near_ref.shape[0]
    step = pl.program_id(0)

    @pl.when(step == 0)
    def _():
        acc_ref[...] = jnp.zeros_like(acc_ref)

    near, distant = halves(gr_ref[...])
    go = (nn(near, near_ref[:, 4 * PAIR :]) + nn(distant, far_ref[:, 4 * PAIR :])).astype(BF16)
    qn, kv = q_ref[...], kv_ref[...]
    first, values, second = kv[:, :PAIR], kv[:, PAIR : 2 * PAIR], kv[:, 2 * PAIR :]
    first_t, second_t = first.T, second.T
    grad_q, grad_k, grad_v = [], [], []
    for head in range(3):
        go_head = only(go[:, PAIR:], head) if head < 2 else only(go[:, :PAIR], 1)
        query = only(qn[:, PAIR * (head // 2) : PAIR * (head // 2 + 1)] * HD ** (-0.5), head % 2).astype(BF16)
        stored = p_ref[head]
        probs = stored.astype(F32)
        grad_probs = nt((values, values, second)[head], go_head)
        delta = jnp.sum(probs * grad_probs, axis=0, keepdims=True)
        grad_scores = (probs * (grad_probs - delta)).astype(BF16)
        grad_v.append(nn(stored, go_head))
        grad_k.append(nn(grad_scores, query))
        grad_q.append(nn((first_t[:HD], first_t[HD:], second_t[:HD])[head], grad_scores))
    zero = jnp.zeros_like(grad_q[2])
    grad_q = (jnp.concatenate(grad_q + [zero], axis=0) * HD ** (-0.5)).T
    grad_k = side(grad_k[0] + grad_k[1], grad_k[2])
    pair_v, last_v = grad_v[0] + grad_v[1], grad_v[2]
    q_hat = q_hat_ref[...].astype(F32)
    k_hat = k_hat_ref[...].astype(F32)
    gain = lambda which: line(heads_ref, rows_of.head_gain(layer, which), 0, 2 * PAIR)
    gq = head_norm_back(grad_q * gain(0), q_hat, q_scale_ref[...].astype(F32)).astype(BF16)
    gk = head_norm_back(grad_k * gain(1), k_hat, k_scale_ref[...].astype(F32)).astype(BF16)
    gkv = side(gk[:, :PAIR], pair_v.astype(BF16), gk[:, PAIR:] + last_v.astype(BF16))
    gq_ref[...] = gq
    gkv_ref[...] = gkv
    total = lambda value: jnp.sum(value.astype(F32), axis=0, keepdims=True)
    small_ref[...] = jnp.zeros_like(small_ref)
    small_ref[0:1, : 2 * PAIR] = total(grad_q * q_hat)
    small_ref[1:2, : 2 * PAIR] = total(grad_k * k_hat)
    small_ref[2:3, : 2 * PAIR] = total(grad_q)
    small_ref[3:4, : 2 * PAIR] = total(gq)
    small_ref[4:5, : 2 * PAIR] = total(gk)
    small_ref[5:6, :PAIR] = total(pair_v.astype(BF16))
    small_ref[5:6, 2 * PAIR :] = total(last_v.astype(BF16))
    acc_ref[:, :half] += nt(gkv, near_ref[:, PAIR : 4 * PAIR])
    acc_ref[:, half:] += nt(gkv, far_ref[:, PAIR : 4 * PAIR])
    own = slice(REACH, REACH + rows)
    for ref, cols in ((near_ref, slice(0, half)), (far_ref, slice(half, 2 * half))):
        acc_ref[own, cols] += nt(gq[:, :PAIR], ref[:, :PAIR]) + nt(gq[:, PAIR:], ref[:, 4 * PAIR : 5 * PAIR])

    @pl.when(step == pl.num_programs(0) - 1)
    def _():
        left_ref[...] = acc_ref[:REACH, :].astype(BF16)
        mine_ref[...] = acc_ref[own, :]
        right_ref[...] = acc_ref[REACH + rows :, :].astype(BF16)


def attend_back(gr, stored, near, far, heads, rows_of, layer):
    rows, width = gr.shape
    half = width // 2
    window = rows + 2 * REACH
    pieces = near.shape[1] // (6 * PAIR)
    full = whole((rows, width))
    return pl.pallas_call(
        functools.partial(attend_back_kernel, rows_of=rows_of, layer=layer),
        grid=(pieces,),
        in_specs=[
            full, column(rows, 2 * PAIR), column(window, 3 * PAIR), column(rows, 2 * PAIR), column(window, 2 * PAIR),
            column(rows, 2 * PAIR), column(window, 2 * PAIR), pl.BlockSpec((3, window, rows), lambda step: (step, 0, 0)),
            column(half, 6 * PAIR), column(half, 6 * PAIR), column(heads.shape[0], 3 * PAIR),
        ],
        out_specs=[
            column(rows, 2 * PAIR), column(window, 3 * PAIR), full, whole((REACH, width)), whole((REACH, width)),
            column(8, 3 * PAIR),
        ],
        out_shape=[
            shaped((rows, pieces * 2 * PAIR)), shaped((window, pieces * 3 * PAIR)), shaped((rows, width), F32),
            shaped((REACH, width)), shaped((REACH, width)), shaped((8, pieces * 3 * PAIR), F32),
        ],
        scratch_shapes=[pltpu.VMEM((window, width), F32)],
        cost_estimate=pl.CostEstimate(
            flops=2 * window * width * width * 2 + 20 * window * rows * width * 2,
            bytes_accessed=20 * window * width,
            transcendentals=0,
        ),
        name="attend_back",
    )(gr, *stored, near, far, heads)


def attn_weight_kernel(a_ref, gq_ref, gkv_ref, gr_ref, o_ref, keep_ref, send_ref, a_t_ref, gr_t_ref):
    rows = gq_ref.shape[0]
    half = keep_ref.shape[0]

    @pl.when(pl.program_id(0) == 0)
    def _():
        a_t_ref[...] = a_ref[...].T
        gr_t_ref[...] = gr_ref[...].T

    for part, ref in ((slice(0, half), keep_ref), (slice(half, 2 * half), send_ref)):
        from_q = nn(a_t_ref[part, REACH : REACH + rows], gq_ref[...])
        from_o = nn(gr_t_ref[part, :], o_ref[...])
        ref[:, :PAIR] = from_q[:, :PAIR].astype(BF16)
        ref[:, PAIR : 4 * PAIR] = nn(a_t_ref[part, :], gkv_ref[...]).astype(BF16)
        ref[:, 4 * PAIR : 5 * PAIR] = (from_q[:, PAIR:] + from_o[:, :PAIR]).astype(BF16)
        ref[:, 5 * PAIR :] = from_o[:, PAIR:].astype(BF16)


def attn_weight_grads(a_win, gq, gkv, gr, o):
    window, width = a_win.shape
    rows = gr.shape[0]
    half = width // 2
    pieces = gq.shape[1] // (2 * PAIR)
    out = column(half, 6 * PAIR)
    return pl.pallas_call(
        attn_weight_kernel,
        grid=(pieces,),
        in_specs=[
            whole((window, width)), column(rows, 2 * PAIR), column(window, 3 * PAIR), whole((rows, width)),
            column(rows, 2 * PAIR),
        ],
        out_specs=[out, out],
        out_shape=[shaped((half, pieces * 6 * PAIR))] * 2,
        scratch_shapes=[pltpu.VMEM((width, window), BF16), pltpu.VMEM((width, rows), BF16)],
        cost_estimate=pl.CostEstimate(
            flops=2 * width * width * (2 * window + 2 * rows), bytes_accessed=8 * width * width, transcendentals=0
        ),
        name="attn_weight_grads",
    )(a_win, gq, gkv, gr, o)


def mlp_weight_kernel(m_ref, gh_ref, gz_ref, act_ref, keep_ref, send_ref, m_t_ref, gz_t_ref):
    half = keep_ref.shape[0]
    wide = gh_ref.shape[1]

    @pl.when(pl.program_id(0) == 0)
    def _():
        m_t_ref[...] = m_ref[...].T
        gz_t_ref[...] = gz_ref[...].T

    for part, ref in ((slice(0, half), keep_ref), (slice(half, 2 * half), send_ref)):
        ref[:, :wide] = nn(m_t_ref[part, :], gh_ref[...]).astype(BF16)
        ref[:, wide:] = nn(gz_t_ref[part, :], act_ref[...]).astype(BF16)


def mlp_weight_grads(m, gh, gz, act):
    rows, width = m.shape
    half = width // 2
    hidden = gh.shape[1]
    pieces = lax.axis_size("tp")
    wide = hidden // pieces
    out = column(half, 2 * wide)
    return pl.pallas_call(
        mlp_weight_kernel,
        grid=(pieces,),
        in_specs=[whole((rows, width)), column(rows, wide), whole((rows, width)), column(rows, wide)],
        out_specs=[out, out],
        out_shape=[shaped((half, 2 * hidden))] * 2,
        scratch_shapes=[pltpu.VMEM((width, rows), BF16), pltpu.VMEM((width, rows), BF16)],
        cost_estimate=pl.CostEstimate(
            flops=4 * width * hidden * rows, bytes_accessed=4 * width * hidden, transcendentals=0
        ),
        name="mlp_weight_grads",
    )(m, gh, gz, act)


def flip(array, bit, axis="fsdp"):
    size = lax.axis_size(axis)
    return lax.ppermute(array, axis, [(i, i ^ (1 << bit)) for i in range(size)])


def ring(array):
    size = lax.axis_size("tp")
    return lax.ppermute(array, "tp", [(i, (i + 1) % size) for i in range(size)])


def hop(array, distance):
    size = lax.axis_size("tp")
    return lax.ppermute(array, "tp", [(i, i + distance) for i in range(size) if 0 <= i + distance < size])


def bits_of(size):
    return size.bit_length() - 1


def row_bits(first_top):
    count = bits_of(lax.axis_size("fsdp"))
    tops = [count - 1, count - 2] if first_top else [count - 2, count - 1]
    return list(range(1, count - 2)), tops


def gather_by_permutes(block, first_top):
    pieces = [block]
    for _ in range(lax.axis_size("tp") - 1):
        pieces.append(ring(pieces[-1]))
    block = jnp.concatenate(pieces, axis=1)
    low, tops = row_bits(first_top)
    have = []
    for bit in low + tops:
        axis = sum(other > bit for other in have)
        block = jnp.stack([block, flip(block, bit)], axis=axis)
        have.append(bit)
    block = block.reshape((-1, block.shape[-1]))
    return block, flip(block, 0)


def add(left, right, kind=BF16):
    return (left.astype(F32) + right.astype(F32)).astype(kind)


def reduce_by_permutes(keep, send, first_top):
    low, tops = row_bits(first_top)
    block = add(keep, flip(send, 0))
    order = tops + low[::-1]
    have = sorted(order, reverse=True)
    block = block.reshape((2,) * len(have) + (-1, block.shape[-1]))
    for bit in order:
        axis = have.index(bit)
        mine = lax.index_in_dim(block, 0, axis, keepdims=False)
        other = lax.index_in_dim(block, 1, axis, keepdims=False)
        block = add(mine, flip(other, bit))
        have.remove(bit)
    pieces = jnp.split(block, lax.axis_size("tp"), axis=1)
    total = pieces[1]
    for piece in pieces[2:]:
        total = add(ring(total), piece)
    return add(ring(total), pieces[0], F32)


def attn_shard(w_qkv, w_out):
    q, k, v = (w_qkv[:, which] for which in range(3))
    o = w_out.T
    return side(q[:, :PAIR], k[:, :PAIR], v[:, :PAIR], k[:, PAIR:], v[:, PAIR:], q[:, PAIR:], o[:, PAIR:], o[:, :PAIR])


def attn_unshard(block):
    tile = lambda start, wide=PAIR: block[:, start : start + wide]
    q = side(tile(0), tile(4 * PAIR, HD))
    k = side(tile(PAIR), tile(3 * PAIR, HD))
    v = side(tile(2 * PAIR), tile(3 * PAIR + HD, HD))
    o = side(tile(5 * PAIR), tile(4 * PAIR + HD, HD))
    return jnp.stack([q, k, v], axis=1), o.T


def body(
    tokens, segment_ids, patch_pos, row_table, col_table, ln_gain, ln_bias, qkv_bias, qk_gain, query_bias, out_bias,
    fc1_bias, fc2_bias, w_qkv, w_out, w_fc1, w_fc2, cotangent,
):
    layers = w_qkv.shape[0]
    rows, width = tokens.shape
    half = width // 2
    fsdp, tp = lax.axis_size("fsdp"), lax.axis_size("tp")
    f_index, t_index = lax.axis_index("fsdp"), lax.axis_index("tp")
    hidden = fc1_bias.shape[1] * fsdp * tp
    grid = row_table.shape[0]
    fine = width // (fsdp * tp)
    parts = hidden // width
    in_kernel = fsdp == 8
    rows_of = Rows(layers, grid)

    place = jnp.arange(width, dtype=jnp.int32)
    chunk = width // fsdp
    slot = place // chunk
    away = (slot % (fsdp // 2)) * 2 + slot // (fsdp // 2)
    feature_at = (f_index ^ away) * chunk + place % chunk
    head_cols = width // tp
    spot = jnp.arange(tp * 3 * PAIR, dtype=jnp.int32)
    tile, part = spot % (3 * PAIR) // PAIR, spot % PAIR // HD
    head = jnp.where(tile == 0, part, jnp.where(tile == part + 1, 2, -fsdp * tp))
    head_at = ((t_index - spot // (3 * PAIR)) % tp) * head_cols + head * HD + spot % HD
    far = place // fine
    arrived_at = ((f_index ^ (far // tp)) * tp + (t_index ^ (far % tp))) * fine + place % fine
    to_feature = (arrived_at[:, None] == feature_at[None, :]).astype(BF16)
    to_head = (arrived_at[:, None] == head_at[None, :]).astype(BF16)
    reorder = (place[:, None] == feature_at[None, :]).astype(BF16)
    device = jnp.arange(fsdp * tp, dtype=jnp.int32)
    device_at = (f_index ^ (device // tp)) * tp + (t_index ^ (device % tp))
    wanted = ((t_index - device // fsdp) % tp) * fsdp + device % fsdp
    to_hidden = (wanted[:, None] == device_at[None, :]).astype(BF16)

    shares = [row_table, col_table] + [
        item.reshape(-1, fine) for item in (ln_gain, ln_bias, out_bias, fc2_bias, qkv_bias, qk_gain, query_bias)
    ]
    small = jnp.concatenate(shares + [fc1_bias.reshape(layers * parts, fine)], axis=0)
    count = small.shape[0]
    flat = small.reshape(1, -1)
    for bit in range(bits_of(tp)):
        flat = jnp.concatenate([flat, flip(flat, bit, "tp")], axis=0)
    for bit in range(bits_of(fsdp)):
        flat = jnp.concatenate([flat, flip(flat, bit)], axis=0)
    gathered = flat.reshape(fsdp * tp, count, fine)
    lined = gathered.transpose(1, 0, 2).reshape(count, width)
    wide = 2 * grid + 6 * layers
    feats = jnp.dot(lined[:wide], to_feature, preferred_element_type=F32)
    heads = jnp.dot(lined[wide : wide + 6 * layers], to_head, preferred_element_type=F32)
    up_shift = jnp.einsum(
        "or,rlsi->losi",
        to_hidden,
        gathered[:, wide + 6 * layers :].reshape(fsdp * tp, layers, parts, fine),
        preferred_element_type=F32,
    ).reshape(layers, 1, hidden)

    attn_shards = [attn_shard(w_qkv[layer], w_out[layer]) for layer in range(layers)]
    mlp_shards = [side(w_fc1[layer], w_fc2[layer].T) for layer in range(layers)]
    if in_kernel:
        attn_near, attn_far = gather_alone(attn_shards[0], tp, half, 0)

    grid_ids = jnp.arange(grid, dtype=jnp.int32)
    row_hot = patch_pos[0][:, None] == grid_ids[None, :]
    col_hot = patch_pos[1][:, None] == grid_ids[None, :]
    residual = (
        jnp.dot(tokens, reorder, preferred_element_type=F32)
        + jnp.dot(row_hot.astype(BF16), feats[:grid].astype(BF16), preferred_element_type=F32)
        + jnp.dot(col_hot.astype(BF16), feats[grid : 2 * grid].astype(BF16), preferred_element_type=F32)
    )
    segments = segment_ids[0]
    padded = jnp.pad(segments, (REACH, REACH), constant_values=-1)
    seg_k = lax.dynamic_slice_in_dim(padded, t_index * rows, rows + 2 * REACH).reshape(-1, 1)
    seg_q = lax.dynamic_slice_in_dim(segments, t_index * rows, rows).reshape(1, -1)
    spill = REACH - rows

    hat, _ = row_norm(residual)
    a_own = (hat * feats[rows_of.ln_gain(0, 0)] + feats[rows_of.ln_bias(0, 0)]).astype(BF16)
    saved, weights = [], []
    for layer in range(layers):
        if in_kernel:
            a_win = halo(a_own, 10 + layer)
            *kept, mid, m, mlp_near, mlp_far = attend(
                a_win, attn_near, attn_far, heads, feats, residual, seg_k, seg_q, rows_of, layer, mlp_shards[layer],
                20 + layer,
            )
        else:
            a_win = jnp.concatenate(
                [hop(a_own[rows - spill :], 2), hop(a_own, 1), a_own, hop(a_own, -1), hop(a_own[:spill], -2)], axis=0
            )
            attn_near, attn_far = gather_by_permutes(attn_shards[layer], layer % 2 == 0)
            *kept, mid, m = attend(a_win, attn_near, attn_far, heads, feats, residual, seg_k, seg_q, rows_of, layer)
            mlp_near, mlp_far = gather_by_permutes(mlp_shards[layer], layer % 2 == 1)
        weights.append((attn_near, attn_far, mlp_near, mlp_far))
        if in_kernel and layer + 1 < layers:
            act, slope, x2, a_own, attn_near, attn_far = mlp(
                m, mid, mlp_near, mlp_far, up_shift[layer], feats, rows_of, layer, attn_shards[layer + 1], 30 + layer
            )
        else:
            act, slope, x2, a_own = mlp(m, mid, mlp_near, mlp_far, up_shift[layer], feats, rows_of, layer)
        saved.append((residual, a_win, kept, mid, m, act, slope))
        residual = x2

    restore = functools.partial(
        lax.dot_general, dimension_numbers=(((1,), (1,)), ((), ())), precision=HIGHEST, preferred_element_type=F32
    )
    exact = reorder.astype(F32)
    activations = restore(residual, exact)
    grad = jnp.dot(cotangent, exact, precision=HIGHEST, preferred_element_type=F32)
    kept_sums = [None] * layers
    w_qkv_grad, w_out_grad, w_fc1_grad, w_fc2_grad = ([None] * layers for _ in range(4))
    for layer in reversed(range(layers)):
        attn_near, attn_far, mlp_near, mlp_far = weights[layer]
        x, a_win, kept, mid, m, act, slope = saved[layer]
        *stored, o = kept
        gz, gh, up_grad, g1, gr, mlp_small = mlp_back(
            grad, mlp_near, mlp_far, slope, mid, feats, rows_of.ln_gain(layer, 1)
        )
        keep, send = mlp_weight_grads(m, gh, gz, act)
        block = reduce_by_permutes(keep, send, layer % 2 == 0)
        middle = block.shape[1] // 2
        w_fc1_grad[layer], w_fc2_grad[layer] = block[:, :middle], block[:, middle:].T
        gq, gkv, mine, left, right, attn_small = attend_back(gr, stored, attn_near, attn_far, heads, rows_of, layer)
        keep, send = attn_weight_grads(a_win, gq, gkv, gr, o)
        w_qkv_grad[layer], w_out_grad[layer] = attn_unshard(reduce_by_permutes(keep, send, layer % 2 == 1))
        ends = jnp.concatenate([hop(right[rows:], 2), hop(left[:spill], -2)], axis=0).astype(F32)
        attn_grad = mine + hop(right[:rows], 1).astype(F32) + hop(left[spill:], -1).astype(F32) + ends
        hat, scale = row_norm(x)
        grad = g1 + row_norm_back(attn_grad * feats[rows_of.ln_gain(layer, 0)], hat, scale)
        kept_sums[layer] = (
            jnp.sum(attn_grad * hat, axis=0), jnp.sum(attn_grad, axis=0), mlp_small, attn_small,
            up_grad.reshape(parts, width),
        )

    token_grad = restore(grad, exact)
    row_grad = jnp.einsum("tg,td->gd", row_hot.astype(F32), grad, precision=HIGHEST)
    col_grad = jnp.einsum("tg,td->gd", col_hot.astype(F32), grad, precision=HIGHEST)
    featured = [row_grad, col_grad]
    featured.append(jnp.stack([item for a_gain, _, sums, _, _ in kept_sums for item in (a_gain, sums[2])]))
    featured.append(jnp.stack([item for _, a_shift, sums, _, _ in kept_sums for item in (a_shift, sums[3])]))
    featured.append(jnp.stack([sums[1] for _, _, sums, _, _ in kept_sums]))
    featured.append(jnp.stack([sums[0] for _, _, sums, _, _ in kept_sums]))
    headed = jnp.concatenate(
        [sums[3:6] for _, _, _, sums, _ in kept_sums]
        + [sums[0:2] for _, _, _, sums, _ in kept_sums]
        + [sums[2:3] for _, _, _, sums, _ in kept_sums]
    )
    spread = jnp.concatenate(
        [restore(jnp.concatenate(featured), to_feature.astype(F32)), restore(headed, to_head.astype(F32))]
    )
    spread = spread.reshape(-1, fsdp * tp, fine).transpose(1, 0, 2)
    up_all = jnp.stack([item[4] for item in kept_sums]).reshape(layers, fsdp * tp, parts * fine)
    up_all = jnp.einsum("or,lok->rlk", to_hidden.astype(F32), up_all, precision=HIGHEST)
    flat = jnp.concatenate([spread.reshape(fsdp * tp, -1), up_all.reshape(fsdp * tp, -1)], axis=1)
    for bit in reversed(range(bits_of(fsdp))):
        middle = flat.shape[0] // 2
        flat = flat[:middle] + flip(flat[middle:], bit)
    for bit in reversed(range(bits_of(tp))):
        middle = flat.shape[0] // 2
        flat = flat[:middle] + flip(flat[middle:], bit, "tp")
    flat = flat.reshape(-1)
    sizes = [grid, grid, 2 * layers, 2 * layers, layers, layers, 3 * layers, 2 * layers, layers, layers * parts]
    shapes = [
        (grid, fine), (grid, fine), (layers, 2, fine), (layers, 2, fine), (layers, fine), (layers, fine),
        (layers, 3, fine), (layers, 2, fine), (layers, fine), (layers, parts * fine),
    ]
    found = []
    start = 0
    for lines, shape in zip(sizes, shapes):
        found.append(flat[start : start + lines * fine].reshape(shape))
        start += lines * fine
    rows_g, cols_g, gain_g, shift_g, out_g, last_g, proj_g, head_gain_g, head_shift_g, up_g = found
    return (
        activations, token_grad, rows_g, cols_g, gain_g, shift_g, proj_g, head_gain_g, head_shift_g, out_g, up_g, last_g,
        jnp.stack(w_qkv_grad), jnp.stack(w_out_grad), jnp.stack(w_fc1_grad), jnp.stack(w_fc2_grad),
    )


def solution(mesh):
    both = ("fsdp", "tp")
    in_specs = (
        P(both, None), P("fsdp", None), P(None, both), P(None, both), P(None, both), P(None, None, both),
        P(None, None, both), P(None, None, both), P(None, None, both), P(None, both), P(None, both), P(None, both),
        P(None, both), P(None, "fsdp", None, "tp"), P(None, "tp", "fsdp"), P(None, "fsdp", "tp"), P(None, "tp", "fsdp"),
        P(both, None),
    )
    out_specs = (
        P(both, None), P(both, None), P(None, both), P(None, both), P(None, None, both), P(None, None, both),
        P(None, None, both), P(None, None, both), P(None, both), P(None, both), P(None, both), P(None, both),
        P(None, "fsdp", None, "tp"), P(None, "tp", "fsdp"), P(None, "fsdp", "tp"), P(None, "tp", "fsdp"),
    )
    return jax.shard_map(body, mesh=mesh, in_specs=in_specs, out_specs=out_specs, check_vma=False)
```

```python
import functools

import jax
import jax.numpy as jnp
from jax import lax
from jax.experimental import pallas as pl
from jax.experimental.pallas import tpu as pltpu
from jax.sharding import PartitionSpec as P

HD = 64
PAIR = 128
REACH = 384
EPS = 1e-06
FILL = -1e30
ROOT_HALF = 0.7071067811865476
INV_ROOT_TWO_PI = 0.3989422804014327
HIGHEST = lax.Precision.HIGHEST
F32 = jnp.float32
BF16 = jnp.bfloat16
MESH = pl.DeviceIdType.MESH
ANY = pl.BlockSpec(memory_space=pl.ANY)


def nn(left, right):
    return lax.dot_general(left, right, (((1,), (0,)), ((), ())), preferred_element_type=F32)


def nt(left, right):
    return lax.dot_general(left, right, (((1,), (1,)), ((), ())), preferred_element_type=F32)


def halves(array):
    middle = array.shape[1] // 2
    return array[:, :middle], array[:, middle:]


def row_norm(value):
    centered = value - jnp.mean(value, axis=-1, keepdims=True)
    scale = lax.rsqrt(jnp.mean(centered * centered, axis=-1, keepdims=True) + EPS)
    return centered * scale, scale


def row_norm_back(grad_hat, normed, scale):
    return scale * (
        grad_hat
        - jnp.mean(grad_hat, axis=-1, keepdims=True)
        - normed * jnp.mean(grad_hat * normed, axis=-1, keepdims=True)
    )


def head_mean(value, exact=False):
    wide = value.shape[1]
    rows = lax.broadcasted_iota(jnp.int32, (wide, wide), 0) // HD
    cols = lax.broadcasted_iota(jnp.int32, (wide, wide), 1) // HD
    spread = jnp.where(rows == cols, 1.0 / HD, 0.0).astype(BF16)
    high = value.astype(BF16)
    mean = nn(high, spread)
    if exact:
        mean += nn((value - high.astype(F32)).astype(BF16), spread)
    return mean


def head_norm(value):
    centered = value - head_mean(value, exact=True)
    scale = lax.rsqrt(head_mean(centered * centered) + EPS)
    return centered * scale, scale


def head_norm_back(grad_hat, normed, scale):
    return scale * (grad_hat - head_mean(grad_hat) - normed * head_mean(grad_hat * normed))


def only(array, part):
    return jnp.where(lax.broadcasted_iota(jnp.int32, (1, PAIR), 1) // HD == part, array, jnp.zeros_like(array))


def side(*parts):
    return jnp.concatenate(parts, axis=1)


def whole(shape):
    return pl.BlockSpec(shape, lambda step: (0,) * len(shape))


def column(height, wide, every=1, first=0):
    return pl.BlockSpec((height, wide), lambda step: (0, step * every + first))


def shaped(shape, kind=BF16):
    return jax.ShapeDtypeStruct(shape, kind)


class Neighbours:
    def __init__(self):
        fsdp, tp = lax.axis_index("fsdp"), lax.axis_index("tp")
        self.size = lax.axis_size("tp")
        self.tp = tp
        self.x, self.y, self.core = ({"fsdp": jnp.bitwise_xor(fsdp, bit)} for bit in (2, 4, 1))
        self.right = self.along(1)

    def along(self, distance):
        return {"tp": lax.rem(self.tp + distance, self.size)}

    def greet(self, all_tp=False):
        distances = range(1, self.size) if all_tp else [self.size - 1]
        targets = [self.x, self.y, self.core] + [self.along(distance) for distance in distances]
        barrier = pltpu.get_barrier_semaphore()
        for target in targets:
            pl.semaphore_signal(barrier, inc=1, device_id=target, device_id_type=MESH)
        pl.semaphore_wait(barrier, len(targets))


class Gather:
    KINDS = 7

    def __init__(self, shard, near, far, send, recv, local):
        self.shard, self.near, self.far, self.send, self.recv, self.local = shard, near, far, send, recv, local
        self.chunk, self.wide = shard.shape
        self.pieces = near.shape[1] // self.wide
        self.peers = Neighbours()

    def at(self, piece, start, count, half=None):
        first, wide = piece * self.wide, self.wide
        if half is not None:
            wide //= 2
            first += half * wide
        return self.near.at[pl.ds(start * self.chunk, count * self.chunk), pl.ds(first, wide)]

    def copy(self, piece, kind, source, target, device):
        return pltpu.make_async_remote_copy(
            src_ref=source, dst_ref=target, send_sem=self.send.at[piece, kind], recv_sem=self.recv.at[piece, kind],
            device_id=device, device_id_type=MESH,
        )

    def copies(self, piece, stage):
        if stage == "z":
            source = self.shard if piece == 0 else self.at(piece, 0, 1)
            return [self.copy(piece, 0, source, self.at(piece + 1, 0, 1), self.peers.right)]
        if stage == "first":
            half = self.wide // 2
            left = self.shard.at[:, pl.ds(0, half)] if piece == 0 else self.at(piece, 0, 1, 0)
            right = self.shard.at[:, pl.ds(half, half)] if piece == 0 else self.at(piece, 0, 1, 1)
            return [
                self.copy(piece, 1, left, self.at(piece, 1, 1, 0), self.peers.x),
                self.copy(piece, 2, right, self.at(piece, 2, 1, 1), self.peers.y),
            ]
        if stage == "second":
            return [
                self.copy(piece, 3, self.at(piece, 0, 2, 0), self.at(piece, 2, 2, 0), self.peers.y),
                self.copy(piece, 4, self.at(piece, 0, 1, 1), self.at(piece, 1, 1, 1), self.peers.x),
                self.copy(piece, 5, self.at(piece, 2, 1, 1), self.at(piece, 3, 1, 1), self.peers.x),
            ]
        span = pl.ds(piece * self.wide, self.wide)
        return [self.copy(piece, 6, self.near.at[:, span], self.far.at[:, span], self.peers.core)]

    def start(self, piece, stage):
        for copy in self.copies(piece, stage):
            copy.start()

    def arrived(self, piece, stage):
        for copy in self.copies(piece, stage):
            copy.wait_recv()

    def run(self, event):
        name, piece = event
        if name == "begin":
            self.peers.greet()
            own = pltpu.make_async_copy(self.shard, self.at(0, 0, 1), self.local)
            own.start()
            self.start(0, "z")
            self.start(0, "first")
            own.wait()
        elif name == "A":
            self.arrived(piece - 1, "z")
            if piece + 1 < self.pieces:
                self.start(piece, "z")
            self.start(piece, "first")
        elif name == "B":
            self.arrived(piece, "first")
            self.start(piece, "second")
        elif name == "C":
            self.arrived(piece, "second")
            self.start(piece, "core")
        else:
            for piece in range(self.pieces):
                self.arrived(piece, "core")
                for stage in ("z", "first", "second", "core"):
                    if stage != "z" or piece + 1 < self.pieces:
                        for copy in self.copies(piece, stage):
                            copy.wait_send()


def gather_events(pieces):
    order = [("begin", 0)]
    for piece in range(pieces):
        if piece:
            order.append(("A", piece))
        if piece > 1:
            order.append(("C", piece - 2))
        if piece:
            order.append(("B", piece - 1))
    order += [("C", pieces - 2), ("B", pieces - 1), ("C", pieces - 1), ("end", 0)]
    return order


def spaced(events, counts):
    table = []
    for count in counts:
        table.append(events[:count])
        events = events[count:]
    return table + [events]


def gather_specs(shard, pieces, halved):
    chunk, wide = shard.shape
    full = shaped((halved, pieces * wide))
    semaphores = pltpu.SemaphoreType.DMA((pieces, Gather.KINDS))
    return [whole((chunk, wide))], [full, full], [semaphores, semaphores, pltpu.SemaphoreType.DMA]


def gather_kernel(shard_ref, near_ref, far_ref, send, recv, local):
    gather = Gather(shard_ref, near_ref, far_ref, send, recv, local)
    for event in gather_events(gather.pieces):
        gather.run(event)


def params(collective=None):
    if collective is None:
        return pltpu.CompilerParams()
    return pltpu.CompilerParams(collective_id=collective, has_side_effects=True)


def gather_alone(shard, pieces, halved, collective):
    operands, results, scratch = gather_specs(shard, pieces, halved)
    return pl.pallas_call(
        gather_kernel,
        grid=(1,),
        in_specs=operands,
        out_specs=[ANY] * 2,
        out_shape=results,
        scratch_shapes=scratch,
        compiler_params=params(collective),
        name="gather_block",
    )(shard)


def halo_kernel(a_ref, out_ref, send, recv):
    rows = a_ref.shape[0]
    spill = REACH - rows
    place, size = lax.axis_index("tp"), lax.axis_size("tp")
    out_ref[REACH : REACH + rows, :] = a_ref[...]
    moves = [
        (1, pl.ds(0, rows), pl.ds(spill, rows)),
        (-1, pl.ds(0, rows), pl.ds(REACH + rows, rows)),
        (2, pl.ds(rows - spill, spill), pl.ds(0, spill)),
        (-2, pl.ds(0, spill), pl.ds(REACH + 2 * rows, spill)),
    ]
    barrier = pltpu.get_barrier_semaphore()
    inside = lambda other: jnp.logical_and(other >= 0, other < size)
    for distance, _, _ in moves:

        @pl.when(inside(place + distance))
        def _():
            pl.semaphore_signal(barrier, inc=1, device_id={"tp": place + distance}, device_id_type=MESH)

    pl.semaphore_wait(barrier, jnp.minimum(place, 2) + jnp.minimum(size - 1 - place, 2))

    def copy(index):
        distance, source, target = moves[index]
        return pltpu.make_async_remote_copy(
            src_ref=a_ref.at[source, :], dst_ref=out_ref.at[target, :], send_sem=send.at[index], recv_sem=recv.at[index],
            device_id={"tp": place + distance}, device_id_type=MESH,
        )

    for index, (distance, _, _) in enumerate(moves):

        @pl.when(inside(place + distance))
        def _():
            copy(index).start()

        @pl.when(jnp.logical_not(inside(place - distance)))
        def _():
            target = moves[index][2]
            out_ref[target, :] = jnp.zeros((target.size, out_ref.shape[1]), BF16)

    for index, (distance, _, _) in enumerate(moves):

        @pl.when(inside(place + distance))
        def _():
            copy(index).wait_send()

        @pl.when(inside(place - distance))
        def _():
            copy(index).wait_recv()


def halo(a_own, collective):
    rows, width = a_own.shape
    return pl.pallas_call(
        halo_kernel,
        grid=(1,),
        in_specs=[whole((rows, width))],
        out_specs=whole((rows + 2 * REACH, width)),
        out_shape=shaped((rows + 2 * REACH, width)),
        scratch_shapes=[pltpu.SemaphoreType.DMA((4,)), pltpu.SemaphoreType.DMA((4,))],
        compiler_params=params(collective),
        name="halo",
    )(a_own)


class Rows:
    def __init__(self, layers, grid):
        self.layers, self.grid = layers, grid

    def ln_gain(self, layer, which):
        return 2 * self.grid + 2 * layer + which

    def ln_bias(self, layer, which):
        return 2 * self.grid + 2 * self.layers + 2 * layer + which

    def out_bias(self, layer):
        return 2 * self.grid + 4 * self.layers + layer

    def last_bias(self, layer):
        return 2 * self.grid + 5 * self.layers + layer

    def proj_bias(self, layer, which):
        return 3 * layer + which

    def head_gain(self, layer, which):
        return 3 * self.layers + 2 * layer + which

    def head_bias(self, layer):
        return 5 * self.layers + layer


def line(ref, row, start=0, wide=None):
    return ref[row : row + 1, start : start + (wide or ref.shape[1] - start)]


def hooked(gather, table, slots):
    step = pl.program_id(0)

    def at(slot):
        if gather is None:
            return
        for index in range(slot, len(table) - 1, slots):
            if table[index]:

                @pl.when(step == index // slots)
                def _(events=table[index]):
                    for event in events:
                        gather.run(event)

    def after():
        if gather is None:
            return

        @pl.when(step == pl.num_programs(0) - 1)
        def _():
            for event in table[-1]:
                gather.run(event)

    return at, after


def attend_kernel(*refs, rows_of, layer, table):
    a_ref, near_ref, far_ref, heads_ref, feats_ref, x_ref, seg_k_ref, seg_q_ref = refs[:8]
    rest = refs[8:]
    gather = None
    if table:
        gather = Gather(rest[0], *rest[11:13], *rest[-3:])
        rest = rest[1:11] + rest[13:-3]
    q_ref, kv_ref, q_hat_ref, k_hat_ref, q_scale_ref, k_scale_ref, p_ref, o_ref, mid_ref, m_ref = rest[:10]
    mask_ref, acc_ref = rest[10:]
    rows = q_ref.shape[0]
    half = near_ref.shape[0]
    step = pl.program_id(0)
    at, after = hooked(gather, table, 2)
    at(0)

    @pl.when(step == 0)
    def _():
        mask_ref[...] = jnp.where(seg_k_ref[...] == seg_q_ref[...], 0.0, FILL)
        acc_ref[...] = jnp.zeros_like(acc_ref)

    tile = lambda row, which: line(heads_ref, row, which * PAIR, PAIR)
    bias = [rows_of.proj_bias(layer, which) for which in range(3)]
    q_gain, k_gain = (rows_of.head_gain(layer, which) for which in range(2))
    q_shift = rows_of.head_bias(layer)
    near, distant = halves(a_ref[...])
    own, own_far = halves(a_ref[REACH : REACH + rows, :])
    kv = nn(near, near_ref[:, PAIR : 4 * PAIR]) + nn(distant, far_ref[:, PAIR : 4 * PAIR])
    kv += side(tile(bias[1], 0), tile(bias[2], 0), tile(bias[1], 1) + tile(bias[2], 2))
    q = side(
        nn(own, near_ref[:, :PAIR]) + nn(own_far, far_ref[:, :PAIR]),
        nn(own, near_ref[:, 4 * PAIR : 5 * PAIR]) + nn(own_far, far_ref[:, 4 * PAIR : 5 * PAIR]),
    ) + line(heads_ref, bias[0], 0, 2 * PAIR)
    q_hat, q_scale = head_norm(q)
    k_hat, k_scale = head_norm(side(kv[:, :PAIR], kv[:, 2 * PAIR :]))
    qn = (q_hat * line(heads_ref, q_gain, 0, 2 * PAIR) + line(heads_ref, q_shift, 0, 2 * PAIR)).astype(BF16)
    qn = side(qn[:, :PAIR], only(qn[:, PAIR:], 0))
    kn = (k_hat * line(heads_ref, k_gain, 0, 2 * PAIR)).astype(BF16)
    v = kv[:, PAIR:].astype(BF16)
    low = lax.broadcasted_iota(jnp.int32, (1, PAIR), 1) < HD
    first, second = kn[:, :PAIR], jnp.where(low, kn[:, PAIR:], v[:, PAIR:])
    values = v[:, :PAIR]
    q_ref[...] = qn
    kv_ref[...] = side(first, values, second)
    q_hat_ref[...] = q_hat.astype(BF16)
    k_hat_ref[...] = k_hat.astype(BF16)
    q_scale_ref[...] = q_scale.astype(BF16)
    k_scale_ref[...] = k_scale.astype(BF16)
    at(1)
    values_t, second_t = values.T, second.T
    mixed = []
    for head in range(3):
        keys = (first, first, second)[head]
        query = only(qn[:, PAIR * (head // 2) : PAIR * (head // 2 + 1)] * HD ** (-0.5), head % 2).astype(BF16)
        scores = nt(keys, query) + mask_ref[...]
        weights = jnp.exp(scores - jnp.max(scores, axis=0, keepdims=True))
        total = jnp.sum(weights, axis=0, keepdims=True)
        probs = (weights * (1.0 / total)).astype(BF16)
        p_ref[head] = probs
        mixed.append(nn((values_t[:HD], values_t[HD:], second_t[HD:])[head], probs))
    o = jnp.concatenate([jnp.zeros_like(mixed[2]), mixed[2], mixed[0], mixed[1]], axis=0).T.astype(BF16)
    o_ref[...] = o
    acc_ref[:, :half] += nt(o, near_ref[:, 4 * PAIR :])
    acc_ref[:, half:] += nt(o, far_ref[:, 4 * PAIR :])

    @pl.when(step == pl.num_programs(0) - 1)
    def _():
        mid = x_ref[...] + (acc_ref[...] + line(feats_ref, rows_of.out_bias(layer)))
        mid_ref[...] = mid
        hat, _ = row_norm(mid)
        m_ref[...] = (
            hat * line(feats_ref, rows_of.ln_gain(layer, 1)) + line(feats_ref, rows_of.ln_bias(layer, 1))
        ).astype(BF16)

    after()


def attend(a_win, near, far, heads, feats, x, seg_k, seg_q, rows_of, layer, shard=None, collective=None):
    window, width = a_win.shape
    rows = x.shape[0]
    half = width // 2
    pieces = near.shape[1] // (6 * PAIR)
    extra = gather_specs(shard, pieces, half) if shard is not None else ([], [], [])
    table = spaced(gather_events(pieces), [1, 0, 1, 1, 1, 1, 1, 2]) if shard is not None else None
    outs = [(rows, 2 * PAIR), (window, 3 * PAIR), (rows, 2 * PAIR), (window, 2 * PAIR), (rows, 2 * PAIR), (window, 2 * PAIR)]
    return pl.pallas_call(
        functools.partial(attend_kernel, rows_of=rows_of, layer=layer, table=table),
        grid=(pieces,),
        in_specs=[
            whole((window, width)), column(half, 6 * PAIR), column(half, 6 * PAIR), column(heads.shape[0], 3 * PAIR),
            whole(feats.shape), whole((rows, width)), whole((window, 1)), whole((1, rows)), *extra[0],
        ],
        out_specs=[column(*shape) for shape in outs]
        + [pl.BlockSpec((3, window, rows), lambda step: (step, 0, 0)), column(rows, 2 * PAIR)]
        + [whole((rows, width))] * 2 + [ANY] * len(extra[1]),
        out_shape=[shaped((height, pieces * wide)) for height, wide in outs]
        + [shaped((3 * pieces, window, rows)), shaped((rows, pieces * 2 * PAIR)), shaped((rows, width), F32), shaped((rows, width))]
        + extra[1],
        scratch_shapes=[pltpu.VMEM((window, rows), F32), pltpu.VMEM((rows, width), F32), *extra[2]],
        compiler_params=params(collective),
        cost_estimate=pl.CostEstimate(
            flops=2 * window * width * width * 2 + 8 * window * rows * width * 4,
            bytes_accessed=20 * window * width,
            transcendentals=3 * pieces * window * rows,
        ),
        name="attend",
    )(a_win, near, far, heads, feats, x, seg_k, seg_q, *([] if shard is None else [shard]))


def mlp_kernel(*refs, rows_of, layer, table):
    m_ref, mid_ref, up_near_ref, up_far_ref, down_near_ref, down_far_ref, up_shift_ref, feats_ref = refs[:8]
    rest = refs[8:]
    gather = None
    if table:
        gather = Gather(rest[0], *rest[5:7], *rest[-3:])
        rest = rest[1:5] + rest[7:-3]
    act_ref, slope_ref, x2_ref, a_ref, acc_ref = rest
    half = up_near_ref.shape[0]
    step = pl.program_id(0)
    at, after = hooked(gather, table, 2)
    at(0)

    @pl.when(step == 0)
    def _():
        acc_ref[...] = jnp.zeros_like(acc_ref)

    near, distant = halves(m_ref[...])
    hidden = nn(near, up_near_ref[...]) + nn(distant, up_far_ref[...]) + up_shift_ref[...]
    at(1)
    phi = 0.5 * (1.0 + lax.erf(hidden * ROOT_HALF))
    act = (hidden * phi).astype(BF16)
    act_ref[...] = act
    slope_ref[...] = (phi + hidden * jnp.exp(-0.5 * hidden * hidden) * INV_ROOT_TWO_PI).astype(BF16)
    acc_ref[:, :half] += nt(act, down_near_ref[...])
    acc_ref[:, half:] += nt(act, down_far_ref[...])

    @pl.when(step == pl.num_programs(0) - 1)
    def _():
        x2 = mid_ref[...] + (acc_ref[...] + line(feats_ref, rows_of.last_bias(layer)))
        x2_ref[...] = x2
        hat, _ = row_norm(x2)
        after = min(layer + 1, rows_of.layers - 1)
        a_ref[...] = (
            hat * line(feats_ref, rows_of.ln_gain(after, 0)) + line(feats_ref, rows_of.ln_bias(after, 0))
        ).astype(BF16)

    after()


def mlp(m, mid, near, far, up_shift, feats, rows_of, layer, shard=None, collective=None):
    rows, width = mid.shape
    half = width // 2
    hidden = up_shift.shape[1]
    pieces = lax.axis_size("tp")
    wide = hidden // pieces
    extra = gather_specs(shard, pieces, half) if shard is not None else ([], [], [])
    table = spaced(gather_events(pieces), [1, 0, 1, 1, 1, 1, 1, 2]) if shard is not None else None
    full = whole((rows, width))
    return pl.pallas_call(
        functools.partial(mlp_kernel, rows_of=rows_of, layer=layer, table=table),
        grid=(pieces,),
        in_specs=[
            full, full, column(half, wide, 2), column(half, wide, 2), column(half, wide, 2, 1), column(half, wide, 2, 1),
            column(1, wide), whole(feats.shape), *extra[0],
        ],
        out_specs=[column(rows, wide), column(rows, wide), full, full] + [ANY] * len(extra[1]),
        out_shape=[shaped((rows, hidden)), shaped((rows, hidden)), shaped((rows, width), F32), shaped((rows, width))] + extra[1],
        scratch_shapes=[pltpu.VMEM((rows, width), F32), *extra[2]],
        compiler_params=params(collective),
        cost_estimate=pl.CostEstimate(
            flops=4 * rows * width * hidden, bytes_accessed=4 * width * hidden, transcendentals=2 * rows * hidden
        ),
        name="mlp",
    )(m, mid, near, far, near, far, up_shift, feats, *([] if shard is None else [shard]))


def mlp_back_kernel(*refs, gain_row):
    step = pl.program_id(0)
    mlp_back_work(*refs, gain_row, step == 0, step == pl.num_programs(0) - 1)


def mlp_back_work(
    g_ref, down_near_ref, down_far_ref, slope_ref, up_near_ref, up_far_ref, mid_ref, feats_ref,
    gz_ref, gh_ref, up_shift_grad_ref, g1_ref, gr_ref, small_ref, acc_ref, gain_row, opening, closing,
):
    half = up_near_ref.shape[0]

    @pl.when(opening)
    def _():
        gz_ref[...] = g_ref[...].astype(BF16)
        acc_ref[...] = jnp.zeros_like(acc_ref)

    near, distant = halves(gz_ref[...])
    gh = ((nn(near, down_near_ref[...]) + nn(distant, down_far_ref[...])) * slope_ref[...].astype(F32)).astype(BF16)
    gh_ref[...] = gh
    up_shift_grad_ref[...] = jnp.sum(gh.astype(F32), axis=0, keepdims=True)
    acc_ref[:, :half] += nt(gh, up_near_ref[...])
    acc_ref[:, half:] += nt(gh, up_far_ref[...])

    @pl.when(closing)
    def _():
        gm = acc_ref[...]
        hat, scale = row_norm(mid_ref[...])
        g1 = g_ref[...] + row_norm_back(gm * line(feats_ref, gain_row), hat, scale)
        gr = g1.astype(BF16)
        g1_ref[...] = g1
        gr_ref[...] = gr
        small_ref[...] = jnp.zeros_like(small_ref)
        small_ref[0:1, :] = jnp.sum(gz_ref[...].astype(F32), axis=0, keepdims=True)
        small_ref[1:2, :] = jnp.sum(gr.astype(F32), axis=0, keepdims=True)
        small_ref[2:3, :] = jnp.sum(gm * hat, axis=0, keepdims=True)
        small_ref[3:4, :] = jnp.sum(gm, axis=0, keepdims=True)


def mlp_back(grad, near, far, slope, mid, feats, gain_row):
    rows, width = grad.shape
    half = width // 2
    hidden = slope.shape[1]
    pieces = lax.axis_size("tp")
    wide = hidden // pieces
    full = whole((rows, width))
    return pl.pallas_call(
        functools.partial(mlp_back_kernel, gain_row=gain_row),
        grid=(pieces,),
        in_specs=[
            full, column(half, wide, 2, 1), column(half, wide, 2, 1), column(rows, wide), column(half, wide, 2),
            column(half, wide, 2), full, whole(feats.shape),
        ],
        out_specs=[full, column(rows, wide), column(1, wide), full, full, whole((8, width))],
        out_shape=[
            shaped((rows, width)), shaped((rows, hidden)), shaped((1, hidden), F32), shaped((rows, width), F32),
            shaped((rows, width)), shaped((8, width), F32),
        ],
        scratch_shapes=[pltpu.VMEM((rows, width), F32)],
        cost_estimate=pl.CostEstimate(
            flops=4 * rows * width * hidden, bytes_accessed=4 * width * hidden, transcendentals=0
        ),
        name="mlp_back",
    )(grad, near, far, slope, near, far, mid, feats)


def attend_back_kernel(*refs, rows_of, layer):
    attend_back_work(*refs, rows_of, layer, lambda: None)


def attend_back_work(
    gr_ref, q_ref, kv_ref, q_hat_ref, k_hat_ref, q_scale_ref, k_scale_ref, p_ref, near_ref, far_ref, heads_ref,
    gq_ref, gkv_ref, mine_ref, left_ref, right_ref, small_ref, acc_ref, rows_of, layer, middle,
):
    rows = gr_ref.shape[0]
    half = near_ref.shape[0]
    step = pl.program_id(0)

    @pl.when(step == 0)
    def _():
        acc_ref[...] = jnp.zeros_like(acc_ref)

    near, distant = halves(gr_ref[...])
    go = (nn(near, near_ref[:, 4 * PAIR :]) + nn(distant, far_ref[:, 4 * PAIR :])).astype(BF16)
    qn, kv = q_ref[...], kv_ref[...]
    first, values, second = kv[:, :PAIR], kv[:, PAIR : 2 * PAIR], kv[:, 2 * PAIR :]
    first_t, second_t = first.T, second.T
    grad_q, grad_k, grad_v = [], [], []
    for head in range(3):
        if head == 1:
            middle()
        go_head = only(go[:, PAIR:], head) if head < 2 else only(go[:, :PAIR], 1)
        query = only(qn[:, PAIR * (head // 2) : PAIR * (head // 2 + 1)] * HD ** (-0.5), head % 2).astype(BF16)
        stored = p_ref[head]
        probs = stored.astype(F32)
        grad_probs = nt((values, values, second)[head], go_head)
        delta = jnp.sum(probs * grad_probs, axis=0, keepdims=True)
        grad_scores = (probs * (grad_probs - delta)).astype(BF16)
        grad_v.append(nn(stored, go_head))
        grad_k.append(nn(grad_scores, query))
        grad_q.append(nn((first_t[:HD], first_t[HD:], second_t[:HD])[head], grad_scores))
    zero = jnp.zeros_like(grad_q[2])
    grad_q = (jnp.concatenate(grad_q + [zero], axis=0) * HD ** (-0.5)).T
    grad_k = side(grad_k[0] + grad_k[1], grad_k[2])
    pair_v, last_v = grad_v[0] + grad_v[1], grad_v[2]
    q_hat = q_hat_ref[...].astype(F32)
    k_hat = k_hat_ref[...].astype(F32)
    gain = lambda which: line(heads_ref, rows_of.head_gain(layer, which), 0, 2 * PAIR)
    gq = head_norm_back(grad_q * gain(0), q_hat, q_scale_ref[...].astype(F32)).astype(BF16)
    gk = head_norm_back(grad_k * gain(1), k_hat, k_scale_ref[...].astype(F32)).astype(BF16)
    gkv = side(gk[:, :PAIR], pair_v.astype(BF16), gk[:, PAIR:] + last_v.astype(BF16))
    gq_ref[...] = gq
    gkv_ref[...] = gkv
    total = lambda value: jnp.sum(value.astype(F32), axis=0, keepdims=True)
    small_ref[...] = jnp.zeros_like(small_ref)
    small_ref[0:1, : 2 * PAIR] = total(grad_q * q_hat)
    small_ref[1:2, : 2 * PAIR] = total(grad_k * k_hat)
    small_ref[2:3, : 2 * PAIR] = total(grad_q)
    small_ref[3:4, : 2 * PAIR] = total(gq)
    small_ref[4:5, : 2 * PAIR] = total(gk)
    small_ref[5:6, :PAIR] = total(pair_v.astype(BF16))
    small_ref[5:6, 2 * PAIR :] = total(last_v.astype(BF16))
    acc_ref[:, :half] += nt(gkv, near_ref[:, PAIR : 4 * PAIR])
    acc_ref[:, half:] += nt(gkv, far_ref[:, PAIR : 4 * PAIR])
    own = slice(REACH, REACH + rows)
    for ref, cols in ((near_ref, slice(0, half)), (far_ref, slice(half, 2 * half))):
        acc_ref[own, cols] += nt(gq[:, :PAIR], ref[:, :PAIR]) + nt(gq[:, PAIR:], ref[:, 4 * PAIR : 5 * PAIR])

    @pl.when(step == pl.num_programs(0) - 1)
    def _():
        left_ref[...] = acc_ref[:REACH, :].astype(BF16)
        mine_ref[...] = acc_ref[own, :]
        right_ref[...] = acc_ref[REACH + rows :, :].astype(BF16)


def attend_back_specs(rows, width, pieces, lines):
    half = width // 2
    window = rows + 2 * REACH
    full = whole((rows, width))
    in_specs = [
        full, column(rows, 2 * PAIR), column(window, 3 * PAIR), column(rows, 2 * PAIR), column(window, 2 * PAIR),
        column(rows, 2 * PAIR), column(window, 2 * PAIR), pl.BlockSpec((3, window, rows), lambda step: (step, 0, 0)),
        column(half, 6 * PAIR), column(half, 6 * PAIR), column(lines, 3 * PAIR),
    ]
    out_specs = [
        column(rows, 2 * PAIR), column(window, 3 * PAIR), full, whole((REACH, width)), whole((REACH, width)), column(8, 3 * PAIR),
    ]
    out_shape = [
        shaped((rows, pieces * 2 * PAIR)), shaped((window, pieces * 3 * PAIR)), shaped((rows, width), F32),
        shaped((REACH, width)), shaped((REACH, width)), shaped((8, pieces * 3 * PAIR), F32),
    ]
    cost = pl.CostEstimate(
        flops=2 * window * width * width * 2 + 20 * window * rows * width * 2,
        bytes_accessed=20 * window * width,
        transcendentals=0,
    )
    return in_specs, out_specs, out_shape, [pltpu.VMEM((window, width), F32)], cost


def attend_back(gr, stored, near, far, heads, rows_of, layer):
    rows, width = gr.shape
    pieces = near.shape[1] // (6 * PAIR)
    in_specs, out_specs, out_shape, scratch, cost = attend_back_specs(rows, width, pieces, heads.shape[0])
    return pl.pallas_call(
        functools.partial(attend_back_kernel, rows_of=rows_of, layer=layer),
        grid=(pieces,),
        in_specs=in_specs,
        out_specs=out_specs,
        out_shape=out_shape,
        scratch_shapes=scratch,
        cost_estimate=cost,
        name="attend_back",
    )(gr, *stored, near, far, heads)


def attn_weight_kernel(a_ref, gq_ref, gkv_ref, gr_ref, o_ref, keep_ref, send_ref, a_t_ref, gr_t_ref):
    rows = gq_ref.shape[0]
    half = keep_ref.shape[0]

    @pl.when(pl.program_id(0) == 0)
    def _():
        a_t_ref[...] = a_ref[...].T
        gr_t_ref[...] = gr_ref[...].T

    for part, ref in ((slice(0, half), keep_ref), (slice(half, 2 * half), send_ref)):
        from_q = nn(a_t_ref[part, REACH : REACH + rows], gq_ref[...])
        from_o = nn(gr_t_ref[part, :], o_ref[...])
        ref[:, :PAIR] = from_q[:, :PAIR].astype(BF16)
        ref[:, PAIR : 4 * PAIR] = nn(a_t_ref[part, :], gkv_ref[...]).astype(BF16)
        ref[:, 4 * PAIR : 5 * PAIR] = (from_q[:, PAIR:] + from_o[:, :PAIR]).astype(BF16)
        ref[:, 5 * PAIR :] = from_o[:, PAIR:].astype(BF16)


def attn_weight_grads(a_win, gq, gkv, gr, o):
    window, width = a_win.shape
    rows = gr.shape[0]
    half = width // 2
    pieces = gq.shape[1] // (2 * PAIR)
    out = column(half, 6 * PAIR)
    return pl.pallas_call(
        attn_weight_kernel,
        grid=(pieces,),
        in_specs=[
            whole((window, width)), column(rows, 2 * PAIR), column(window, 3 * PAIR), whole((rows, width)),
            column(rows, 2 * PAIR),
        ],
        out_specs=[out, out],
        out_shape=[shaped((half, pieces * 6 * PAIR))] * 2,
        scratch_shapes=[pltpu.VMEM((width, window), BF16), pltpu.VMEM((width, rows), BF16)],
        cost_estimate=pl.CostEstimate(
            flops=2 * width * width * (2 * window + 2 * rows), bytes_accessed=8 * width * width, transcendentals=0
        ),
        name="attn_weight_grads",
    )(a_win, gq, gkv, gr, o)


def mlp_weight_kernel(m_ref, gh_ref, gz_ref, act_ref, keep_ref, send_ref, m_t_ref, gz_t_ref):
    half = keep_ref.shape[0]
    wide = gh_ref.shape[1]

    @pl.when(pl.program_id(0) == 0)
    def _():
        m_t_ref[...] = m_ref[...].T
        gz_t_ref[...] = gz_ref[...].T

    for part, ref in ((slice(0, half), keep_ref), (slice(half, 2 * half), send_ref)):
        ref[:, :wide] = nn(m_t_ref[part, :], gh_ref[...]).astype(BF16)
        ref[:, wide:] = nn(gz_t_ref[part, :], act_ref[...]).astype(BF16)


def mlp_weight_grads(m, gh, gz, act):
    rows, width = m.shape
    half = width // 2
    hidden = gh.shape[1]
    pieces = lax.axis_size("tp")
    wide = hidden // pieces
    out = column(half, 2 * wide)
    return pl.pallas_call(
        mlp_weight_kernel,
        grid=(pieces,),
        in_specs=[whole((rows, width)), column(rows, wide), whole((rows, width)), column(rows, wide)],
        out_specs=[out, out],
        out_shape=[shaped((half, 2 * hidden))] * 2,
        scratch_shapes=[pltpu.VMEM((width, rows), BF16), pltpu.VMEM((width, rows), BF16)],
        cost_estimate=pl.CostEstimate(
            flops=4 * width * hidden * rows, bytes_accessed=4 * width * hidden, transcendentals=0
        ),
        name="mlp_weight_grads",
    )(m, gh, gz, act)


class Scatter:
    KINDS = 7

    def __init__(self, out, away, keep, core, first, second, ring_in, send, recv):
        self.out, self.away, self.keep, self.core_in = out, away, keep, core
        self.first_in, self.second_in, self.ring_in, self.send, self.recv = first, second, ring_in, send, recv
        self.chunk, self.wide = out.shape
        self.half = self.wide // 2
        self.pieces = keep.shape[0]
        self.near = Neighbours()

    def copy(self, piece, kind, source, target, device):
        return pltpu.make_async_remote_copy(
            src_ref=source, dst_ref=target, send_sem=self.send.at[piece, kind], recv_sem=self.recv.at[piece, kind],
            device_id=device, device_id_type=MESH,
        )

    def copies(self, piece, stage):
        c, left, right = self.chunk, pl.ds(0, self.half), pl.ds(self.half, self.half)
        rows = lambda start, count=1: pl.ds(start * c, count * c)
        if stage == "core":
            return [self.copy(piece, 0, self.away.at[piece], self.core_in.at[piece], self.near.core)]
        if stage == "first":
            source, target = self.keep.at[piece], self.first_in.at[piece]
            return [
                self.copy(piece, 1, source.at[rows(2, 2), left], target.at[:, left], self.near.y),
                self.copy(piece, 2, source.at[rows(1), right], target.at[rows(0), right], self.near.x),
                self.copy(piece, 3, source.at[rows(3), right], target.at[rows(1), right], self.near.x),
            ]
        if stage == "second":
            source, target = self.keep.at[piece], self.second_in.at[piece]
            return [
                self.copy(piece, 4, source.at[rows(1), left], target.at[:, left], self.near.x),
                self.copy(piece, 5, source.at[rows(2), right], target.at[:, right], self.near.y),
            ]
        target = self.ring_in.at[lax.rem(piece + 1, self.pieces)]
        return [self.copy(piece, 6, self.keep.at[piece, rows(0), :], target, self.near.right)]

    def start(self, piece, stage):
        for copy in self.copies(piece, stage):
            copy.start()

    def arrived(self, piece, stage):
        for copy in self.copies(piece, stage):
            copy.wait_recv()

    def add(self, piece, start, count, cols, source):
        step = 32

        @pl.loop(0, count * self.chunk // step)
        def _(index):
            row = pl.multiple_of(index * step, step)
            into = (piece, pl.ds(start * self.chunk + row, step), cols)
            self.keep[into] = (self.keep[into].astype(F32) + source[pl.ds(row, step), cols].astype(F32)).astype(BF16)

    def place(self, index):
        return lax.rem(index + 1, self.pieces)

    def core(self, index):
        self.start(self.place(index), "core")

    def first(self, index):
        piece = self.place(index)
        self.arrived(piece, "core")
        self.add(piece, 0, 4, pl.ds(0, self.wide), self.core_in.at[piece])
        self.start(piece, "first")

    def second(self, index):
        piece = self.place(index)
        left, right = pl.ds(0, self.half), pl.ds(self.half, self.half)
        self.arrived(piece, "first")
        source = self.first_in.at[piece]
        self.add(piece, 0, 2, left, source)
        self.add(piece, 0, 1, right, source)
        self.add(piece, 2, 1, right, source.at[pl.ds(self.chunk, self.chunk)])
        self.start(piece, "second")

    def last(self, index):
        piece = self.place(index)
        self.arrived(piece, "second")
        kept = pl.ds(0, self.chunk)

        def ring():
            self.arrived(lax.rem(piece + self.pieces - 1, self.pieces), "ring")

        def total(with_ring):
            value = self.keep[piece, kept, :].astype(F32) + self.second_in[piece].astype(F32)
            return value + self.ring_in[piece].astype(F32) if with_ring else value

        if isinstance(index, int):
            if index:
                ring()
            if index == self.pieces - 1:
                self.out[...] = total(True)
            else:
                self.keep[piece, kept, :] = total(index > 0).astype(BF16)
                self.start(piece, "ring")
            return
        raise NotImplementedError

    def done(self):
        for piece in range(self.pieces):
            for stage in ("core", "first", "second", "ring"):
                if stage != "ring" or piece:
                    for copy in self.copies(piece, stage):
                        copy.wait_send()


def scatter_specs(pieces, chunk, wide):
    buffer = lambda rows: pltpu.VMEM((pieces, rows * chunk, wide), BF16)
    semaphores = pltpu.SemaphoreType.DMA((pieces, Scatter.KINDS))
    return shaped((chunk, wide), F32), [buffer(4), buffer(4), buffer(4), buffer(2), buffer(1), buffer(1), semaphores, semaphores]


def at_step(index, work):
    @pl.when(pl.program_id(0) == index)
    def _():
        work()


def attend_back_scatter_kernel(
    gr_ref, q_ref, kv_ref, q_hat_ref, k_hat_ref, q_scale_ref, k_scale_ref, p_ref, near_ref, far_ref, heads_ref,
    m_ref, gh_ref, gz_ref, act_ref, gq_ref, gkv_ref, mine_ref, left_ref, right_ref, small_ref, out_ref,
    acc_ref, m_t_ref, gz_t_ref, *scratch, rows_of, layer,
):
    scatter = Scatter(out_ref, *scratch)
    pieces, half, wide = scatter.pieces, near_ref.shape[0], gh_ref.shape[1]
    step = pl.program_id(0)

    @pl.when(step == 0)
    def _():
        scatter.near.greet()
        m_t_ref[...] = m_ref[...].T
        gz_t_ref[...] = gz_ref[...].T

    piece = scatter.place(step)
    for part, ref in ((slice(0, half), scatter.keep), (slice(half, 2 * half), scatter.away)):
        ref[piece, :, :wide] = nn(m_t_ref[part, :], gh_ref[...]).astype(BF16)
        ref[piece, :, wide:] = nn(gz_t_ref[part, :], act_ref[...]).astype(BF16)
    scatter.core(step)
    for index in range(2, pieces):
        at_step(index, lambda: scatter.last(index - 2))

    def middle():
        scatter.first(step)

        @pl.when(step > 0)
        def _():
            scatter.second(step - 1)

    attend_back_work(
        gr_ref, q_ref, kv_ref, q_hat_ref, k_hat_ref, q_scale_ref, k_scale_ref, p_ref, near_ref, far_ref, heads_ref,
        gq_ref, gkv_ref, mine_ref, left_ref, right_ref, small_ref, acc_ref, rows_of, layer, middle,
    )

    @pl.when(step == pieces - 1)
    def _():
        scatter.last(pieces - 2)
        scatter.second(pieces - 1)
        scatter.last(pieces - 1)
        scatter.done()


def attend_back_scatter(gr, stored, near, far, heads, m, gh, gz, act, rows_of, layer, collective):
    rows, width = gr.shape
    half = width // 2
    hidden = gh.shape[1]
    pieces = near.shape[1] // (6 * PAIR)
    wide = hidden // pieces
    in_specs, out_specs, out_shape, scratch, cost = attend_back_specs(rows, width, pieces, heads.shape[0])
    turned = pl.BlockSpec((rows, wide), lambda step: (0, lax.rem(step + 1, pieces)))
    full = whole((rows, width))
    result, extra = scatter_specs(pieces, half // 4, 2 * wide)
    return pl.pallas_call(
        functools.partial(attend_back_scatter_kernel, rows_of=rows_of, layer=layer),
        grid=(pieces,),
        in_specs=in_specs + [full, turned, full, turned],
        out_specs=out_specs + [whole(result.shape)],
        out_shape=out_shape + [result],
        scratch_shapes=scratch + [pltpu.VMEM((width, rows), BF16)] * 2 + extra,
        compiler_params=params(collective),
        cost_estimate=cost,
        name="attend_back_scatter",
    )(gr, *stored, near, far, heads, m, gh, gz, act)


def give_back_kernel(*refs, rows_of, layer, with_mlp):
    a_ref, gq_ref, gkv_ref, gr_ref, o_ref, x_ref, g1_ref, mine_ref, left_ref, right_ref, feats_ref = refs[:11]
    rest = refs[11:]
    if with_mlp:
        down_near_ref, down_far_ref, slope_ref, up_near_ref, up_far_ref, mid_ref = rest[:6]
        rest = rest[6:]
    g_ref, sums_ref, out_ref = rest[:3]
    rest = rest[3:]
    if with_mlp:
        mlp_outs, rest = rest[:6], rest[6:]
        acc_ref, rest = rest[0], rest[1:]
    a_t_ref, gr_t_ref, total_ref, landed_ref, halo_send, halo_recv, *scratch = rest
    scatter = Scatter(out_ref, *scratch)
    pieces, rows = scatter.pieces, gr_ref.shape[0]
    half = gr_ref.shape[1] // 2
    spill = REACH - rows
    step = pl.program_id(0)
    moves = [
        (1, right_ref, pl.ds(0, rows), pl.ds(0, rows), 0),
        (-1, left_ref, pl.ds(spill, rows), pl.ds(0, rows), 0),
        (2, right_ref, pl.ds(rows, spill), pl.ds(0, spill), 0),
        (-2, left_ref, pl.ds(0, spill), pl.ds(0, spill), rows - spill),
    ]
    place, size = lax.axis_index("tp"), lax.axis_size("tp")
    inside = lambda other: jnp.logical_and(other >= 0, other < size)

    def halo_copy(index):
        distance, ref, source, target, _ = moves[index]
        return pltpu.make_async_remote_copy(
            src_ref=ref.at[source, :], dst_ref=landed_ref.at[index, target, :], send_sem=halo_send.at[index],
            recv_sem=halo_recv.at[index], device_id={"tp": place + distance}, device_id_type=MESH,
        )

    @pl.when(step == 0)
    def _():
        scatter.near.greet(all_tp=True)
        for index, (distance, *_) in enumerate(moves):

            @pl.when(inside(place + distance))
            def _():
                halo_copy(index).start()

        a_t_ref[...] = a_ref[...].T
        gr_t_ref[...] = gr_ref[...].T

    @pl.when(step < pieces)
    def _():
        piece = scatter.place(step)
        for part, ref in ((slice(0, half), scatter.keep), (slice(half, 2 * half), scatter.away)):
            from_q = nn(a_t_ref[part, REACH : REACH + rows], gq_ref[...])
            from_o = nn(gr_t_ref[part, :], o_ref[...])
            ref[piece, :, :PAIR] = from_q[:, :PAIR].astype(BF16)
            ref[piece, :, PAIR : 4 * PAIR] = nn(a_t_ref[part, :], gkv_ref[...]).astype(BF16)
            ref[piece, :, 4 * PAIR : 5 * PAIR] = (from_q[:, PAIR:] + from_o[:, :PAIR]).astype(BF16)
            ref[piece, :, 5 * PAIR :] = from_o[:, PAIR:].astype(BF16)
        scatter.core(step)

        @pl.when(step > 0)
        def _():
            scatter.first(step - 1)

        @pl.when(step > 1)
        def _():
            scatter.second(step - 2)

    @pl.when(step == pieces - 1)
    def _():
        scatter.first(pieces - 1)
        scatter.last(0)
        scatter.second(pieces - 2)
        total_ref[...] = mine_ref[...]
        for index, (distance, _, _, target, start) in enumerate(moves):

            @pl.when(inside(place + distance))
            def _():
                halo_copy(index).wait_send()

            @pl.when(inside(place - distance))
            def _():
                halo_copy(index).wait_recv()
                total_ref[pl.ds(start, target.size), :] += landed_ref[index, target, :].astype(F32)

        scatter.last(1)
        total = total_ref[...]
        hat, scale = row_norm(x_ref[...])
        g_ref[...] = g1_ref[...] + row_norm_back(total * line(feats_ref, rows_of.ln_gain(layer, 0)), hat, scale)
        sums_ref[...] = jnp.zeros_like(sums_ref)
        sums_ref[0:1, :] = jnp.sum(total * hat, axis=0, keepdims=True)
        sums_ref[1:2, :] = jnp.sum(total, axis=0, keepdims=True)
        scatter.second(pieces - 1)

    if with_mlp:

        @pl.when(step >= pieces)
        def _():
            mlp_back_work(
                g_ref, down_near_ref, down_far_ref, slope_ref, up_near_ref, up_far_ref, mid_ref, feats_ref, *mlp_outs,
                acc_ref, rows_of.ln_gain(layer - 1, 1), step == pieces, step == 2 * pieces - 1,
            )

    @pl.when(step == pl.num_programs(0) - 1)
    def _():
        scatter.last(pieces - 2)
        scatter.last(pieces - 1)
        scatter.done()


def give_back(a_win, gq, gkv, gr, o, x, g1, mine, left, right, feats, rows_of, layer, collective, before=None):
    window, width = a_win.shape
    rows = gr.shape[0]
    half = width // 2
    pieces = gq.shape[1] // (2 * PAIR)
    full = whole((rows, width))
    turned = lambda height, wide: pl.BlockSpec(
        (height, wide), lambda step: (0, lax.rem(jnp.minimum(step, pieces - 1) + 1, pieces))
    )
    in_specs = [
        whole((window, width)), turned(rows, 2 * PAIR), turned(window, 3 * PAIR), full, turned(rows, 2 * PAIR), full, full,
        full, whole((REACH, width)), whole((REACH, width)), whole(feats.shape),
    ]
    operands = [a_win, gq, gkv, gr, o, x, g1, mine, left, right, feats]
    result, extra = scatter_specs(pieces, half // 4, 6 * PAIR)
    out_specs = [full, whole((8, width)), whole(result.shape)]
    out_shape = [shaped((rows, width), F32), shaped((8, width), F32), result]
    scratch = []
    if before is not None:
        near, far, slope, mid = before
        hidden = slope.shape[1]
        wide = hidden // pieces
        late = lambda height, every=1, first=0: pl.BlockSpec(
            (height, wide), lambda step: (0, jnp.maximum(step - pieces, 0) * every + first)
        )
        in_specs += [late(half, 2, 1), late(half, 2, 1), late(rows), late(half, 2), late(half, 2), full]
        operands += [near, far, slope, near, far, mid]
        out_specs += [full, late(rows), late(1), full, full, whole((8, width))]
        out_shape += [
            shaped((rows, width)), shaped((rows, hidden)), shaped((1, hidden), F32), shaped((rows, width), F32),
            shaped((rows, width)), shaped((8, width), F32),
        ]
        scratch = [pltpu.VMEM((rows, width), F32)]
    scratch += [
        pltpu.VMEM((width, window), BF16), pltpu.VMEM((width, rows), BF16), pltpu.VMEM((rows, width), F32),
        pltpu.VMEM((4, rows, width), BF16), pltpu.SemaphoreType.DMA((4,)), pltpu.SemaphoreType.DMA((4,)), *extra,
    ]
    return pl.pallas_call(
        functools.partial(give_back_kernel, rows_of=rows_of, layer=layer, with_mlp=before is not None),
        grid=(pieces if before is None else 2 * pieces,),
        in_specs=in_specs,
        out_specs=out_specs,
        out_shape=out_shape,
        scratch_shapes=scratch,
        compiler_params=params(collective),
        cost_estimate=pl.CostEstimate(
            flops=2 * width * width * (2 * window + 2 * rows), bytes_accessed=20 * width * width, transcendentals=0
        ),
        name="give_back",
    )(*operands)


def flip(array, bit, axis="fsdp"):
    size = lax.axis_size(axis)
    return lax.ppermute(array, axis, [(i, i ^ (1 << bit)) for i in range(size)])


def ring(array):
    size = lax.axis_size("tp")
    return lax.ppermute(array, "tp", [(i, (i + 1) % size) for i in range(size)])


def hop(array, distance):
    size = lax.axis_size("tp")
    return lax.ppermute(array, "tp", [(i, i + distance) for i in range(size) if 0 <= i + distance < size])


def bits_of(size):
    return size.bit_length() - 1


def row_bits(first_top):
    count = bits_of(lax.axis_size("fsdp"))
    tops = [count - 1, count - 2] if first_top else [count - 2, count - 1]
    return list(range(1, count - 2)), tops


def gather_by_permutes(block, first_top):
    pieces = [block]
    for _ in range(lax.axis_size("tp") - 1):
        pieces.append(ring(pieces[-1]))
    block = jnp.concatenate(pieces, axis=1)
    low, tops = row_bits(first_top)
    have = []
    for bit in low + tops:
        axis = sum(other > bit for other in have)
        block = jnp.stack([block, flip(block, bit)], axis=axis)
        have.append(bit)
    block = block.reshape((-1, block.shape[-1]))
    return block, flip(block, 0)


def add(left, right, kind=BF16):
    return (left.astype(F32) + right.astype(F32)).astype(kind)


def reduce_by_permutes(keep, send, first_top):
    low, tops = row_bits(first_top)
    block = add(keep, flip(send, 0))
    order = tops + low[::-1]
    have = sorted(order, reverse=True)
    block = block.reshape((2,) * len(have) + (-1, block.shape[-1]))
    for bit in order:
        axis = have.index(bit)
        mine = lax.index_in_dim(block, 0, axis, keepdims=False)
        other = lax.index_in_dim(block, 1, axis, keepdims=False)
        block = add(mine, flip(other, bit))
        have.remove(bit)
    pieces = jnp.split(block, lax.axis_size("tp"), axis=1)
    total = pieces[1]
    for piece in pieces[2:]:
        total = add(ring(total), piece)
    return add(ring(total), pieces[0], F32)


def attn_shard(w_qkv, w_out):
    q, k, v = (w_qkv[:, which] for which in range(3))
    o = w_out.T
    return side(q[:, :PAIR], k[:, :PAIR], v[:, :PAIR], k[:, PAIR:], v[:, PAIR:], q[:, PAIR:], o[:, PAIR:], o[:, :PAIR])


def attn_unshard(block):
    tile = lambda start, wide=PAIR: block[:, start : start + wide]
    q = side(tile(0), tile(4 * PAIR, HD))
    k = side(tile(PAIR), tile(3 * PAIR, HD))
    v = side(tile(2 * PAIR), tile(3 * PAIR + HD, HD))
    o = side(tile(5 * PAIR), tile(4 * PAIR + HD, HD))
    return jnp.stack([q, k, v], axis=1), o.T


def body(
    tokens, segment_ids, patch_pos, row_table, col_table, ln_gain, ln_bias, qkv_bias, qk_gain, query_bias, out_bias,
    fc1_bias, fc2_bias, w_qkv, w_out, w_fc1, w_fc2, cotangent,
):
    layers = w_qkv.shape[0]
    rows, width = tokens.shape
    half = width // 2
    fsdp, tp = lax.axis_size("fsdp"), lax.axis_size("tp")
    f_index, t_index = lax.axis_index("fsdp"), lax.axis_index("tp")
    hidden = fc1_bias.shape[1] * fsdp * tp
    grid = row_table.shape[0]
    fine = width // (fsdp * tp)
    parts = hidden // width
    in_kernel = fsdp == 8
    rows_of = Rows(layers, grid)

    place = jnp.arange(width, dtype=jnp.int32)
    chunk = width // fsdp
    slot = place // chunk
    away = (slot % (fsdp // 2)) * 2 + slot // (fsdp // 2)
    feature_at = (f_index ^ away) * chunk + place % chunk
    head_cols = width // tp
    spot = jnp.arange(tp * 3 * PAIR, dtype=jnp.int32)
    tile, part = spot % (3 * PAIR) // PAIR, spot % PAIR // HD
    head = jnp.where(tile == 0, part, jnp.where(tile == part + 1, 2, -fsdp * tp))
    head_at = ((t_index - spot // (3 * PAIR)) % tp) * head_cols + head * HD + spot % HD
    far = place // fine
    arrived_at = ((f_index ^ (far // tp)) * tp + (t_index ^ (far % tp))) * fine + place % fine
    to_feature = (arrived_at[:, None] == feature_at[None, :]).astype(BF16)
    to_head = (arrived_at[:, None] == head_at[None, :]).astype(BF16)
    reorder = (place[:, None] == feature_at[None, :]).astype(BF16)
    device = jnp.arange(fsdp * tp, dtype=jnp.int32)
    device_at = (f_index ^ (device // tp)) * tp + (t_index ^ (device % tp))
    wanted = ((t_index - device // fsdp) % tp) * fsdp + device % fsdp
    to_hidden = (wanted[:, None] == device_at[None, :]).astype(BF16)

    shares = [row_table, col_table] + [
        item.reshape(-1, fine) for item in (ln_gain, ln_bias, out_bias, fc2_bias, qkv_bias, qk_gain, query_bias)
    ]
    small = jnp.concatenate(shares + [fc1_bias.reshape(layers * parts, fine)], axis=0)
    count = small.shape[0]
    flat = small.reshape(1, -1)
    for bit in range(bits_of(tp)):
        flat = jnp.concatenate([flat, flip(flat, bit, "tp")], axis=0)
    for bit in range(bits_of(fsdp)):
        flat = jnp.concatenate([flat, flip(flat, bit)], axis=0)
    gathered = flat.reshape(fsdp * tp, count, fine)
    lined = gathered.transpose(1, 0, 2).reshape(count, width)
    wide = 2 * grid + 6 * layers
    feats = jnp.dot(lined[:wide], to_feature, preferred_element_type=F32)
    heads = jnp.dot(lined[wide : wide + 6 * layers], to_head, preferred_element_type=F32)
    up_shift = jnp.einsum(
        "or,rlsi->losi",
        to_hidden,
        gathered[:, wide + 6 * layers :].reshape(fsdp * tp, layers, parts, fine),
        preferred_element_type=F32,
    ).reshape(layers, 1, hidden)

    attn_shards = [attn_shard(w_qkv[layer], w_out[layer]) for layer in range(layers)]
    mlp_shards = [side(w_fc1[layer], w_fc2[layer].T) for layer in range(layers)]
    if in_kernel:
        attn_near, attn_far = gather_alone(attn_shards[0], tp, half, 0)

    grid_ids = jnp.arange(grid, dtype=jnp.int32)
    row_hot = patch_pos[0][:, None] == grid_ids[None, :]
    col_hot = patch_pos[1][:, None] == grid_ids[None, :]
    residual = (
        jnp.dot(tokens, reorder, preferred_element_type=F32)
        + jnp.dot(row_hot.astype(BF16), feats[:grid].astype(BF16), preferred_element_type=F32)
        + jnp.dot(col_hot.astype(BF16), feats[grid : 2 * grid].astype(BF16), preferred_element_type=F32)
    )
    segments = segment_ids[0]
    padded = jnp.pad(segments, (REACH, REACH), constant_values=-1)
    seg_k = lax.dynamic_slice_in_dim(padded, t_index * rows, rows + 2 * REACH).reshape(-1, 1)
    seg_q = lax.dynamic_slice_in_dim(segments, t_index * rows, rows).reshape(1, -1)
    spill = REACH - rows

    hat, _ = row_norm(residual)
    a_own = (hat * feats[rows_of.ln_gain(0, 0)] + feats[rows_of.ln_bias(0, 0)]).astype(BF16)
    saved, weights = [], []
    for layer in range(layers):
        if in_kernel:
            a_win = halo(a_own, 10 + layer)
            *kept, mid, m, mlp_near, mlp_far = attend(
                a_win, attn_near, attn_far, heads, feats, residual, seg_k, seg_q, rows_of, layer, mlp_shards[layer],
                20 + layer,
            )
        else:
            a_win = jnp.concatenate(
                [hop(a_own[rows - spill :], 2), hop(a_own, 1), a_own, hop(a_own, -1), hop(a_own[:spill], -2)], axis=0
            )
            attn_near, attn_far = gather_by_permutes(attn_shards[layer], layer % 2 == 0)
            *kept, mid, m = attend(a_win, attn_near, attn_far, heads, feats, residual, seg_k, seg_q, rows_of, layer)
            mlp_near, mlp_far = gather_by_permutes(mlp_shards[layer], layer % 2 == 1)
        weights.append((attn_near, attn_far, mlp_near, mlp_far))
        if in_kernel and layer + 1 < layers:
            act, slope, x2, a_own, attn_near, attn_far = mlp(
                m, mid, mlp_near, mlp_far, up_shift[layer], feats, rows_of, layer, attn_shards[layer + 1], 30 + layer
            )
        else:
            act, slope, x2, a_own = mlp(m, mid, mlp_near, mlp_far, up_shift[layer], feats, rows_of, layer)
        saved.append((residual, a_win, kept, mid, m, act, slope))
        residual = x2

    restore = functools.partial(
        lax.dot_general, dimension_numbers=(((1,), (1,)), ((), ())), precision=HIGHEST, preferred_element_type=F32
    )
    exact = reorder.astype(F32)
    activations = restore(residual, exact)
    grad = jnp.dot(cotangent, exact, precision=HIGHEST, preferred_element_type=F32)
    kept_sums = [None] * layers
    w_qkv_grad, w_out_grad, w_fc1_grad, w_fc2_grad = ([None] * layers for _ in range(4))
    back = None
    for layer in reversed(range(layers)):
        attn_near, attn_far, mlp_near, mlp_far = weights[layer]
        x, a_win, kept, mid, m, act, slope = saved[layer]
        *stored, o = kept
        if back is None:
            back = mlp_back(grad, mlp_near, mlp_far, slope, mid, feats, rows_of.ln_gain(layer, 1))
        gz, gh, up_grad, g1, gr, mlp_small = back
        back = None
        if in_kernel:
            gq, gkv, mine, left, right, attn_small, mlp_block = attend_back_scatter(
                gr, stored, attn_near, attn_far, heads, m, gh, gz, act, rows_of, layer, 40 + layer
            )
            before = None
            if layer:
                before = (*weights[layer - 1][2:], saved[layer - 1][6], saved[layer - 1][3])
            grad, norm_sums, attn_block, *back = give_back(
                a_win, gq, gkv, gr, o, x, g1, mine, left, right, feats, rows_of, layer, 50 + layer, before
            )
            back = back or None
            norm_sums = norm_sums[0], norm_sums[1]
        else:
            mlp_block = reduce_by_permutes(*mlp_weight_grads(m, gh, gz, act), layer % 2 == 0)
            gq, gkv, mine, left, right, attn_small = attend_back(gr, stored, attn_near, attn_far, heads, rows_of, layer)
            attn_block = reduce_by_permutes(*attn_weight_grads(a_win, gq, gkv, gr, o), layer % 2 == 1)
            ends = jnp.concatenate([hop(right[rows:], 2), hop(left[:spill], -2)], axis=0).astype(F32)
            attn_grad = mine + hop(right[:rows], 1).astype(F32) + hop(left[spill:], -1).astype(F32) + ends
            hat, scale = row_norm(x)
            grad = g1 + row_norm_back(attn_grad * feats[rows_of.ln_gain(layer, 0)], hat, scale)
            norm_sums = jnp.sum(attn_grad * hat, axis=0), jnp.sum(attn_grad, axis=0)
        middle = mlp_block.shape[1] // 2
        w_fc1_grad[layer], w_fc2_grad[layer] = mlp_block[:, :middle], mlp_block[:, middle:].T
        w_qkv_grad[layer], w_out_grad[layer] = attn_unshard(attn_block)
        kept_sums[layer] = (*norm_sums, mlp_small, attn_small, up_grad.reshape(parts, width))

    token_grad = restore(grad, exact)
    row_grad = jnp.einsum("tg,td->gd", row_hot.astype(F32), grad, precision=HIGHEST)
    col_grad = jnp.einsum("tg,td->gd", col_hot.astype(F32), grad, precision=HIGHEST)
    featured = [row_grad, col_grad]
    featured.append(jnp.stack([item for a_gain, _, sums, _, _ in kept_sums for item in (a_gain, sums[2])]))
    featured.append(jnp.stack([item for _, a_shift, sums, _, _ in kept_sums for item in (a_shift, sums[3])]))
    featured.append(jnp.stack([sums[1] for _, _, sums, _, _ in kept_sums]))
    featured.append(jnp.stack([sums[0] for _, _, sums, _, _ in kept_sums]))
    headed = jnp.concatenate(
        [sums[3:6] for _, _, _, sums, _ in kept_sums]
        + [sums[0:2] for _, _, _, sums, _ in kept_sums]
        + [sums[2:3] for _, _, _, sums, _ in kept_sums]
    )
    spread = jnp.concatenate(
        [restore(jnp.concatenate(featured), to_feature.astype(F32)), restore(headed, to_head.astype(F32))]
    )
    spread = spread.reshape(-1, fsdp * tp, fine).transpose(1, 0, 2)
    up_all = jnp.stack([item[4] for item in kept_sums]).reshape(layers, fsdp * tp, parts * fine)
    up_all = jnp.einsum("or,lok->rlk", to_hidden.astype(F32), up_all, precision=HIGHEST)
    flat = jnp.concatenate([spread.reshape(fsdp * tp, -1), up_all.reshape(fsdp * tp, -1)], axis=1)
    for bit in reversed(range(bits_of(fsdp))):
        middle = flat.shape[0] // 2
        flat = flat[:middle] + flip(flat[middle:], bit)
    for bit in reversed(range(bits_of(tp))):
        middle = flat.shape[0] // 2
        flat = flat[:middle] + flip(flat[middle:], bit, "tp")
    flat = flat.reshape(-1)
    sizes = [grid, grid, 2 * layers, 2 * layers, layers, layers, 3 * layers, 2 * layers, layers, layers * parts]
    shapes = [
        (grid, fine), (grid, fine), (layers, 2, fine), (layers, 2, fine), (layers, fine), (layers, fine),
        (layers, 3, fine), (layers, 2, fine), (layers, fine), (layers, parts * fine),
    ]
    found = []
    start = 0
    for lines, shape in zip(sizes, shapes):
        found.append(flat[start : start + lines * fine].reshape(shape))
        start += lines * fine
    rows_g, cols_g, gain_g, shift_g, out_g, last_g, proj_g, head_gain_g, head_shift_g, up_g = found
    return (
        activations, token_grad, rows_g, cols_g, gain_g, shift_g, proj_g, head_gain_g, head_shift_g, out_g, up_g, last_g,
        jnp.stack(w_qkv_grad), jnp.stack(w_out_grad), jnp.stack(w_fc1_grad), jnp.stack(w_fc2_grad),
    )


def solution(mesh):
    both = ("fsdp", "tp")
    in_specs = (
        P(both, None), P("fsdp", None), P(None, both), P(None, both), P(None, both), P(None, None, both),
        P(None, None, both), P(None, None, both), P(None, None, both), P(None, both), P(None, both), P(None, both),
        P(None, both), P(None, "fsdp", None, "tp"), P(None, "tp", "fsdp"), P(None, "fsdp", "tp"), P(None, "tp", "fsdp"),
        P(both, None),
    )
    out_specs = (
        P(both, None), P(both, None), P(None, both), P(None, both), P(None, None, both), P(None, None, both),
        P(None, None, both), P(None, None, both), P(None, both), P(None, both), P(None, both), P(None, both),
        P(None, "fsdp", None, "tp"), P(None, "tp", "fsdp"), P(None, "fsdp", "tp"), P(None, "tp", "fsdp"),
    )
    return jax.shard_map(body, mesh=mesh, in_specs=in_specs, out_specs=out_specs, check_vma=False)
```

```python
import functools

import jax
import jax.numpy as jnp
from jax import lax
from jax.experimental import pallas as pl
from jax.experimental.pallas import tpu as pltpu
from jax.sharding import PartitionSpec as P

HD = 64
PAIR = 128
REACH = 384
EPS = 1e-06
FILL = -1e30
ROOT_HALF = 0.7071067811865476
INV_ROOT_TWO_PI = 0.3989422804014327
HIGHEST = lax.Precision.HIGHEST
F32 = jnp.float32
BF16 = jnp.bfloat16
MESH = pl.DeviceIdType.MESH
ANY = pl.BlockSpec(memory_space=pl.ANY)


def nn(left, right):
    return lax.dot_general(left, right, (((1,), (0,)), ((), ())), preferred_element_type=F32)


def nt(left, right):
    return lax.dot_general(left, right, (((1,), (1,)), ((), ())), preferred_element_type=F32)


def halves(array):
    middle = array.shape[1] // 2
    return array[:, :middle], array[:, middle:]


def row_norm(value):
    centered = value - jnp.mean(value, axis=-1, keepdims=True)
    scale = lax.rsqrt(jnp.mean(centered * centered, axis=-1, keepdims=True) + EPS)
    return centered * scale, scale


def row_norm_back(grad_hat, normed, scale):
    return scale * (
        grad_hat
        - jnp.mean(grad_hat, axis=-1, keepdims=True)
        - normed * jnp.mean(grad_hat * normed, axis=-1, keepdims=True)
    )


def head_mean(value, exact=False):
    wide = value.shape[1]
    rows = lax.broadcasted_iota(jnp.int32, (wide, wide), 0) // HD
    cols = lax.broadcasted_iota(jnp.int32, (wide, wide), 1) // HD
    spread = jnp.where(rows == cols, 1.0 / HD, 0.0).astype(BF16)
    high = value.astype(BF16)
    mean = nn(high, spread)
    if exact:
        mean += nn((value - high.astype(F32)).astype(BF16), spread)
    return mean


def head_norm(value):
    centered = value - head_mean(value, exact=True)
    scale = lax.rsqrt(head_mean(centered * centered) + EPS)
    return centered * scale, scale


def head_norm_back(grad_hat, normed, scale):
    return scale * (grad_hat - head_mean(grad_hat) - normed * head_mean(grad_hat * normed))


def only(array, part):
    return jnp.where(lax.broadcasted_iota(jnp.int32, (1, PAIR), 1) // HD == part, array, jnp.zeros_like(array))


def side(*parts):
    return jnp.concatenate(parts, axis=1)


def whole(shape):
    return pl.BlockSpec(shape, lambda step: (0,) * len(shape))


def column(height, wide, every=1, first=0):
    return pl.BlockSpec((height, wide), lambda step: (0, step * every + first))


def piece_of(layer, height, wide, first=0):
    return pl.BlockSpec((None, None, height, wide), lambda step: (layer, step, 0, first))


def slab(layer, height, wide):
    return pl.BlockSpec((None, height, wide), lambda step: (layer, 0, step))


def heads_of(layer):
    return pl.BlockSpec((None, None, HEADS, 3 * PAIR), lambda step: (step, layer, 0, 0))


def sheet(layer, height, wide):
    return pl.BlockSpec((None, height, wide), lambda step: (layer, 0, 0))


def shaped(shape, kind=BF16):
    return jax.ShapeDtypeStruct(shape, kind)


class Neighbours:
    def __init__(self):
        fsdp, tp = lax.axis_index("fsdp"), lax.axis_index("tp")
        self.size = lax.axis_size("tp")
        self.tp = tp
        self.x, self.y, self.core = ({"fsdp": jnp.bitwise_xor(fsdp, bit)} for bit in (2, 4, 1))

    def along(self, distance):
        return {"tp": lax.rem(self.tp + distance, self.size)}

    def greet(self):
        targets = [self.x, self.y, self.core] + [self.along(distance) for distance in range(1, self.size)]
        barrier = pltpu.get_barrier_semaphore()
        for target in targets:
            pl.semaphore_signal(barrier, inc=1, device_id=target, device_id_type=MESH)
        pl.semaphore_wait(barrier, len(targets))


class Plan:
    LINKS = {"x": (45.5e3, 1.5), "y": (45.5e3, 1.5), "z": (45.5e3, 2.2), "core": (600e3, 1.0)}

    def __init__(self, depth):
        self.depth, self.clock = depth, 0.0
        self.free, self.here, self.jobs, self.table = dict.fromkeys(self.LINKS, 0.0), {}, [], {}

    def add(self, rank, work, needs, copies, gives):
        self.jobs.append((rank, len(self.jobs), work, needs, copies, gives))
        self.jobs.sort(key=lambda job: job[:2])

    def carry(self, copies, gives):
        end = self.clock
        for link, size in copies:
            rate, latency = self.LINKS[link]
            self.free[link] = max(self.free[link], self.clock) + size / rate
            end = max(end, self.free[link] + latency)
        self.here[gives] = end

    def slot(self, *at):
        found = True
        while found:
            found = False
            for job in self.jobs:
                _, _, work, needs, copies, gives = job
                ready = all(self.here.get(need, float("inf")) <= self.clock for need in needs)
                if ready and all(self.free[link] - self.clock < self.depth for link, _ in copies):
                    self.carry(copies, gives)
                    self.table.setdefault(at, []).append(work)
                    self.jobs.remove(job)
                    found = True
                    break

    def wait(self, key, work, *at):
        self.slot(*at)
        while self.here.get(key, float("inf")) > self.clock:
            self.clock += 0.25
            self.slot(*at)
        self.table.setdefault(at, []).append(work)

    def spend(self, time):
        self.clock += time


def turn(index, pieces):
    if isinstance(index, int):
        return (index + 1) // 2 if index % 2 else (pieces - index // 2) % pieces
    return jnp.where(lax.rem(index, 2) == 1, (index + 1) // 2, lax.rem(pieces - index // 2, pieces))


class Gather:
    KINDS = 7

    def __init__(self, peers, shard, near, far, send, recv, local, near_out, far_out, stored):
        self.peers, self.shard, self.near, self.far = peers, shard, near, far
        self.send, self.recv, self.local = send, recv, local
        self.outs, self.stored = (near_out, far_out), stored
        self.chunk, self.wide = shard.shape
        self.pieces = near.shape[0]

    def at(self, piece, start, count, half=None):
        first, wide = (0, self.wide) if half is None else (half * (self.wide // 2), self.wide // 2)
        return self.near.at[piece, pl.ds(start * self.chunk, count * self.chunk), pl.ds(first, wide)]

    def copy(self, piece, kind, source, target, device):
        return pltpu.make_async_remote_copy(
            src_ref=source, dst_ref=target, send_sem=self.send.at[piece, kind], recv_sem=self.recv.at[piece, kind],
            device_id=device, device_id_type=MESH,
        )

    def copies(self, piece, stage):
        if stage == "z":
            return [self.copy(piece, 0, self.shard, self.at(piece, 0, 1), self.peers.along(piece))] if piece else []
        if stage == "first":
            half = self.wide // 2
            left = self.shard.at[:, pl.ds(0, half)] if piece == 0 else self.at(piece, 0, 1, 0)
            right = self.shard.at[:, pl.ds(half, half)] if piece == 0 else self.at(piece, 0, 1, 1)
            return [
                self.copy(piece, 1, left, self.at(piece, 1, 1, 0), self.peers.x),
                self.copy(piece, 2, right, self.at(piece, 2, 1, 1), self.peers.y),
            ]
        if stage == "second":
            return [
                self.copy(piece, 3, self.at(piece, 0, 2, 0), self.at(piece, 2, 2, 0), self.peers.y),
                self.copy(piece, 4, self.at(piece, 0, 1, 1), self.at(piece, 1, 1, 1), self.peers.x),
                self.copy(piece, 5, self.at(piece, 2, 1, 1), self.at(piece, 3, 1, 1), self.peers.x),
            ]
        return [self.copy(piece, 6, self.near.at[piece], self.far.at[piece], self.peers.core)]

    def start(self, piece, stage):
        for copy in self.copies(piece, stage):
            copy.start()

    def arrived(self, piece, stage):
        for copy in self.copies(piece, stage):
            copy.wait_recv()

    def store(self, piece):
        return [
            pltpu.make_async_copy(source.at[piece], target.at[piece], self.stored.at[piece, which])
            for which, (source, target) in enumerate(zip((self.near, self.far), self.outs))
        ]

    def own(self):
        return pltpu.make_async_copy(self.shard, self.at(0, 0, 1), self.local)

    def sent(self, piece):
        self.start(piece, "z")

    def landed(self, piece):
        self.arrived(piece, "z")
        self.start(piece, "first")

    def crossed(self, piece):
        self.arrived(piece, "first")
        self.start(piece, "second")

    def shared(self, piece):
        self.arrived(piece, "second")
        self.start(piece, "core")

    def need(self, piece):
        self.arrived(piece, "core")
        for copy in self.store(piece):
            copy.start()

    def jobs(self, plan, index):
        size = self.chunk * self.wide * 2
        for place in range(self.pieces):
            piece = turn(place, self.pieces)
            key = (index, piece)
            rank = index * self.pieces + place
            if piece:
                plan.add(rank, (self.sent, piece), [], [("z", size * self.pieces / (self.pieces - 1))], ("z", *key))
            both = lambda count: [("x", count * size), ("y", count * size)]
            plan.add(rank, (self.landed, piece), [("z", *key)] if piece else [], both(0.5), ("first", *key))
            plan.add(rank, (self.crossed, piece), [("first", *key)], both(1), ("second", *key))
            plan.add(rank, (self.shared, piece), [("second", *key)], [("core", 4 * size)], ("core", *key))

    def end(self):
        for piece in range(self.pieces):
            for stage in ("z", "first", "second", "core"):
                for copy in self.copies(piece, stage):
                    copy.wait_send()
            for copy in self.store(piece):
                copy.wait()


class Halo:
    def __init__(self, ref, rows, send, recv):
        self.ref, self.send, self.recv = ref, send, recv
        self.place, self.size = lax.axis_index("tp"), lax.axis_size("tp")
        spill = REACH - rows
        self.moves = [
            (1, pl.ds(REACH, rows), pl.ds(spill, rows)),
            (-1, pl.ds(REACH, rows), pl.ds(REACH + rows, rows)),
            (2, pl.ds(2 * rows, spill), pl.ds(0, spill)),
            (-2, pl.ds(REACH, spill), pl.ds(REACH + 2 * rows, spill)),
        ]

    def inside(self, distance):
        other = self.place + distance
        return jnp.logical_and(other >= 0, other < self.size)

    def copy(self, index):
        distance, source, target = self.moves[index]
        return pltpu.make_async_remote_copy(
            src_ref=self.ref.at[source, :], dst_ref=self.ref.at[target, :], send_sem=self.send.at[index],
            recv_sem=self.recv.at[index], device_id={"tp": self.place + distance}, device_id_type=MESH,
        )

    def begin(self):
        for index, (distance, _, target) in enumerate(self.moves):

            @pl.when(self.inside(distance))
            def _():
                self.copy(index).start()

            @pl.when(jnp.logical_not(self.inside(-distance)))
            def _():
                self.ref[target, :] = jnp.zeros((target.size, self.ref.shape[1]), BF16)

    def end(self, _=None):
        for index, (distance, _, _) in enumerate(self.moves):

            @pl.when(self.inside(distance))
            def _():
                self.copy(index).wait_send()

            @pl.when(self.inside(-distance))
            def _():
                self.copy(index).wait_recv()


def params(collective=None):
    if collective is None:
        return pltpu.CompilerParams()
    return pltpu.CompilerParams(collective_id=collective, has_side_effects=True)


LN_GAIN, LN_BIAS, OUT_BIAS, LAST_BIAS, FEATS = (0, 1), (2, 3), 4, 5, 6
PROJ_BIAS, HEAD_GAIN, HEAD_BIAS, HEADS = (0, 1, 2), (3, 4), 5, 6


def line(ref, row, start=0, wide=None):
    return ref[pl.ds(row, 1), pl.ds(start, wide or ref.shape[1] - start)]


def attend_work(
    a_ref, near_ref, far_ref, heads_ref, feats_ref, x_ref, q_ref, kv_ref, q_hat_ref, k_hat_ref, q_scale_ref, k_scale_ref,
    p_ref, o_ref, mid_ref, m_ref, mask_ref, acc_ref, opening, closing, hook,
):
    rows = q_ref.shape[0]
    half = near_ref.shape[0]

    @pl.when(opening)
    def _():
        acc_ref[...] = jnp.zeros_like(acc_ref)

    tile = lambda row, which: line(heads_ref, row, which * PAIR, PAIR)
    bias, (q_gain, k_gain), q_shift = PROJ_BIAS, HEAD_GAIN, HEAD_BIAS
    near, distant = halves(a_ref[...])
    own, own_far = halves(a_ref[REACH : REACH + rows, :])
    kv = nn(near, near_ref[:, PAIR : 4 * PAIR]) + nn(distant, far_ref[:, PAIR : 4 * PAIR])
    kv += side(tile(bias[1], 0), tile(bias[2], 0), tile(bias[1], 1) + tile(bias[2], 2))
    q = side(
        nn(own, near_ref[:, :PAIR]) + nn(own_far, far_ref[:, :PAIR]),
        nn(own, near_ref[:, 4 * PAIR : 5 * PAIR]) + nn(own_far, far_ref[:, 4 * PAIR : 5 * PAIR]),
    ) + line(heads_ref, bias[0], 0, 2 * PAIR)
    q_hat, q_scale = head_norm(q)
    k_hat, k_scale = head_norm(side(kv[:, :PAIR], kv[:, 2 * PAIR :]))
    qn = (q_hat * line(heads_ref, q_gain, 0, 2 * PAIR) + line(heads_ref, q_shift, 0, 2 * PAIR)).astype(BF16)
    qn = side(qn[:, :PAIR], only(qn[:, PAIR:], 0))
    kn = (k_hat * line(heads_ref, k_gain, 0, 2 * PAIR)).astype(BF16)
    v = kv[:, PAIR:].astype(BF16)
    low = lax.broadcasted_iota(jnp.int32, (1, PAIR), 1) < HD
    first, second = kn[:, :PAIR], jnp.where(low, kn[:, PAIR:], v[:, PAIR:])
    values = v[:, :PAIR]
    q_ref[...] = qn
    kv_ref[...] = side(first, values, second)
    q_hat_ref[...] = q_hat.astype(BF16)
    k_hat_ref[...] = k_hat.astype(BF16)
    q_scale_ref[...] = q_scale.astype(BF16)
    k_scale_ref[...] = k_scale.astype(BF16)
    hook(1)
    values_t, second_t = values.T, second.T
    mixed = []
    for head in range(3):
        if head:
            hook(head + 1)
        keys = (first, first, second)[head]
        query = only(qn[:, PAIR * (head // 2) : PAIR * (head // 2 + 1)] * HD ** (-0.5), head % 2).astype(BF16)
        scores = nt(keys, query) + mask_ref[...]
        weights = jnp.exp(scores - jnp.max(scores, axis=0, keepdims=True))
        total = jnp.sum(weights, axis=0, keepdims=True)
        probs = (weights * (1.0 / total)).astype(BF16)
        p_ref[head] = probs
        mixed.append(nn((values_t[:HD], values_t[HD:], second_t[HD:])[head], probs))
    o = jnp.concatenate([jnp.zeros_like(mixed[2]), mixed[2], mixed[0], mixed[1]], axis=0).T.astype(BF16)
    o_ref[...] = o
    acc_ref[:, :half] += nt(o, near_ref[:, 4 * PAIR :])
    acc_ref[:, half:] += nt(o, far_ref[:, 4 * PAIR :])

    @pl.when(closing)
    def _():
        mid = x_ref[...] + (acc_ref[...] + line(feats_ref, OUT_BIAS))
        mid_ref[...] = mid
        hat, _ = row_norm(mid)
        m_ref[...] = (hat * line(feats_ref, LN_GAIN[1]) + line(feats_ref, LN_BIAS[1])).astype(BF16)


def mlp_work(
    m_ref, mid_ref, near_ref, far_ref, up_shift, feats_ref, act_ref, slope_ref, x2_ref, acc_ref, opening, closing, hook,
):
    half = near_ref.shape[0]
    wide = act_ref.shape[1]

    @pl.when(opening)
    def _():
        acc_ref[...] = jnp.zeros_like(acc_ref)

    near, distant = halves(m_ref[...])
    hidden = nn(near, near_ref[:, :wide]) + nn(distant, far_ref[:, :wide]) + up_shift
    hook(1)
    phi = 0.5 * (1.0 + lax.erf(hidden * ROOT_HALF))
    act = (hidden * phi).astype(BF16)
    act_ref[...] = act
    slope_ref[...] = (phi + hidden * jnp.exp(-0.5 * hidden * hidden) * INV_ROOT_TWO_PI).astype(BF16)
    acc_ref[:, :half] += nt(act, near_ref[:, wide:])
    acc_ref[:, half:] += nt(act, far_ref[:, wide:])

    @pl.when(closing)
    def _():
        x2_ref[...] = mid_ref[...] + (acc_ref[...] + line(feats_ref, LAST_BIAS))


def norm_rows(x, feats_ref):
    hat, _ = row_norm(x)
    return (hat * line(feats_ref, LN_GAIN[0]) + line(feats_ref, LN_BIAS[0])).astype(BF16)


def quiet(slot):
    pass


def attend_kernel(
    a_ref, near_ref, far_ref, heads_ref, feats_ref, x_ref, seg_k_ref, seg_q_ref, *rest
):
    step = pl.program_id(0)
    mask_ref = rest[-2]

    @pl.when(step == 0)
    def _():
        mask_ref[...] = jnp.where(seg_k_ref[...] == seg_q_ref[...], 0.0, FILL)

    attend_work(
        a_ref, near_ref, far_ref, heads_ref, feats_ref, x_ref, *rest, step == 0, step == pl.num_programs(0) - 1, quiet
    )


def attend_shapes(rows, window):
    return [
        (rows, 2 * PAIR), (window, 3 * PAIR), (rows, 2 * PAIR), (window, 2 * PAIR), (rows, 2 * PAIR), (window, 2 * PAIR),
    ]


def attend(a_win, near, far, heads, feats, x, seg_k, seg_q, layer):
    window, width = a_win.shape
    rows = x.shape[0]
    half = width // 2
    pieces = near.shape[1]
    outs = attend_shapes(rows, window)
    return pl.pallas_call(
        attend_kernel,
        grid=(pieces,),
        in_specs=[
            whole((window, width)), piece_of(0, half, 6 * PAIR), piece_of(0, half, 6 * PAIR), heads_of(layer), sheet(layer, FEATS, width),
            whole((rows, width)), whole((window, 1)), whole((1, rows)),
        ],
        out_specs=[column(*shape) for shape in outs]
        + [pl.BlockSpec((3, window, rows), lambda step: (step, 0, 0)), column(rows, 2 * PAIR)] + [whole((rows, width))] * 2,
        out_shape=[shaped((height, pieces * wide)) for height, wide in outs]
        + [shaped((3 * pieces, window, rows)), shaped((rows, pieces * 2 * PAIR)), shaped((rows, width), F32), shaped((rows, width))],
        scratch_shapes=[pltpu.VMEM((window, rows), F32), pltpu.VMEM((rows, width), F32)],
        name="attend",
    )(a_win, near, far, heads, feats, x, seg_k, seg_q)


def mlp_kernel(m_ref, mid_ref, near_ref, far_ref, up_shift_ref, feats_ref, *rest):
    step = pl.program_id(0)
    mlp_work(
        m_ref, mid_ref, near_ref, far_ref, up_shift_ref[...], feats_ref, *rest, step == 0, step == pl.num_programs(0) - 1, quiet
    )


def mlp(m, mid, near, far, up_shift, feats, layer):
    rows, width = mid.shape
    half = width // 2
    _, pieces, _, wide = up_shift.shape
    hidden = pieces * wide
    full = whole((rows, width))
    return pl.pallas_call(
        mlp_kernel,
        grid=(pieces,),
        in_specs=[
            full, full, piece_of(0, half, 2 * wide), piece_of(0, half, 2 * wide), piece_of(layer, 1, wide), sheet(layer, FEATS, width),
        ],
        out_specs=[column(rows, wide), column(rows, wide), full],
        out_shape=[shaped((rows, hidden)), shaped((rows, hidden)), shaped((rows, width), F32)],
        scratch_shapes=[pltpu.VMEM((rows, width), F32)],
        name="mlp",
    )(m, mid, near, far, up_shift, feats)


def forward_kernel(
    a_ref, x_ref, heads_ref, feats_ref, up_shift_ref, seg_k_ref, seg_q_ref, attn_shard_ref, mlp_shard_ref,
    q_ref, kv_ref, q_hat_ref, k_hat_ref, q_scale_ref, k_scale_ref, p_ref, o_ref, act_ref, slope_ref, mid_ref, m_ref, x2_ref,
    a_win_out, attn_near_out, attn_far_out, mlp_near_out, mlp_far_out,
    mask_ref, acc_ref, now_ref, a_win_ref, kept, attn_near, attn_far, mlp_near, mlp_far, send, recv, local, stored, halo_send, halo_recv,
):
    layers, pieces, rows = attn_near.shape[0], attn_near.shape[1], a_ref.shape[0]
    step = pl.program_id(0)
    peers = Neighbours()
    halo = lambda layer: Halo(a_win_ref.at[layer], rows, halo_send.at[layer], halo_recv.at[layer])
    keep_window = lambda layer: pltpu.make_async_copy(a_win_ref.at[layer], a_win_out.at[layer], kept.at[layer])

    def window(layer):
        halo(layer).end()
        keep_window(layer).start()

    gathers = []
    for layer in range(layers):
        for which, (shard, near, far, near_out, far_out) in enumerate((
            (attn_shard_ref, attn_near, attn_far, attn_near_out, attn_far_out),
            (mlp_shard_ref, mlp_near, mlp_far, mlp_near_out, mlp_far_out),
        )):
            index = 2 * layer + which
            gathers.append(
                Gather(
                    peers, shard.at[layer], near.at[layer], far.at[layer], send.at[index], recv.at[index], local.at[index],
                    near_out.at[layer], far_out.at[layer], stored.at[index],
                )
            )

    plan = Plan(5.0)
    for index, gather in enumerate(gathers):
        gather.jobs(plan, index)
    halo_size = a_ref.shape[1] * 2 * 2 * rows
    plan.spend(2.5)
    plan.slot(0, 0)
    for layer in range(layers):
        plan.carry([("z", halo_size)], ("halo", layer))
        first = 1 + 2 * layer * pieces
        plan.wait(("halo", layer), (window, layer), *((first, 0) if layer else (0, 1)))
        for index in range(pieces):
            piece = turn(index, pieces)
            plan.wait(("core", 2 * layer, piece), (gathers[2 * layer].need, piece), first + index, 0)
            for slot, time in enumerate((2.0, 1.4, 1.4)):
                plan.spend(time)
                plan.slot(first + index, slot + 1)
            plan.spend(1.4)
        first += pieces
        for index in range(pieces):
            piece = turn(index, pieces)
            plan.wait(("core", 2 * layer + 1, piece), (gathers[2 * layer + 1].need, piece), first + index, 0)
            plan.spend(1.0)
            plan.slot(first + index, 1)
            plan.spend(1.5)
    table = plan.table

    def run(at, slot):
        if (at, slot) in table:

            @pl.when(step == at)
            def _():
                for work, piece in table[at, slot]:
                    work(piece)

    @pl.when(step == 0)
    def _():
        peers.greet()
        mask_ref[...] = jnp.where(seg_k_ref[...] == seg_q_ref[...], 0.0, FILL)
        now_ref[...] = x_ref[...]
        a_win_ref[0, REACH : REACH + rows, :] = a_ref[...]
        for gather in gathers:
            gather.own().start()
        for gather in gathers:
            gather.own().wait()

    run(0, 0)

    @pl.when(step == 0)
    def _():
        halo(0).begin()

    run(0, 1)

    count = jnp.maximum(step - 1, 0)
    layer = count // (2 * pieces)
    inner = lax.rem(count, 2 * pieces)
    index = lax.rem(inner, pieces)
    piece = turn(index, pieces)
    steps_of = lambda which: [
        1 + (2 * layer + which) * pieces + index for layer in range(layers) for index in range(pieces)
    ]

    @pl.when(jnp.logical_and(step > 0, inner < pieces))
    def _():
        def hook(slot):
            for at in steps_of(0):
                run(at, slot)

        hook(0)
        attend_work(
            a_win_ref.at[layer], attn_near.at[layer, piece], attn_far.at[layer, piece], heads_ref.at[piece, layer],
            feats_ref.at[layer], now_ref,
            q_ref, kv_ref, q_hat_ref, k_hat_ref, q_scale_ref, k_scale_ref, p_ref, o_ref, mid_ref.at[layer], m_ref.at[layer],
            mask_ref, acc_ref, index == 0, index == pieces - 1, hook,
        )

    @pl.when(inner >= pieces)
    def _():
        def hook(slot):
            for at in steps_of(1):
                run(at, slot)

        hook(0)
        mlp_work(
            m_ref.at[layer], mid_ref.at[layer], mlp_near.at[layer, piece], mlp_far.at[layer, piece],
            up_shift_ref[layer, piece], feats_ref.at[layer], act_ref, slope_ref, now_ref, acc_ref, index == 0,
            index == pieces - 1, hook,
        )

        @pl.when(index == pieces - 1)
        def _():
            x2_ref[layer] = now_ref[...]

            @pl.when(layer + 1 < layers)
            def _():
                a_win_ref[layer + 1, REACH : REACH + rows, :] = norm_rows(now_ref[...], feats_ref.at[layer + 1])
                halo(layer + 1).begin()

    @pl.when(step == pl.num_programs(0) - 1)
    def _():
        for gather in gathers:
            gather.end()
        for layer in range(layers):
            keep_window(layer).wait()


def forward(a_own, x, heads, feats, up_shift, seg_k, seg_q, attn_shards, mlp_shards):
    rows, width = x.shape
    layers, chunk, wide = mlp_shards.shape
    half = width // 2
    window = rows + 2 * REACH
    _, pieces, _, part = up_shift.shape
    hidden = pieces * part

    def attend_at(step):
        count = jnp.maximum(step - 1, 0)
        layer, inner = count // (2 * pieces), lax.rem(count, 2 * pieces)
        return layer, turn(jnp.minimum(inner, pieces - 1), pieces)

    def mlp_at(step):
        count = jnp.maximum(step - 1, 0)
        layer, inner = count // (2 * pieces), lax.rem(count, 2 * pieces)
        done = jnp.where(inner >= pieces, layer * pieces + inner - pieces, jnp.maximum(layer * pieces - 1, 0))
        return done // pieces, turn(lax.rem(done, pieces), pieces)

    def attend_block(height, wide):
        return pl.BlockSpec((None, height, wide), lambda step: (attend_at(step)[0], 0, attend_at(step)[1]))

    mlp_block = pl.BlockSpec((None, rows, part), lambda step: (mlp_at(step)[0], 0, mlp_at(step)[1]))
    heads_at = lambda step: attend_at(step)[0] * pieces + attend_at(step)[1]
    once = lambda shape: pl.BlockSpec(shape, lambda step: (0,) * len(shape), pipeline_mode=pl.Buffered(1))
    outs = attend_shapes(rows, window) + [(rows, 2 * PAIR)]
    specs = [attend_block(*shape) for shape in outs]
    shapes = [shaped((layers, height, pieces * wide)) for height, wide in outs]
    specs.insert(6, pl.BlockSpec((3, window, rows), lambda step: (heads_at(step), 0, 0)))
    shapes.insert(6, shaped((3 * layers * pieces, window, rows)))
    held = [((layers, rows, width), F32), ((layers, rows, width), BF16), ((layers, rows, width), F32)]
    weights = [(layers, pieces, half, 6 * PAIR)] * 2 + [(layers, pieces, half, wide)] * 2
    semaphores = pltpu.SemaphoreType.DMA((2 * layers, pieces, Gather.KINDS))
    inputs = (a_own, x, heads, feats, up_shift, seg_k, seg_q, attn_shards, mlp_shards)
    return pl.pallas_call(
        forward_kernel,
        grid=(1 + 2 * layers * pieces,),
        in_specs=[once(item.shape) for item in inputs],
        out_specs=specs + [mlp_block] * 2 + [once(shape) for shape, _ in held] + [ANY] * 5,
        out_shape=shapes + [shaped((layers, rows, hidden))] * 2 + [shaped(*item) for item in held]
        + [shaped(shape) for shape in [(layers, window, width)] + weights],
        scratch_shapes=[
            pltpu.VMEM((window, rows), F32), pltpu.VMEM((rows, width), F32), pltpu.VMEM((rows, width), F32),
            pltpu.VMEM((layers, window, width), BF16), pltpu.SemaphoreType.DMA((layers,)),
            *[pltpu.VMEM(shape, BF16) for shape in weights], semaphores, semaphores, pltpu.SemaphoreType.DMA((2 * layers,)),
            pltpu.SemaphoreType.DMA((2 * layers, pieces, 2)), pltpu.SemaphoreType.DMA((layers, 4)),
            pltpu.SemaphoreType.DMA((layers, 4)),
        ],
        compiler_params=params(20),
        name="forward",
    )(*inputs)


def mlp_back_kernel(*refs):
    step = pl.program_id(0)
    mlp_back_work(*refs, step == 0, step == pl.num_programs(0) - 1)


def mlp_back_work(
    g_ref, down_near_ref, down_far_ref, slope_ref, up_near_ref, up_far_ref, mid_ref, feats_ref,
    gz_ref, gh_ref, up_shift_grad_ref, g1_ref, gr_ref, small_ref, acc_ref, opening, closing,
):
    half = up_near_ref.shape[0]

    @pl.when(opening)
    def _():
        gz_ref[...] = g_ref[...].astype(BF16)
        acc_ref[...] = jnp.zeros_like(acc_ref)

    near, distant = halves(gz_ref[...])
    gh = ((nn(near, down_near_ref[...]) + nn(distant, down_far_ref[...])) * slope_ref[...].astype(F32)).astype(BF16)
    gh_ref[...] = gh
    up_shift_grad_ref[...] = jnp.sum(gh.astype(F32), axis=0, keepdims=True)
    acc_ref[:, :half] += nt(gh, up_near_ref[...])
    acc_ref[:, half:] += nt(gh, up_far_ref[...])

    @pl.when(closing)
    def _():
        gm = acc_ref[...]
        hat, scale = row_norm(mid_ref[...])
        g1 = g_ref[...] + row_norm_back(gm * line(feats_ref, LN_GAIN[1]), hat, scale)
        gr = g1.astype(BF16)
        g1_ref[...] = g1
        gr_ref[...] = gr
        small_ref[...] = jnp.zeros_like(small_ref)
        small_ref[0:1, :] = jnp.sum(gz_ref[...].astype(F32), axis=0, keepdims=True)
        small_ref[1:2, :] = jnp.sum(gr.astype(F32), axis=0, keepdims=True)
        small_ref[2:3, :] = jnp.sum(gm * hat, axis=0, keepdims=True)
        small_ref[3:4, :] = jnp.sum(gm, axis=0, keepdims=True)


def mlp_back(grad, near, far, slope, mid, feats, layer, index):
    rows, width = grad.shape
    half = width // 2
    hidden = slope.shape[2]
    pieces = near.shape[1]
    wide = hidden // pieces
    full = whole((rows, width))
    return pl.pallas_call(
        mlp_back_kernel,
        grid=(pieces,),
        in_specs=[
            full, piece_of(index, half, wide, 1), piece_of(index, half, wide, 1), slab(index, rows, wide),
            piece_of(index, half, wide), piece_of(index, half, wide), sheet(index, rows, width), sheet(layer, FEATS, width),
        ],
        out_specs=[full, column(rows, wide), column(1, wide), full, full, whole((8, width))],
        out_shape=[
            shaped((rows, width)), shaped((rows, hidden)), shaped((1, hidden), F32), shaped((rows, width), F32),
            shaped((rows, width)), shaped((8, width), F32),
        ],
        scratch_shapes=[pltpu.VMEM((rows, width), F32)],
        cost_estimate=pl.CostEstimate(
            flops=4 * rows * width * hidden, bytes_accessed=4 * width * hidden, transcendentals=0
        ),
        name="mlp_back",
    )(grad, near, far, slope, near, far, mid, feats)


def attend_back_kernel(*refs):
    attend_back_work(*refs, quiet)


def attend_back_work(
    gr_ref, q_ref, kv_ref, q_hat_ref, k_hat_ref, q_scale_ref, k_scale_ref, p_ref, near_ref, far_ref, heads_ref,
    gq_ref, gkv_ref, mine_ref, left_ref, right_ref, small_ref, acc_ref, hook,
):
    rows = gr_ref.shape[0]
    half = near_ref.shape[0]
    step = pl.program_id(0)

    @pl.when(step == 0)
    def _():
        acc_ref[...] = jnp.zeros_like(acc_ref)

    near, distant = halves(gr_ref[...])
    go = (nn(near, near_ref[:, 4 * PAIR :]) + nn(distant, far_ref[:, 4 * PAIR :])).astype(BF16)
    qn, kv = q_ref[...], kv_ref[...]
    first, values, second = kv[:, :PAIR], kv[:, PAIR : 2 * PAIR], kv[:, 2 * PAIR :]
    first_t, second_t = first.T, second.T
    grad_q, grad_k, grad_v = [], [], []
    for head in range(3):
        hook(head)
        go_head = only(go[:, PAIR:], head) if head < 2 else only(go[:, :PAIR], 1)
        query = only(qn[:, PAIR * (head // 2) : PAIR * (head // 2 + 1)] * HD ** (-0.5), head % 2).astype(BF16)
        stored = p_ref[head]
        probs = stored.astype(F32)
        grad_probs = nt((values, values, second)[head], go_head)
        delta = jnp.sum(probs * grad_probs, axis=0, keepdims=True)
        grad_scores = (probs * (grad_probs - delta)).astype(BF16)
        grad_v.append(nn(stored, go_head))
        grad_k.append(nn(grad_scores, query))
        grad_q.append(nn((first_t[:HD], first_t[HD:], second_t[:HD])[head], grad_scores))
    hook(3)
    zero = jnp.zeros_like(grad_q[2])
    grad_q = (jnp.concatenate(grad_q + [zero], axis=0) * HD ** (-0.5)).T
    grad_k = side(grad_k[0] + grad_k[1], grad_k[2])
    pair_v, last_v = grad_v[0] + grad_v[1], grad_v[2]
    q_hat = q_hat_ref[...].astype(F32)
    k_hat = k_hat_ref[...].astype(F32)
    gain = lambda which: line(heads_ref, HEAD_GAIN[which], 0, 2 * PAIR)
    gq = head_norm_back(grad_q * gain(0), q_hat, q_scale_ref[...].astype(F32)).astype(BF16)
    gk = head_norm_back(grad_k * gain(1), k_hat, k_scale_ref[...].astype(F32)).astype(BF16)
    gkv = side(gk[:, :PAIR], pair_v.astype(BF16), gk[:, PAIR:] + last_v.astype(BF16))
    gq_ref[...] = gq
    gkv_ref[...] = gkv
    total = lambda value: jnp.sum(value.astype(F32), axis=0, keepdims=True)
    small_ref[...] = jnp.zeros_like(small_ref)
    small_ref[0:1, : 2 * PAIR] = total(grad_q * q_hat)
    small_ref[1:2, : 2 * PAIR] = total(grad_k * k_hat)
    small_ref[2:3, : 2 * PAIR] = total(grad_q)
    small_ref[3:4, : 2 * PAIR] = total(gq)
    small_ref[4:5, : 2 * PAIR] = total(gk)
    small_ref[5:6, :PAIR] = total(pair_v.astype(BF16))
    small_ref[5:6, 2 * PAIR :] = total(last_v.astype(BF16))
    acc_ref[:, :half] += nt(gkv, near_ref[:, PAIR : 4 * PAIR])
    acc_ref[:, half:] += nt(gkv, far_ref[:, PAIR : 4 * PAIR])
    own = slice(REACH, REACH + rows)
    for ref, cols in ((near_ref, slice(0, half)), (far_ref, slice(half, 2 * half))):
        acc_ref[own, cols] += nt(gq[:, :PAIR], ref[:, :PAIR]) + nt(gq[:, PAIR:], ref[:, 4 * PAIR : 5 * PAIR])

    @pl.when(step == pl.num_programs(0) - 1)
    def _():
        left_ref[...] = acc_ref[:REACH, :].astype(BF16)
        mine_ref[...] = acc_ref[own, :]
        right_ref[...] = acc_ref[REACH + rows :, :].astype(BF16)


def attend_back_specs(rows, width, pieces, layer, index):
    half = width // 2
    window = rows + 2 * REACH
    full = whole((rows, width))
    in_specs = [
        full, *[slab(index, *shape) for shape in attend_shapes(rows, window)],
        pl.BlockSpec((3, window, rows), lambda step: (index * pieces + step, 0, 0)), piece_of(index, half, 6 * PAIR),
        piece_of(index, half, 6 * PAIR), heads_of(layer),
    ]
    out_specs = [
        column(rows, 2 * PAIR), column(window, 3 * PAIR), full, whole((REACH, width)), whole((REACH, width)), column(8, 3 * PAIR),
    ]
    out_shape = [
        shaped((rows, pieces * 2 * PAIR)), shaped((window, pieces * 3 * PAIR)), shaped((rows, width), F32),
        shaped((REACH, width)), shaped((REACH, width)), shaped((8, pieces * 3 * PAIR), F32),
    ]
    cost = pl.CostEstimate(
        flops=2 * window * width * width * 2 + 20 * window * rows * width * 2,
        bytes_accessed=20 * window * width,
        transcendentals=0,
    )
    return in_specs, out_specs, out_shape, [pltpu.VMEM((window, width), F32)], cost


def attend_back(gr, stored, near, far, heads, layer, index):
    rows, width = gr.shape
    pieces = near.shape[1]
    in_specs, out_specs, out_shape, scratch, cost = attend_back_specs(rows, width, pieces, layer, index)
    return pl.pallas_call(
        attend_back_kernel,
        grid=(pieces,),
        in_specs=in_specs,
        out_specs=out_specs,
        out_shape=out_shape,
        scratch_shapes=scratch,
        cost_estimate=cost,
        name="attend_back",
    )(gr, *stored, near, far, heads)


def attn_weight_kernel(a_ref, gq_ref, gkv_ref, gr_ref, o_ref, keep_ref, send_ref, a_t_ref, gr_t_ref):
    rows = gq_ref.shape[0]
    half = keep_ref.shape[0]

    @pl.when(pl.program_id(0) == 0)
    def _():
        a_t_ref[...] = a_ref[...].T
        gr_t_ref[...] = gr_ref[...].T

    for part, ref in ((slice(0, half), keep_ref), (slice(half, 2 * half), send_ref)):
        from_q = nn(a_t_ref[part, REACH : REACH + rows], gq_ref[...])
        from_o = nn(gr_t_ref[part, :], o_ref[...])
        ref[:, :PAIR] = from_q[:, :PAIR].astype(BF16)
        ref[:, PAIR : 4 * PAIR] = nn(a_t_ref[part, :], gkv_ref[...]).astype(BF16)
        ref[:, 4 * PAIR : 5 * PAIR] = (from_q[:, PAIR:] + from_o[:, :PAIR]).astype(BF16)
        ref[:, 5 * PAIR :] = from_o[:, PAIR:].astype(BF16)


def attn_weight_grads(a_win, gq, gkv, gr, o):
    _, window, width = a_win.shape
    rows = gr.shape[0]
    half = width // 2
    pieces = gq.shape[1] // (2 * PAIR)
    out = column(half, 6 * PAIR)
    return pl.pallas_call(
        attn_weight_kernel,
        grid=(pieces,),
        in_specs=[
            sheet(0, window, width), column(rows, 2 * PAIR), column(window, 3 * PAIR), whole((rows, width)),
            slab(0, rows, 2 * PAIR),
        ],
        out_specs=[out, out],
        out_shape=[shaped((half, pieces * 6 * PAIR))] * 2,
        scratch_shapes=[pltpu.VMEM((width, window), BF16), pltpu.VMEM((width, rows), BF16)],
        cost_estimate=pl.CostEstimate(
            flops=2 * width * width * (2 * window + 2 * rows), bytes_accessed=8 * width * width, transcendentals=0
        ),
        name="attn_weight_grads",
    )(a_win, gq, gkv, gr, o)


def mlp_weight_kernel(m_ref, gh_ref, gz_ref, act_ref, keep_ref, send_ref, m_t_ref, gz_t_ref):
    half = keep_ref.shape[0]
    wide = gh_ref.shape[1]

    @pl.when(pl.program_id(0) == 0)
    def _():
        m_t_ref[...] = m_ref[...].T
        gz_t_ref[...] = gz_ref[...].T

    for part, ref in ((slice(0, half), keep_ref), (slice(half, 2 * half), send_ref)):
        ref[:, :wide] = nn(m_t_ref[part, :], gh_ref[...]).astype(BF16)
        ref[:, wide:] = nn(gz_t_ref[part, :], act_ref[...]).astype(BF16)


def mlp_weight_grads(m, gh, gz, act):
    _, rows, width = m.shape
    half = width // 2
    hidden = gh.shape[1]
    pieces = lax.axis_size("tp")
    wide = hidden // pieces
    out = column(half, 2 * wide)
    return pl.pallas_call(
        mlp_weight_kernel,
        grid=(pieces,),
        in_specs=[sheet(0, rows, width), column(rows, wide), whole((rows, width)), slab(0, rows, wide)],
        out_specs=[out, out],
        out_shape=[shaped((half, 2 * hidden))] * 2,
        scratch_shapes=[pltpu.VMEM((width, rows), BF16), pltpu.VMEM((width, rows), BF16)],
        cost_estimate=pl.CostEstimate(
            flops=4 * width * hidden * rows, bytes_accessed=4 * width * hidden, transcendentals=0
        ),
        name="mlp_weight_grads",
    )(m, gh, gz, act)


class Scatter:
    KINDS = 7

    def __init__(self, out, away, keep, core, first, second, given, send, recv):
        self.out, self.away, self.keep, self.core_in = out, away, keep, core
        self.first_in, self.second_in, self.given, self.send, self.recv = first, second, given, send, recv
        self.chunk, self.wide = out.shape
        self.half = self.wide // 2
        self.pieces = keep.shape[0]
        self.near = Neighbours()

    def copy(self, piece, kind, source, target, device):
        return pltpu.make_async_remote_copy(
            src_ref=source, dst_ref=target, send_sem=self.send.at[piece, kind], recv_sem=self.recv.at[piece, kind],
            device_id=device, device_id_type=MESH,
        )

    def copies(self, piece, stage):
        c, left, right = self.chunk, pl.ds(0, self.half), pl.ds(self.half, self.half)
        rows = lambda start, count=1: pl.ds(start * c, count * c)
        if stage == "core":
            return [self.copy(piece, 0, self.away.at[piece], self.core_in.at[piece], self.near.core)]
        if stage == "first":
            source, target = self.keep.at[piece], self.first_in.at[piece]
            return [
                self.copy(piece, 1, source.at[rows(2, 2), left], target.at[:, left], self.near.y),
                self.copy(piece, 2, source.at[rows(1), right], target.at[rows(0), right], self.near.x),
                self.copy(piece, 3, source.at[rows(3), right], target.at[rows(1), right], self.near.x),
            ]
        if stage == "second":
            source, target = self.keep.at[piece], self.second_in.at[piece]
            return [
                self.copy(piece, 4, source.at[rows(1), left], target.at[:, left], self.near.x),
                self.copy(piece, 5, source.at[rows(2), right], target.at[:, right], self.near.y),
            ]
        owner = self.near.along(self.pieces - piece)
        return [self.copy(piece, 6, self.keep.at[piece, rows(0), :], self.given.at[piece], owner)]

    def start(self, piece, stage):
        for copy in self.copies(piece, stage):
            copy.start()

    def arrived(self, piece, stage):
        for copy in self.copies(piece, stage):
            copy.wait_recv()

    def add(self, piece, start, count, cols, source):
        step = 32

        @pl.loop(0, count * self.chunk // step)
        def _(index):
            row = pl.multiple_of(index * step, step)
            into = (piece, pl.ds(start * self.chunk + row, step), cols)
            self.keep[into] = self.keep[into] + source[pl.ds(row, step), cols]

    def place(self, index):
        return lax.rem(index + 1, self.pieces)

    def core(self, index):
        self.start(self.place(index), "core")

    def first(self, index):
        piece = self.place(index)
        self.arrived(piece, "core")
        self.add(piece, 0, 4, pl.ds(0, self.wide), self.core_in.at[piece])
        self.start(piece, "first")

    def second(self, index):
        piece = self.place(index)
        left, right = pl.ds(0, self.half), pl.ds(self.half, self.half)
        self.arrived(piece, "first")
        source = self.first_in.at[piece]
        self.add(piece, 0, 2, left, source)
        self.add(piece, 0, 1, right, source)
        self.add(piece, 2, 1, right, source.at[pl.ds(self.chunk, self.chunk)])
        self.start(piece, "second")

    def last(self, index):
        piece = (index + 1) % self.pieces
        self.arrived(piece, "second")
        kept = pl.ds(0, self.chunk)
        total = self.keep[piece, kept, :].astype(F32) + self.second_in[piece].astype(F32)
        if piece:
            self.keep[piece, kept, :] = total.astype(BF16)
            self.start(piece, "give")
        else:
            for other in range(1, self.pieces):
                self.arrived(other, "give")
                total += self.given[other].astype(F32)
            self.out[...] = total

    def done(self):
        for piece in range(self.pieces):
            for stage in ("core", "first", "second", "give"):
                if stage != "give" or piece:
                    for copy in self.copies(piece, stage):
                        copy.wait_send()


def scatter_specs(pieces, chunk, wide):
    buffer = lambda rows: pltpu.VMEM((pieces, rows * chunk, wide), BF16)
    semaphores = pltpu.SemaphoreType.DMA((pieces, Scatter.KINDS))
    return shaped((chunk, wide), F32), [buffer(4), buffer(4), buffer(4), buffer(2), buffer(1), buffer(1), semaphores, semaphores]


def at_step(index, work):
    @pl.when(pl.program_id(0) == index)
    def _():
        work()


def attend_back_scatter_kernel(
    gr_ref, q_ref, kv_ref, q_hat_ref, k_hat_ref, q_scale_ref, k_scale_ref, p_ref, near_ref, far_ref, heads_ref,
    m_ref, gh_ref, gz_ref, act_ref, gq_ref, gkv_ref, mine_ref, left_ref, right_ref, small_ref, out_ref,
    acc_ref, m_t_ref, gz_t_ref, *scratch,
):
    scatter = Scatter(out_ref, *scratch)
    pieces, half = scatter.pieces, near_ref.shape[0]
    wide = gh_ref.shape[1] // pieces
    step = pl.program_id(0)

    @pl.when(step == 0)
    def _():
        scatter.near.greet()
        m_t_ref[...] = m_ref[...].T
        gz_t_ref[...] = gz_ref[...].T

    @pl.loop(jnp.where(step == 0, 0, step + 1), jnp.minimum(step + 2, pieces))
    def _(index):
        piece = scatter.place(index)
        cols = pl.ds(pl.multiple_of(piece * wide, wide), wide)
        for part, ref in ((slice(0, half), scatter.keep), (slice(half, 2 * half), scatter.away)):
            ref[piece, :, :wide] = nn(m_t_ref[part, :], gh_ref[:, cols]).astype(BF16)
            ref[piece, :, wide:] = nn(gz_t_ref[part, :], act_ref[:, cols]).astype(BF16)
        scatter.core(index)

    table = {
        (0, 1): [(scatter.first, 0)],
        (0, 3): [(scatter.first, 1)],
        (1, 1): [(scatter.second, 0), (scatter.first, 2)],
        (2, 1): [(scatter.second, 1), (scatter.last, 0), (scatter.first, 3)],
        (3, 1): [(scatter.last, 1), (scatter.second, 2)],
    }

    def hook(slot):
        for (when, where), events in table.items():
            if where == slot:

                @pl.when(step == when)
                def _():
                    for work, index in events:
                        work(index)

    attend_back_work(
        gr_ref, q_ref, kv_ref, q_hat_ref, k_hat_ref, q_scale_ref, k_scale_ref, p_ref, near_ref, far_ref, heads_ref,
        gq_ref, gkv_ref, mine_ref, left_ref, right_ref, small_ref, acc_ref, hook,
    )

    @pl.when(step == pieces - 1)
    def _():
        scatter.last(pieces - 2)
        scatter.second(pieces - 1)
        scatter.last(pieces - 1)
        scatter.done()


def attend_back_scatter(gr, stored, near, far, heads, m, gh, gz, act, layer, collective):
    rows, width = gr.shape
    half = width // 2
    hidden = gh.shape[1]
    pieces = near.shape[1]
    wide = hidden // pieces
    in_specs, out_specs, out_shape, scratch, cost = attend_back_specs(rows, width, pieces, layer, layer)
    full, all_hidden = whole((rows, width)), whole((rows, hidden))
    result, extra = scatter_specs(pieces, half // 4, 2 * wide)
    return pl.pallas_call(
        attend_back_scatter_kernel,
        grid=(pieces,),
        in_specs=in_specs + [sheet(layer, rows, width), all_hidden, full, sheet(layer, rows, hidden)],
        out_specs=out_specs + [whole(result.shape)],
        out_shape=out_shape + [result],
        scratch_shapes=scratch + [pltpu.VMEM((width, rows), BF16)] * 2 + extra,
        compiler_params=params(collective),
        cost_estimate=cost,
        name="attend_back_scatter",
    )(gr, *stored, near, far, heads, m, gh, gz, act)


def give_back_kernel(*refs, layer, with_mlp):
    a_ref, gq_ref, gkv_ref, gr_ref, o_ref, x_ref, g1_ref, mine_ref, left_ref, right_ref, feats_ref = refs[:11]
    rest = refs[11:]
    if with_mlp:
        down_near_ref, down_far_ref, slope_ref, up_near_ref, up_far_ref, mid_ref = rest[:6]
        rest = rest[6:]
    g_ref, sums_ref, out_ref = rest[:3]
    rest = rest[3:]
    if with_mlp:
        mlp_outs, rest = rest[:6], rest[6:]
        acc_ref, rest = rest[0], rest[1:]
    a_t_ref, gr_t_ref, total_ref, landed_ref, halo_send, halo_recv, *scratch = rest
    scatter = Scatter(out_ref, *scratch)
    pieces, rows = scatter.pieces, gr_ref.shape[0]
    half = gr_ref.shape[1] // 2
    spill = REACH - rows
    step = pl.program_id(0)
    moves = [
        (1, right_ref, pl.ds(0, rows), pl.ds(0, rows), 0),
        (-1, left_ref, pl.ds(spill, rows), pl.ds(0, rows), 0),
        (2, right_ref, pl.ds(rows, spill), pl.ds(0, spill), 0),
        (-2, left_ref, pl.ds(0, spill), pl.ds(0, spill), rows - spill),
    ]
    place, size = lax.axis_index("tp"), lax.axis_size("tp")
    inside = lambda other: jnp.logical_and(other >= 0, other < size)

    def halo_copy(index):
        distance, ref, source, target, _ = moves[index]
        return pltpu.make_async_remote_copy(
            src_ref=ref.at[source, :], dst_ref=landed_ref.at[index, target, :], send_sem=halo_send.at[index],
            recv_sem=halo_recv.at[index], device_id={"tp": place + distance}, device_id_type=MESH,
        )

    @pl.when(step == 0)
    def _():
        scatter.near.greet()
        for index, (distance, *_) in enumerate(moves):

            @pl.when(inside(place + distance))
            def _():
                halo_copy(index).start()

        a_t_ref[...] = a_ref[...].T
        gr_t_ref[...] = gr_ref[...].T

    @pl.when(step < pieces)
    def _():
        piece = scatter.place(step)
        for part, ref in ((slice(0, half), scatter.keep), (slice(half, 2 * half), scatter.away)):
            from_q = nn(a_t_ref[part, REACH : REACH + rows], gq_ref[...])
            from_o = nn(gr_t_ref[part, :], o_ref[...])
            ref[piece, :, :PAIR] = from_q[:, :PAIR].astype(BF16)
            ref[piece, :, PAIR : 4 * PAIR] = nn(a_t_ref[part, :], gkv_ref[...]).astype(BF16)
            ref[piece, :, 4 * PAIR : 5 * PAIR] = (from_q[:, PAIR:] + from_o[:, :PAIR]).astype(BF16)
            ref[piece, :, 5 * PAIR :] = from_o[:, PAIR:].astype(BF16)
        scatter.core(step)

        @pl.when(step > 0)
        def _():
            scatter.first(step - 1)

        @pl.when(step > 1)
        def _():
            scatter.second(step - 2)

    @pl.when(step == pieces - 1)
    def _():
        scatter.first(pieces - 1)
        scatter.last(0)
        scatter.second(pieces - 2)
        total_ref[...] = mine_ref[...]
        for index, (distance, _, _, target, start) in enumerate(moves):

            @pl.when(inside(place + distance))
            def _():
                halo_copy(index).wait_send()

            @pl.when(inside(place - distance))
            def _():
                halo_copy(index).wait_recv()
                total_ref[pl.ds(start, target.size), :] += landed_ref[index, target, :].astype(F32)

        scatter.last(1)
        total = total_ref[...]
        hat, scale = row_norm(x_ref[...])
        g_ref[...] = g1_ref[...] + row_norm_back(total * line(feats_ref.at[layer], LN_GAIN[0]), hat, scale)
        sums_ref[...] = jnp.zeros_like(sums_ref)
        sums_ref[0:1, :] = jnp.sum(total * hat, axis=0, keepdims=True)
        sums_ref[1:2, :] = jnp.sum(total, axis=0, keepdims=True)
        scatter.second(pieces - 1)

    if with_mlp:

        @pl.when(step >= pieces)
        def _():
            mlp_back_work(
                g_ref, down_near_ref, down_far_ref, slope_ref, up_near_ref, up_far_ref, mid_ref,
                feats_ref.at[layer - 1], *mlp_outs, acc_ref, step == pieces, step == 2 * pieces - 1,
            )

    @pl.when(step == pl.num_programs(0) - 1)
    def _():
        scatter.last(pieces - 2)
        scatter.last(pieces - 1)
        scatter.done()


def give_back(a_win, gq, gkv, gr, o, x, g1, mine, left, right, feats, layer, collective, before=None):
    _, window, width = a_win.shape
    rows = gr.shape[0]
    half = width // 2
    pieces = gq.shape[1] // (2 * PAIR)
    full = whole((rows, width))
    turned_at = lambda step: lax.rem(jnp.minimum(step, pieces - 1) + 1, pieces)
    turned = lambda height, wide: pl.BlockSpec((height, wide), lambda step: (0, turned_at(step)))
    in_specs = [
        sheet(layer, window, width), turned(rows, 2 * PAIR), turned(window, 3 * PAIR), full,
        pl.BlockSpec((None, rows, 2 * PAIR), lambda step: (layer, 0, turned_at(step))),
        full if layer == 0 else sheet(layer - 1, rows, width), full, full, whole((REACH, width)), whole((REACH, width)),
        whole(feats.shape),
    ]
    operands = [a_win, gq, gkv, gr, o, x, g1, mine, left, right, feats]
    result, extra = scatter_specs(pieces, half // 4, 6 * PAIR)
    out_specs = [full, whole((8, width)), whole(result.shape)]
    out_shape = [shaped((rows, width), F32), shaped((8, width), F32), result]
    scratch = []
    if before is not None:
        near, far, slope, mid = before
        hidden = slope.shape[2]
        wide = hidden // pieces
        below = layer - 1
        late_at = lambda step: jnp.maximum(step - pieces, 0)
        late = lambda height: pl.BlockSpec((height, wide), lambda step: (0, late_at(step)))
        late_piece = lambda first: pl.BlockSpec((None, None, half, wide), lambda step: (below, late_at(step), 0, first))
        in_specs += [
            late_piece(1), late_piece(1), pl.BlockSpec((None, rows, wide), lambda step: (below, 0, late_at(step))),
            late_piece(0), late_piece(0), sheet(below, rows, width),
        ]
        operands += [near, far, slope, near, far, mid]
        out_specs += [full, late(rows), late(1), full, full, whole((8, width))]
        out_shape += [
            shaped((rows, width)), shaped((rows, hidden)), shaped((1, hidden), F32), shaped((rows, width), F32),
            shaped((rows, width)), shaped((8, width), F32),
        ]
        scratch = [pltpu.VMEM((rows, width), F32)]
    scratch += [
        pltpu.VMEM((width, window), BF16), pltpu.VMEM((width, rows), BF16), pltpu.VMEM((rows, width), F32),
        pltpu.VMEM((4, rows, width), BF16), pltpu.SemaphoreType.DMA((4,)), pltpu.SemaphoreType.DMA((4,)), *extra,
    ]
    return pl.pallas_call(
        functools.partial(give_back_kernel, layer=layer, with_mlp=before is not None),
        grid=(pieces if before is None else 2 * pieces,),
        in_specs=in_specs,
        out_specs=out_specs,
        out_shape=out_shape,
        scratch_shapes=scratch,
        compiler_params=params(collective),
        cost_estimate=pl.CostEstimate(
            flops=2 * width * width * (2 * window + 2 * rows), bytes_accessed=20 * width * width, transcendentals=0
        ),
        name="give_back",
    )(*operands)


def flip(array, bit, axis="fsdp"):
    size = lax.axis_size(axis)
    return lax.ppermute(array, axis, [(i, i ^ (1 << bit)) for i in range(size)])


def ring(array):
    size = lax.axis_size("tp")
    return lax.ppermute(array, "tp", [(i, (i + 1) % size) for i in range(size)])


def hop(array, distance):
    size = lax.axis_size("tp")
    return lax.ppermute(array, "tp", [(i, i + distance) for i in range(size) if 0 <= i + distance < size])


def bits_of(size):
    return size.bit_length() - 1


def row_bits(first_top):
    count = bits_of(lax.axis_size("fsdp"))
    tops = [count - 1, count - 2] if first_top else [count - 2, count - 1]
    return list(range(1, count - 2)), tops


def gather_by_permutes(block, first_top):
    pieces = [block]
    for _ in range(lax.axis_size("tp") - 1):
        pieces.append(ring(pieces[-1]))
    block = jnp.concatenate(pieces, axis=1)
    low, tops = row_bits(first_top)
    have = []
    for bit in low + tops:
        axis = sum(other > bit for other in have)
        block = jnp.stack([block, flip(block, bit)], axis=axis)
        have.append(bit)
    block = block.reshape((-1, len(pieces), pieces[0].shape[1])).transpose(1, 0, 2)[None]
    return block, flip(block, 0)


def add(left, right, kind=BF16):
    return (left.astype(F32) + right.astype(F32)).astype(kind)


def reduce_by_permutes(keep, send, first_top):
    low, tops = row_bits(first_top)
    block = add(keep, flip(send, 0))
    order = tops + low[::-1]
    have = sorted(order, reverse=True)
    block = block.reshape((2,) * len(have) + (-1, block.shape[-1]))
    for bit in order:
        axis = have.index(bit)
        mine = lax.index_in_dim(block, 0, axis, keepdims=False)
        other = lax.index_in_dim(block, 1, axis, keepdims=False)
        block = add(mine, flip(other, bit))
        have.remove(bit)
    pieces = jnp.split(block, lax.axis_size("tp"), axis=1)
    total = pieces[1]
    for piece in pieces[2:]:
        total = add(ring(total), piece)
    return add(ring(total), pieces[0], F32)


def attn_shard(w_qkv, w_out):
    q, k, v = (w_qkv[:, which] for which in range(3))
    o = w_out.T
    return side(q[:, :PAIR], k[:, :PAIR], v[:, :PAIR], k[:, PAIR:], v[:, PAIR:], q[:, PAIR:], o[:, PAIR:], o[:, :PAIR])


def attn_unshard(block):
    tile = lambda start, wide=PAIR: block[:, start : start + wide]
    q = side(tile(0), tile(4 * PAIR, HD))
    k = side(tile(PAIR), tile(3 * PAIR, HD))
    v = side(tile(2 * PAIR), tile(3 * PAIR + HD, HD))
    o = side(tile(5 * PAIR), tile(4 * PAIR + HD, HD))
    return jnp.stack([q, k, v], axis=1), o.T


def body(
    tokens, segment_ids, patch_pos, row_table, col_table, ln_gain, ln_bias, qkv_bias, qk_gain, query_bias, out_bias,
    fc1_bias, fc2_bias, w_qkv, w_out, w_fc1, w_fc2, cotangent,
):
    layers = w_qkv.shape[0]
    rows, width = tokens.shape
    half = width // 2
    fsdp, tp = lax.axis_size("fsdp"), lax.axis_size("tp")
    f_index, t_index = lax.axis_index("fsdp"), lax.axis_index("tp")
    hidden = fc1_bias.shape[1] * fsdp * tp
    grid = row_table.shape[0]
    fine = width // (fsdp * tp)
    parts = hidden // width
    in_kernel = fsdp == 8

    place = jnp.arange(width, dtype=jnp.int32)
    chunk = width // fsdp
    slot = place // chunk
    away = (slot % (fsdp // 2)) * 2 + slot // (fsdp // 2)
    feature_at = (f_index ^ away) * chunk + place % chunk
    head_cols = width // tp
    spot = jnp.arange(tp * 3 * PAIR, dtype=jnp.int32)
    tile, part = spot % (3 * PAIR) // PAIR, spot % PAIR // HD
    head = jnp.where(tile == 0, part, jnp.where(tile == part + 1, 2, -fsdp * tp))
    head_at = ((t_index - spot // (3 * PAIR)) % tp) * head_cols + head * HD + spot % HD
    far = place // fine
    arrived_at = ((f_index ^ (far // tp)) * tp + (t_index ^ (far % tp))) * fine + place % fine
    to_feature = (arrived_at[:, None] == feature_at[None, :]).astype(BF16)
    to_head = (arrived_at[:, None] == head_at[None, :]).astype(BF16)
    reorder = (place[:, None] == feature_at[None, :]).astype(BF16)
    device = jnp.arange(fsdp * tp, dtype=jnp.int32)
    device_at = (f_index ^ (device // tp)) * tp + (t_index ^ (device % tp))
    wanted = ((t_index - device // fsdp) % tp) * fsdp + device % fsdp
    to_hidden = (wanted[:, None] == device_at[None, :]).astype(BF16)

    by_layer = lambda *items: jnp.concatenate([item.reshape(layers, -1, fine) for item in items], axis=1).reshape(-1, fine)
    shares = [
        row_table, col_table, by_layer(ln_gain, ln_bias, out_bias, fc2_bias), by_layer(qkv_bias, qk_gain, query_bias),
        fc1_bias.reshape(layers * parts, fine),
    ]
    small = jnp.concatenate(shares, axis=0)
    count = small.shape[0]
    flat = small.reshape(1, -1)
    for bit in range(bits_of(tp)):
        flat = jnp.concatenate([flat, flip(flat, bit, "tp")], axis=0)
    for bit in range(bits_of(fsdp)):
        flat = jnp.concatenate([flat, flip(flat, bit)], axis=0)
    gathered = flat.reshape(fsdp * tp, count, fine)
    lined = gathered.transpose(1, 0, 2).reshape(count, width)
    wide = 2 * grid + 6 * layers
    feats = jnp.dot(lined[:wide], to_feature, preferred_element_type=F32)
    heads = jnp.dot(lined[wide : wide + 6 * layers], to_head, preferred_element_type=F32)
    up_shift = jnp.einsum(
        "or,rlsi->losi",
        to_hidden,
        gathered[:, wide + 6 * layers :].reshape(fsdp * tp, layers, parts, fine),
        preferred_element_type=F32,
    ).reshape(layers, tp, 1, hidden // tp)
    tables = feats[: 2 * grid].astype(BF16)
    feats = feats[2 * grid :].reshape(layers, FEATS, width)

    heads = heads.reshape(layers, HEADS, tp, 3 * PAIR).transpose(2, 0, 1, 3)
    attn_shards = jnp.stack([attn_shard(w_qkv[layer], w_out[layer]) for layer in range(layers)])
    mlp_shards = jnp.concatenate([w_fc1, w_fc2.transpose(0, 2, 1)], axis=2)

    grid_ids = jnp.arange(grid, dtype=jnp.int32)
    row_hot = patch_pos[0][:, None] == grid_ids[None, :]
    col_hot = patch_pos[1][:, None] == grid_ids[None, :]
    residual = (
        jnp.dot(tokens, reorder, preferred_element_type=F32)
        + jnp.dot(row_hot.astype(BF16), tables[:grid], preferred_element_type=F32)
        + jnp.dot(col_hot.astype(BF16), tables[grid:], preferred_element_type=F32)
    )
    segments = segment_ids[0]
    padded = jnp.pad(segments, (REACH, REACH), constant_values=-1)
    seg_k = lax.dynamic_slice_in_dim(padded, t_index * rows, rows + 2 * REACH).reshape(-1, 1)
    seg_q = lax.dynamic_slice_in_dim(segments, t_index * rows, rows).reshape(1, -1)
    spill = REACH - rows

    hat, _ = row_norm(residual)
    a_own = (hat * feats[0, LN_GAIN[0]] + feats[0, LN_BIAS[0]]).astype(BF16)
    if in_kernel:
        *stored, o, act, slope, mid, m, x2, a_win, attn_near, attn_far, mlp_near, mlp_far = forward(
            a_own, residual, heads, feats, up_shift, seg_k, seg_q, attn_shards, mlp_shards
        )
        start, residual = residual, x2[layers - 1]
        saved = [
            (x2 if layer else start, a_win, stored, o, mid, m, act, slope, attn_near, attn_far, mlp_near, mlp_far)
            for layer in range(layers)
        ]
    else:
        saved = []
        for layer in range(layers):
            a_win = jnp.concatenate(
                [hop(a_own[rows - spill :], 2), hop(a_own, 1), a_own, hop(a_own, -1), hop(a_own[:spill], -2)], axis=0
            )
            attn_near, attn_far = gather_by_permutes(attn_shards[layer], layer % 2 == 0)
            *stored, probs, o, mid, m = attend(
                a_win, attn_near, attn_far, heads, feats, residual, seg_k, seg_q, layer
            )
            mlp_near, mlp_far = gather_by_permutes(mlp_shards[layer], layer % 2 == 1)
            act, slope, x2 = mlp(m, mid, mlp_near, mlp_far, up_shift, feats, layer)
            stored = [item[None] for item in stored] + [probs]
            kept = [item[None] for item in (o, mid, m, act, slope)]
            saved.append((residual, a_win[None], stored, *kept, attn_near, attn_far, mlp_near, mlp_far))
            residual = x2
            if layer + 1 < layers:
                hat, _ = row_norm(residual)
                a_own = (
                    hat * feats[layer + 1, LN_GAIN[0]] + feats[layer + 1, LN_BIAS[0]]
                ).astype(BF16)

    restore = functools.partial(
        lax.dot_general, dimension_numbers=(((1,), (1,)), ((), ())), precision=HIGHEST, preferred_element_type=F32
    )
    exact = reorder.astype(F32)
    activations = restore(residual, exact)
    grad = jnp.dot(cotangent, exact, precision=HIGHEST, preferred_element_type=F32)
    kept_sums = [None] * layers
    w_qkv_grad, w_out_grad, w_fc1_grad, w_fc2_grad = ([None] * layers for _ in range(4))
    back = None
    for layer in reversed(range(layers)):
        x, a_win, stored, o, mid, m, act, slope, attn_near, attn_far, mlp_near, mlp_far = saved[layer]
        if back is None:
            index = layer if in_kernel else 0
            back = mlp_back(grad, mlp_near, mlp_far, slope, mid, feats, layer, index)
        gz, gh, up_grad, g1, gr, mlp_small = back
        back = None
        if in_kernel:
            gq, gkv, mine, left, right, attn_small, mlp_block = attend_back_scatter(
                gr, stored, attn_near, attn_far, heads, m, gh, gz, act, layer, 40 + layer
            )
            before = None
            if layer:
                before = mlp_near, mlp_far, slope, mid
            grad, norm_sums, attn_block, *back = give_back(
                a_win, gq, gkv, gr, o, x, g1, mine, left, right, feats, layer, 50 + layer, before
            )
            back = back or None
            norm_sums = norm_sums[0], norm_sums[1]
        else:
            mlp_block = reduce_by_permutes(*mlp_weight_grads(m, gh, gz, act), layer % 2 == 0)
            gq, gkv, mine, left, right, attn_small = attend_back(
                gr, stored, attn_near, attn_far, heads, layer, 0
            )
            attn_block = reduce_by_permutes(*attn_weight_grads(a_win, gq, gkv, gr, o), layer % 2 == 1)
            ends = jnp.concatenate([hop(right[rows:], 2), hop(left[:spill], -2)], axis=0).astype(F32)
            attn_grad = mine + hop(right[:rows], 1).astype(F32) + hop(left[spill:], -1).astype(F32) + ends
            hat, scale = row_norm(x)
            grad = g1 + row_norm_back(attn_grad * feats[layer, LN_GAIN[0]], hat, scale)
            norm_sums = jnp.sum(attn_grad * hat, axis=0), jnp.sum(attn_grad, axis=0)
        middle = mlp_block.shape[1] // 2
        w_fc1_grad[layer], w_fc2_grad[layer] = mlp_block[:, :middle], mlp_block[:, middle:].T
        w_qkv_grad[layer], w_out_grad[layer] = attn_unshard(attn_block)
        kept_sums[layer] = (*norm_sums, mlp_small, attn_small, up_grad.reshape(parts, width))

    token_grad = restore(grad, exact)
    row_grad = jnp.einsum("tg,td->gd", row_hot.astype(F32), grad, precision=HIGHEST)
    col_grad = jnp.einsum("tg,td->gd", col_hot.astype(F32), grad, precision=HIGHEST)
    featured = [row_grad, col_grad]
    headed = []
    for a_gain, a_shift, sums, head_sums, _ in kept_sums:
        featured.append(jnp.stack([a_gain, sums[2], a_shift, sums[3], sums[1], sums[0]]))
        headed += [head_sums[3:6], head_sums[0:2], head_sums[2:3]]
    headed = jnp.concatenate(headed)
    spread = jnp.concatenate(
        [restore(jnp.concatenate(featured), to_feature.astype(F32)), restore(headed, to_head.astype(F32))]
    )
    spread = spread.reshape(-1, fsdp * tp, fine).transpose(1, 0, 2)
    up_all = jnp.stack([item[4] for item in kept_sums]).reshape(layers, fsdp * tp, parts * fine)
    up_all = jnp.einsum("or,lok->rlk", to_hidden.astype(F32), up_all, precision=HIGHEST)
    flat = jnp.concatenate([spread.reshape(fsdp * tp, -1), up_all.reshape(fsdp * tp, -1)], axis=1)
    for bit in reversed(range(bits_of(fsdp))):
        middle = flat.shape[0] // 2
        flat = flat[:middle] + flip(flat[middle:], bit)
    for bit in reversed(range(bits_of(tp))):
        middle = flat.shape[0] // 2
        flat = flat[:middle] + flip(flat[middle:], bit, "tp")
    flat = flat.reshape(-1)
    found = flat.reshape(-1, fine)
    rows_g, cols_g, rest = found[:grid], found[grid : 2 * grid], found[2 * grid :]
    by_feature = rest[: layers * FEATS].reshape(layers, FEATS, fine)
    by_head = rest[layers * FEATS : layers * (FEATS + HEADS)].reshape(layers, HEADS, fine)
    up_g = rest[layers * (FEATS + HEADS) :].reshape(layers, parts * fine)
    gain_g, shift_g, out_g, last_g = by_feature[:, :2], by_feature[:, 2:4], by_feature[:, OUT_BIAS], by_feature[:, LAST_BIAS]
    proj_g, head_gain_g, head_shift_g = by_head[:, :3], by_head[:, 3:5], by_head[:, HEAD_BIAS]
    return (
        activations, token_grad, rows_g, cols_g, gain_g, shift_g, proj_g, head_gain_g, head_shift_g, out_g, up_g, last_g,
        jnp.stack(w_qkv_grad), jnp.stack(w_out_grad), jnp.stack(w_fc1_grad), jnp.stack(w_fc2_grad),
    )


def solution(mesh):
    both = ("fsdp", "tp")
    in_specs = (
        P(both, None), P("fsdp", None), P(None, both), P(None, both), P(None, both), P(None, None, both),
        P(None, None, both), P(None, None, both), P(None, None, both), P(None, both), P(None, both), P(None, both),
        P(None, both), P(None, "fsdp", None, "tp"), P(None, "tp", "fsdp"), P(None, "fsdp", "tp"), P(None, "tp", "fsdp"),
        P(both, None),
    )
    out_specs = (
        P(both, None), P(both, None), P(None, both), P(None, both), P(None, None, both), P(None, None, both),
        P(None, None, both), P(None, None, both), P(None, both), P(None, both), P(None, both), P(None, both),
        P(None, "fsdp", None, "tp"), P(None, "tp", "fsdp"), P(None, "fsdp", "tp"), P(None, "tp", "fsdp"),
    )
    return jax.shard_map(body, mesh=mesh, in_specs=in_specs, out_specs=out_specs, check_vma=False)
```

```python
import functools

import jax
import jax.numpy as jnp
from jax import lax
from jax.experimental import pallas as pl
from jax.experimental.pallas import tpu as pltpu
from jax.sharding import PartitionSpec as P

HD = 64
PAIR = 128
REACH = 384
EPS = 1e-06
FILL = -1e30
ROOT_HALF = 0.7071067811865476
INV_ROOT_TWO_PI = 0.3989422804014327
HIGHEST = lax.Precision.HIGHEST
F32 = jnp.float32
BF16 = jnp.bfloat16
MESH = pl.DeviceIdType.MESH
VMEM = 67043328
ANY = pl.BlockSpec(memory_space=pl.ANY)


def nn(left, right):
    return lax.dot_general(left, right, (((1,), (0,)), ((), ())), preferred_element_type=F32)


def nt(left, right):
    return lax.dot_general(left, right, (((1,), (1,)), ((), ())), preferred_element_type=F32)


def halves(array):
    middle = array.shape[1] // 2
    return array[:, :middle], array[:, middle:]


def row_norm(value):
    centered = value - jnp.mean(value, axis=-1, keepdims=True)
    scale = lax.rsqrt(jnp.mean(centered * centered, axis=-1, keepdims=True) + EPS)
    return centered * scale, scale


def row_norm_back(grad_hat, normed, scale):
    return scale * (
        grad_hat
        - jnp.mean(grad_hat, axis=-1, keepdims=True)
        - normed * jnp.mean(grad_hat * normed, axis=-1, keepdims=True)
    )


def head_mean(value, exact=False):
    wide = value.shape[1]
    rows = lax.broadcasted_iota(jnp.int32, (wide, wide), 0) // HD
    cols = lax.broadcasted_iota(jnp.int32, (wide, wide), 1) // HD
    spread = jnp.where(rows == cols, 1.0 / HD, 0.0).astype(BF16)
    high = value.astype(BF16)
    mean = nn(high, spread)
    if exact:
        mean += nn((value - high.astype(F32)).astype(BF16), spread)
    return mean


def head_norm(value):
    centered = value - head_mean(value, exact=True)
    scale = lax.rsqrt(head_mean(centered * centered) + EPS)
    return centered * scale, scale


def head_norm_back(grad_hat, normed, scale):
    return scale * (grad_hat - head_mean(grad_hat) - normed * head_mean(grad_hat * normed))


def only(array, part):
    return jnp.where(lax.broadcasted_iota(jnp.int32, (1, PAIR), 1) // HD == part, array, jnp.zeros_like(array))


def side(*parts):
    return jnp.concatenate(parts, axis=1)


def whole(shape):
    return pl.BlockSpec(shape, lambda step: (0,) * len(shape))


def column(height, wide, every=1, first=0):
    return pl.BlockSpec((height, wide), lambda step: (0, step * every + first))


def piece_of(layer, height, wide, first=0):
    return pl.BlockSpec((None, None, height, wide), lambda step: (layer, step, 0, first))


def slab(layer, height, wide):
    return pl.BlockSpec((None, height, wide), lambda step: (layer, 0, step))


def heads_of(layer):
    return pl.BlockSpec((None, None, HEADS, 3 * PAIR), lambda step: (step, layer, 0, 0))


def sheet(layer, height, wide):
    return pl.BlockSpec((None, height, wide), lambda step: (layer, 0, 0))


def shaped(shape, kind=BF16):
    return jax.ShapeDtypeStruct(shape, kind)


class Neighbours:
    def __init__(self):
        fsdp, tp = lax.axis_index("fsdp"), lax.axis_index("tp")
        self.size = lax.axis_size("tp")
        self.tp = tp
        self.x, self.y, self.core = ({"fsdp": jnp.bitwise_xor(fsdp, bit)} for bit in (2, 4, 1))

    def along(self, distance):
        return {"tp": lax.rem(self.tp + distance, self.size)}

    def all(self):
        return [self.x, self.y, self.core] + [self.along(distance) for distance in range(1, self.size)]

    def greet(self):
        targets = self.all()
        barrier = pltpu.get_barrier_semaphore()
        for target in targets:
            pl.semaphore_signal(barrier, inc=1, device_id=target, device_id_type=MESH)
        pl.semaphore_wait(barrier, len(targets))


class Plan:
    LINKS = {"x": (45.5e3, 1.5), "y": (45.5e3, 1.5), "z": (45.5e3, 2.2), "core": (600e3, 1.0)}

    def __init__(self):
        self.depth, self.clock = {"x": 5.0, "y": 5.0, "z": 5.0, "core": 20.0}, 0.0
        self.free, self.here, self.jobs, self.table = dict.fromkeys(self.LINKS, 0.0), {}, [], {}

    def add(self, rank, work, needs, copies, gives, group):
        self.jobs.append((rank, len(self.jobs), work, needs, copies, gives, group))
        self.jobs.sort(key=lambda job: job[:2])

    def carry(self, copies, gives):
        end = self.clock
        for link, size in copies:
            rate, latency = self.LINKS[link]
            self.free[link] = max(self.free[link], self.clock) + size / rate
            end = max(end, self.free[link] + latency)
        self.here[gives] = end

    def slot(self, *at):
        found = True
        while found:
            found = False
            for job in self.jobs:
                _, _, work, needs, copies, gives, _ = job
                ready = all(self.here.get(need, float("inf")) <= self.clock for need in needs)
                if ready and all(self.free[link] - self.clock < self.depth[link] for link, _ in copies):
                    self.carry(copies, gives)
                    self.table.setdefault(at, []).append(work)
                    self.jobs.remove(job)
                    found = True
                    break

    def wait(self, key, work, *at):
        self.slot(*at)
        while self.here.get(key, float("inf")) > self.clock:
            self.clock += 0.25
            self.slot(*at)
        self.table.setdefault(at, []).append(work)

    def finish(self, group, *at):
        self.slot(*at)
        while any(group in (None, job[-1]) for job in self.jobs):
            self.clock += 0.25
            self.slot(*at)

    def spend(self, time):
        self.clock += time


def turn(index, pieces):
    if isinstance(index, int):
        return (index + 1) // 2 if index % 2 else (pieces - index // 2) % pieces
    return jnp.where(lax.rem(index, 2) == 1, (index + 1) // 2, lax.rem(pieces - index // 2, pieces))


class Gather:
    KINDS = 7

    def __init__(self, peers, shard, near, far, send, recv, local, near_out, far_out, stored):
        self.peers, self.shard, self.near, self.far = peers, shard, near, far
        self.send, self.recv, self.local = send, recv, local
        self.outs, self.stored = (near_out, far_out), stored
        self.chunk, self.wide = shard.shape
        self.pieces = near.shape[0]

    def at(self, piece, start, count, half=None):
        first, wide = (0, self.wide) if half is None else (half * (self.wide // 2), self.wide // 2)
        return self.near.at[piece, pl.ds(start * self.chunk, count * self.chunk), pl.ds(first, wide)]

    def copy(self, piece, kind, source, target, device):
        return pltpu.make_async_remote_copy(
            src_ref=source, dst_ref=target, send_sem=self.send.at[piece, kind], recv_sem=self.recv.at[piece, kind],
            device_id=device, device_id_type=MESH,
        )

    def copies(self, piece, stage):
        if stage == "z":
            return [self.copy(piece, 0, self.shard, self.at(piece, 0, 1), self.peers.along(piece))] if piece else []
        if stage == "first":
            half = self.wide // 2
            left = self.shard.at[:, pl.ds(0, half)] if piece == 0 else self.at(piece, 0, 1, 0)
            right = self.shard.at[:, pl.ds(half, half)] if piece == 0 else self.at(piece, 0, 1, 1)
            return [
                self.copy(piece, 1, left, self.at(piece, 1, 1, 0), self.peers.x),
                self.copy(piece, 2, right, self.at(piece, 2, 1, 1), self.peers.y),
            ]
        if stage == "second":
            return [
                self.copy(piece, 3, self.at(piece, 0, 2, 0), self.at(piece, 2, 2, 0), self.peers.y),
                self.copy(piece, 4, self.at(piece, 0, 1, 1), self.at(piece, 1, 1, 1), self.peers.x),
                self.copy(piece, 5, self.at(piece, 2, 1, 1), self.at(piece, 3, 1, 1), self.peers.x),
            ]
        return [self.copy(piece, 6, self.near.at[piece], self.far.at[piece], self.peers.core)]

    def start(self, piece, stage):
        for copy in self.copies(piece, stage):
            copy.start()

    def arrived(self, piece, stage):
        for copy in self.copies(piece, stage):
            copy.wait_recv()

    def store(self, piece):
        return [
            pltpu.make_async_copy(source.at[piece], target.at[piece], self.stored.at[piece, which])
            for which, (source, target) in enumerate(zip((self.near, self.far), self.outs))
        ]

    def own(self):
        return pltpu.make_async_copy(self.shard, self.at(0, 0, 1), self.local)

    def sent(self, piece):
        self.start(piece, "z")

    def landed(self, piece):
        self.arrived(piece, "z")
        self.start(piece, "first")

    def crossed(self, piece):
        self.arrived(piece, "first")
        self.start(piece, "second")

    def shared(self, piece):
        self.arrived(piece, "second")
        self.start(piece, "core")

    def need(self, piece):
        self.arrived(piece, "core")
        for copy in self.store(piece):
            copy.start()

    def jobs(self, plan, index):
        size = self.chunk * self.wide * 2
        for place in range(self.pieces):
            piece = turn(place, self.pieces)
            key = (index, piece)
            rank = index * self.pieces + place
            if piece:
                plan.add(rank, (self.sent, piece), [], [("z", size * self.pieces / (self.pieces - 1))], ("z", *key), index)
            both = lambda count: [("x", count * size), ("y", count * size)]
            plan.add(rank, (self.landed, piece), [("z", *key)] if piece else [], both(0.5), ("first", *key), index)
            plan.add(rank, (self.crossed, piece), [("first", *key)], both(1), ("second", *key), index)
            plan.add(rank, (self.shared, piece), [("second", *key)], [("core", 4 * size)], ("core", *key), index)

    def end(self):
        for piece in range(self.pieces):
            for stage in ("z", "first", "second", "core"):
                for copy in self.copies(piece, stage):
                    copy.wait_send()
            for copy in self.store(piece):
                copy.wait()


class Halo:
    def __init__(self, ref, rows, send, recv):
        self.ref, self.send, self.recv = ref, send, recv
        self.place, self.size = lax.axis_index("tp"), lax.axis_size("tp")
        spill = REACH - rows
        self.moves = [
            (1, pl.ds(REACH, rows), pl.ds(spill, rows)),
            (-1, pl.ds(REACH, rows), pl.ds(REACH + rows, rows)),
            (2, pl.ds(2 * rows, spill), pl.ds(0, spill)),
            (-2, pl.ds(REACH, spill), pl.ds(REACH + 2 * rows, spill)),
        ]

    def inside(self, distance):
        other = self.place + distance
        return jnp.logical_and(other >= 0, other < self.size)

    def copy(self, index):
        distance, source, target = self.moves[index]
        return pltpu.make_async_remote_copy(
            src_ref=self.ref.at[source, :], dst_ref=self.ref.at[target, :], send_sem=self.send.at[index],
            recv_sem=self.recv.at[index], device_id={"tp": self.place + distance}, device_id_type=MESH,
        )

    def begin(self):
        for index, (distance, _, target) in enumerate(self.moves):

            @pl.when(self.inside(distance))
            def _():
                self.copy(index).start()

            @pl.when(jnp.logical_not(self.inside(-distance)))
            def _():
                self.ref[target, :] = jnp.zeros((target.size, self.ref.shape[1]), BF16)

    def end(self, _=None):
        for index, (distance, _, _) in enumerate(self.moves):

            @pl.when(self.inside(distance))
            def _():
                self.copy(index).wait_send()

            @pl.when(self.inside(-distance))
            def _():
                self.copy(index).wait_recv()


def exchange_kernel(x_ref, out_ref, landed, send, recv, *, to_sum):
    size, tp = landed.shape[0], lax.axis_size("tp")
    me = lax.axis_index("fsdp") * tp + lax.axis_index("tp")
    place = lambda device: {"fsdp": device // tp, "tp": lax.rem(device, tp)}
    barrier = pltpu.get_barrier_semaphore()

    @pl.loop(1, size)
    def _(distance):
        target = place(lax.rem(me + distance, size))
        pl.semaphore_signal(barrier, inc=1, device_id=target, device_id_type=MESH)

    pl.semaphore_wait(barrier, size - 1)

    def copy(distance):
        target = lax.rem(me + distance, size)
        return pltpu.make_async_remote_copy(
            src_ref=x_ref.at[target] if to_sum else x_ref, dst_ref=landed.at[me], send_sem=send.at[distance],
            recv_sem=recv.at[distance], device_id=place(target), device_id_type=MESH,
        )

    @pl.loop(1, size)
    def _(distance):
        copy(distance).start()

    landed[me] = x_ref[me] if to_sum else x_ref[...]

    @pl.loop(1, size)
    def _(distance):
        copy(distance).wait()

    if to_sum:
        out_ref[...] = landed[0]

        @pl.loop(1, size)
        def _(device):
            out_ref[...] += landed[device]

    else:
        out_ref[...] = landed[...]


def exchange(x, size, to_sum, collective):
    shape = x.shape[1:] if to_sum else x.shape
    result = shaped(shape if to_sum else (size, *shape), x.dtype)
    return pl.pallas_call(
        functools.partial(exchange_kernel, to_sum=to_sum),
        grid=(1,),
        in_specs=[whole(x.shape)],
        out_specs=whole(result.shape),
        out_shape=result,
        scratch_shapes=[
            pltpu.VMEM((size, *shape), x.dtype), pltpu.SemaphoreType.DMA((size,)), pltpu.SemaphoreType.DMA((size,)),
        ],
        compiler_params=params(collective),
        name="exchange",
    )(x)


def lanes(block):
    size = block.shape[-1]
    tall = -(-size // (16 * PAIR)) * 16
    block = jnp.pad(block, [(0, 0)] * (block.ndim - 1) + [(0, tall * PAIR - size)])
    return block.reshape(*block.shape[:-1], tall, PAIR)


def params(collective, memory=None):
    return pltpu.CompilerParams(collective_id=collective, has_side_effects=True, vmem_limit_bytes=memory)


LN_GAIN, LN_BIAS, OUT_BIAS, LAST_BIAS, FEATS = (0, 1), (2, 3), 4, 5, 6
PROJ_BIAS, HEAD_GAIN, HEAD_BIAS, HEADS = (0, 1, 2), (3, 4), 5, 6


def line(ref, row, start=0, wide=None):
    return ref[pl.ds(row, 1), pl.ds(start, wide or ref.shape[1] - start)]


def attend_work(
    a_ref, near_ref, far_ref, heads_ref, feats_ref, x_ref, q_ref, kv_ref, q_hat_ref, k_hat_ref, q_scale_ref, k_scale_ref,
    p_ref, o_ref, mid_ref, m_ref, mask_ref, acc_ref, opening, closing, hook,
):
    rows = q_ref.shape[0]
    half = near_ref.shape[0]

    @pl.when(opening)
    def _():
        acc_ref[...] = jnp.zeros_like(acc_ref)

    tile = lambda row, which: line(heads_ref, row, which * PAIR, PAIR)
    bias, (q_gain, k_gain), q_shift = PROJ_BIAS, HEAD_GAIN, HEAD_BIAS
    near, distant = halves(a_ref[...])
    own, own_far = halves(a_ref[REACH : REACH + rows, :])
    kv = nn(near, near_ref[:, PAIR : 4 * PAIR]) + nn(distant, far_ref[:, PAIR : 4 * PAIR])
    kv += side(tile(bias[1], 0), tile(bias[2], 0), tile(bias[1], 1) + tile(bias[2], 2))
    q = side(
        nn(own, near_ref[:, :PAIR]) + nn(own_far, far_ref[:, :PAIR]),
        nn(own, near_ref[:, 4 * PAIR : 5 * PAIR]) + nn(own_far, far_ref[:, 4 * PAIR : 5 * PAIR]),
    ) + line(heads_ref, bias[0], 0, 2 * PAIR)
    q_hat, q_scale = head_norm(q)
    k_hat, k_scale = head_norm(side(kv[:, :PAIR], kv[:, 2 * PAIR :]))
    qn = (q_hat * line(heads_ref, q_gain, 0, 2 * PAIR) + line(heads_ref, q_shift, 0, 2 * PAIR)).astype(BF16)
    qn = side(qn[:, :PAIR], only(qn[:, PAIR:], 0))
    kn = (k_hat * line(heads_ref, k_gain, 0, 2 * PAIR)).astype(BF16)
    v = kv[:, PAIR:].astype(BF16)
    low = lax.broadcasted_iota(jnp.int32, (1, PAIR), 1) < HD
    first, second = kn[:, :PAIR], jnp.where(low, kn[:, PAIR:], v[:, PAIR:])
    values = v[:, :PAIR]
    q_ref[...] = qn
    kv_ref[...] = side(first, values, second)
    q_hat_ref[...] = q_hat.astype(BF16)
    k_hat_ref[...] = k_hat.astype(BF16)
    q_scale_ref[...] = q_scale.astype(BF16)
    k_scale_ref[...] = k_scale.astype(BF16)
    hook(1)
    values_t, second_t = values.T, second.T
    mixed = []
    for head in range(3):
        if head:
            hook(head + 1)
        keys = (first, first, second)[head]
        query = only(qn[:, PAIR * (head // 2) : PAIR * (head // 2 + 1)] * HD ** (-0.5), head % 2).astype(BF16)
        scores = nt(keys, query) + mask_ref[...]
        weights = jnp.exp(scores - jnp.max(scores, axis=0, keepdims=True))
        total = jnp.sum(weights, axis=0, keepdims=True)
        probs = (weights * (1.0 / total)).astype(BF16)
        p_ref[head] = probs
        mixed.append(nn((values_t[:HD], values_t[HD:], second_t[HD:])[head], probs))
    o = jnp.concatenate([jnp.zeros_like(mixed[2]), mixed[2], mixed[0], mixed[1]], axis=0).T.astype(BF16)
    o_ref[...] = o
    acc_ref[:, :half] += nt(o, near_ref[:, 4 * PAIR :])
    acc_ref[:, half:] += nt(o, far_ref[:, 4 * PAIR :])

    @pl.when(closing)
    def _():
        mid = x_ref[...] + (acc_ref[...] + line(feats_ref, OUT_BIAS))
        mid_ref[...] = mid
        hat, _ = row_norm(mid)
        m_ref[...] = (hat * line(feats_ref, LN_GAIN[1]) + line(feats_ref, LN_BIAS[1])).astype(BF16)


def mlp_work(
    m_ref, mid_ref, near_ref, far_ref, up_shift, feats_ref, act_ref, slope_ref, x2_ref, acc_ref, opening, closing, hook,
):
    half = near_ref.shape[0]
    wide = act_ref.shape[1]

    @pl.when(opening)
    def _():
        acc_ref[...] = jnp.zeros_like(acc_ref)

    near, distant = halves(m_ref[...])
    hidden = nn(near, near_ref[:, :wide]) + nn(distant, far_ref[:, :wide]) + up_shift
    hook(1)
    phi = 0.5 * (1.0 + lax.erf(hidden * ROOT_HALF))
    act = (hidden * phi).astype(BF16)
    act_ref[...] = act
    slope_ref[...] = (phi + hidden * jnp.exp(-0.5 * hidden * hidden) * INV_ROOT_TWO_PI).astype(BF16)
    acc_ref[:, :half] += nt(act, near_ref[:, wide:])
    acc_ref[:, half:] += nt(act, far_ref[:, wide:])

    @pl.when(closing)
    def _():
        x2_ref[...] = mid_ref[...] + (acc_ref[...] + line(feats_ref, LAST_BIAS))


def norm_rows(x, feats_ref):
    hat, _ = row_norm(x)
    return (hat * line(feats_ref, LN_GAIN[0]) + line(feats_ref, LN_BIAS[0])).astype(BF16)


def quiet(slot):
    pass


def attend_kernel(
    a_ref, near_ref, far_ref, heads_ref, feats_ref, x_ref, seg_k_ref, seg_q_ref, *rest
):
    step = pl.program_id(0)
    mask_ref = rest[-2]

    @pl.when(step == 0)
    def _():
        mask_ref[...] = jnp.where(seg_k_ref[...] == seg_q_ref[...], 0.0, FILL)

    attend_work(
        a_ref, near_ref, far_ref, heads_ref, feats_ref, x_ref, *rest, step == 0, step == pl.num_programs(0) - 1, quiet
    )


def attend_shapes(rows, window):
    return [
        (rows, 2 * PAIR), (window, 3 * PAIR), (rows, 2 * PAIR), (window, 2 * PAIR), (rows, 2 * PAIR), (window, 2 * PAIR),
    ]


def attend(a_win, near, far, heads, feats, x, seg_k, seg_q, layer):
    window, width = a_win.shape
    rows = x.shape[0]
    half = width // 2
    pieces = near.shape[1]
    outs = attend_shapes(rows, window)
    return pl.pallas_call(
        attend_kernel,
        grid=(pieces,),
        in_specs=[
            whole((window, width)), piece_of(0, half, 6 * PAIR), piece_of(0, half, 6 * PAIR), heads_of(layer), sheet(layer, FEATS, width),
            whole((rows, width)), whole((window, 1)), whole((1, rows)),
        ],
        out_specs=[column(*shape) for shape in outs]
        + [pl.BlockSpec((3, window, rows), lambda step: (step, 0, 0)), column(rows, 2 * PAIR)] + [whole((rows, width))] * 2,
        out_shape=[shaped((height, pieces * wide)) for height, wide in outs]
        + [shaped((3 * pieces, window, rows)), shaped((rows, pieces * 2 * PAIR)), shaped((rows, width), F32), shaped((rows, width))],
        scratch_shapes=[pltpu.VMEM((window, rows), F32), pltpu.VMEM((rows, width), F32)],
        name="attend",
    )(a_win, near, far, heads, feats, x, seg_k, seg_q)


def mlp_kernel(m_ref, mid_ref, near_ref, far_ref, up_shift_ref, feats_ref, *rest):
    step = pl.program_id(0)
    mlp_work(
        m_ref, mid_ref, near_ref, far_ref, up_shift_ref[...], feats_ref, *rest, step == 0, step == pl.num_programs(0) - 1, quiet
    )


def mlp(m, mid, near, far, up_shift, feats, layer):
    rows, width = mid.shape
    half = width // 2
    _, pieces, _, wide = up_shift.shape
    hidden = pieces * wide
    full = whole((rows, width))
    return pl.pallas_call(
        mlp_kernel,
        grid=(pieces,),
        in_specs=[
            full, full, piece_of(0, half, 2 * wide), piece_of(0, half, 2 * wide), piece_of(layer, 1, wide), sheet(layer, FEATS, width),
        ],
        out_specs=[column(rows, wide), column(rows, wide), full],
        out_shape=[shaped((rows, hidden)), shaped((rows, hidden)), shaped((rows, width), F32)],
        scratch_shapes=[pltpu.VMEM((rows, width), F32)],
        name="mlp",
    )(m, mid, near, far, up_shift, feats)


class Share:
    def __init__(self, peers, mine, landed, chunks, send, recv):
        self.peers, self.mine, self.landed, self.chunks, self.send, self.recv = peers, mine, landed, chunks, send, recv
        self.pieces, self.lines = landed.shape[0], mine.shape[0]

    def copy(self, index, source, target, device):
        return pltpu.make_async_remote_copy(
            src_ref=source, dst_ref=target, send_sem=self.send.at[index], recv_sem=self.recv.at[index], device_id=device,
            device_id_type=MESH,
        )

    def along(self):
        place = self.landed.at[self.peers.tp]
        return [self.copy(d - 1, self.mine, place, self.peers.along(d)) for d in range(1, self.pieces)]

    def across(self, stage):
        count = 1 << stage
        device = (self.peers.x, self.peers.y, self.peers.core)[stage]
        source, target = self.chunks.at[pl.ds(0, count)], self.chunks.at[pl.ds(count, count)]
        return self.copy(self.pieces - 1 + stage, source, target, device)

    def begin(self):
        for copy in self.along():
            copy.start()
        self.landed[self.peers.tp] = self.mine[...]

    def meet(self, fine):
        for copy in self.along():
            copy.wait_recv()
        row, col = (lax.broadcasted_iota(jnp.int32, (PAIR, PAIR), axis) for axis in range(2))
        total = 0.0
        for place in range(self.pieces):
            spread = jnp.logical_and(row < fine, col == row + place * fine)
            total += nn(self.landed[place], spread.astype(F32).astype(BF16))
        self.chunks[0] = total.astype(BF16)
        self.across(0).start()

    def spread(self, stage):
        self.across(stage - 1).wait_recv()
        self.across(stage).start()

    def end(self):
        self.across(2).wait_recv()
        for copy in self.along() + [self.across(stage) for stage in range(3)]:
            copy.wait_send()

    def chunk_of(self, fsdp):
        away = jnp.bitwise_xor(lax.axis_index("fsdp"), fsdp)
        return lax.rem(away, 2) * (self.chunks.shape[0] // 2) + away // 2

    def features(self, lines, width):
        chunk = width // self.chunks.shape[0]
        row, col = (lax.broadcasted_iota(jnp.int32, (2 * PAIR, width), axis) for axis in range(2))
        total = 0.0
        for place in range(0, self.chunks.shape[0], 2):
            lane = lax.rem(row, PAIR)
            spread = jnp.logical_and(lane < chunk, col == (place + row // PAIR) * chunk + lane)
            both = side(self.chunks[place, :lines, :], self.chunks[place + 1, :lines, :])
            total += nn(both, spread.astype(F32).astype(BF16))
        return total

    def owner(self, place):
        return lax.rem(self.peers.tp + self.pieces - place, self.pieces)

    def heads(self, place, start, chunk):
        owner = self.owner(place)
        rows = pl.ds(start, 16)
        both = side(self.chunks[self.chunk_of(2 * owner), rows, :], self.chunks[self.chunk_of(2 * owner + 1), rows, :])
        row, col = (lax.broadcasted_iota(jnp.int32, (2 * PAIR, 3 * PAIR), axis) for axis in range(2))
        lane = lax.rem(row, PAIR)
        feature = row // PAIR * chunk + lane
        last = jnp.logical_and(feature >= PAIR, col == feature + 3 * HD)
        spread = jnp.logical_and(lane < chunk, jnp.logical_or(col == feature, last))
        return nn(both, spread.astype(F32).astype(BF16))

    def hidden(self, start, layers, parts, fine):
        rows = pl.ds(start, 16)
        block = jnp.concatenate(
            [self.chunks[self.chunk_of(2 * self.owner(i // 2) + i % 2), rows, :] for i in range(2 * self.pieces)], axis=0
        )
        wide = self.pieces * parts * fine
        row, col = (lax.broadcasted_iota(jnp.int32, (PAIR, wide), axis) for axis in range(2))
        line_of = lax.broadcasted_iota(jnp.int32, (block.shape[0], 1), 0)
        total = 0.0
        for part in range(parts):
            target = row // fine * (parts * fine) + part * fine + lax.rem(row, fine)
            spread = jnp.logical_and(row < self.pieces * fine, col == target)
            here = nn(block, spread.astype(F32).astype(BF16))
            total += jnp.where(lax.rem(line_of, parts) == part, here, 0.0)
        row, col = (lax.broadcasted_iota(jnp.int32, (2 * self.pieces * layers, block.shape[0]), axis) for axis in range(2))
        group = jnp.logical_and(row // layers == col // 16, lax.rem(row, layers) == lax.rem(col, 16) // parts)
        return nn(group.astype(F32).astype(BF16), total.astype(BF16))


def forward_kernel(
    token_ref, hot_ref, share_ref, seg_k_ref, seg_q_ref, attn_shard_ref, mlp_shard_ref,
    q_ref, kv_ref, q_hat_ref, k_hat_ref, q_scale_ref, k_scale_ref, p_ref, o_ref, act_ref, slope_ref, mid_ref, m_ref, x2_ref,
    x0_ref, feats_ref, heads_ref, a_win_out, attn_near_out, attn_far_out, mlp_near_out, mlp_far_out,
    mask_ref, acc_ref, now_ref, a_win_ref, kept, attn_near, attn_far, mlp_near, mlp_far, send, recv, local, stored, halo_send, halo_recv,
    up_shift_ref, landed, chunks, share_send, share_recv,
):
    layers, pieces, (rows, width) = attn_near.shape[0], attn_near.shape[1], token_ref.shape
    chunk = width // chunks.shape[0]
    fine, parts, tables = chunk // pieces, act_ref.shape[1] * pieces // width, hot_ref.shape[1]
    step = pl.program_id(0)
    peers = Neighbours()
    halo = lambda layer: Halo(a_win_ref.at[layer], rows, halo_send.at[layer], halo_recv.at[layer])
    keep_window = lambda layer: pltpu.make_async_copy(a_win_ref.at[layer], a_win_out.at[layer], kept.at[layer])

    def window(layer):
        halo(layer).end()
        keep_window(layer).start()

    gathers = []
    for layer in range(layers):
        for which, (shard, near, far, near_out, far_out) in enumerate((
            (attn_shard_ref, attn_near, attn_far, attn_near_out, attn_far_out),
            (mlp_shard_ref, mlp_near, mlp_far, mlp_near_out, mlp_far_out),
        )):
            index = 2 * layer + which
            gathers.append(
                Gather(
                    peers, shard.at[layer], near.at[layer], far.at[layer], send.at[index], recv.at[index], local.at[index],
                    near_out.at[layer], far_out.at[layer], stored.at[index],
                )
            )

    share = Share(peers, share_ref, landed, chunks, share_send, share_recv)

    def open_up(_):
        share.end()
        lines = tables + 16
        found = share.features(lines, width)
        for layer in range(layers):
            feats_ref[layer] = found[tables + layer * FEATS : tables + (layer + 1) * FEATS]
        x0 = token_ref[...] + nn(hot_ref[...], found[:tables].astype(BF16))
        x0_ref[...] = x0
        now_ref[...] = x0
        a_win_ref[0, REACH : REACH + rows, :] = norm_rows(x0, feats_ref.at[0])
        halo(0).begin()
        for piece in range(pieces):
            found = share.heads(piece, lines, chunk)
            for layer in range(layers):
                heads_ref[piece, layer] = found[layer * HEADS : (layer + 1) * HEADS]
        found = share.hidden(lines + 16, layers, parts, fine)
        half = pieces * parts * fine
        for index in range(2 * pieces):
            for layer in range(layers):
                at = index * layers + layer
                up_shift_ref[layer, index // 2, :, index % 2 * half : (index % 2 + 1) * half] = found[at : at + 1]

    plan = Plan()
    for index, gather in enumerate(gathers):
        gather.jobs(plan, index)
    halo_size = width * 2 * 2 * rows
    share_size = share_ref.shape[0] * PAIR * 2
    plan.spend(2.5)
    plan.carry([("z", pieces * share_size)], ("share", 0))
    plan.wait(("share", 0), (share.meet, fine), 0, 0)
    plan.carry([("x", share_size)], ("share", 1))
    plan.wait(("share", 1), (share.spread, 1), 0, 0)
    plan.carry([("y", 2 * share_size)], ("share", 2))
    plan.wait(("share", 2), (share.spread, 2), 0, 0)
    plan.carry([("core", 4 * share_size)], ("share", 3))
    plan.wait(("share", 3), (open_up, 0), 0, 0)
    for layer in range(layers):
        plan.carry([("z", halo_size)], ("halo", layer))
        first = 1 + 2 * layer * pieces
        if layer == 0:
            plan.spend(5.0)
        plan.wait(("halo", layer), (window, layer), *((first, 0) if layer else (0, 0)))
        for index in range(pieces):
            piece = turn(index, pieces)
            plan.wait(("core", 2 * layer, piece), (gathers[2 * layer].need, piece), first + index, 0)
            for slot, time in enumerate((2.0, 1.4, 1.4)):
                plan.spend(time)
                plan.slot(first + index, slot + 1)
            plan.spend(1.4)
        first += pieces
        for index in range(pieces):
            piece = turn(index, pieces)
            plan.wait(("core", 2 * layer + 1, piece), (gathers[2 * layer + 1].need, piece), first + index, 0)
            plan.spend(1.0)
            plan.slot(first + index, 1)
            plan.spend(1.5)
    table = plan.table

    def run(at, slot):
        if (at, slot) in table:

            @pl.when(step == at)
            def _():
                for work, piece in table[at, slot]:
                    work(piece)

    @pl.when(step == 0)
    def _():
        peers.greet()
        mask_ref[...] = jnp.where(seg_k_ref[...] == seg_q_ref[...], 0.0, FILL)
        share.begin()
        for gather in gathers:
            gather.own().start()
        for gather in gathers:
            gather.own().wait()

    run(0, 0)

    count = jnp.maximum(step - 1, 0)
    layer = count // (2 * pieces)
    inner = lax.rem(count, 2 * pieces)
    index = lax.rem(inner, pieces)
    piece = turn(index, pieces)
    steps_of = lambda which: [
        1 + (2 * layer + which) * pieces + index for layer in range(layers) for index in range(pieces)
    ]

    @pl.when(jnp.logical_and(step > 0, inner < pieces))
    def _():
        def hook(slot):
            for at in steps_of(0):
                run(at, slot)

        hook(0)
        attend_work(
            a_win_ref.at[layer], attn_near.at[layer, piece], attn_far.at[layer, piece], heads_ref.at[piece, layer],
            feats_ref.at[layer], now_ref,
            q_ref, kv_ref, q_hat_ref, k_hat_ref, q_scale_ref, k_scale_ref, p_ref, o_ref, mid_ref.at[layer], m_ref.at[layer],
            mask_ref, acc_ref, index == 0, index == pieces - 1, hook,
        )

    @pl.when(inner >= pieces)
    def _():
        def hook(slot):
            for at in steps_of(1):
                run(at, slot)

        hook(0)
        mlp_work(
            m_ref.at[layer], mid_ref.at[layer], mlp_near.at[layer, piece], mlp_far.at[layer, piece],
            up_shift_ref[layer, piece], feats_ref.at[layer], act_ref, slope_ref, now_ref, acc_ref, index == 0,
            index == pieces - 1, hook,
        )

        @pl.when(index == pieces - 1)
        def _():
            x2_ref[layer] = now_ref[...]

            @pl.when(layer + 1 < layers)
            def _():
                a_win_ref[layer + 1, REACH : REACH + rows, :] = norm_rows(now_ref[...], feats_ref.at[layer + 1])
                halo(layer + 1).begin()

    @pl.when(step == pl.num_programs(0) - 1)
    def _():
        for gather in gathers:
            gather.end()
        for layer in range(layers):
            keep_window(layer).wait()


def forward(tokens, hot, share, seg_k, seg_q, attn_shards, mlp_shards):
    rows, width = tokens.shape
    layers, chunk, wide = mlp_shards.shape
    half = width // 2
    window = rows + 2 * REACH
    pieces, chunks, part = lax.axis_size("tp"), lax.axis_size("fsdp"), wide // 2
    hidden = pieces * part

    def attend_at(step):
        count = jnp.maximum(step - 1, 0)
        layer, inner = count // (2 * pieces), lax.rem(count, 2 * pieces)
        return layer, turn(jnp.minimum(inner, pieces - 1), pieces)

    def mlp_at(step):
        count = jnp.maximum(step - 1, 0)
        layer, inner = count // (2 * pieces), lax.rem(count, 2 * pieces)
        done = jnp.where(inner >= pieces, layer * pieces + inner - pieces, jnp.maximum(layer * pieces - 1, 0))
        return done // pieces, turn(lax.rem(done, pieces), pieces)

    def attend_block(height, wide):
        return pl.BlockSpec((None, height, wide), lambda step: (attend_at(step)[0], 0, attend_at(step)[1]))

    mlp_block = pl.BlockSpec((None, rows, part), lambda step: (mlp_at(step)[0], 0, mlp_at(step)[1]))
    heads_at = lambda step: attend_at(step)[0] * pieces + attend_at(step)[1]
    once = lambda shape: pl.BlockSpec(shape, lambda step: (0,) * len(shape), pipeline_mode=pl.Buffered(1))
    outs = attend_shapes(rows, window) + [(rows, 2 * PAIR)]
    specs = [attend_block(*shape) for shape in outs]
    shapes = [shaped((layers, height, pieces * wide)) for height, wide in outs]
    specs.insert(6, pl.BlockSpec((3, window, rows), lambda step: (heads_at(step), 0, 0)))
    shapes.insert(6, shaped((3 * layers * pieces, window, rows)))
    held = [((layers, rows, width), F32), ((layers, rows, width), BF16), ((layers, rows, width), F32)]
    weights = [(layers, pieces, half, 6 * PAIR)] * 2 + [(layers, pieces, half, wide)] * 2
    semaphores = pltpu.SemaphoreType.DMA((2 * layers, pieces, Gather.KINDS))
    held += [((rows, width), F32), ((layers, FEATS, width), F32), ((pieces, layers, HEADS, 3 * PAIR), F32)]
    inputs = (tokens, hot, share, seg_k, seg_q, attn_shards, mlp_shards)
    return pl.pallas_call(
        forward_kernel,
        grid=(1 + 2 * layers * pieces,),
        in_specs=[once(item.shape) for item in inputs],
        out_specs=specs + [mlp_block] * 2 + [once(shape) for shape, _ in held] + [ANY] * 5,
        out_shape=shapes + [shaped((layers, rows, hidden))] * 2 + [shaped(*item) for item in held]
        + [shaped(shape) for shape in [(layers, window, width)] + weights],
        scratch_shapes=[
            pltpu.VMEM((window, rows), F32), pltpu.VMEM((rows, width), F32), pltpu.VMEM((rows, width), F32),
            pltpu.VMEM((layers, window, width), BF16), pltpu.SemaphoreType.DMA((layers,)),
            *[pltpu.VMEM(shape, BF16) for shape in weights], semaphores, semaphores, pltpu.SemaphoreType.DMA((2 * layers,)),
            pltpu.SemaphoreType.DMA((2 * layers, pieces, 2)), pltpu.SemaphoreType.DMA((layers, 4)),
            pltpu.SemaphoreType.DMA((layers, 4)), pltpu.VMEM((layers, pieces, 1, part), F32),
            pltpu.VMEM((pieces, *share.shape), BF16), pltpu.VMEM((chunks, *share.shape), BF16),
            pltpu.SemaphoreType.DMA((pieces + 2,)), pltpu.SemaphoreType.DMA((pieces + 2,)),
        ],
        compiler_params=params(20, VMEM),
        name="forward",
    )(*inputs)


def mlp_back_kernel(*refs):
    step = pl.program_id(0)
    mlp_back_work(*refs, step == 0, step == pl.num_programs(0) - 1, quiet)


def mlp_back_work(
    g_ref, down_near_ref, down_far_ref, slope_ref, up_near_ref, up_far_ref, mid_ref, feats_ref,
    gz_ref, gh_ref, up_shift_grad_ref, g1_ref, gr_ref, small_ref, acc_ref, opening, closing, hook,
):
    half = up_near_ref.shape[0]

    @pl.when(opening)
    def _():
        gz_ref[...] = g_ref[...].astype(BF16)
        acc_ref[...] = jnp.zeros_like(acc_ref)

    near, distant = halves(gz_ref[...])
    gh = ((nn(near, down_near_ref[...]) + nn(distant, down_far_ref[...])) * slope_ref[...].astype(F32)).astype(BF16)
    gh_ref[...] = gh
    hook(1)
    up_shift_grad_ref[...] = jnp.sum(gh.astype(F32), axis=0, keepdims=True)
    acc_ref[:, :half] += nt(gh, up_near_ref[...])
    acc_ref[:, half:] += nt(gh, up_far_ref[...])

    @pl.when(closing)
    def _():
        gm = acc_ref[...]
        hat, scale = row_norm(mid_ref[...])
        g1 = g_ref[...] + row_norm_back(gm * line(feats_ref, LN_GAIN[1]), hat, scale)
        gr = g1.astype(BF16)
        g1_ref[...] = g1
        gr_ref[...] = gr
        small_ref[...] = jnp.zeros_like(small_ref)
        small_ref[0:1, :] = jnp.sum(gz_ref[...].astype(F32), axis=0, keepdims=True)
        small_ref[1:2, :] = jnp.sum(gr.astype(F32), axis=0, keepdims=True)
        small_ref[2:3, :] = jnp.sum(gm * hat, axis=0, keepdims=True)
        small_ref[3:4, :] = jnp.sum(gm, axis=0, keepdims=True)


def mlp_back(grad, near, far, slope, mid, feats, layer, index):
    rows, width = grad.shape
    half = width // 2
    hidden = slope.shape[2]
    pieces = near.shape[1]
    wide = hidden // pieces
    full = whole((rows, width))
    return pl.pallas_call(
        mlp_back_kernel,
        grid=(pieces,),
        in_specs=[
            full, piece_of(index, half, wide, 1), piece_of(index, half, wide, 1), slab(index, rows, wide),
            piece_of(index, half, wide), piece_of(index, half, wide), sheet(index, rows, width), sheet(layer, FEATS, width),
        ],
        out_specs=[full, column(rows, wide), column(1, wide), full, full, whole((8, width))],
        out_shape=[
            shaped((rows, width)), shaped((rows, hidden)), shaped((1, hidden), F32), shaped((rows, width), F32),
            shaped((rows, width)), shaped((8, width), F32),
        ],
        scratch_shapes=[pltpu.VMEM((rows, width), F32)],
        cost_estimate=pl.CostEstimate(
            flops=4 * rows * width * hidden, bytes_accessed=4 * width * hidden, transcendentals=0
        ),
        name="mlp_back",
    )(grad, near, far, slope, near, far, mid, feats)


def attend_back_kernel(*refs):
    *ins, gq_ref, gkv_ref, mine_ref, left_ref, right_ref, small_ref, acc_ref = refs
    rows = gq_ref.shape[0]
    step = pl.program_id(0)

    @pl.when(step == 0)
    def _():
        acc_ref[...] = jnp.zeros_like(acc_ref)

    attend_back_work(*ins, gq_ref, gkv_ref, small_ref, acc_ref, quiet)

    @pl.when(step == pl.num_programs(0) - 1)
    def _():
        left_ref[...] = acc_ref[:REACH, :].astype(BF16)
        mine_ref[...] = acc_ref[REACH : REACH + rows, :]
        right_ref[...] = acc_ref[REACH + rows :, :].astype(BF16)


def attend_back_work(
    gr_ref, q_ref, kv_ref, q_hat_ref, k_hat_ref, q_scale_ref, k_scale_ref, p_ref, near_ref, far_ref, heads_ref,
    gq_ref, gkv_ref, small_ref, acc_ref, hook,
):
    rows = gr_ref.shape[0]
    half = near_ref.shape[0]
    near, distant = halves(gr_ref[...])
    go = (nn(near, near_ref[:, 4 * PAIR :]) + nn(distant, far_ref[:, 4 * PAIR :])).astype(BF16)
    qn, kv = q_ref[...], kv_ref[...]
    first, values, second = kv[:, :PAIR], kv[:, PAIR : 2 * PAIR], kv[:, 2 * PAIR :]
    first_t, second_t = first.T, second.T
    grad_q, grad_k, grad_v = [], [], []
    for head in range(3):
        if head:
            hook(head)
        go_head = only(go[:, PAIR:], head) if head < 2 else only(go[:, :PAIR], 1)
        query = only(qn[:, PAIR * (head // 2) : PAIR * (head // 2 + 1)] * HD ** (-0.5), head % 2).astype(BF16)
        stored = p_ref[head]
        probs = stored.astype(F32)
        grad_probs = nt((values, values, second)[head], go_head)
        delta = jnp.sum(probs * grad_probs, axis=0, keepdims=True)
        grad_scores = (probs * (grad_probs - delta)).astype(BF16)
        grad_v.append(nn(stored, go_head))
        grad_k.append(nn(grad_scores, query))
        grad_q.append(nn((first_t[:HD], first_t[HD:], second_t[:HD])[head], grad_scores))
    hook(3)
    zero = jnp.zeros_like(grad_q[2])
    grad_q = (jnp.concatenate(grad_q + [zero], axis=0) * HD ** (-0.5)).T
    grad_k = side(grad_k[0] + grad_k[1], grad_k[2])
    pair_v, last_v = grad_v[0] + grad_v[1], grad_v[2]
    q_hat = q_hat_ref[...].astype(F32)
    k_hat = k_hat_ref[...].astype(F32)
    gain = lambda which: line(heads_ref, HEAD_GAIN[which], 0, 2 * PAIR)
    gq = head_norm_back(grad_q * gain(0), q_hat, q_scale_ref[...].astype(F32)).astype(BF16)
    gk = head_norm_back(grad_k * gain(1), k_hat, k_scale_ref[...].astype(F32)).astype(BF16)
    gkv = side(gk[:, :PAIR], pair_v.astype(BF16), gk[:, PAIR:] + last_v.astype(BF16))
    gq_ref[...] = gq
    gkv_ref[...] = gkv
    total = lambda value: jnp.sum(value.astype(F32), axis=0, keepdims=True)
    small_ref[...] = jnp.zeros_like(small_ref)
    small_ref[0:1, : 2 * PAIR] = total(grad_q * q_hat)
    small_ref[1:2, : 2 * PAIR] = total(grad_k * k_hat)
    small_ref[2:3, : 2 * PAIR] = total(grad_q)
    small_ref[3:4, : 2 * PAIR] = total(gq)
    small_ref[4:5, : 2 * PAIR] = total(gk)
    small_ref[5:6, :PAIR] = total(pair_v.astype(BF16))
    small_ref[5:6, 2 * PAIR :] = total(last_v.astype(BF16))
    acc_ref[:, :half] += nt(gkv, near_ref[:, PAIR : 4 * PAIR])
    acc_ref[:, half:] += nt(gkv, far_ref[:, PAIR : 4 * PAIR])
    own = slice(REACH, REACH + rows)
    for ref, cols in ((near_ref, slice(0, half)), (far_ref, slice(half, 2 * half))):
        acc_ref[own, cols] += nt(gq[:, :PAIR], ref[:, :PAIR]) + nt(gq[:, PAIR:], ref[:, 4 * PAIR : 5 * PAIR])


def attend_back_specs(rows, width, pieces, layer, index):
    half = width // 2
    window = rows + 2 * REACH
    full = whole((rows, width))
    in_specs = [
        full, *[slab(index, *shape) for shape in attend_shapes(rows, window)],
        pl.BlockSpec((3, window, rows), lambda step: (index * pieces + step, 0, 0)), piece_of(index, half, 6 * PAIR),
        piece_of(index, half, 6 * PAIR), heads_of(layer),
    ]
    out_specs = [
        column(rows, 2 * PAIR), column(window, 3 * PAIR), full, whole((REACH, width)), whole((REACH, width)), column(8, 3 * PAIR),
    ]
    out_shape = [
        shaped((rows, pieces * 2 * PAIR)), shaped((window, pieces * 3 * PAIR)), shaped((rows, width), F32),
        shaped((REACH, width)), shaped((REACH, width)), shaped((8, pieces * 3 * PAIR), F32),
    ]
    cost = pl.CostEstimate(
        flops=2 * window * width * width * 2 + 20 * window * rows * width * 2,
        bytes_accessed=20 * window * width,
        transcendentals=0,
    )
    return in_specs, out_specs, out_shape, [pltpu.VMEM((window, width), F32)], cost


def attend_back(gr, stored, near, far, heads, layer, index):
    rows, width = gr.shape
    pieces = near.shape[1]
    in_specs, out_specs, out_shape, scratch, cost = attend_back_specs(rows, width, pieces, layer, index)
    return pl.pallas_call(
        attend_back_kernel,
        grid=(pieces,),
        in_specs=in_specs,
        out_specs=out_specs,
        out_shape=out_shape,
        scratch_shapes=scratch,
        cost_estimate=cost,
        name="attend_back",
    )(gr, *stored, near, far, heads)


def attn_weight_kernel(a_ref, gq_ref, gkv_ref, gr_ref, o_ref, keep_ref, send_ref, a_t_ref, gr_t_ref):
    rows = gq_ref.shape[0]
    half = keep_ref.shape[0]

    @pl.when(pl.program_id(0) == 0)
    def _():
        a_t_ref[...] = a_ref[...].T
        gr_t_ref[...] = gr_ref[...].T

    for part, ref in ((slice(0, half), keep_ref), (slice(half, 2 * half), send_ref)):
        from_q = nn(a_t_ref[part, REACH : REACH + rows], gq_ref[...])
        from_o = nn(gr_t_ref[part, :], o_ref[...])
        ref[:, :PAIR] = from_q[:, :PAIR].astype(BF16)
        ref[:, PAIR : 4 * PAIR] = nn(a_t_ref[part, :], gkv_ref[...]).astype(BF16)
        ref[:, 4 * PAIR : 5 * PAIR] = (from_q[:, PAIR:] + from_o[:, :PAIR]).astype(BF16)
        ref[:, 5 * PAIR :] = from_o[:, PAIR:].astype(BF16)


def attn_weight_grads(a_win, gq, gkv, gr, o):
    _, window, width = a_win.shape
    rows = gr.shape[0]
    half = width // 2
    pieces = gq.shape[1] // (2 * PAIR)
    out = column(half, 6 * PAIR)
    return pl.pallas_call(
        attn_weight_kernel,
        grid=(pieces,),
        in_specs=[
            sheet(0, window, width), column(rows, 2 * PAIR), column(window, 3 * PAIR), whole((rows, width)),
            slab(0, rows, 2 * PAIR),
        ],
        out_specs=[out, out],
        out_shape=[shaped((half, pieces * 6 * PAIR))] * 2,
        scratch_shapes=[pltpu.VMEM((width, window), BF16), pltpu.VMEM((width, rows), BF16)],
        cost_estimate=pl.CostEstimate(
            flops=2 * width * width * (2 * window + 2 * rows), bytes_accessed=8 * width * width, transcendentals=0
        ),
        name="attn_weight_grads",
    )(a_win, gq, gkv, gr, o)


def mlp_weight_kernel(m_ref, gh_ref, gz_ref, act_ref, keep_ref, send_ref, m_t_ref, gz_t_ref):
    half = keep_ref.shape[0]
    wide = gh_ref.shape[1]

    @pl.when(pl.program_id(0) == 0)
    def _():
        m_t_ref[...] = m_ref[...].T
        gz_t_ref[...] = gz_ref[...].T

    for part, ref in ((slice(0, half), keep_ref), (slice(half, 2 * half), send_ref)):
        ref[:, :wide] = nn(m_t_ref[part, :], gh_ref[...]).astype(BF16)
        ref[:, wide:] = nn(gz_t_ref[part, :], act_ref[...]).astype(BF16)


def mlp_weight_grads(m, gh, gz, act):
    _, rows, width = m.shape
    half = width // 2
    hidden = gh.shape[1]
    pieces = lax.axis_size("tp")
    wide = hidden // pieces
    out = column(half, 2 * wide)
    return pl.pallas_call(
        mlp_weight_kernel,
        grid=(pieces,),
        in_specs=[sheet(0, rows, width), column(rows, wide), whole((rows, width)), slab(0, rows, wide)],
        out_specs=[out, out],
        out_shape=[shaped((half, 2 * hidden))] * 2,
        scratch_shapes=[pltpu.VMEM((width, rows), BF16), pltpu.VMEM((width, rows), BF16)],
        cost_estimate=pl.CostEstimate(
            flops=4 * width * hidden * rows, bytes_accessed=4 * width * hidden, transcendentals=0
        ),
        name="mlp_weight_grads",
    )(m, gh, gz, act)


class Scatter:
    KINDS = 7

    def __init__(self, peers, out, away, keep, core, first, second, given, send, recv):
        self.peers, self.out, self.away, self.keep, self.core_in = peers, out, away, keep, core
        self.first_in, self.second_in, self.given, self.send, self.recv = first, second, given, send, recv
        self.chunk, self.wide = out.shape
        self.half = self.wide // 2
        self.pieces = keep.shape[0]

    def copy(self, piece, kind, source, target, device):
        return pltpu.make_async_remote_copy(
            src_ref=source, dst_ref=target, send_sem=self.send.at[piece, kind], recv_sem=self.recv.at[piece, kind],
            device_id=device, device_id_type=MESH,
        )

    def copies(self, piece, stage):
        c, left, right = self.chunk, pl.ds(0, self.half), pl.ds(self.half, self.half)
        rows = lambda start, count=1: pl.ds(start * c, count * c)
        if stage == "core":
            return [self.copy(piece, 0, self.away.at[self.slot(piece)], self.core_in.at[piece], self.peers.core)]
        if stage == "first":
            source, target = self.keep.at[piece], self.first_in.at[piece]
            return [
                self.copy(piece, 1, source.at[rows(2, 2), left], target.at[:, left], self.peers.y),
                self.copy(piece, 2, source.at[rows(1), right], target.at[rows(0), right], self.peers.x),
                self.copy(piece, 3, source.at[rows(3), right], target.at[rows(1), right], self.peers.x),
            ]
        if stage == "second":
            source, target = self.keep.at[piece], self.second_in.at[piece]
            return [
                self.copy(piece, 4, source.at[rows(1), left], target.at[:, left], self.peers.x),
                self.copy(piece, 5, source.at[rows(2), right], target.at[:, right], self.peers.y),
            ]
        target = self.given.at[(piece + 1) % self.pieces]
        return [self.copy(piece, 6, self.keep.at[piece, rows(0), :], target, self.peers.along(1))]

    def start(self, piece, stage):
        for copy in self.copies(piece, stage):
            copy.start()

    def arrived(self, piece, stage):
        for copy in self.copies(piece, stage):
            copy.wait_recv()

    def add(self, piece, start, count, cols, source):
        step = 32

        @pl.loop(0, count * self.chunk // step)
        def _(index):
            row = pl.multiple_of(index * step, step)
            into = (piece, pl.ds(start * self.chunk + row, step), cols)
            self.keep[into] = self.keep[into] + source[pl.ds(row, step), cols]

    def slot(self, piece):
        return (piece + self.pieces - 1) % self.pieces % 2

    def room(self, index, piece):
        @pl.when(index > 1)
        def _():
            for copy in self.copies(lax.rem(piece + self.pieces - 2, self.pieces), "core"):
                copy.wait_send()

    def first(self, piece):
        self.arrived(piece, "core")
        self.add(piece, 0, 4, pl.ds(0, self.wide), self.core_in.at[piece])
        self.start(piece, "first")

    def second(self, piece):
        left, right = pl.ds(0, self.half), pl.ds(self.half, self.half)
        self.arrived(piece, "first")
        source = self.first_in.at[piece]
        self.add(piece, 0, 2, left, source)
        self.add(piece, 0, 1, right, source)
        self.add(piece, 2, 1, right, source.at[pl.ds(self.chunk, self.chunk)])
        self.start(piece, "second")

    def last(self, piece):
        self.arrived(piece, "second")
        kept = pl.ds(0, self.chunk)
        total = self.keep[piece, kept, :].astype(F32) + self.second_in[piece].astype(F32)
        if piece != 1:
            self.arrived((piece - 1) % self.pieces, "give")
            total += self.given[piece].astype(F32)
        if piece:
            self.keep[piece, kept, :] = total.astype(BF16)
            self.start(piece, "give")
        else:
            self.out[...] = total

    def done(self):
        for piece in range(self.pieces):
            for stage in ("core", "first", "second", "give"):
                if (stage != "give" or piece) and (stage != "core" or piece in (0, self.pieces - 1)):
                    for copy in self.copies(piece, stage):
                        copy.wait_send()

    def made(self, plan, index, piece):
        size = self.chunk * self.wide * 2
        both = lambda count: [("x", count * size), ("y", count * size)]
        key = (index, piece)
        rank = index * self.pieces + (piece - 1) % self.pieces
        plan.carry([("core", 4 * size)], ("core", *key))
        plan.add(rank, (self.first, piece), [("core", *key)], both(1), ("first", *key), index)
        plan.add(rank, (self.second, piece), [("first", *key)], both(0.5), ("second", *key), index)
        needs = [("second", *key)] + ([("give", index, (piece - 1) % self.pieces)] if piece != 1 else [])
        plan.add(rank, (self.last, piece), needs, [("z", size)] if piece else [], ("give", *key), index)


class Return:
    def __init__(self, edges, landed, rows, send, recv):
        self.edges, self.landed, self.send, self.recv = edges, landed, send, recv
        self.place, self.size = lax.axis_index("tp"), lax.axis_size("tp")
        spill = REACH - rows
        self.moves = [
            (1, 1, pl.ds(0, rows), pl.ds(0, rows), 0),
            (-1, 0, pl.ds(spill, rows), pl.ds(rows, rows), 0),
            (2, 1, pl.ds(rows, spill), pl.ds(2 * rows, spill), 0),
            (-2, 0, pl.ds(0, spill), pl.ds(2 * rows + spill, spill), rows - spill),
        ]

    def inside(self, distance):
        other = self.place + distance
        return jnp.logical_and(other >= 0, other < self.size)

    def copy(self, index):
        distance, which, source, target, _ = self.moves[index]
        return pltpu.make_async_remote_copy(
            src_ref=self.edges.at[which, source, :], dst_ref=self.landed.at[target, :], send_sem=self.send.at[index],
            recv_sem=self.recv.at[index], device_id={"tp": self.place + distance}, device_id_type=MESH,
        )

    def begin(self):
        for index, (distance, *_) in enumerate(self.moves):

            @pl.when(self.inside(distance))
            def _():
                self.copy(index).start()

    def end(self, total_ref):
        for index, (distance, _, _, target, start) in enumerate(self.moves):

            @pl.when(self.inside(distance))
            def _():
                self.copy(index).wait_send()

            @pl.when(self.inside(-distance))
            def _():
                self.copy(index).wait_recv()
                total_ref[pl.ds(start, target.size), :] += self.landed[target, :].astype(F32)


def backward_kernel(
    cot_ref, feats_ref, m_ref, mid_ref, a_win_ref, x0_ref, x2_ref,
    mlp_near_ref, mlp_far_ref, slope_ref, act_ref,
    q_ref, kv_ref, q_hat_ref, k_hat_ref, q_scale_ref, k_scale_ref, p_ref, attn_near_ref, attn_far_ref, heads_ref, o_ref,
    g_ref, up_grad_ref, head_sums_ref, mlp_sums_ref, norm_sums_ref, mlp_out, attn_out,
    gz_ref, gh_ref, g1_ref, gr_ref, acc_ref, window_ref, gq_ref, gkv_ref, total_ref, turned_ref, a_t_ref, edges_ref,
    landed_ref, halo_send, halo_recv, free, fetched, *buffers,
):
    layers, pieces, rows = up_grad_ref.shape[0], up_grad_ref.shape[1], g_ref.shape[0]
    half = g_ref.shape[1] // 2
    wide = slope_ref.shape[1]
    own = slice(REACH, REACH + rows)
    step = pl.program_id(0)
    peers = Neighbours()
    scatter_of = lambda layer, which: Scatter(
        peers, (mlp_out, attn_out)[which].at[layer], *buffers[8 * which : 8 * which + 6],
        *[item.at[layer] for item in buffers[8 * which + 6 : 8 * which + 8]],
    )
    back = lambda layer: Return(edges_ref, landed_ref.at[layer], rows, halo_send.at[layer], halo_recv.at[layer])

    def fetch(source, target):
        copy = pltpu.make_async_copy(source, target, fetched)
        copy.start()
        copy.wait()

    def halo_back(layer):
        back(layer).end(total_ref)

    def made_free(item):
        layer, which = item
        scatter_of(layer + 1, which).done()
        for target in peers.all():
            pl.semaphore_signal(free.at[layer, which], inc=1, device_id=target, device_id_type=MESH)
        pl.semaphore_wait(free.at[layer, which], len(peers.all()))

    plan = Plan()
    plan.spend(2.5)
    halo_size = 2 * half * 2 * 2 * rows
    order = [(index + 1) % pieces for index in range(pieces)]
    for layer in reversed(range(layers)):
        for which in range(2):
            for index, piece in enumerate(order):
                at = (2 * (layers - 1 - layer) + which) * pieces + index
                if index == 0 and layer + 1 < layers:
                    if which == 0:
                        plan.wait(("halo", layer + 1), (halo_back, layer + 1), at, 0)
                    plan.finish(2 * (layers - 2 - layer) + which, at, 0)
                    plan.table.setdefault((at, 0), []).append((made_free, (layer, which)))
                plan.slot(at, 0)
                for slot, time in enumerate(((1.5,), (2.2, 1.3, 1.3))[which]):
                    plan.spend(time)
                    plan.slot(at, slot + 1)
                plan.spend((2.6, 3.0)[which])
                scatter_of(layer, which).made(plan, 2 * (layers - 1 - layer) + which, piece)
        plan.carry([("z", halo_size)], ("halo", layer))
    ending = 2 * layers * pieces
    plan.wait(("halo", 0), (halo_back, 0), ending, 0)
    plan.finish(None, ending, 1)
    table = plan.table

    def run(at, slot):
        if (at, slot) in table:

            @pl.when(step == at)
            def _():
                for work, item in table[at, slot]:
                    work(item)

    phase = step // pieces
    layer = jnp.maximum(layers - 1 - phase // 2, 0)
    index = lax.rem(step, pieces)
    piece = lax.rem(index + 1, pieces)
    in_mlp, in_attend = lax.rem(phase, 2) == 0, lax.rem(phase, 2) == 1
    is_ending = step == ending

    @pl.when(step == 0)
    def _():
        peers.greet()
        fetch(cot_ref, g_ref)

    run(ending, 0)
    for at in range(2 * pieces, ending, 2 * pieces):
        run(at, 0)

    def through_norm(layer, x):
        fetch(x, acc_ref)
        total = total_ref[...]
        hat, scale = row_norm(acc_ref[...])
        g_ref[...] = g1_ref[...] + row_norm_back(total * line(feats_ref.at[layer], LN_GAIN[0]), hat, scale)
        norm_sums_ref[layer] = jnp.zeros(norm_sums_ref.shape[1:], F32)
        norm_sums_ref[layer, 0:1, :] = jnp.sum(total * hat, axis=0, keepdims=True)
        norm_sums_ref[layer, 1:2, :] = jnp.sum(total, axis=0, keepdims=True)

    for above in range(1, layers):

        @pl.when(step == 2 * (layers - above) * pieces)
        def _():
            through_norm(above, x2_ref.at[above - 1])

    @pl.when(is_ending)
    def _():
        through_norm(0, x0_ref)

    @pl.when(jnp.logical_and(in_mlp, step < ending))
    def _():
        def hook(slot):
            for at in range(ending):
                if at // pieces % 2 == 0 and not (slot == 0 and at % (2 * pieces) == 0 and at):
                    run(at, slot)

        hook(0)
        up, down = pl.ds(0, wide), pl.ds(wide, wide)
        mlp_back_work(
            g_ref, mlp_near_ref.at[:, down], mlp_far_ref.at[:, down], slope_ref, mlp_near_ref.at[:, up], mlp_far_ref.at[:, up],
            mid_ref, feats_ref.at[layer], gz_ref, gh_ref, up_grad_ref.at[layer, piece], g1_ref, gr_ref,
            mlp_sums_ref.at[layer], acc_ref, index == 0, index == pieces - 1, hook,
        )

        @pl.when(index == 0)
        def _():
            turned_ref[0] = m_ref[...].T
            turned_ref[1] = gz_ref[...].T

        away, keep = buffers[0], buffers[1]
        scatter = scatter_of(layer, 0)
        scatter.room(index, piece)
        for part, ref in ((slice(0, half), keep.at[piece]), (slice(half, 2 * half), away.at[scatter.slot(piece)])):
            ref[:, :wide] = nn(turned_ref[0, part, :], gh_ref[...]).astype(BF16)
            ref[:, wide:] = nn(turned_ref[1, part, :], act_ref[...]).astype(BF16)
        scatter.start(piece, "core")

    @pl.when(in_attend)
    def _():
        def hook(slot):
            for at in range(ending):
                if at // pieces % 2 == 1:
                    run(at, slot)

        hook(0)

        @pl.when(index == 0)
        def _():
            window_ref[...] = jnp.zeros_like(window_ref)
            a_t_ref[...] = a_win_ref[...].T
            turned_ref[0] = gr_ref[...].T

        attend_back_work(
            gr_ref, q_ref, kv_ref, q_hat_ref, k_hat_ref, q_scale_ref, k_scale_ref, p_ref, attn_near_ref, attn_far_ref,
            heads_ref, gq_ref, gkv_ref, head_sums_ref.at[layer, piece], window_ref, hook,
        )
        away, keep = buffers[8], buffers[9]
        scatter = scatter_of(layer, 1)
        scatter.room(index, piece)
        for part, ref in ((slice(0, half), keep.at[piece]), (slice(half, 2 * half), away.at[scatter.slot(piece)])):
            from_q = nn(a_t_ref[part, own], gq_ref[...])
            from_o = nn(turned_ref[0, part, :], o_ref[...])
            ref[:, :PAIR] = from_q[:, :PAIR].astype(BF16)
            ref[:, PAIR : 4 * PAIR] = nn(a_t_ref[part, :], gkv_ref[...]).astype(BF16)
            ref[:, 4 * PAIR : 5 * PAIR] = (from_q[:, PAIR:] + from_o[:, :PAIR]).astype(BF16)
            ref[:, 5 * PAIR :] = from_o[:, PAIR:].astype(BF16)
        scatter.start(piece, "core")

        @pl.when(index == pieces - 1)
        def _():
            edges_ref[0] = window_ref[:REACH, :].astype(BF16)
            edges_ref[1] = window_ref[REACH + rows :, :].astype(BF16)
            total_ref[...] = window_ref[own, :]
            back(layer).begin()

    run(ending, 1)

    @pl.when(is_ending)
    def _():
        for which in range(2):
            scatter_of(0, which).done()


def scatter_buffers(layers, pieces, chunk, wide):
    buffer = lambda rows: pltpu.VMEM((pieces, rows * chunk, wide), BF16)
    semaphores = pltpu.SemaphoreType.DMA((layers, pieces, Scatter.KINDS))
    away = pltpu.VMEM((2, 4 * chunk, wide), BF16)
    return [away, buffer(4), buffer(4), buffer(2), buffer(1), buffer(1), semaphores, semaphores]


def backward(cotangent, feats, heads, start, saved):
    *stored, o, act, slope, mid, m, x2, a_win, attn_near, attn_far, mlp_near, mlp_far = saved
    layers, window, width = a_win.shape
    rows, half, pieces = m.shape[1], width // 2, attn_near.shape[1]
    hidden = act.shape[2]
    wide, chunk = hidden // pieces, half // 4

    def mlp_at(step):
        phase = jnp.minimum(step // pieces, 2 * layers - 1)
        index = jnp.where(lax.rem(phase, 2) == 0, lax.rem(step, pieces), pieces - 1)
        return layers - 1 - phase // 2, lax.rem(index + 1, pieces)

    def attend_at(step):
        phase = jnp.minimum(step // pieces, 2 * layers - 1)
        index = jnp.where(lax.rem(phase, 2) == 1, lax.rem(step, pieces), 0)
        index = jnp.where(step == 2 * layers * pieces, pieces - 1, index)
        return layers - 1 - phase // 2, lax.rem(index + 1, pieces)

    once = lambda shape: pl.BlockSpec(shape, lambda step: (0,) * len(shape), pipeline_mode=pl.Buffered(1))
    weight = lambda at, wide: pl.BlockSpec((None, None, half, wide), lambda step: (*at(step), 0, 0))
    cols = lambda at, height, wide: pl.BlockSpec((None, height, wide), lambda step: (at(step)[0], 0, at(step)[1]))
    by_heads = pl.BlockSpec((3, window, rows), lambda step: (attend_at(step)[0] * pieces + attend_at(step)[1], 0, 0))
    layer_heads = pl.BlockSpec((None, None, HEADS, 3 * PAIR), lambda step: (attend_at(step)[1], attend_at(step)[0], 0, 0))
    layer_sheet = lambda at, height: pl.BlockSpec(
        (None, height, width), lambda step: (at(step)[0], 0, 0), pipeline_mode=pl.Buffered(1)
    )
    outs = [
        (rows, width), (layers, pieces, 1, wide), (layers, pieces, 8, 3 * PAIR), (layers, 8, width), (layers, 8, width),
        (layers, chunk, 2 * wide), (layers, chunk, 6 * PAIR),
    ]
    vmem = lambda shape, kind=BF16: pltpu.VMEM(shape, kind)
    inputs = (cotangent, feats, m, mid, a_win, start, x2, mlp_near, mlp_far, slope, act, *stored, attn_near, attn_far, heads, o)
    return pl.pallas_call(
        backward_kernel,
        grid=(2 * layers * pieces + 1,),
        in_specs=[
            ANY, once(feats.shape), layer_sheet(mlp_at, rows), layer_sheet(mlp_at, rows), layer_sheet(attend_at, window), ANY, ANY,
            weight(mlp_at, 2 * wide), weight(mlp_at, 2 * wide), cols(mlp_at, rows, wide),
            cols(mlp_at, rows, wide), *[cols(attend_at, *shape) for shape in attend_shapes(rows, window)], by_heads,
            weight(attend_at, 6 * PAIR), weight(attend_at, 6 * PAIR), layer_heads, cols(attend_at, rows, 2 * PAIR),
        ],
        out_specs=[once(shape) for shape in outs],
        out_shape=[shaped(shape, F32) for shape in outs],
        scratch_shapes=[
            vmem((rows, width)), vmem((rows, wide)), vmem((rows, width), F32), vmem((rows, width)),
            vmem((rows, width), F32), vmem((window, width), F32), vmem((rows, 2 * PAIR)), vmem((window, 3 * PAIR)),
            vmem((rows, width), F32), vmem((2, width, rows)), vmem((width, window)), vmem((2, REACH, width)),
            vmem((layers, 2 * REACH, width)), pltpu.SemaphoreType.DMA((layers, 4)), pltpu.SemaphoreType.DMA((layers, 4)),
            pltpu.SemaphoreType.REGULAR((layers, 2)), pltpu.SemaphoreType.DMA, *scatter_buffers(layers, pieces, chunk, 2 * wide),
            *scatter_buffers(layers, pieces, chunk, 6 * PAIR),
        ],
        compiler_params=params(40, VMEM),
        name="backward",
    )(*inputs)


def flip(array, bit, axis="fsdp"):
    size = lax.axis_size(axis)
    return lax.ppermute(array, axis, [(i, i ^ (1 << bit)) for i in range(size)])


def ring(array):
    size = lax.axis_size("tp")
    return lax.ppermute(array, "tp", [(i, (i + 1) % size) for i in range(size)])


def hop(array, distance):
    size = lax.axis_size("tp")
    return lax.ppermute(array, "tp", [(i, i + distance) for i in range(size) if 0 <= i + distance < size])


def bits_of(size):
    return size.bit_length() - 1


def row_bits(first_top):
    count = bits_of(lax.axis_size("fsdp"))
    tops = [count - 1, count - 2] if first_top else [count - 2, count - 1]
    return list(range(1, count - 2)), tops


def gather_by_permutes(block, first_top):
    pieces = [block]
    for _ in range(lax.axis_size("tp") - 1):
        pieces.append(ring(pieces[-1]))
    block = jnp.concatenate(pieces, axis=1)
    low, tops = row_bits(first_top)
    have = []
    for bit in low + tops:
        axis = sum(other > bit for other in have)
        block = jnp.stack([block, flip(block, bit)], axis=axis)
        have.append(bit)
    block = block.reshape((-1, len(pieces), pieces[0].shape[1])).transpose(1, 0, 2)[None]
    return block, flip(block, 0)


def add(left, right, kind=BF16):
    return (left.astype(F32) + right.astype(F32)).astype(kind)


def reduce_by_permutes(keep, send, first_top):
    low, tops = row_bits(first_top)
    block = add(keep, flip(send, 0))
    order = tops + low[::-1]
    have = sorted(order, reverse=True)
    block = block.reshape((2,) * len(have) + (-1, block.shape[-1]))
    for bit in order:
        axis = have.index(bit)
        mine = lax.index_in_dim(block, 0, axis, keepdims=False)
        other = lax.index_in_dim(block, 1, axis, keepdims=False)
        block = add(mine, flip(other, bit))
        have.remove(bit)
    pieces = jnp.split(block, lax.axis_size("tp"), axis=1)
    total = pieces[1]
    for piece in pieces[2:]:
        total = add(ring(total), piece)
    return add(ring(total), pieces[0], F32)


def attn_shard(w_qkv, w_out):
    q, k, v = (w_qkv[:, which] for which in range(3))
    o = w_out.T
    return side(q[:, :PAIR], k[:, :PAIR], v[:, :PAIR], k[:, PAIR:], v[:, PAIR:], q[:, PAIR:], o[:, PAIR:], o[:, :PAIR])


def attn_unshard(block):
    tile = lambda start, wide=PAIR: block[:, start : start + wide]
    q = side(tile(0), tile(4 * PAIR, HD))
    k = side(tile(PAIR), tile(3 * PAIR, HD))
    v = side(tile(2 * PAIR), tile(3 * PAIR + HD, HD))
    o = side(tile(5 * PAIR), tile(4 * PAIR + HD, HD))
    return jnp.stack([q, k, v], axis=1), o.T


def body(
    tokens, segment_ids, patch_pos, row_table, col_table, ln_gain, ln_bias, qkv_bias, qk_gain, query_bias, out_bias,
    fc1_bias, fc2_bias, w_qkv, w_out, w_fc1, w_fc2, cotangent,
):
    layers = w_qkv.shape[0]
    rows, width = tokens.shape
    half = width // 2
    fsdp, tp = lax.axis_size("fsdp"), lax.axis_size("tp")
    f_index, t_index = lax.axis_index("fsdp"), lax.axis_index("tp")
    hidden = fc1_bias.shape[1] * fsdp * tp
    grid = row_table.shape[0]
    fine = width // (fsdp * tp)
    parts = hidden // width
    in_kernel = fsdp == 8

    place = jnp.arange(width, dtype=jnp.int32)
    chunk = width // fsdp
    slot = place // chunk
    away = (slot % (fsdp // 2)) * 2 + slot // (fsdp // 2)
    feature_at = (f_index ^ away) * chunk + place % chunk
    head_cols = width // tp
    spot = jnp.arange(tp * 3 * PAIR, dtype=jnp.int32)
    tile, part = spot % (3 * PAIR) // PAIR, spot % PAIR // HD
    head = jnp.where(tile == 0, part, jnp.where(tile == part + 1, 2, -fsdp * tp))
    head_at = ((t_index - spot // (3 * PAIR)) % tp) * head_cols + head * HD + spot % HD
    to_feature = (place[:, None] == feature_at[None, :]).astype(BF16)
    to_head = (place[:, None] == head_at[None, :]).astype(BF16)
    device = jnp.arange(fsdp * tp, dtype=jnp.int32)
    wanted = ((t_index - device // fsdp) % tp) * fsdp + device % fsdp
    to_hidden = (wanted[:, None] == device[None, :]).astype(BF16)

    by_layer = lambda *items: jnp.concatenate([item.reshape(layers, -1, fine) for item in items], axis=1).reshape(-1, fine)
    shares = [
        row_table, col_table, by_layer(ln_gain, ln_bias, out_bias, fc2_bias), by_layer(qkv_bias, qk_gain, query_bias),
        fc1_bias.reshape(layers * parts, fine),
    ]
    count = sum(item.shape[0] for item in shares)
    attn_shards = jnp.stack([attn_shard(w_qkv[layer], w_out[layer]) for layer in range(layers)])
    mlp_shards = jnp.concatenate([w_fc1, w_fc2.transpose(0, 2, 1)], axis=2)
    grid_ids = jnp.arange(grid, dtype=jnp.int32)
    row_hot = patch_pos[0][:, None] == grid_ids[None, :]
    col_hot = patch_pos[1][:, None] == grid_ids[None, :]
    hot = side(row_hot, col_hot).astype(BF16)
    tokens = jnp.dot(tokens, to_feature, preferred_element_type=F32)
    segments = segment_ids[0]
    padded = jnp.pad(segments, (REACH, REACH), constant_values=-1)
    seg_k = lax.dynamic_slice_in_dim(padded, t_index * rows, rows + 2 * REACH).reshape(-1, 1)
    seg_q = lax.dynamic_slice_in_dim(segments, t_index * rows, rows).reshape(1, -1)
    spill = REACH - rows

    if in_kernel:
        share = jnp.concatenate([jnp.pad(item, ((0, -item.shape[0] % 16), (0, PAIR - fine))) for item in shares], axis=0)
        *kept, start, feats, heads, a_win, attn_near, attn_far, mlp_near, mlp_far = forward(
            tokens, hot, share, seg_k, seg_q, attn_shards, mlp_shards
        )
        residual = kept[-1][layers - 1]
        kept += [a_win, attn_near, attn_far, mlp_near, mlp_far]
    else:
        small = jnp.concatenate(shares, axis=0)
        flat = small.reshape(1, -1)
        for bit in range(bits_of(tp)):
            flat = jnp.concatenate([flat, flip(flat, bit, "tp")], axis=0)
        for bit in range(bits_of(fsdp)):
            flat = jnp.concatenate([flat, flip(flat, bit)], axis=0)
        flat = flat[jnp.arange(fsdp * tp) ^ (f_index * tp + t_index)]
        gathered = flat.reshape(fsdp * tp, count, fine)
        lined = gathered.transpose(1, 0, 2).reshape(count, width)
        wide = 2 * grid + 6 * layers
        feats = jnp.dot(lined[:wide], to_feature, preferred_element_type=F32)
        heads = jnp.dot(lined[wide : wide + 6 * layers], to_head, preferred_element_type=F32)
        up_shift = jnp.einsum(
            "or,rlsi->losi",
            to_hidden,
            gathered[:, wide + 6 * layers :].reshape(fsdp * tp, layers, parts, fine),
            preferred_element_type=F32,
        ).reshape(layers, tp, 1, hidden // tp)
        tables = feats[: 2 * grid].astype(BF16)
        feats = feats[2 * grid :].reshape(layers, FEATS, width)

        heads = heads.reshape(layers, HEADS, tp, 3 * PAIR).transpose(2, 0, 1, 3)
        residual = tokens + jnp.dot(hot, tables, preferred_element_type=F32)
        hat, _ = row_norm(residual)
        a_own = (hat * feats[0, LN_GAIN[0]] + feats[0, LN_BIAS[0]]).astype(BF16)
        saved = []
        for layer in range(layers):
            a_win = jnp.concatenate(
                [hop(a_own[rows - spill :], 2), hop(a_own, 1), a_own, hop(a_own, -1), hop(a_own[:spill], -2)], axis=0
            )
            attn_near, attn_far = gather_by_permutes(attn_shards[layer], layer % 2 == 0)
            *stored, probs, o, mid, m = attend(
                a_win, attn_near, attn_far, heads, feats, residual, seg_k, seg_q, layer
            )
            mlp_near, mlp_far = gather_by_permutes(mlp_shards[layer], layer % 2 == 1)
            act, slope, x2 = mlp(m, mid, mlp_near, mlp_far, up_shift, feats, layer)
            stored = [item[None] for item in stored] + [probs]
            kept = [item[None] for item in (o, mid, m, act, slope)]
            saved.append((residual, a_win[None], stored, *kept, attn_near, attn_far, mlp_near, mlp_far))
            residual = x2
            if layer + 1 < layers:
                hat, _ = row_norm(residual)
                a_own = (
                    hat * feats[layer + 1, LN_GAIN[0]] + feats[layer + 1, LN_BIAS[0]]
                ).astype(BF16)

    restore = functools.partial(
        lax.dot_general, dimension_numbers=(((1,), (1,)), ((), ())), precision=HIGHEST, preferred_element_type=F32
    )
    exact = to_feature.astype(F32)
    activations = restore(residual, exact)
    cotangent_here = jnp.dot(cotangent, exact, precision=HIGHEST, preferred_element_type=F32)
    kept_sums = [None] * layers
    if in_kernel:
        grad, up_grads, attn_sums, mlp_sums, norm_sums, mlp_blocks, attn_blocks = backward(cotangent_here, feats, heads, start, kept)
        attn_sums = attn_sums.transpose(0, 2, 1, 3).reshape(layers, 8, -1)
        kept_sums = [
            (norm_sums[layer, 0], norm_sums[layer, 1], mlp_sums[layer], attn_sums[layer], up_grads[layer].reshape(parts, width))
            for layer in range(layers)
        ]
    else:
        grad, mlp_blocks, attn_blocks = cotangent_here, [None] * layers, [None] * layers
        for layer in reversed(range(layers)):
            x, a_win, stored, o, mid, m, act, slope, attn_near, attn_far, mlp_near, mlp_far = saved[layer]
            gz, gh, up_grad, g1, gr, mlp_small = mlp_back(grad, mlp_near, mlp_far, slope, mid, feats, layer, 0)
            mlp_blocks[layer] = reduce_by_permutes(*mlp_weight_grads(m, gh, gz, act), layer % 2 == 0)
            gq, gkv, mine, left, right, attn_small = attend_back(gr, stored, attn_near, attn_far, heads, layer, 0)
            attn_blocks[layer] = reduce_by_permutes(*attn_weight_grads(a_win, gq, gkv, gr, o), layer % 2 == 1)
            ends = jnp.concatenate([hop(right[rows:], 2), hop(left[:spill], -2)], axis=0).astype(F32)
            attn_grad = mine + hop(right[:rows], 1).astype(F32) + hop(left[spill:], -1).astype(F32) + ends
            hat, scale = row_norm(x)
            grad = g1 + row_norm_back(attn_grad * feats[layer, LN_GAIN[0]], hat, scale)
            kept_sums[layer] = (
                jnp.sum(attn_grad * hat, axis=0), jnp.sum(attn_grad, axis=0), mlp_small, attn_small,
                up_grad.reshape(parts, width),
            )
    middle = mlp_blocks[0].shape[1] // 2
    w_fc1_grad = [block[:, :middle] for block in mlp_blocks]
    w_fc2_grad = [block[:, middle:].T for block in mlp_blocks]
    w_qkv_grad, w_out_grad = zip(*[attn_unshard(block) for block in attn_blocks])

    token_grad = restore(grad, exact)
    row_grad = jnp.einsum("tg,td->gd", row_hot.astype(F32), grad, precision=HIGHEST)
    col_grad = jnp.einsum("tg,td->gd", col_hot.astype(F32), grad, precision=HIGHEST)
    featured = [row_grad, col_grad]
    headed = []
    for a_gain, a_shift, sums, head_sums, _ in kept_sums:
        featured.append(jnp.stack([a_gain, sums[2], a_shift, sums[3], sums[1], sums[0]]))
        headed += [head_sums[3:6], head_sums[0:2], head_sums[2:3]]
    headed = jnp.concatenate(headed)
    spread = jnp.concatenate(
        [restore(jnp.concatenate(featured), to_feature.astype(F32)), restore(headed, to_head.astype(F32))]
    )
    spread = spread.reshape(-1, fsdp * tp, fine).transpose(1, 0, 2)
    up_all = jnp.stack([item[4] for item in kept_sums]).reshape(layers, fsdp * tp, parts * fine)
    up_all = jnp.einsum("or,lok->rlk", to_hidden.astype(F32), up_all, precision=HIGHEST)
    flat = jnp.concatenate([spread.reshape(fsdp * tp, -1), up_all.reshape(fsdp * tp, -1)], axis=1)
    if in_kernel:
        flat = exchange(lanes(flat), fsdp * tp, True, 60).reshape(-1)[: count * fine]
    else:
        flat = flat[jnp.arange(fsdp * tp) ^ (f_index * tp + t_index)]
        for bit in reversed(range(bits_of(fsdp))):
            middle = flat.shape[0] // 2
            flat = flat[:middle] + flip(flat[middle:], bit)
        for bit in reversed(range(bits_of(tp))):
            middle = flat.shape[0] // 2
            flat = flat[:middle] + flip(flat[middle:], bit, "tp")
    found = flat.reshape(-1, fine)
    rows_g, cols_g, rest = found[:grid], found[grid : 2 * grid], found[2 * grid :]
    by_feature = rest[: layers * FEATS].reshape(layers, FEATS, fine)
    by_head = rest[layers * FEATS : layers * (FEATS + HEADS)].reshape(layers, HEADS, fine)
    up_g = rest[layers * (FEATS + HEADS) :].reshape(layers, parts * fine)
    gain_g, shift_g, out_g, last_g = by_feature[:, :2], by_feature[:, 2:4], by_feature[:, OUT_BIAS], by_feature[:, LAST_BIAS]
    proj_g, head_gain_g, head_shift_g = by_head[:, :3], by_head[:, 3:5], by_head[:, HEAD_BIAS]
    return (
        activations, token_grad, rows_g, cols_g, gain_g, shift_g, proj_g, head_gain_g, head_shift_g, out_g, up_g, last_g,
        jnp.stack(w_qkv_grad), jnp.stack(w_out_grad), jnp.stack(w_fc1_grad), jnp.stack(w_fc2_grad),
    )


def solution(mesh):
    both = ("fsdp", "tp")
    in_specs = (
        P(both, None), P("fsdp", None), P(None, both), P(None, both), P(None, both), P(None, None, both),
        P(None, None, both), P(None, None, both), P(None, None, both), P(None, both), P(None, both), P(None, both),
        P(None, both), P(None, "fsdp", None, "tp"), P(None, "tp", "fsdp"), P(None, "fsdp", "tp"), P(None, "tp", "fsdp"),
        P(both, None),
    )
    out_specs = (
        P(both, None), P(both, None), P(None, both), P(None, both), P(None, None, both), P(None, None, both),
        P(None, None, both), P(None, None, both), P(None, both), P(None, both), P(None, both), P(None, both),
        P(None, "fsdp", None, "tp"), P(None, "tp", "fsdp"), P(None, "fsdp", "tp"), P(None, "tp", "fsdp"),
    )
    return jax.shard_map(body, mesh=mesh, in_specs=in_specs, out_specs=out_specs, check_vma=False)
```

```python
import functools

import jax
import jax.numpy as jnp
from jax import lax
from jax.experimental import pallas as pl
from jax.experimental.pallas import tpu as pltpu
from jax.sharding import PartitionSpec as P

HD = 64
PAIR = 128
REACH = 384
EPS = 1e-06
FILL = -1e30
ROOT_HALF = 0.7071067811865476
INV_ROOT_TWO_PI = 0.3989422804014327
HIGHEST = lax.Precision.HIGHEST
F32 = jnp.float32
BF16 = jnp.bfloat16
MESH = pl.DeviceIdType.MESH
VMEM = 67043328
ANY = pl.BlockSpec(memory_space=pl.ANY)


def nn(left, right):
    return lax.dot_general(left, right, (((1,), (0,)), ((), ())), preferred_element_type=F32)


def nt(left, right):
    return lax.dot_general(left, right, (((1,), (1,)), ((), ())), preferred_element_type=F32)


def halves(array):
    middle = array.shape[1] // 2
    return array[:, :middle], array[:, middle:]


def row_norm(value):
    centered = value - jnp.mean(value, axis=-1, keepdims=True)
    scale = lax.rsqrt(jnp.mean(centered * centered, axis=-1, keepdims=True) + EPS)
    return centered * scale, scale


def row_norm_back(grad_hat, normed, scale):
    return scale * (
        grad_hat
        - jnp.mean(grad_hat, axis=-1, keepdims=True)
        - normed * jnp.mean(grad_hat * normed, axis=-1, keepdims=True)
    )


def head_mean(value, exact=False):
    wide = value.shape[1]
    rows = lax.broadcasted_iota(jnp.int32, (wide, wide), 0) // HD
    cols = lax.broadcasted_iota(jnp.int32, (wide, wide), 1) // HD
    spread = jnp.where(rows == cols, 1.0 / HD, 0.0).astype(BF16)
    high = value.astype(BF16)
    mean = nn(high, spread)
    if exact:
        mean += nn((value - high.astype(F32)).astype(BF16), spread)
    return mean


def head_norm(value):
    centered = value - head_mean(value, exact=True)
    scale = lax.rsqrt(head_mean(centered * centered) + EPS)
    return centered * scale, scale


def head_norm_back(grad_hat, normed, scale):
    return scale * (grad_hat - head_mean(grad_hat) - normed * head_mean(grad_hat * normed))


def only(array, part):
    return jnp.where(lax.broadcasted_iota(jnp.int32, (1, PAIR), 1) // HD == part, array, jnp.zeros_like(array))


def side(*parts):
    return jnp.concatenate(parts, axis=1)


def whole(shape):
    return pl.BlockSpec(shape, lambda step: (0,) * len(shape))


def column(height, wide, every=1, first=0):
    return pl.BlockSpec((height, wide), lambda step: (0, step * every + first))


def piece_of(layer, height, wide, first=0):
    return pl.BlockSpec((None, None, height, wide), lambda step: (layer, step, 0, first))


def slab(layer, height, wide):
    return pl.BlockSpec((None, height, wide), lambda step: (layer, 0, step))


def heads_of(layer):
    return pl.BlockSpec((None, None, HEADS, 3 * PAIR), lambda step: (step, layer, 0, 0))


def sheet(layer, height, wide):
    return pl.BlockSpec((None, height, wide), lambda step: (layer, 0, 0))


def shaped(shape, kind=BF16):
    return jax.ShapeDtypeStruct(shape, kind)


class Neighbours:
    def __init__(self):
        fsdp, tp = lax.axis_index("fsdp"), lax.axis_index("tp")
        self.size = lax.axis_size("tp")
        self.tp = tp
        self.x, self.y, self.core = ({"fsdp": jnp.bitwise_xor(fsdp, bit)} for bit in (2, 4, 1))

    def along(self, distance):
        return {"tp": lax.rem(self.tp + distance, self.size)}

    def all(self):
        return [self.x, self.y, self.core] + [self.along(distance) for distance in range(1, self.size)]

    def greet(self):
        targets = self.all()
        barrier = pltpu.get_barrier_semaphore()
        for target in targets:
            pl.semaphore_signal(barrier, inc=1, device_id=target, device_id_type=MESH)
        pl.semaphore_wait(barrier, len(targets))


class Plan:
    LINKS = {"x": (45.5e3, 1.5), "y": (45.5e3, 1.5), "z": (45.5e3, 2.2), "core": (600e3, 1.0)}

    def __init__(self):
        self.depth, self.clock = {"x": 5.0, "y": 5.0, "z": 5.0, "core": 20.0}, 0.0
        self.free, self.here, self.jobs, self.table = dict.fromkeys(self.LINKS, 0.0), {}, [], {}

    def add(self, rank, work, needs, copies, gives, group):
        self.jobs.append((rank, len(self.jobs), work, needs, copies, gives, group))
        self.jobs.sort(key=lambda job: job[:2])

    def carry(self, copies, gives):
        end = self.clock
        for link, size in copies:
            rate, latency = self.LINKS[link]
            self.free[link] = max(self.free[link], self.clock) + size / rate
            end = max(end, self.free[link] + latency)
        self.here[gives] = end

    def slot(self, *at):
        found = True
        while found:
            found = False
            for job in self.jobs:
                _, _, work, needs, copies, gives, _ = job
                ready = all(self.here.get(need, float("inf")) <= self.clock for need in needs)
                if ready and all(self.free[link] - self.clock < self.depth[link] for link, _ in copies):
                    self.carry(copies, gives)
                    self.table.setdefault(at, []).append(work)
                    self.jobs.remove(job)
                    found = True
                    break

    def wait(self, key, work, *at):
        self.slot(*at)
        while self.here.get(key, float("inf")) > self.clock:
            self.clock += 0.25
            self.slot(*at)
        self.table.setdefault(at, []).append(work)

    def finish(self, group, *at):
        self.slot(*at)
        while any(group in (None, job[-1]) for job in self.jobs):
            self.clock += 0.25
            self.slot(*at)

    def spend(self, time):
        self.clock += time


def turn(index, pieces):
    if isinstance(index, int):
        return (index + 1) // 2 if index % 2 else (pieces - index // 2) % pieces
    return jnp.where(lax.rem(index, 2) == 1, (index + 1) // 2, lax.rem(pieces - index // 2, pieces))


class Gather:
    KINDS = 7

    def __init__(self, peers, shard, near, far, send, recv, local, near_out, far_out, stored):
        self.peers, self.shard, self.near, self.far = peers, shard, near, far
        self.send, self.recv, self.local = send, recv, local
        self.outs, self.stored = (near_out, far_out), stored
        self.chunk, self.wide = shard.shape
        self.pieces = near.shape[0]

    def at(self, piece, start, count, half=None):
        first, wide = (0, self.wide) if half is None else (half * (self.wide // 2), self.wide // 2)
        return self.near.at[piece, pl.ds(start * self.chunk, count * self.chunk), pl.ds(first, wide)]

    def copy(self, piece, kind, source, target, device):
        return pltpu.make_async_remote_copy(
            src_ref=source, dst_ref=target, send_sem=self.send.at[piece, kind], recv_sem=self.recv.at[piece, kind],
            device_id=device, device_id_type=MESH,
        )

    def copies(self, piece, stage):
        if stage == "z":
            return [self.copy(piece, 0, self.shard, self.at(piece, 0, 1), self.peers.along(piece))] if piece else []
        if stage == "first":
            half = self.wide // 2
            left = self.shard.at[:, pl.ds(0, half)] if piece == 0 else self.at(piece, 0, 1, 0)
            right = self.shard.at[:, pl.ds(half, half)] if piece == 0 else self.at(piece, 0, 1, 1)
            return [
                self.copy(piece, 1, left, self.at(piece, 1, 1, 0), self.peers.x),
                self.copy(piece, 2, right, self.at(piece, 2, 1, 1), self.peers.y),
            ]
        if stage == "second":
            return [
                self.copy(piece, 3, self.at(piece, 0, 2, 0), self.at(piece, 2, 2, 0), self.peers.y),
                self.copy(piece, 4, self.at(piece, 0, 1, 1), self.at(piece, 1, 1, 1), self.peers.x),
                self.copy(piece, 5, self.at(piece, 2, 1, 1), self.at(piece, 3, 1, 1), self.peers.x),
            ]
        return [self.copy(piece, 6, self.near.at[piece], self.far.at[piece], self.peers.core)]

    def start(self, piece, stage):
        for copy in self.copies(piece, stage):
            copy.start()

    def arrived(self, piece, stage):
        for copy in self.copies(piece, stage):
            copy.wait_recv()

    def store(self, piece):
        return [
            pltpu.make_async_copy(source.at[piece], target.at[piece], self.stored.at[piece, which])
            for which, (source, target) in enumerate(zip((self.near, self.far), self.outs))
        ]

    def own(self):
        return pltpu.make_async_copy(self.shard, self.at(0, 0, 1), self.local)

    def sent(self, piece):
        self.start(piece, "z")

    def landed(self, piece):
        self.arrived(piece, "z")
        self.start(piece, "first")

    def crossed(self, piece):
        self.arrived(piece, "first")
        self.start(piece, "second")

    def shared(self, piece):
        self.arrived(piece, "second")
        self.start(piece, "core")

    def need(self, piece):
        self.arrived(piece, "core")
        for copy in self.store(piece):
            copy.start()

    def jobs(self, plan, index):
        size = self.chunk * self.wide * 2
        for place in range(self.pieces):
            piece = turn(place, self.pieces)
            key = (index, piece)
            rank = index * self.pieces + place
            if piece:
                plan.add(rank, (self.sent, piece), [], [("z", size * self.pieces / (self.pieces - 1))], ("z", *key), index)
            both = lambda count: [("x", count * size), ("y", count * size)]
            plan.add(rank, (self.landed, piece), [("z", *key)] if piece else [], both(0.5), ("first", *key), index)
            plan.add(rank, (self.crossed, piece), [("first", *key)], both(1), ("second", *key), index)
            plan.add(rank, (self.shared, piece), [("second", *key)], [("core", 4 * size)], ("core", *key), index)

    def end(self):
        for piece in range(self.pieces):
            for stage in ("z", "first", "second", "core"):
                for copy in self.copies(piece, stage):
                    copy.wait_send()
            for copy in self.store(piece):
                copy.wait()


class Halo:
    def __init__(self, ref, rows, send, recv):
        self.ref, self.send, self.recv = ref, send, recv
        self.place, self.size = lax.axis_index("tp"), lax.axis_size("tp")
        spill = REACH - rows
        self.moves = [
            (1, pl.ds(REACH, rows), pl.ds(spill, rows)),
            (-1, pl.ds(REACH, rows), pl.ds(REACH + rows, rows)),
            (2, pl.ds(2 * rows, spill), pl.ds(0, spill)),
            (-2, pl.ds(REACH, spill), pl.ds(REACH + 2 * rows, spill)),
        ]

    def inside(self, distance):
        other = self.place + distance
        return jnp.logical_and(other >= 0, other < self.size)

    def copy(self, index):
        distance, source, target = self.moves[index]
        return pltpu.make_async_remote_copy(
            src_ref=self.ref.at[source, :], dst_ref=self.ref.at[target, :], send_sem=self.send.at[index],
            recv_sem=self.recv.at[index], device_id={"tp": self.place + distance}, device_id_type=MESH,
        )

    def begin(self):
        for index, (distance, _, target) in enumerate(self.moves):

            @pl.when(self.inside(distance))
            def _():
                self.copy(index).start()

            @pl.when(jnp.logical_not(self.inside(-distance)))
            def _():
                self.ref[target, :] = jnp.zeros((target.size, self.ref.shape[1]), BF16)

    def end(self, _=None):
        for index, (distance, _, _) in enumerate(self.moves):

            @pl.when(self.inside(distance))
            def _():
                self.copy(index).wait_send()

            @pl.when(self.inside(-distance))
            def _():
                self.copy(index).wait_recv()


def params(collective, memory=None):
    return pltpu.CompilerParams(collective_id=collective, has_side_effects=True, vmem_limit_bytes=memory)


LN_GAIN, LN_BIAS, OUT_BIAS, LAST_BIAS, FEATS = (0, 1), (2, 3), 4, 5, 6
PROJ_BIAS, HEAD_GAIN, HEAD_BIAS, HEADS = (0, 1, 2), (3, 4), 5, 6


def line(ref, row, start=0, wide=None):
    return ref[pl.ds(row, 1), pl.ds(start, wide or ref.shape[1] - start)]


def attend_work(
    a_ref, near_ref, far_ref, heads_ref, feats_ref, x_ref, q_ref, kv_ref, q_hat_ref, k_hat_ref, q_scale_ref, k_scale_ref,
    p_ref, o_ref, mid_ref, m_ref, mask_ref, acc_ref, opening, closing, hook,
):
    rows = q_ref.shape[0]
    half = near_ref.shape[0]

    @pl.when(opening)
    def _():
        acc_ref[...] = jnp.zeros_like(acc_ref)

    tile = lambda row, which: line(heads_ref, row, which * PAIR, PAIR)
    bias, (q_gain, k_gain), q_shift = PROJ_BIAS, HEAD_GAIN, HEAD_BIAS
    near, distant = halves(a_ref[...])
    own, own_far = halves(a_ref[REACH : REACH + rows, :])
    kv = nn(near, near_ref[:, PAIR : 4 * PAIR]) + nn(distant, far_ref[:, PAIR : 4 * PAIR])
    kv += side(tile(bias[1], 0), tile(bias[2], 0), tile(bias[1], 1) + tile(bias[2], 2))
    q = side(
        nn(own, near_ref[:, :PAIR]) + nn(own_far, far_ref[:, :PAIR]),
        nn(own, near_ref[:, 4 * PAIR : 5 * PAIR]) + nn(own_far, far_ref[:, 4 * PAIR : 5 * PAIR]),
    ) + line(heads_ref, bias[0], 0, 2 * PAIR)
    q_hat, q_scale = head_norm(q)
    k_hat, k_scale = head_norm(side(kv[:, :PAIR], kv[:, 2 * PAIR :]))
    qn = (q_hat * line(heads_ref, q_gain, 0, 2 * PAIR) + line(heads_ref, q_shift, 0, 2 * PAIR)).astype(BF16)
    qn = side(qn[:, :PAIR], only(qn[:, PAIR:], 0))
    kn = (k_hat * line(heads_ref, k_gain, 0, 2 * PAIR)).astype(BF16)
    v = kv[:, PAIR:].astype(BF16)
    low = lax.broadcasted_iota(jnp.int32, (1, PAIR), 1) < HD
    first, second = kn[:, :PAIR], jnp.where(low, kn[:, PAIR:], v[:, PAIR:])
    values = v[:, :PAIR]
    q_ref[...] = qn
    kv_ref[...] = side(first, values, second)
    q_hat_ref[...] = q_hat.astype(BF16)
    k_hat_ref[...] = k_hat.astype(BF16)
    q_scale_ref[...] = q_scale.astype(BF16)
    k_scale_ref[...] = k_scale.astype(BF16)
    hook(1)
    values_t, second_t = values.T, second.T
    mixed = []
    for head in range(3):
        if head:
            hook(head + 1)
        keys = (first, first, second)[head]
        query = only(qn[:, PAIR * (head // 2) : PAIR * (head // 2 + 1)] * HD ** (-0.5), head % 2).astype(BF16)
        scores = nt(keys, query) + mask_ref[...]
        weights = jnp.exp(scores - jnp.max(scores, axis=0, keepdims=True))
        total = jnp.sum(weights, axis=0, keepdims=True)
        probs = (weights * (1.0 / total)).astype(BF16)
        p_ref[head] = probs
        mixed.append(nn((values_t[:HD], values_t[HD:], second_t[HD:])[head], probs))
    o = jnp.concatenate([jnp.zeros_like(mixed[2]), mixed[2], mixed[0], mixed[1]], axis=0).T.astype(BF16)
    o_ref[...] = o
    acc_ref[:, :half] += nt(o, near_ref[:, 4 * PAIR :])
    acc_ref[:, half:] += nt(o, far_ref[:, 4 * PAIR :])

    @pl.when(closing)
    def _():
        mid = x_ref[...] + (acc_ref[...] + line(feats_ref, OUT_BIAS))
        mid_ref[...] = mid
        hat, _ = row_norm(mid)
        m_ref[...] = (hat * line(feats_ref, LN_GAIN[1]) + line(feats_ref, LN_BIAS[1])).astype(BF16)


def mlp_work(
    m_ref, mid_ref, near_ref, far_ref, up_shift, feats_ref, act_ref, slope_ref, x2_ref, acc_ref, opening, closing, hook,
):
    half = near_ref.shape[0]
    wide = act_ref.shape[1]

    @pl.when(opening)
    def _():
        acc_ref[...] = jnp.zeros_like(acc_ref)

    near, distant = halves(m_ref[...])
    hidden = nn(near, near_ref[:, :wide]) + nn(distant, far_ref[:, :wide]) + up_shift
    hook(1)
    phi = 0.5 * (1.0 + lax.erf(hidden * ROOT_HALF))
    act = (hidden * phi).astype(BF16)
    act_ref[...] = act
    slope_ref[...] = (phi + hidden * jnp.exp(-0.5 * hidden * hidden) * INV_ROOT_TWO_PI).astype(BF16)
    acc_ref[:, :half] += nt(act, near_ref[:, wide:])
    acc_ref[:, half:] += nt(act, far_ref[:, wide:])

    @pl.when(closing)
    def _():
        x2_ref[...] = mid_ref[...] + (acc_ref[...] + line(feats_ref, LAST_BIAS))


def norm_rows(x, feats_ref):
    hat, _ = row_norm(x)
    return (hat * line(feats_ref, LN_GAIN[0]) + line(feats_ref, LN_BIAS[0])).astype(BF16)


def quiet(slot):
    pass


def attend_kernel(
    a_ref, near_ref, far_ref, heads_ref, feats_ref, x_ref, seg_k_ref, seg_q_ref, *rest
):
    step = pl.program_id(0)
    mask_ref = rest[-2]

    @pl.when(step == 0)
    def _():
        mask_ref[...] = jnp.where(seg_k_ref[...] == seg_q_ref[...], 0.0, FILL)

    attend_work(
        a_ref, near_ref, far_ref, heads_ref, feats_ref, x_ref, *rest, step == 0, step == pl.num_programs(0) - 1, quiet
    )


def attend_shapes(rows, window):
    return [
        (rows, 2 * PAIR), (window, 3 * PAIR), (rows, 2 * PAIR), (window, 2 * PAIR), (rows, 2 * PAIR), (window, 2 * PAIR),
    ]


def attend(a_win, near, far, heads, feats, x, seg_k, seg_q, layer):
    window, width = a_win.shape
    rows = x.shape[0]
    half = width // 2
    pieces = near.shape[1]
    outs = attend_shapes(rows, window)
    return pl.pallas_call(
        attend_kernel,
        grid=(pieces,),
        in_specs=[
            whole((window, width)), piece_of(0, half, 6 * PAIR), piece_of(0, half, 6 * PAIR), heads_of(layer), sheet(layer, FEATS, width),
            whole((rows, width)), whole((window, 1)), whole((1, rows)),
        ],
        out_specs=[column(*shape) for shape in outs]
        + [pl.BlockSpec((3, window, rows), lambda step: (step, 0, 0)), column(rows, 2 * PAIR)] + [whole((rows, width))] * 2,
        out_shape=[shaped((height, pieces * wide)) for height, wide in outs]
        + [shaped((3 * pieces, window, rows)), shaped((rows, pieces * 2 * PAIR)), shaped((rows, width), F32), shaped((rows, width))],
        scratch_shapes=[pltpu.VMEM((window, rows), F32), pltpu.VMEM((rows, width), F32)],
        name="attend",
    )(a_win, near, far, heads, feats, x, seg_k, seg_q)


def mlp_kernel(m_ref, mid_ref, near_ref, far_ref, up_shift_ref, feats_ref, *rest):
    step = pl.program_id(0)
    mlp_work(
        m_ref, mid_ref, near_ref, far_ref, up_shift_ref[...], feats_ref, *rest, step == 0, step == pl.num_programs(0) - 1, quiet
    )


def mlp(m, mid, near, far, up_shift, feats, layer):
    rows, width = mid.shape
    half = width // 2
    _, pieces, _, wide = up_shift.shape
    hidden = pieces * wide
    full = whole((rows, width))
    return pl.pallas_call(
        mlp_kernel,
        grid=(pieces,),
        in_specs=[
            full, full, piece_of(0, half, 2 * wide), piece_of(0, half, 2 * wide), piece_of(layer, 1, wide), sheet(layer, FEATS, width),
        ],
        out_specs=[column(rows, wide), column(rows, wide), full],
        out_shape=[shaped((rows, hidden)), shaped((rows, hidden)), shaped((rows, width), F32)],
        scratch_shapes=[pltpu.VMEM((rows, width), F32)],
        name="mlp",
    )(m, mid, near, far, up_shift, feats)


class Share:
    def __init__(self, peers, mine, landed, chunks, send, recv):
        self.peers, self.mine, self.landed, self.chunks, self.send, self.recv = peers, mine, landed, chunks, send, recv
        self.pieces, self.lines = landed.shape[0], mine.shape[0]

    def copy(self, index, source, target, device):
        return pltpu.make_async_remote_copy(
            src_ref=source, dst_ref=target, send_sem=self.send.at[index], recv_sem=self.recv.at[index], device_id=device,
            device_id_type=MESH,
        )

    def along(self):
        place = self.landed.at[self.peers.tp]
        return [self.copy(d - 1, self.mine, place, self.peers.along(d)) for d in range(1, self.pieces)]

    def across(self, stage):
        count = 1 << stage
        device = (self.peers.x, self.peers.y, self.peers.core)[stage]
        source, target = self.chunks.at[pl.ds(0, count)], self.chunks.at[pl.ds(count, count)]
        return self.copy(self.pieces - 1 + stage, source, target, device)

    def begin(self):
        for copy in self.along():
            copy.start()
        self.landed[self.peers.tp] = self.mine[...]

    def meet(self, fine):
        for copy in self.along():
            copy.wait_recv()
        row, col = (lax.broadcasted_iota(jnp.int32, (PAIR, PAIR), axis) for axis in range(2))
        total = 0.0
        for place in range(self.pieces):
            spread = jnp.logical_and(row < fine, col == row + place * fine)
            total += nn(self.landed[place], spread.astype(F32).astype(BF16))
        self.chunks[0] = total.astype(BF16)
        self.across(0).start()

    def spread(self, stage):
        self.across(stage - 1).wait_recv()
        self.across(stage).start()

    def end(self):
        self.across(2).wait_recv()
        for copy in self.along() + [self.across(stage) for stage in range(3)]:
            copy.wait_send()

    def chunk_of(self, fsdp):
        away = jnp.bitwise_xor(lax.axis_index("fsdp"), fsdp)
        return lax.rem(away, 2) * (self.chunks.shape[0] // 2) + away // 2

    def features(self, lines, width):
        chunk = width // self.chunks.shape[0]
        row, col = (lax.broadcasted_iota(jnp.int32, (2 * PAIR, width), axis) for axis in range(2))
        total = 0.0
        for place in range(0, self.chunks.shape[0], 2):
            lane = lax.rem(row, PAIR)
            spread = jnp.logical_and(lane < chunk, col == (place + row // PAIR) * chunk + lane)
            both = side(self.chunks[place, :lines, :], self.chunks[place + 1, :lines, :])
            total += nn(both, spread.astype(F32).astype(BF16))
        return total

    def owner(self, place):
        return lax.rem(self.peers.tp + self.pieces - place, self.pieces)

    def heads(self, place, start, chunk):
        owner = self.owner(place)
        rows = pl.ds(start, 16)
        both = side(self.chunks[self.chunk_of(2 * owner), rows, :], self.chunks[self.chunk_of(2 * owner + 1), rows, :])
        row, col = (lax.broadcasted_iota(jnp.int32, (2 * PAIR, 3 * PAIR), axis) for axis in range(2))
        lane = lax.rem(row, PAIR)
        feature = row // PAIR * chunk + lane
        last = jnp.logical_and(feature >= PAIR, col == feature + 3 * HD)
        spread = jnp.logical_and(lane < chunk, jnp.logical_or(col == feature, last))
        return nn(both, spread.astype(F32).astype(BF16))

    def hidden(self, start, layers, parts, fine):
        rows = pl.ds(start, 16)
        block = jnp.concatenate(
            [self.chunks[self.chunk_of(2 * self.owner(i // 2) + i % 2), rows, :] for i in range(2 * self.pieces)], axis=0
        )
        wide = self.pieces * parts * fine
        row, col = (lax.broadcasted_iota(jnp.int32, (PAIR, wide), axis) for axis in range(2))
        line_of = lax.broadcasted_iota(jnp.int32, (block.shape[0], 1), 0)
        total = 0.0
        for part in range(parts):
            target = row // fine * (parts * fine) + part * fine + lax.rem(row, fine)
            spread = jnp.logical_and(row < self.pieces * fine, col == target)
            here = nn(block, spread.astype(F32).astype(BF16))
            total += jnp.where(lax.rem(line_of, parts) == part, here, 0.0)
        row, col = (lax.broadcasted_iota(jnp.int32, (2 * self.pieces * layers, block.shape[0]), axis) for axis in range(2))
        group = jnp.logical_and(row // layers == col // 16, lax.rem(row, layers) == lax.rem(col, 16) // parts)
        return nn(group.astype(F32).astype(BF16), total.astype(BF16))


def forward_kernel(
    token_ref, hot_ref, share_ref, seg_k_ref, seg_q_ref, attn_shard_ref, mlp_shard_ref,
    q_ref, kv_ref, q_hat_ref, k_hat_ref, q_scale_ref, k_scale_ref, p_ref, o_ref, act_ref, slope_ref, mid_ref, m_ref, x2_ref,
    x0_ref, feats_ref, heads_ref, a_win_out, attn_near_out, attn_far_out, mlp_near_out, mlp_far_out,
    mask_ref, acc_ref, now_ref, a_win_ref, kept, attn_near, attn_far, mlp_near, mlp_far, send, recv, local, stored, halo_send, halo_recv,
    up_shift_ref, landed, chunks, share_send, share_recv,
):
    layers, pieces, (rows, width) = attn_near.shape[0], attn_near.shape[1], token_ref.shape
    chunk = width // chunks.shape[0]
    fine, parts, tables = chunk // pieces, act_ref.shape[1] * pieces // width, hot_ref.shape[1]
    step = pl.program_id(0)
    peers = Neighbours()
    halo = lambda layer: Halo(a_win_ref.at[layer], rows, halo_send.at[layer], halo_recv.at[layer])
    keep_window = lambda layer: pltpu.make_async_copy(a_win_ref.at[layer], a_win_out.at[layer], kept.at[layer])

    def window(layer):
        halo(layer).end()
        keep_window(layer).start()

    gathers = []
    for layer in range(layers):
        for which, (shard, near, far, near_out, far_out) in enumerate((
            (attn_shard_ref, attn_near, attn_far, attn_near_out, attn_far_out),
            (mlp_shard_ref, mlp_near, mlp_far, mlp_near_out, mlp_far_out),
        )):
            index = 2 * layer + which
            gathers.append(
                Gather(
                    peers, shard.at[layer], near.at[layer], far.at[layer], send.at[index], recv.at[index], local.at[index],
                    near_out.at[layer], far_out.at[layer], stored.at[index],
                )
            )

    share = Share(peers, share_ref, landed, chunks, share_send, share_recv)

    def open_up(_):
        share.end()
        lines = tables + 16
        found = share.features(lines, width)
        for layer in range(layers):
            feats_ref[layer] = found[tables + layer * FEATS : tables + (layer + 1) * FEATS]
        x0 = token_ref[...] + nn(hot_ref[...], found[:tables].astype(BF16))
        x0_ref[...] = x0
        now_ref[...] = x0
        a_win_ref[0, REACH : REACH + rows, :] = norm_rows(x0, feats_ref.at[0])
        halo(0).begin()
        for piece in range(pieces):
            found = share.heads(piece, lines, chunk)
            for layer in range(layers):
                heads_ref[piece, layer] = found[layer * HEADS : (layer + 1) * HEADS]
        found = share.hidden(lines + 16, layers, parts, fine)
        half = pieces * parts * fine
        for index in range(2 * pieces):
            for layer in range(layers):
                at = index * layers + layer
                up_shift_ref[layer, index // 2, :, index % 2 * half : (index % 2 + 1) * half] = found[at : at + 1]

    plan = Plan()
    for index, gather in enumerate(gathers):
        gather.jobs(plan, index)
    halo_size = width * 2 * 2 * rows
    share_size = share_ref.shape[0] * PAIR * 2
    plan.spend(2.5)
    plan.carry([("z", pieces * share_size)], ("share", 0))
    plan.wait(("share", 0), (share.meet, fine), 0, 0)
    plan.carry([("x", share_size)], ("share", 1))
    plan.wait(("share", 1), (share.spread, 1), 0, 0)
    plan.carry([("y", 2 * share_size)], ("share", 2))
    plan.wait(("share", 2), (share.spread, 2), 0, 0)
    plan.carry([("core", 4 * share_size)], ("share", 3))
    plan.wait(("share", 3), (open_up, 0), 0, 0)
    for layer in range(layers):
        plan.carry([("z", halo_size)], ("halo", layer))
        first = 1 + 2 * layer * pieces
        if layer == 0:
            plan.spend(5.0)
        plan.wait(("halo", layer), (window, layer), *((first, 0) if layer else (0, 0)))
        for index in range(pieces):
            piece = turn(index, pieces)
            plan.wait(("core", 2 * layer, piece), (gathers[2 * layer].need, piece), first + index, 0)
            for slot, time in enumerate((2.0, 1.4, 1.4)):
                plan.spend(time)
                plan.slot(first + index, slot + 1)
            plan.spend(1.4)
        first += pieces
        for index in range(pieces):
            piece = turn(index, pieces)
            plan.wait(("core", 2 * layer + 1, piece), (gathers[2 * layer + 1].need, piece), first + index, 0)
            plan.spend(1.0)
            plan.slot(first + index, 1)
            plan.spend(1.5)
    table = plan.table

    def run(at, slot):
        if (at, slot) in table:

            @pl.when(step == at)
            def _():
                for work, piece in table[at, slot]:
                    work(piece)

    @pl.when(step == 0)
    def _():
        peers.greet()
        mask_ref[...] = jnp.where(seg_k_ref[...] == seg_q_ref[...], 0.0, FILL)
        share.begin()
        for gather in gathers:
            gather.own().start()
        for gather in gathers:
            gather.own().wait()

    run(0, 0)

    count = jnp.maximum(step - 1, 0)
    layer = count // (2 * pieces)
    inner = lax.rem(count, 2 * pieces)
    index = lax.rem(inner, pieces)
    piece = turn(index, pieces)
    steps_of = lambda which: [
        1 + (2 * layer + which) * pieces + index for layer in range(layers) for index in range(pieces)
    ]

    @pl.when(jnp.logical_and(step > 0, inner < pieces))
    def _():
        def hook(slot):
            for at in steps_of(0):
                run(at, slot)

        hook(0)
        attend_work(
            a_win_ref.at[layer], attn_near.at[layer, piece], attn_far.at[layer, piece], heads_ref.at[piece, layer],
            feats_ref.at[layer], now_ref,
            q_ref, kv_ref, q_hat_ref, k_hat_ref, q_scale_ref, k_scale_ref, p_ref, o_ref, mid_ref.at[layer], m_ref.at[layer],
            mask_ref, acc_ref, index == 0, index == pieces - 1, hook,
        )

    @pl.when(inner >= pieces)
    def _():
        def hook(slot):
            for at in steps_of(1):
                run(at, slot)

        hook(0)
        mlp_work(
            m_ref.at[layer], mid_ref.at[layer], mlp_near.at[layer, piece], mlp_far.at[layer, piece],
            up_shift_ref[layer, piece], feats_ref.at[layer], act_ref, slope_ref, now_ref, acc_ref, index == 0,
            index == pieces - 1, hook,
        )

        @pl.when(index == pieces - 1)
        def _():
            x2_ref[layer] = now_ref[...]

            @pl.when(layer + 1 < layers)
            def _():
                a_win_ref[layer + 1, REACH : REACH + rows, :] = norm_rows(now_ref[...], feats_ref.at[layer + 1])
                halo(layer + 1).begin()

    @pl.when(step == pl.num_programs(0) - 1)
    def _():
        for gather in gathers:
            gather.end()
        for layer in range(layers):
            keep_window(layer).wait()


def forward(tokens, hot, share, seg_k, seg_q, attn_shards, mlp_shards):
    rows, width = tokens.shape
    layers, chunk, wide = mlp_shards.shape
    half = width // 2
    window = rows + 2 * REACH
    pieces, chunks, part = lax.axis_size("tp"), lax.axis_size("fsdp"), wide // 2
    hidden = pieces * part

    def attend_at(step):
        count = jnp.maximum(step - 1, 0)
        layer, inner = count // (2 * pieces), lax.rem(count, 2 * pieces)
        return layer, turn(jnp.minimum(inner, pieces - 1), pieces)

    def mlp_at(step):
        count = jnp.maximum(step - 1, 0)
        layer, inner = count // (2 * pieces), lax.rem(count, 2 * pieces)
        done = jnp.where(inner >= pieces, layer * pieces + inner - pieces, jnp.maximum(layer * pieces - 1, 0))
        return done // pieces, turn(lax.rem(done, pieces), pieces)

    def attend_block(height, wide):
        return pl.BlockSpec((None, height, wide), lambda step: (attend_at(step)[0], 0, attend_at(step)[1]))

    mlp_block = pl.BlockSpec((None, rows, part), lambda step: (mlp_at(step)[0], 0, mlp_at(step)[1]))
    heads_at = lambda step: attend_at(step)[0] * pieces + attend_at(step)[1]
    once = lambda shape: pl.BlockSpec(shape, lambda step: (0,) * len(shape), pipeline_mode=pl.Buffered(1))
    outs = attend_shapes(rows, window) + [(rows, 2 * PAIR)]
    specs = [attend_block(*shape) for shape in outs]
    shapes = [shaped((layers, height, pieces * wide)) for height, wide in outs]
    specs.insert(6, pl.BlockSpec((3, window, rows), lambda step: (heads_at(step), 0, 0)))
    shapes.insert(6, shaped((3 * layers * pieces, window, rows)))
    held = [((layers, rows, width), F32), ((layers, rows, width), BF16), ((layers, rows, width), F32)]
    weights = [(layers, pieces, half, 6 * PAIR)] * 2 + [(layers, pieces, half, wide)] * 2
    semaphores = pltpu.SemaphoreType.DMA((2 * layers, pieces, Gather.KINDS))
    held += [((rows, width), F32), ((layers, FEATS, width), F32), ((pieces, layers, HEADS, 3 * PAIR), F32)]
    inputs = (tokens, hot, share, seg_k, seg_q, attn_shards, mlp_shards)
    return pl.pallas_call(
        forward_kernel,
        grid=(1 + 2 * layers * pieces,),
        in_specs=[once(item.shape) for item in inputs],
        out_specs=specs + [mlp_block] * 2 + [once(shape) for shape, _ in held] + [ANY] * 5,
        out_shape=shapes + [shaped((layers, rows, hidden))] * 2 + [shaped(*item) for item in held]
        + [shaped(shape) for shape in [(layers, window, width)] + weights],
        scratch_shapes=[
            pltpu.VMEM((window, rows), F32), pltpu.VMEM((rows, width), F32), pltpu.VMEM((rows, width), F32),
            pltpu.VMEM((layers, window, width), BF16), pltpu.SemaphoreType.DMA((layers,)),
            *[pltpu.VMEM(shape, BF16) for shape in weights], semaphores, semaphores, pltpu.SemaphoreType.DMA((2 * layers,)),
            pltpu.SemaphoreType.DMA((2 * layers, pieces, 2)), pltpu.SemaphoreType.DMA((layers, 4)),
            pltpu.SemaphoreType.DMA((layers, 4)), pltpu.VMEM((layers, pieces, 1, part), F32),
            pltpu.VMEM((pieces, *share.shape), BF16), pltpu.VMEM((chunks, *share.shape), BF16),
            pltpu.SemaphoreType.DMA((pieces + 2,)), pltpu.SemaphoreType.DMA((pieces + 2,)),
        ],
        compiler_params=params(20, VMEM),
        name="forward",
    )(*inputs)


def mlp_back_kernel(*refs):
    step = pl.program_id(0)
    mlp_back_work(*refs, step == 0, step == pl.num_programs(0) - 1, quiet)


def mlp_back_work(
    g_ref, down_near_ref, down_far_ref, slope_ref, up_near_ref, up_far_ref, mid_ref, feats_ref,
    gz_ref, gh_ref, up_shift_grad_ref, g1_ref, gr_ref, small_ref, acc_ref, opening, closing, hook,
):
    half = up_near_ref.shape[0]

    @pl.when(opening)
    def _():
        gz_ref[...] = g_ref[...].astype(BF16)
        acc_ref[...] = jnp.zeros_like(acc_ref)

    near, distant = halves(gz_ref[...])
    gh = ((nn(near, down_near_ref[...]) + nn(distant, down_far_ref[...])) * slope_ref[...].astype(F32)).astype(BF16)
    gh_ref[...] = gh
    hook(1)
    up_shift_grad_ref[...] = jnp.sum(gh.astype(F32), axis=0, keepdims=True)
    acc_ref[:, :half] += nt(gh, up_near_ref[...])
    acc_ref[:, half:] += nt(gh, up_far_ref[...])

    @pl.when(closing)
    def _():
        gm = acc_ref[...]
        hat, scale = row_norm(mid_ref[...])
        g1 = g_ref[...] + row_norm_back(gm * line(feats_ref, LN_GAIN[1]), hat, scale)
        gr = g1.astype(BF16)
        g1_ref[...] = g1
        gr_ref[...] = gr
        small_ref[...] = jnp.zeros_like(small_ref)
        small_ref[0:1, :] = jnp.sum(gz_ref[...].astype(F32), axis=0, keepdims=True)
        small_ref[1:2, :] = jnp.sum(gr.astype(F32), axis=0, keepdims=True)
        small_ref[2:3, :] = jnp.sum(gm * hat, axis=0, keepdims=True)
        small_ref[3:4, :] = jnp.sum(gm, axis=0, keepdims=True)


def mlp_back(grad, near, far, slope, mid, feats, layer, index):
    rows, width = grad.shape
    half = width // 2
    hidden = slope.shape[2]
    pieces = near.shape[1]
    wide = hidden // pieces
    full = whole((rows, width))
    return pl.pallas_call(
        mlp_back_kernel,
        grid=(pieces,),
        in_specs=[
            full, piece_of(index, half, wide, 1), piece_of(index, half, wide, 1), slab(index, rows, wide),
            piece_of(index, half, wide), piece_of(index, half, wide), sheet(index, rows, width), sheet(layer, FEATS, width),
        ],
        out_specs=[full, column(rows, wide), column(1, wide), full, full, whole((8, width))],
        out_shape=[
            shaped((rows, width)), shaped((rows, hidden)), shaped((1, hidden), F32), shaped((rows, width), F32),
            shaped((rows, width)), shaped((8, width), F32),
        ],
        scratch_shapes=[pltpu.VMEM((rows, width), F32)],
        cost_estimate=pl.CostEstimate(
            flops=4 * rows * width * hidden, bytes_accessed=4 * width * hidden, transcendentals=0
        ),
        name="mlp_back",
    )(grad, near, far, slope, near, far, mid, feats)


def attend_back_kernel(*refs):
    *ins, gq_ref, gkv_ref, mine_ref, left_ref, right_ref, small_ref, acc_ref = refs
    rows = gq_ref.shape[0]
    step = pl.program_id(0)

    @pl.when(step == 0)
    def _():
        acc_ref[...] = jnp.zeros_like(acc_ref)

    attend_back_work(*ins, gq_ref, gkv_ref, small_ref, acc_ref, quiet)

    @pl.when(step == pl.num_programs(0) - 1)
    def _():
        left_ref[...] = acc_ref[:REACH, :].astype(BF16)
        mine_ref[...] = acc_ref[REACH : REACH + rows, :]
        right_ref[...] = acc_ref[REACH + rows :, :].astype(BF16)


def attend_back_work(
    gr_ref, q_ref, kv_ref, q_hat_ref, k_hat_ref, q_scale_ref, k_scale_ref, p_ref, near_ref, far_ref, heads_ref,
    gq_ref, gkv_ref, small_ref, acc_ref, hook,
):
    rows = gr_ref.shape[0]
    half = near_ref.shape[0]
    near, distant = halves(gr_ref[...])
    go = (nn(near, near_ref[:, 4 * PAIR :]) + nn(distant, far_ref[:, 4 * PAIR :])).astype(BF16)
    qn, kv = q_ref[...], kv_ref[...]
    first, values, second = kv[:, :PAIR], kv[:, PAIR : 2 * PAIR], kv[:, 2 * PAIR :]
    first_t, second_t = first.T, second.T
    grad_q, grad_k, grad_v = [], [], []
    for head in range(3):
        if head:
            hook(head)
        go_head = only(go[:, PAIR:], head) if head < 2 else only(go[:, :PAIR], 1)
        query = only(qn[:, PAIR * (head // 2) : PAIR * (head // 2 + 1)] * HD ** (-0.5), head % 2).astype(BF16)
        stored = p_ref[head]
        probs = stored.astype(F32)
        grad_probs = nt((values, values, second)[head], go_head)
        delta = jnp.sum(probs * grad_probs, axis=0, keepdims=True)
        grad_scores = (probs * (grad_probs - delta)).astype(BF16)
        grad_v.append(nn(stored, go_head))
        grad_k.append(nn(grad_scores, query))
        grad_q.append(nn((first_t[:HD], first_t[HD:], second_t[:HD])[head], grad_scores))
    hook(3)
    zero = jnp.zeros_like(grad_q[2])
    grad_q = (jnp.concatenate(grad_q + [zero], axis=0) * HD ** (-0.5)).T
    grad_k = side(grad_k[0] + grad_k[1], grad_k[2])
    pair_v, last_v = grad_v[0] + grad_v[1], grad_v[2]
    q_hat = q_hat_ref[...].astype(F32)
    k_hat = k_hat_ref[...].astype(F32)
    gain = lambda which: line(heads_ref, HEAD_GAIN[which], 0, 2 * PAIR)
    gq = head_norm_back(grad_q * gain(0), q_hat, q_scale_ref[...].astype(F32)).astype(BF16)
    gk = head_norm_back(grad_k * gain(1), k_hat, k_scale_ref[...].astype(F32)).astype(BF16)
    gkv = side(gk[:, :PAIR], pair_v.astype(BF16), gk[:, PAIR:] + last_v.astype(BF16))
    gq_ref[...] = gq
    gkv_ref[...] = gkv
    total = lambda value: jnp.sum(value.astype(F32), axis=0, keepdims=True)
    small_ref[...] = jnp.zeros_like(small_ref)
    small_ref[0:1, : 2 * PAIR] = total(grad_q * q_hat)
    small_ref[1:2, : 2 * PAIR] = total(grad_k * k_hat)
    small_ref[2:3, : 2 * PAIR] = total(grad_q)
    small_ref[3:4, : 2 * PAIR] = total(gq)
    small_ref[4:5, : 2 * PAIR] = total(gk)
    small_ref[5:6, :PAIR] = total(pair_v.astype(BF16))
    small_ref[5:6, 2 * PAIR :] = total(last_v.astype(BF16))
    acc_ref[:, :half] += nt(gkv, near_ref[:, PAIR : 4 * PAIR])
    acc_ref[:, half:] += nt(gkv, far_ref[:, PAIR : 4 * PAIR])
    own = slice(REACH, REACH + rows)
    for ref, cols in ((near_ref, slice(0, half)), (far_ref, slice(half, 2 * half))):
        acc_ref[own, cols] += nt(gq[:, :PAIR], ref[:, :PAIR]) + nt(gq[:, PAIR:], ref[:, 4 * PAIR : 5 * PAIR])


def attend_back_specs(rows, width, pieces, layer, index):
    half = width // 2
    window = rows + 2 * REACH
    full = whole((rows, width))
    in_specs = [
        full, *[slab(index, *shape) for shape in attend_shapes(rows, window)],
        pl.BlockSpec((3, window, rows), lambda step: (index * pieces + step, 0, 0)), piece_of(index, half, 6 * PAIR),
        piece_of(index, half, 6 * PAIR), heads_of(layer),
    ]
    out_specs = [
        column(rows, 2 * PAIR), column(window, 3 * PAIR), full, whole((REACH, width)), whole((REACH, width)), column(8, 3 * PAIR),
    ]
    out_shape = [
        shaped((rows, pieces * 2 * PAIR)), shaped((window, pieces * 3 * PAIR)), shaped((rows, width), F32),
        shaped((REACH, width)), shaped((REACH, width)), shaped((8, pieces * 3 * PAIR), F32),
    ]
    cost = pl.CostEstimate(
        flops=2 * window * width * width * 2 + 20 * window * rows * width * 2,
        bytes_accessed=20 * window * width,
        transcendentals=0,
    )
    return in_specs, out_specs, out_shape, [pltpu.VMEM((window, width), F32)], cost


def attend_back(gr, stored, near, far, heads, layer, index):
    rows, width = gr.shape
    pieces = near.shape[1]
    in_specs, out_specs, out_shape, scratch, cost = attend_back_specs(rows, width, pieces, layer, index)
    return pl.pallas_call(
        attend_back_kernel,
        grid=(pieces,),
        in_specs=in_specs,
        out_specs=out_specs,
        out_shape=out_shape,
        scratch_shapes=scratch,
        cost_estimate=cost,
        name="attend_back",
    )(gr, *stored, near, far, heads)


def attn_weight_kernel(a_ref, gq_ref, gkv_ref, gr_ref, o_ref, keep_ref, send_ref, a_t_ref, gr_t_ref):
    rows = gq_ref.shape[0]
    half = keep_ref.shape[0]

    @pl.when(pl.program_id(0) == 0)
    def _():
        a_t_ref[...] = a_ref[...].T
        gr_t_ref[...] = gr_ref[...].T

    for part, ref in ((slice(0, half), keep_ref), (slice(half, 2 * half), send_ref)):
        from_q = nn(a_t_ref[part, REACH : REACH + rows], gq_ref[...])
        from_o = nn(gr_t_ref[part, :], o_ref[...])
        ref[:, :PAIR] = from_q[:, :PAIR].astype(BF16)
        ref[:, PAIR : 4 * PAIR] = nn(a_t_ref[part, :], gkv_ref[...]).astype(BF16)
        ref[:, 4 * PAIR : 5 * PAIR] = (from_q[:, PAIR:] + from_o[:, :PAIR]).astype(BF16)
        ref[:, 5 * PAIR :] = from_o[:, PAIR:].astype(BF16)


def attn_weight_grads(a_win, gq, gkv, gr, o):
    _, window, width = a_win.shape
    rows = gr.shape[0]
    half = width // 2
    pieces = gq.shape[1] // (2 * PAIR)
    out = column(half, 6 * PAIR)
    return pl.pallas_call(
        attn_weight_kernel,
        grid=(pieces,),
        in_specs=[
            sheet(0, window, width), column(rows, 2 * PAIR), column(window, 3 * PAIR), whole((rows, width)),
            slab(0, rows, 2 * PAIR),
        ],
        out_specs=[out, out],
        out_shape=[shaped((half, pieces * 6 * PAIR))] * 2,
        scratch_shapes=[pltpu.VMEM((width, window), BF16), pltpu.VMEM((width, rows), BF16)],
        cost_estimate=pl.CostEstimate(
            flops=2 * width * width * (2 * window + 2 * rows), bytes_accessed=8 * width * width, transcendentals=0
        ),
        name="attn_weight_grads",
    )(a_win, gq, gkv, gr, o)


def mlp_weight_kernel(m_ref, gh_ref, gz_ref, act_ref, keep_ref, send_ref, m_t_ref, gz_t_ref):
    half = keep_ref.shape[0]
    wide = gh_ref.shape[1]

    @pl.when(pl.program_id(0) == 0)
    def _():
        m_t_ref[...] = m_ref[...].T
        gz_t_ref[...] = gz_ref[...].T

    for part, ref in ((slice(0, half), keep_ref), (slice(half, 2 * half), send_ref)):
        ref[:, :wide] = nn(m_t_ref[part, :], gh_ref[...]).astype(BF16)
        ref[:, wide:] = nn(gz_t_ref[part, :], act_ref[...]).astype(BF16)


def mlp_weight_grads(m, gh, gz, act):
    _, rows, width = m.shape
    half = width // 2
    hidden = gh.shape[1]
    pieces = lax.axis_size("tp")
    wide = hidden // pieces
    out = column(half, 2 * wide)
    return pl.pallas_call(
        mlp_weight_kernel,
        grid=(pieces,),
        in_specs=[sheet(0, rows, width), column(rows, wide), whole((rows, width)), slab(0, rows, wide)],
        out_specs=[out, out],
        out_shape=[shaped((half, 2 * hidden))] * 2,
        scratch_shapes=[pltpu.VMEM((width, rows), BF16), pltpu.VMEM((width, rows), BF16)],
        cost_estimate=pl.CostEstimate(
            flops=4 * width * hidden * rows, bytes_accessed=4 * width * hidden, transcendentals=0
        ),
        name="mlp_weight_grads",
    )(m, gh, gz, act)


class Scatter:
    KINDS = 7

    def __init__(self, peers, out, away, keep, core, first, second, given, send, recv):
        self.peers, self.out, self.away, self.keep, self.core_in = peers, out, away, keep, core
        self.first_in, self.second_in, self.given, self.send, self.recv = first, second, given, send, recv
        self.chunk, self.wide = out.shape
        self.half = self.wide // 2
        self.pieces = keep.shape[0]

    def copy(self, piece, kind, source, target, device):
        return pltpu.make_async_remote_copy(
            src_ref=source, dst_ref=target, send_sem=self.send.at[piece, kind], recv_sem=self.recv.at[piece, kind],
            device_id=device, device_id_type=MESH,
        )

    def copies(self, piece, stage):
        c, left, right = self.chunk, pl.ds(0, self.half), pl.ds(self.half, self.half)
        rows = lambda start, count=1: pl.ds(start * c, count * c)
        if stage == "core":
            return [self.copy(piece, 0, self.away.at[self.slot(piece)], self.core_in.at[piece], self.peers.core)]
        if stage == "first":
            source, target = self.keep.at[piece], self.first_in.at[piece]
            return [
                self.copy(piece, 1, source.at[rows(2, 2), left], target.at[:, left], self.peers.y),
                self.copy(piece, 2, source.at[rows(1), right], target.at[rows(0), right], self.peers.x),
                self.copy(piece, 3, source.at[rows(3), right], target.at[rows(1), right], self.peers.x),
            ]
        if stage == "second":
            source, target = self.keep.at[piece], self.second_in.at[piece]
            return [
                self.copy(piece, 4, source.at[rows(1), left], target.at[:, left], self.peers.x),
                self.copy(piece, 5, source.at[rows(2), right], target.at[:, right], self.peers.y),
            ]
        target = self.given.at[(piece - 1) % self.pieces]
        return [self.copy(piece, 6, self.keep.at[piece, rows(0), :], target, self.peers.along(1))]

    def start(self, piece, stage):
        for copy in self.copies(piece, stage):
            copy.start()

    def arrived(self, piece, stage):
        for copy in self.copies(piece, stage):
            copy.wait_recv()

    def add(self, piece, start, count, cols, source):
        step = 32

        @pl.loop(0, count * self.chunk // step)
        def _(index):
            row = pl.multiple_of(index * step, step)
            into = (piece, pl.ds(start * self.chunk + row, step), cols)
            self.keep[into] = self.keep[into] + source[pl.ds(row, step), cols]

    def slot(self, piece):
        return (piece + self.pieces - 1) % self.pieces % 2

    def room(self, index, piece):
        @pl.when(index > 1)
        def _():
            for copy in self.copies(lax.rem(piece + self.pieces - 2, self.pieces), "core"):
                copy.wait_send()

    def first(self, piece):
        self.arrived(piece, "core")
        self.add(piece, 0, 4, pl.ds(0, self.wide), self.core_in.at[piece])
        self.start(piece, "first")

    def second(self, piece):
        left, right = pl.ds(0, self.half), pl.ds(self.half, self.half)
        self.arrived(piece, "first")
        source = self.first_in.at[piece]
        self.add(piece, 0, 2, left, source)
        self.add(piece, 0, 1, right, source)
        self.add(piece, 2, 1, right, source.at[pl.ds(self.chunk, self.chunk)])
        self.start(piece, "second")

    def last(self, piece):
        self.arrived(piece, "second")
        kept = pl.ds(0, self.chunk)
        total = self.keep[piece, kept, :].astype(F32) + self.second_in[piece].astype(F32)
        if piece != 1:
            self.arrived((piece - 1) % self.pieces, "give")
            total += self.given[(piece - 2) % self.pieces].astype(F32)
        if piece:
            self.keep[piece, kept, :] = total.astype(BF16)
            self.start(piece, "give")
        else:
            self.out[...] = total

    def done(self):
        for piece in range(self.pieces):
            for stage in ("core", "first", "second", "give"):
                if (stage != "give" or piece) and (stage != "core" or piece in (0, self.pieces - 1)):
                    for copy in self.copies(piece, stage):
                        copy.wait_send()

    def made(self, plan, index, piece):
        size = self.chunk * self.wide * 2
        both = lambda count: [("x", count * size), ("y", count * size)]
        key = (index, piece)
        rank = index * self.pieces + (piece - 1) % self.pieces
        plan.carry([("core", 4 * size)], ("core", *key))
        plan.add(rank, (self.first, piece), [("core", *key)], both(1), ("first", *key), index)
        plan.add(rank, (self.second, piece), [("first", *key)], both(0.5), ("second", *key), index)
        needs = [("second", *key)] + ([("give", index, (piece - 1) % self.pieces)] if piece != 1 else [])
        plan.add(rank, (self.last, piece), needs, [("z", size)] if piece else [], ("give", *key), index)


class Return:
    def __init__(self, edges, landed, rows, send, recv):
        self.edges, self.landed, self.send, self.recv = edges, landed, send, recv
        self.place, self.size = lax.axis_index("tp"), lax.axis_size("tp")
        spill = REACH - rows
        self.moves = [
            (1, 1, pl.ds(0, rows), pl.ds(0, rows), 0),
            (-1, 0, pl.ds(spill, rows), pl.ds(rows, rows), 0),
            (2, 1, pl.ds(rows, spill), pl.ds(2 * rows, spill), 0),
            (-2, 0, pl.ds(0, spill), pl.ds(2 * rows + spill, spill), rows - spill),
        ]

    def inside(self, distance):
        other = self.place + distance
        return jnp.logical_and(other >= 0, other < self.size)

    def copy(self, index):
        distance, which, source, target, _ = self.moves[index]
        return pltpu.make_async_remote_copy(
            src_ref=self.edges.at[pl.ds(which * REACH + source.start, source.size), pl.ds(0, self.landed.shape[1])],
            dst_ref=self.landed.at[target, :], send_sem=self.send.at[index],
            recv_sem=self.recv.at[index], device_id={"tp": self.place + distance}, device_id_type=MESH,
        )

    def begin(self):
        for index, (distance, *_) in enumerate(self.moves):

            @pl.when(self.inside(distance))
            def _():
                self.copy(index).start()

    def end(self, total_ref):
        for index, (distance, _, _, target, start) in enumerate(self.moves):

            @pl.when(self.inside(distance))
            def _():
                self.copy(index).wait_send()

            @pl.when(self.inside(-distance))
            def _():
                self.copy(index).wait_recv()
                total_ref[pl.ds(start, target.size), :] += self.landed[target, :].astype(F32)


def split_dot(left, right):
    if left.dtype == F32:
        high = left.astype(BF16)
        return nn(high, right) + nn((left - high.astype(F32)).astype(BF16), right)
    high = right.astype(BF16)
    return nn(left, high) + nn(left, (right - high.astype(F32)).astype(BF16))


def picked(mask):
    return mask.astype(F32).astype(BF16)


class Tally:
    def __init__(self, peers, chunks, inbox, send, recv, pieces):
        self.peers, self.chunks, self.inbox, self.send, self.recv, self.pieces = peers, chunks, inbox, send, recv, pieces
        self.share = Share(peers, chunks.at[0], inbox.at[pl.ds(0, pieces)], chunks, send, recv)

    def across(self, stage):
        count = 4 >> stage
        device = (self.peers.core, self.peers.y, self.peers.x)[stage]
        source, target = self.chunks.at[pl.ds(count, count)], self.inbox.at[pl.ds(8 - 2 * count, count)]
        return self.share.copy(stage, source, target, device)

    def along(self):
        place = self.inbox.at[7 + self.peers.tp]
        return [self.share.copy(2 + d, self.chunks.at[0], place, self.peers.along(d)) for d in range(1, self.pieces)]

    def build(self, tables, lines_ref, work_ref, norm_sums, mlp_sums, head_sums, up_grad):
        layers, width = norm_sums.shape[0], lines_ref.shape[1]
        count = self.chunks.shape[0]
        chunk, first = width // count, tables.shape[0]
        fine, parts = chunk // self.pieces, up_grad.shape[3] * self.pieces // width
        lines_ref[:first, :] = tables
        lines_ref[first : first + 16, :] = jnp.zeros((16, width), F32)
        for layer in range(layers):
            sums = [(norm_sums, 0), (mlp_sums, 2), (norm_sums, 1), (mlp_sums, 3), (mlp_sums, 1), (mlp_sums, 0)]
            for index, (ref, row) in enumerate(sums):
                at = first + layer * FEATS + index
                lines_ref[at : at + 1, :] = ref[layer, row : row + 1, :]
        lines = lines_ref[: first + 16, :]
        row, col = (lax.broadcasted_iota(jnp.int32, (width, PAIR), axis) for axis in range(2))
        for place in range(count):
            spread = picked(jnp.logical_and(col < chunk, row == place * chunk + col))
            self.chunks[place, : first + 16, :] = split_dot(lines, spread).astype(BF16)
        row, col = (lax.broadcasted_iota(jnp.int32, (3 * PAIR, 2 * PAIR), axis) for axis in range(2))
        lane = lax.rem(col, PAIR)
        feature = col // PAIR * chunk + lane
        last = jnp.logical_and(feature >= PAIR, row == feature + 3 * HD)
        spread = picked(jnp.logical_and(lane < chunk, jnp.logical_or(row == feature, last)))
        work_ref[:32, :] = jnp.zeros((32, width), F32)
        for piece in range(self.pieces):
            for layer in range(layers):
                for index, line_at in enumerate((3, 4, 5, 0, 1, 2)):
                    at = layer * HEADS + index
                    work_ref[at : at + 1, : 3 * PAIR] = head_sums[layer, piece, line_at : line_at + 1, :]
            both = split_dot(work_ref[:16, : 3 * PAIR], spread).astype(BF16)
            owner = self.share.owner(piece)
            for index in range(2):
                target = self.chunks.at[self.share.chunk_of(2 * owner + index)]
                target[first + 16 : first + 32, :] = both[:, index * PAIR : (index + 1) * PAIR]
        wide = self.pieces * parts * fine
        for index in range(2 * self.pieces):
            for layer in range(layers):
                at = 16 + index * layers + layer
                half = slice(index % 2 * wide, (index % 2 + 1) * wide)
                work_ref[at : at + 1, :wide] = up_grad[layer, index // 2, :, half]
        biases = work_ref[16 : 16 + 2 * self.pieces * layers, :wide]
        row, col = (lax.broadcasted_iota(jnp.int32, (wide, PAIR), axis) for axis in range(2))
        shape = (2 * self.pieces * 16, 2 * self.pieces * layers)
        line_of, from_of = (lax.broadcasted_iota(jnp.int32, shape, axis) for axis in range(2))
        total = 0.0
        for part in range(parts):
            source = col // fine * (parts * fine) + part * fine + lax.rem(col, fine)
            here = split_dot(biases, picked(jnp.logical_and(col < chunk, row == source)))
            group = jnp.logical_and(line_of // 16 == from_of // layers, lax.rem(line_of, 16) == lax.rem(from_of, layers) * parts + part)
            total += split_dot(picked(group), here)
        for index in range(2 * self.pieces):
            target = self.chunks.at[self.share.chunk_of(2 * self.share.owner(index // 2) + index % 2)]
            target[first + 32 : first + 48, :] = total[index * 16 : (index + 1) * 16].astype(BF16)
        self.across(0).start()

    def fold(self, stage):
        count = 4 >> stage
        self.across(stage).wait_recv()
        mine, found = self.chunks[:count], self.inbox[8 - 2 * count : 8 - count]
        self.chunks[:count] = (mine.astype(F32) + found.astype(F32)).astype(BF16)
        if stage < 2:
            self.across(stage + 1).start()
        else:
            for copy in self.along():
                copy.start()

    def total(self, out_ref):
        total = self.chunks[0].astype(F32)
        for copy in self.along():
            copy.wait_recv()
        for distance in range(1, self.pieces):
            total += self.inbox[7 + lax.rem(self.peers.tp + distance, self.pieces)].astype(F32)
        out_ref[...] = total
        for copy in self.along() + [self.across(stage) for stage in range(3)]:
            copy.wait_send()


def backward_kernel(
    cot_ref, hot_ref, feats_ref, m_ref, mid_ref, a_win_ref, x0_ref, x2_ref,
    mlp_near_ref, mlp_far_ref, slope_ref, act_ref,
    q_ref, kv_ref, q_hat_ref, k_hat_ref, q_scale_ref, k_scale_ref, p_ref, attn_near_ref, attn_far_ref, heads_ref, o_ref,
    g_ref, up_grad_ref, head_sums_ref, mlp_sums_ref, norm_sums_ref, tally_ref, mlp_out, attn_out,
    gz_ref, gh_ref, g1_ref, gr_ref, acc_ref, window_ref, gq_ref, gkv_ref, turned_ref, a_t_ref,
    landed_ref, halo_send, halo_recv, free, fetched, chunks, inbox, tally_send, tally_recv, *buffers,
):
    layers, pieces, rows = up_grad_ref.shape[0], up_grad_ref.shape[1], g_ref.shape[0]
    half = g_ref.shape[1] // 2
    wide = slope_ref.shape[1]
    own = slice(REACH, REACH + rows)
    total_ref = window_ref.at[own]
    step = pl.program_id(0)
    peers = Neighbours()
    scatter_of = lambda layer, which: Scatter(
        peers, (mlp_out, attn_out)[which].at[layer], *buffers[8 * which : 8 * which + 6],
        *[item.at[layer] for item in buffers[8 * which + 6 : 8 * which + 8]],
    )
    back = lambda layer: Return(a_t_ref, landed_ref.at[layer], rows, halo_send.at[layer], halo_recv.at[layer])

    def fetch(source, target):
        copy = pltpu.make_async_copy(source, target, fetched)
        copy.start()
        copy.wait()

    def halo_back(layer):
        back(layer).end(total_ref)

    def made_free(item):
        layer, which = item
        scatter_of(layer + 1, which).done()
        for target in peers.all():
            pl.semaphore_signal(free.at[layer, which], inc=1, device_id=target, device_id_type=MESH)
        pl.semaphore_wait(free.at[layer, which], len(peers.all()))

    plan = Plan()
    plan.spend(2.5)
    halo_size = 2 * half * 2 * 2 * rows
    order = [(index + 1) % pieces for index in range(pieces)]
    for layer in reversed(range(layers)):
        for which in range(2):
            for index, piece in enumerate(order):
                at = (2 * (layers - 1 - layer) + which) * pieces + index
                if index == 0 and layer + 1 < layers:
                    if which == 0:
                        plan.wait(("halo", layer + 1), (halo_back, layer + 1), at, 0)
                    plan.finish(2 * (layers - 2 - layer) + which, at, 0)
                    plan.table.setdefault((at, 0), []).append((made_free, (layer, which)))
                plan.slot(at, 0)
                for slot, time in enumerate(((1.5,), (2.2, 1.3, 1.3))[which]):
                    plan.spend(time)
                    plan.slot(at, slot + 1)
                plan.spend((2.6, 3.0)[which])
                scatter_of(layer, which).made(plan, 2 * (layers - 1 - layer) + which, piece)
        plan.carry([("z", halo_size)], ("halo", layer))
    ending = 2 * layers * pieces
    plan.wait(("halo", 0), (halo_back, 0), ending, 0)
    plan.spend(8.0)
    tally = Tally(peers, chunks, inbox, tally_send, tally_recv, pieces)
    size = chunks.shape[1] * PAIR * 2
    for stage, (link, count) in enumerate((("core", 4), ("y", 2), ("x", 1), ("z", pieces))):
        plan.carry([(link, count * size)], ("tally", stage))
        work = (tally.fold, stage) if stage < 3 else (tally.total, tally_ref)
        plan.wait(("tally", stage), work, ending, 1)
    plan.finish(None, ending, 1)
    table = plan.table

    def run(at, slot):
        if (at, slot) in table:

            @pl.when(step == at)
            def _():
                for work, item in table[at, slot]:
                    work(item)

    phase = step // pieces
    layer = jnp.maximum(layers - 1 - phase // 2, 0)
    index = lax.rem(step, pieces)
    piece = lax.rem(index + 1, pieces)
    in_mlp, in_attend = lax.rem(phase, 2) == 0, lax.rem(phase, 2) == 1
    is_ending = step == ending

    @pl.when(step == 0)
    def _():
        peers.greet()
        fetch(cot_ref, g_ref)

    run(ending, 0)
    for at in range(2 * pieces, ending, 2 * pieces):
        run(at, 0)

    def through_norm(layer, x):
        fetch(x, acc_ref)
        total = total_ref[...]
        hat, scale = row_norm(acc_ref[...])
        g_ref[...] = g1_ref[...] + row_norm_back(total * line(feats_ref.at[layer], LN_GAIN[0]), hat, scale)
        norm_sums_ref[layer] = jnp.zeros(norm_sums_ref.shape[1:], F32)
        norm_sums_ref[layer, 0:1, :] = jnp.sum(total * hat, axis=0, keepdims=True)
        norm_sums_ref[layer, 1:2, :] = jnp.sum(total, axis=0, keepdims=True)

    for above in range(1, layers):

        @pl.when(step == 2 * (layers - above) * pieces)
        def _():
            through_norm(above, x2_ref.at[above - 1])

    @pl.when(is_ending)
    def _():
        through_norm(0, x0_ref)
        tables = split_dot(hot_ref[...].T, g_ref[...])
        tally.build(tables, total_ref, acc_ref, norm_sums_ref, mlp_sums_ref, head_sums_ref, up_grad_ref)

    @pl.when(jnp.logical_and(in_mlp, step < ending))
    def _():
        def hook(slot):
            for at in range(ending):
                if at // pieces % 2 == 0 and not (slot == 0 and at % (2 * pieces) == 0 and at):
                    run(at, slot)

        hook(0)
        up, down = pl.ds(0, wide), pl.ds(wide, wide)
        mlp_back_work(
            g_ref, mlp_near_ref.at[:, down], mlp_far_ref.at[:, down], slope_ref, mlp_near_ref.at[:, up], mlp_far_ref.at[:, up],
            mid_ref, feats_ref.at[layer], gz_ref, gh_ref, up_grad_ref.at[layer, piece], g1_ref, gr_ref,
            mlp_sums_ref.at[layer], acc_ref, index == 0, index == pieces - 1, hook,
        )

        @pl.when(index == 0)
        def _():
            turned_ref[0] = m_ref[...].T
            turned_ref[1] = gz_ref[...].T

        away, keep = buffers[0], buffers[1]
        scatter = scatter_of(layer, 0)
        scatter.room(index, piece)
        for part, ref in ((slice(0, half), keep.at[piece]), (slice(half, 2 * half), away.at[scatter.slot(piece)])):
            ref[:, :wide] = nn(turned_ref[0, part, :], gh_ref[...]).astype(BF16)
            ref[:, wide:] = nn(turned_ref[1, part, :], act_ref[...]).astype(BF16)
        scatter.start(piece, "core")

    @pl.when(in_attend)
    def _():
        def hook(slot):
            for at in range(ending):
                if at // pieces % 2 == 1:
                    run(at, slot)

        hook(0)

        @pl.when(index == 0)
        def _():
            window_ref[...] = jnp.zeros_like(window_ref)
            a_t_ref[...] = a_win_ref[...].T
            turned_ref[0] = gr_ref[...].T

        attend_back_work(
            gr_ref, q_ref, kv_ref, q_hat_ref, k_hat_ref, q_scale_ref, k_scale_ref, p_ref, attn_near_ref, attn_far_ref,
            heads_ref, gq_ref, gkv_ref, head_sums_ref.at[layer, piece], window_ref, hook,
        )
        away, keep = buffers[8], buffers[9]
        scatter = scatter_of(layer, 1)
        scatter.room(index, piece)
        for part, ref in ((slice(0, half), keep.at[piece]), (slice(half, 2 * half), away.at[scatter.slot(piece)])):
            from_q = nn(a_t_ref[part, own], gq_ref[...])
            from_o = nn(turned_ref[0, part, :], o_ref[...])
            ref[:, :PAIR] = from_q[:, :PAIR].astype(BF16)
            ref[:, PAIR : 4 * PAIR] = nn(a_t_ref[part, :], gkv_ref[...]).astype(BF16)
            ref[:, 4 * PAIR : 5 * PAIR] = (from_q[:, PAIR:] + from_o[:, :PAIR]).astype(BF16)
            ref[:, 5 * PAIR :] = from_o[:, PAIR:].astype(BF16)
        scatter.start(piece, "core")

        @pl.when(index == pieces - 1)
        def _():
            a_t_ref[:REACH, : 2 * half] = window_ref[:REACH, :].astype(BF16)
            a_t_ref[REACH : 2 * REACH, : 2 * half] = window_ref[REACH + rows :, :].astype(BF16)
            back(layer).begin()

    run(ending, 1)

    @pl.when(is_ending)
    def _():
        for which in range(2):
            scatter_of(0, which).done()


def scatter_buffers(layers, pieces, chunk, wide):
    buffer = lambda rows: pltpu.VMEM((pieces, rows * chunk, wide), BF16)
    semaphores = pltpu.SemaphoreType.DMA((layers, pieces, Scatter.KINDS))
    away = pltpu.VMEM((2, 4 * chunk, wide), BF16)
    given = pltpu.VMEM((pieces - 1, chunk, wide), BF16)
    return [away, buffer(4), buffer(4), buffer(2), buffer(1), given, semaphores, semaphores]


def backward(cotangent, hot, lines, feats, heads, start, saved):
    *stored, o, act, slope, mid, m, x2, a_win, attn_near, attn_far, mlp_near, mlp_far = saved
    layers, window, width = a_win.shape
    rows, half, pieces = m.shape[1], width // 2, attn_near.shape[1]
    hidden = act.shape[2]
    wide, chunk = hidden // pieces, half // 4

    def mlp_at(step):
        phase = jnp.minimum(step // pieces, 2 * layers - 1)
        index = jnp.where(lax.rem(phase, 2) == 0, lax.rem(step, pieces), pieces - 1)
        return layers - 1 - phase // 2, lax.rem(index + 1, pieces)

    def attend_at(step):
        phase = jnp.minimum(step // pieces, 2 * layers - 1)
        index = jnp.where(lax.rem(phase, 2) == 1, lax.rem(step, pieces), 0)
        index = jnp.where(step == 2 * layers * pieces, pieces - 1, index)
        return layers - 1 - phase // 2, lax.rem(index + 1, pieces)

    once = lambda shape: pl.BlockSpec(shape, lambda step: (0,) * len(shape), pipeline_mode=pl.Buffered(1))
    weight = lambda at, wide: pl.BlockSpec((None, None, half, wide), lambda step: (*at(step), 0, 0))
    cols = lambda at, height, wide: pl.BlockSpec((None, height, wide), lambda step: (at(step)[0], 0, at(step)[1]))
    by_heads = pl.BlockSpec((3, window, rows), lambda step: (attend_at(step)[0] * pieces + attend_at(step)[1], 0, 0))
    layer_heads = pl.BlockSpec((None, None, HEADS, 3 * PAIR), lambda step: (attend_at(step)[1], attend_at(step)[0], 0, 0))
    layer_sheet = lambda at, height: pl.BlockSpec(
        (None, height, width), lambda step: (at(step)[0], 0, 0), pipeline_mode=pl.Buffered(1)
    )
    outs = [
        (rows, width), (layers, pieces, 1, wide), (layers, pieces, 8, 3 * PAIR), (layers, 8, width), (layers, 8, width),
        (lines, PAIR), (layers, chunk, 2 * wide), (layers, chunk, 6 * PAIR),
    ]
    vmem = lambda shape, kind=BF16: pltpu.VMEM(shape, kind)
    inputs = (cotangent, hot, feats, m, mid, a_win, start, x2, mlp_near, mlp_far, slope, act, *stored, attn_near, attn_far, heads, o)
    return pl.pallas_call(
        backward_kernel,
        grid=(2 * layers * pieces + 1,),
        in_specs=[
            ANY, once(hot.shape), once(feats.shape), layer_sheet(mlp_at, rows), layer_sheet(mlp_at, rows), layer_sheet(attend_at, window), ANY, ANY,
            weight(mlp_at, 2 * wide), weight(mlp_at, 2 * wide), cols(mlp_at, rows, wide),
            cols(mlp_at, rows, wide), *[cols(attend_at, *shape) for shape in attend_shapes(rows, window)], by_heads,
            weight(attend_at, 6 * PAIR), weight(attend_at, 6 * PAIR), layer_heads, cols(attend_at, rows, 2 * PAIR),
        ],
        out_specs=[once(shape) for shape in outs],
        out_shape=[shaped(shape, F32) for shape in outs],
        scratch_shapes=[
            vmem((rows, width)), vmem((rows, wide)), vmem((rows, width), F32), vmem((rows, width)),
            vmem((rows, width), F32), vmem((window, width), F32), vmem((rows, 2 * PAIR)), vmem((window, 3 * PAIR)),
            vmem((2, width, rows)), vmem((width, window)),
            vmem((layers, 2 * REACH, width)), pltpu.SemaphoreType.DMA((layers, 4)), pltpu.SemaphoreType.DMA((layers, 4)),
            pltpu.SemaphoreType.REGULAR((layers, 2)), pltpu.SemaphoreType.DMA, vmem((8, lines, PAIR)),
            vmem((7 + pieces, lines, PAIR)), pltpu.SemaphoreType.DMA((pieces + 2,)), pltpu.SemaphoreType.DMA((pieces + 2,)), *scatter_buffers(layers, pieces, chunk, 2 * wide),
            *scatter_buffers(layers, pieces, chunk, 6 * PAIR),
        ],
        compiler_params=params(40, VMEM),
        name="backward",
    )(*inputs)


def flip(array, bit, axis="fsdp"):
    size = lax.axis_size(axis)
    return lax.ppermute(array, axis, [(i, i ^ (1 << bit)) for i in range(size)])


def ring(array):
    size = lax.axis_size("tp")
    return lax.ppermute(array, "tp", [(i, (i + 1) % size) for i in range(size)])


def hop(array, distance):
    size = lax.axis_size("tp")
    return lax.ppermute(array, "tp", [(i, i + distance) for i in range(size) if 0 <= i + distance < size])


def bits_of(size):
    return size.bit_length() - 1


def row_bits(first_top):
    count = bits_of(lax.axis_size("fsdp"))
    tops = [count - 1, count - 2] if first_top else [count - 2, count - 1]
    return list(range(1, count - 2)), tops


def gather_by_permutes(block, first_top):
    pieces = [block]
    for _ in range(lax.axis_size("tp") - 1):
        pieces.append(ring(pieces[-1]))
    block = jnp.concatenate(pieces, axis=1)
    low, tops = row_bits(first_top)
    have = []
    for bit in low + tops:
        axis = sum(other > bit for other in have)
        block = jnp.stack([block, flip(block, bit)], axis=axis)
        have.append(bit)
    block = block.reshape((-1, len(pieces), pieces[0].shape[1])).transpose(1, 0, 2)[None]
    return block, flip(block, 0)


def add(left, right, kind=BF16):
    return (left.astype(F32) + right.astype(F32)).astype(kind)


def reduce_by_permutes(keep, send, first_top):
    low, tops = row_bits(first_top)
    block = add(keep, flip(send, 0))
    order = tops + low[::-1]
    have = sorted(order, reverse=True)
    block = block.reshape((2,) * len(have) + (-1, block.shape[-1]))
    for bit in order:
        axis = have.index(bit)
        mine = lax.index_in_dim(block, 0, axis, keepdims=False)
        other = lax.index_in_dim(block, 1, axis, keepdims=False)
        block = add(mine, flip(other, bit))
        have.remove(bit)
    pieces = jnp.split(block, lax.axis_size("tp"), axis=1)
    total = pieces[1]
    for piece in pieces[2:]:
        total = add(ring(total), piece)
    return add(ring(total), pieces[0], F32)


def attn_shard(w_qkv, w_out):
    q, k, v = (w_qkv[:, which] for which in range(3))
    o = w_out.T
    return side(q[:, :PAIR], k[:, :PAIR], v[:, :PAIR], k[:, PAIR:], v[:, PAIR:], q[:, PAIR:], o[:, PAIR:], o[:, :PAIR])


def attn_unshard(block):
    tile = lambda start, wide=PAIR: block[:, start : start + wide]
    q = side(tile(0), tile(4 * PAIR, HD))
    k = side(tile(PAIR), tile(3 * PAIR, HD))
    v = side(tile(2 * PAIR), tile(3 * PAIR + HD, HD))
    o = side(tile(5 * PAIR), tile(4 * PAIR + HD, HD))
    return jnp.stack([q, k, v], axis=1), o.T


def body(
    tokens, segment_ids, patch_pos, row_table, col_table, ln_gain, ln_bias, qkv_bias, qk_gain, query_bias, out_bias,
    fc1_bias, fc2_bias, w_qkv, w_out, w_fc1, w_fc2, cotangent,
):
    layers = w_qkv.shape[0]
    rows, width = tokens.shape
    half = width // 2
    fsdp, tp = lax.axis_size("fsdp"), lax.axis_size("tp")
    f_index, t_index = lax.axis_index("fsdp"), lax.axis_index("tp")
    hidden = fc1_bias.shape[1] * fsdp * tp
    grid = row_table.shape[0]
    fine = width // (fsdp * tp)
    parts = hidden // width
    in_kernel = fsdp == 8

    place = jnp.arange(width, dtype=jnp.int32)
    chunk = width // fsdp
    slot = place // chunk
    away = (slot % (fsdp // 2)) * 2 + slot // (fsdp // 2)
    feature_at = (f_index ^ away) * chunk + place % chunk
    head_cols = width // tp
    spot = jnp.arange(tp * 3 * PAIR, dtype=jnp.int32)
    tile, part = spot % (3 * PAIR) // PAIR, spot % PAIR // HD
    head = jnp.where(tile == 0, part, jnp.where(tile == part + 1, 2, -fsdp * tp))
    head_at = ((t_index - spot // (3 * PAIR)) % tp) * head_cols + head * HD + spot % HD
    to_feature = (place[:, None] == feature_at[None, :]).astype(BF16)
    to_head = (place[:, None] == head_at[None, :]).astype(BF16)
    device = jnp.arange(fsdp * tp, dtype=jnp.int32)
    wanted = ((t_index - device // fsdp) % tp) * fsdp + device % fsdp
    to_hidden = (wanted[:, None] == device[None, :]).astype(BF16)

    by_layer = lambda *items: jnp.concatenate([item.reshape(layers, -1, fine) for item in items], axis=1).reshape(-1, fine)
    shares = [
        row_table, col_table, by_layer(ln_gain, ln_bias, out_bias, fc2_bias), by_layer(qkv_bias, qk_gain, query_bias),
        fc1_bias.reshape(layers * parts, fine),
    ]
    count = sum(item.shape[0] for item in shares)
    attn_shards = jnp.stack([attn_shard(w_qkv[layer], w_out[layer]) for layer in range(layers)])
    mlp_shards = jnp.concatenate([w_fc1, w_fc2.transpose(0, 2, 1)], axis=2)
    grid_ids = jnp.arange(grid, dtype=jnp.int32)
    row_hot = patch_pos[0][:, None] == grid_ids[None, :]
    col_hot = patch_pos[1][:, None] == grid_ids[None, :]
    hot = side(row_hot, col_hot).astype(BF16)
    tokens = jnp.dot(tokens, to_feature, preferred_element_type=F32)
    segments = segment_ids[0]
    padded = jnp.pad(segments, (REACH, REACH), constant_values=-1)
    seg_k = lax.dynamic_slice_in_dim(padded, t_index * rows, rows + 2 * REACH).reshape(-1, 1)
    seg_q = lax.dynamic_slice_in_dim(segments, t_index * rows, rows).reshape(1, -1)
    spill = REACH - rows

    if in_kernel:
        share = jnp.concatenate([jnp.pad(item, ((0, -item.shape[0] % 16), (0, PAIR - fine))) for item in shares], axis=0)
        *kept, start, feats, heads, a_win, attn_near, attn_far, mlp_near, mlp_far = forward(
            tokens, hot, share, seg_k, seg_q, attn_shards, mlp_shards
        )
        residual = kept[-1][layers - 1]
        kept += [a_win, attn_near, attn_far, mlp_near, mlp_far]
    else:
        small = jnp.concatenate(shares, axis=0)
        flat = small.reshape(1, -1)
        for bit in range(bits_of(tp)):
            flat = jnp.concatenate([flat, flip(flat, bit, "tp")], axis=0)
        for bit in range(bits_of(fsdp)):
            flat = jnp.concatenate([flat, flip(flat, bit)], axis=0)
        flat = flat[jnp.arange(fsdp * tp) ^ (f_index * tp + t_index)]
        gathered = flat.reshape(fsdp * tp, count, fine)
        lined = gathered.transpose(1, 0, 2).reshape(count, width)
        wide = 2 * grid + 6 * layers
        feats = jnp.dot(lined[:wide], to_feature, preferred_element_type=F32)
        heads = jnp.dot(lined[wide : wide + 6 * layers], to_head, preferred_element_type=F32)
        up_shift = jnp.einsum(
            "or,rlsi->losi",
            to_hidden,
            gathered[:, wide + 6 * layers :].reshape(fsdp * tp, layers, parts, fine),
            preferred_element_type=F32,
        ).reshape(layers, tp, 1, hidden // tp)
        tables = feats[: 2 * grid].astype(BF16)
        feats = feats[2 * grid :].reshape(layers, FEATS, width)

        heads = heads.reshape(layers, HEADS, tp, 3 * PAIR).transpose(2, 0, 1, 3)
        residual = tokens + jnp.dot(hot, tables, preferred_element_type=F32)
        hat, _ = row_norm(residual)
        a_own = (hat * feats[0, LN_GAIN[0]] + feats[0, LN_BIAS[0]]).astype(BF16)
        saved = []
        for layer in range(layers):
            a_win = jnp.concatenate(
                [hop(a_own[rows - spill :], 2), hop(a_own, 1), a_own, hop(a_own, -1), hop(a_own[:spill], -2)], axis=0
            )
            attn_near, attn_far = gather_by_permutes(attn_shards[layer], layer % 2 == 0)
            *stored, probs, o, mid, m = attend(
                a_win, attn_near, attn_far, heads, feats, residual, seg_k, seg_q, layer
            )
            mlp_near, mlp_far = gather_by_permutes(mlp_shards[layer], layer % 2 == 1)
            act, slope, x2 = mlp(m, mid, mlp_near, mlp_far, up_shift, feats, layer)
            stored = [item[None] for item in stored] + [probs]
            kept = [item[None] for item in (o, mid, m, act, slope)]
            saved.append((residual, a_win[None], stored, *kept, attn_near, attn_far, mlp_near, mlp_far))
            residual = x2
            if layer + 1 < layers:
                hat, _ = row_norm(residual)
                a_own = (
                    hat * feats[layer + 1, LN_GAIN[0]] + feats[layer + 1, LN_BIAS[0]]
                ).astype(BF16)

    restore = functools.partial(
        lax.dot_general, dimension_numbers=(((1,), (1,)), ((), ())), precision=HIGHEST, preferred_element_type=F32
    )
    exact = to_feature.astype(F32)
    activations = restore(residual, exact)
    cotangent_here = jnp.dot(cotangent, exact, precision=HIGHEST, preferred_element_type=F32)
    kept_sums = [None] * layers
    if in_kernel:
        grad, _, _, _, _, tally, mlp_blocks, attn_blocks = backward(
            cotangent_here, hot, share.shape[0], feats, heads, start, kept
        )
    else:
        grad, mlp_blocks, attn_blocks = cotangent_here, [None] * layers, [None] * layers
        for layer in reversed(range(layers)):
            x, a_win, stored, o, mid, m, act, slope, attn_near, attn_far, mlp_near, mlp_far = saved[layer]
            gz, gh, up_grad, g1, gr, mlp_small = mlp_back(grad, mlp_near, mlp_far, slope, mid, feats, layer, 0)
            mlp_blocks[layer] = reduce_by_permutes(*mlp_weight_grads(m, gh, gz, act), layer % 2 == 0)
            gq, gkv, mine, left, right, attn_small = attend_back(gr, stored, attn_near, attn_far, heads, layer, 0)
            attn_blocks[layer] = reduce_by_permutes(*attn_weight_grads(a_win, gq, gkv, gr, o), layer % 2 == 1)
            ends = jnp.concatenate([hop(right[rows:], 2), hop(left[:spill], -2)], axis=0).astype(F32)
            attn_grad = mine + hop(right[:rows], 1).astype(F32) + hop(left[spill:], -1).astype(F32) + ends
            hat, scale = row_norm(x)
            grad = g1 + row_norm_back(attn_grad * feats[layer, LN_GAIN[0]], hat, scale)
            kept_sums[layer] = (
                jnp.sum(attn_grad * hat, axis=0), jnp.sum(attn_grad, axis=0), mlp_small, attn_small,
                up_grad.reshape(parts, width),
            )
    middle = mlp_blocks[0].shape[1] // 2
    w_fc1_grad = [block[:, :middle] for block in mlp_blocks]
    w_fc2_grad = [block[:, middle:].T for block in mlp_blocks]
    w_qkv_grad, w_out_grad = zip(*[attn_unshard(block) for block in attn_blocks])

    token_grad = restore(grad, exact)
    if in_kernel:
        found = lax.dynamic_slice_in_dim(tally, t_index * fine, fine, axis=1)
        rows_g, cols_g, rest = found[:grid], found[grid : 2 * grid], found[2 * grid :]
        by_feature = rest[: layers * FEATS].reshape(layers, FEATS, fine)
        by_head = rest[16 : 16 + layers * HEADS].reshape(layers, HEADS, fine)
        up_g = rest[32 : 32 + layers * parts].reshape(layers, parts * fine)
    else:
        row_grad = jnp.einsum("tg,td->gd", row_hot.astype(F32), grad, precision=HIGHEST)
        col_grad = jnp.einsum("tg,td->gd", col_hot.astype(F32), grad, precision=HIGHEST)
        featured = [row_grad, col_grad]
        headed = []
        for a_gain, a_shift, sums, head_sums, _ in kept_sums:
            featured.append(jnp.stack([a_gain, sums[2], a_shift, sums[3], sums[1], sums[0]]))
            headed += [head_sums[3:6], head_sums[0:2], head_sums[2:3]]
        headed = jnp.concatenate(headed)
        spread = jnp.concatenate(
            [restore(jnp.concatenate(featured), to_feature.astype(F32)), restore(headed, to_head.astype(F32))]
        )
        spread = spread.reshape(-1, fsdp * tp, fine).transpose(1, 0, 2)
        up_all = jnp.stack([item[4] for item in kept_sums]).reshape(layers, fsdp * tp, parts * fine)
        up_all = jnp.einsum("or,lok->rlk", to_hidden.astype(F32), up_all, precision=HIGHEST)
        flat = jnp.concatenate([spread.reshape(fsdp * tp, -1), up_all.reshape(fsdp * tp, -1)], axis=1)
        flat = flat[jnp.arange(fsdp * tp) ^ (f_index * tp + t_index)]
        for bit in reversed(range(bits_of(fsdp))):
            middle = flat.shape[0] // 2
            flat = flat[:middle] + flip(flat[middle:], bit)
        for bit in reversed(range(bits_of(tp))):
            middle = flat.shape[0] // 2
            flat = flat[:middle] + flip(flat[middle:], bit, "tp")
        found = flat.reshape(-1, fine)
        rows_g, cols_g, rest = found[:grid], found[grid : 2 * grid], found[2 * grid :]
        by_feature = rest[: layers * FEATS].reshape(layers, FEATS, fine)
        by_head = rest[layers * FEATS : layers * (FEATS + HEADS)].reshape(layers, HEADS, fine)
        up_g = rest[layers * (FEATS + HEADS) :].reshape(layers, parts * fine)
    gain_g, shift_g, out_g, last_g = by_feature[:, :2], by_feature[:, 2:4], by_feature[:, OUT_BIAS], by_feature[:, LAST_BIAS]
    proj_g, head_gain_g, head_shift_g = by_head[:, :3], by_head[:, 3:5], by_head[:, HEAD_BIAS]
    return (
        activations, token_grad, rows_g, cols_g, gain_g, shift_g, proj_g, head_gain_g, head_shift_g, out_g, up_g, last_g,
        jnp.stack(w_qkv_grad), jnp.stack(w_out_grad), jnp.stack(w_fc1_grad), jnp.stack(w_fc2_grad),
    )


def solution(mesh):
    both = ("fsdp", "tp")
    in_specs = (
        P(both, None), P("fsdp", None), P(None, both), P(None, both), P(None, both), P(None, None, both),
        P(None, None, both), P(None, None, both), P(None, None, both), P(None, both), P(None, both), P(None, both),
        P(None, both), P(None, "fsdp", None, "tp"), P(None, "tp", "fsdp"), P(None, "fsdp", "tp"), P(None, "tp", "fsdp"),
        P(both, None),
    )
    out_specs = (
        P(both, None), P(both, None), P(None, both), P(None, both), P(None, None, both), P(None, None, both),
        P(None, None, both), P(None, None, both), P(None, both), P(None, both), P(None, both), P(None, both),
        P(None, "fsdp", None, "tp"), P(None, "tp", "fsdp"), P(None, "fsdp", "tp"), P(None, "tp", "fsdp"),
    )
    return jax.shard_map(body, mesh=mesh, in_specs=in_specs, out_specs=out_specs, check_vma=False)
```

```python
import functools

import jax
import jax.numpy as jnp
from jax import lax
from jax.experimental import pallas as pl
from jax.experimental.pallas import tpu as pltpu
from jax.sharding import PartitionSpec as P

HD = 64
PAIR = 128
REACH = 384
EPS = 1e-06
FILL = -1e30
ROOT_HALF = 0.7071067811865476
INV_ROOT_TWO_PI = 0.3989422804014327
HIGHEST = lax.Precision.HIGHEST
F32 = jnp.float32
BF16 = jnp.bfloat16
MESH = pl.DeviceIdType.MESH
VMEM = 67043328
ANY = pl.BlockSpec(memory_space=pl.ANY)


def nn(left, right):
    return lax.dot_general(left, right, (((1,), (0,)), ((), ())), preferred_element_type=F32)


def nt(left, right):
    return lax.dot_general(left, right, (((1,), (1,)), ((), ())), preferred_element_type=F32)


def halves(array):
    middle = array.shape[1] // 2
    return array[:, :middle], array[:, middle:]


def row_norm(value):
    centered = value - jnp.mean(value, axis=-1, keepdims=True)
    scale = lax.rsqrt(jnp.mean(centered * centered, axis=-1, keepdims=True) + EPS)
    return centered * scale, scale


def row_norm_back(grad_hat, normed, scale):
    return scale * (
        grad_hat
        - jnp.mean(grad_hat, axis=-1, keepdims=True)
        - normed * jnp.mean(grad_hat * normed, axis=-1, keepdims=True)
    )


def head_mean(value, exact=False):
    wide = value.shape[1]
    rows = lax.broadcasted_iota(jnp.int32, (wide, wide), 0) // HD
    cols = lax.broadcasted_iota(jnp.int32, (wide, wide), 1) // HD
    spread = jnp.where(rows == cols, 1.0 / HD, 0.0).astype(BF16)
    high = value.astype(BF16)
    mean = nn(high, spread)
    if exact:
        mean += nn((value - high.astype(F32)).astype(BF16), spread)
    return mean


def head_norm(value):
    centered = value - head_mean(value, exact=True)
    scale = lax.rsqrt(head_mean(centered * centered) + EPS)
    return centered * scale, scale


def head_norm_back(grad_hat, normed, scale):
    return scale * (grad_hat - head_mean(grad_hat) - normed * head_mean(grad_hat * normed))


def only(array, part):
    return jnp.where(lax.broadcasted_iota(jnp.int32, (1, PAIR), 1) // HD == part, array, jnp.zeros_like(array))


def side(*parts):
    return jnp.concatenate(parts, axis=1)


def whole(shape):
    return pl.BlockSpec(shape, lambda step: (0,) * len(shape))


def column(height, wide, every=1, first=0):
    return pl.BlockSpec((height, wide), lambda step: (0, step * every + first))


def piece_of(layer, height, wide, first=0):
    return pl.BlockSpec((None, None, height, wide), lambda step: (layer, step, 0, first))


def slab(layer, height, wide):
    return pl.BlockSpec((None, height, wide), lambda step: (layer, 0, step))


def heads_of(layer):
    return pl.BlockSpec((None, None, HEADS, 3 * PAIR), lambda step: (step, layer, 0, 0))


def sheet(layer, height, wide):
    return pl.BlockSpec((None, height, wide), lambda step: (layer, 0, 0))


def shaped(shape, kind=BF16):
    return jax.ShapeDtypeStruct(shape, kind)


class Neighbours:
    def __init__(self):
        fsdp, tp = lax.axis_index("fsdp"), lax.axis_index("tp")
        self.size = lax.axis_size("tp")
        self.tp = tp
        self.x, self.y, self.core = ({"fsdp": jnp.bitwise_xor(fsdp, bit)} for bit in (2, 4, 1))

    def along(self, distance):
        return {"tp": lax.rem(self.tp + distance, self.size)}

    def all(self):
        return [self.x, self.y, self.core] + [self.along(distance) for distance in range(1, self.size)]

    def greet(self):
        targets = self.all()
        barrier = pltpu.get_barrier_semaphore()
        for target in targets:
            pl.semaphore_signal(barrier, inc=1, device_id=target, device_id_type=MESH)
        pl.semaphore_wait(barrier, len(targets))


class Plan:
    LINKS = {"x": (45.5e3, 1.5), "y": (45.5e3, 1.5), "z": (45.5e3, 2.2), "core": (600e3, 1.0)}

    def __init__(self, depth):
        self.depth, self.clock = {"x": 3.0, "y": 3.0, "z": depth, "core": 20.0}, 0.0
        self.free, self.here, self.jobs, self.table = dict.fromkeys(self.LINKS, 0.0), {}, [], {}

    def add(self, rank, work, needs, copies, gives, group):
        self.jobs.append((rank, len(self.jobs), work, needs, copies, gives, group))
        self.jobs.sort(key=lambda job: job[:2])

    def carry(self, copies, gives):
        end = self.clock
        for link, size in copies:
            rate, latency = self.LINKS[link]
            self.free[link] = max(self.free[link], self.clock) + size / rate
            end = max(end, self.free[link] + latency)
        self.here[gives] = end

    def slot(self, *at):
        found = True
        while found:
            found = False
            for job in self.jobs:
                _, _, work, needs, copies, gives, _ = job
                ready = all(self.here.get(need, float("inf")) <= self.clock for need in needs)
                if ready and all(self.free[link] - self.clock < self.depth[link] for link, _ in copies):
                    self.carry(copies, gives)
                    self.table.setdefault(at, []).append(work)
                    self.jobs.remove(job)
                    found = True
                    break

    def wait(self, key, work, *at):
        self.slot(*at)
        while self.here.get(key, float("inf")) > self.clock:
            self.clock += 0.25
            self.slot(*at)
        self.table.setdefault(at, []).append(work)

    def finish(self, group, *at):
        self.slot(*at)
        while any(group in (None, job[-1]) for job in self.jobs):
            self.clock += 0.25
            self.slot(*at)

    def spend(self, time):
        self.clock += time


def turn(index, pieces):
    if isinstance(index, int):
        return (index + 1) // 2 if index % 2 else (pieces - index // 2) % pieces
    return jnp.where(lax.rem(index, 2) == 1, (index + 1) // 2, lax.rem(pieces - index // 2, pieces))


class Gather:
    KINDS = 7

    def __init__(self, peers, shard, near, far, send, recv, local, near_out, far_out, stored):
        self.peers, self.shard, self.near, self.far = peers, shard, near, far
        self.send, self.recv, self.local = send, recv, local
        self.outs, self.stored = (near_out, far_out), stored
        self.chunk, self.wide = shard.shape
        self.pieces = near.shape[0]

    def at(self, piece, start, count, half=None):
        first, wide = (0, self.wide) if half is None else (half * (self.wide // 2), self.wide // 2)
        return self.near.at[piece, pl.ds(start * self.chunk, count * self.chunk), pl.ds(first, wide)]

    def copy(self, piece, kind, source, target, device):
        return pltpu.make_async_remote_copy(
            src_ref=source, dst_ref=target, send_sem=self.send.at[piece, kind], recv_sem=self.recv.at[piece, kind],
            device_id=device, device_id_type=MESH,
        )

    def copies(self, piece, stage):
        if stage == "z":
            return [self.copy(piece, 0, self.shard, self.at(piece, 0, 1), self.peers.along(piece))] if piece else []
        if stage == "first":
            half = self.wide // 2
            left = self.shard.at[:, pl.ds(0, half)] if piece == 0 else self.at(piece, 0, 1, 0)
            right = self.shard.at[:, pl.ds(half, half)] if piece == 0 else self.at(piece, 0, 1, 1)
            return [
                self.copy(piece, 1, left, self.at(piece, 1, 1, 0), self.peers.x),
                self.copy(piece, 2, right, self.at(piece, 2, 1, 1), self.peers.y),
            ]
        if stage == "second":
            return [
                self.copy(piece, 3, self.at(piece, 0, 2, 0), self.at(piece, 2, 2, 0), self.peers.y),
                self.copy(piece, 4, self.at(piece, 0, 1, 1), self.at(piece, 1, 1, 1), self.peers.x),
                self.copy(piece, 5, self.at(piece, 2, 1, 1), self.at(piece, 3, 1, 1), self.peers.x),
            ]
        return [self.copy(piece, 6, self.near.at[piece], self.far.at[piece], self.peers.core)]

    def start(self, piece, stage):
        for copy in self.copies(piece, stage):
            copy.start()

    def arrived(self, piece, stage):
        for copy in self.copies(piece, stage):
            copy.wait_recv()

    def store(self, piece):
        return [
            pltpu.make_async_copy(source.at[piece], target.at[piece], self.stored.at[piece, which])
            for which, (source, target) in enumerate(zip((self.near, self.far), self.outs))
        ]

    def own(self):
        return pltpu.make_async_copy(self.shard, self.at(0, 0, 1), self.local)

    def sent(self, piece):
        self.start(piece, "z")

    def landed(self, piece):
        self.arrived(piece, "z")
        self.start(piece, "first")

    def crossed(self, piece):
        self.arrived(piece, "first")
        self.start(piece, "second")

    def shared(self, piece):
        self.arrived(piece, "second")
        self.start(piece, "core")

    def need(self, piece):
        self.arrived(piece, "core")
        for copy in self.store(piece):
            copy.start()

    def jobs(self, plan, index):
        size = self.chunk * self.wide * 2
        for place in range(self.pieces):
            piece = turn(place, self.pieces)
            key = (index, piece)
            rank = index * self.pieces + place
            if piece:
                plan.add(rank, (self.sent, piece), [], [("z", size * self.pieces / (self.pieces - 1))], ("z", *key), index)
            both = lambda count: [("x", count * size), ("y", count * size)]
            plan.add(rank, (self.landed, piece), [("z", *key)] if piece else [], both(0.5), ("first", *key), index)
            plan.add(rank, (self.crossed, piece), [("first", *key)], both(1), ("second", *key), index)
            plan.add(rank, (self.shared, piece), [("second", *key)], [("core", 4 * size)], ("core", *key), index)

    def end(self):
        for piece in range(self.pieces):
            for stage in ("z", "first", "second", "core"):
                for copy in self.copies(piece, stage):
                    copy.wait_send()
            for copy in self.store(piece):
                copy.wait()


class Halo:
    def __init__(self, ref, rows, send, recv):
        self.ref, self.send, self.recv = ref, send, recv
        self.place, self.size = lax.axis_index("tp"), lax.axis_size("tp")
        spill = REACH - rows
        self.moves = [
            (1, 1, pl.ds(REACH, rows), pl.ds(spill, rows)),
            (-1, 1, pl.ds(REACH, rows), pl.ds(REACH + rows, rows)),
            (1, 2, pl.ds(REACH - spill, spill), pl.ds(0, spill)),
            (-1, 2, pl.ds(REACH + rows, spill), pl.ds(REACH + 2 * rows, spill)),
        ]

    def inside(self, distance):
        other = self.place + distance
        return jnp.logical_and(other >= 0, other < self.size)

    def sends(self, index):
        direction, far, *_ = self.moves[index]
        return jnp.logical_and(self.inside(direction), self.inside(direction * (1 - far)))

    def takes(self, index):
        direction, far, *_ = self.moves[index]
        return self.inside(-direction * far)

    def copy(self, index):
        direction, _, source, target = self.moves[index]
        return pltpu.make_async_remote_copy(
            src_ref=self.ref.at[source, :], dst_ref=self.ref.at[target, :], send_sem=self.send.at[index],
            recv_sem=self.recv.at[index], device_id={"tp": self.place + direction}, device_id_type=MESH,
        )

    def start(self, index):
        @pl.when(self.sends(index))
        def _():
            self.copy(index).start()

    def arrived(self, index):
        @pl.when(self.takes(index))
        def _():
            self.copy(index).wait_recv()

    def begin(self):
        for index in range(2):
            self.start(index)
        for index, (*_, target) in enumerate(self.moves):

            @pl.when(jnp.logical_not(self.takes(index)))
            def _():
                self.ref[target, :] = jnp.zeros((target.size, self.ref.shape[1]), BF16)

    def relay(self):
        for index in range(2):
            self.arrived(index)
            self.start(index + 2)

    def end(self):
        for index in range(4):
            if index > 1:
                self.arrived(index)

            @pl.when(self.sends(index))
            def _():
                self.copy(index).wait_send()


def params(collective, memory=None):
    return pltpu.CompilerParams(collective_id=collective, has_side_effects=True, vmem_limit_bytes=memory)


LN_GAIN, LN_BIAS, OUT_BIAS, LAST_BIAS, FEATS = (0, 1), (2, 3), 4, 5, 6
PROJ_BIAS, HEAD_GAIN, HEAD_BIAS, HEADS = (0, 1, 2), (3, 4), 5, 6


def line(ref, row, start=0, wide=None):
    return ref[pl.ds(row, 1), pl.ds(start, wide or ref.shape[1] - start)]


def attend_work(
    a_ref, near_ref, far_ref, heads_ref, feats_ref, x_ref, q_ref, kv_ref, q_hat_ref, k_hat_ref, q_scale_ref, k_scale_ref,
    p_ref, o_ref, mid_ref, m_ref, mask_ref, acc_ref, opening, closing, hook,
):
    rows = q_ref.shape[0]
    half = near_ref.shape[0]

    @pl.when(opening)
    def _():
        acc_ref[...] = jnp.zeros_like(acc_ref)

    tile = lambda row, which: line(heads_ref, row, which * PAIR, PAIR)
    bias, (q_gain, k_gain), q_shift = PROJ_BIAS, HEAD_GAIN, HEAD_BIAS
    near, distant = halves(a_ref[...])
    own, own_far = halves(a_ref[REACH : REACH + rows, :])
    kv = nn(near, near_ref[:, PAIR : 4 * PAIR]) + nn(distant, far_ref[:, PAIR : 4 * PAIR])
    kv += side(tile(bias[1], 0), tile(bias[2], 0), tile(bias[1], 1) + tile(bias[2], 2))
    q = side(
        nn(own, near_ref[:, :PAIR]) + nn(own_far, far_ref[:, :PAIR]),
        nn(own, near_ref[:, 4 * PAIR : 5 * PAIR]) + nn(own_far, far_ref[:, 4 * PAIR : 5 * PAIR]),
    ) + line(heads_ref, bias[0], 0, 2 * PAIR)
    q_hat, q_scale = head_norm(q)
    k_hat, k_scale = head_norm(side(kv[:, :PAIR], kv[:, 2 * PAIR :]))
    qn = (q_hat * line(heads_ref, q_gain, 0, 2 * PAIR) + line(heads_ref, q_shift, 0, 2 * PAIR)).astype(BF16)
    qn = side(qn[:, :PAIR], only(qn[:, PAIR:], 0))
    kn = (k_hat * line(heads_ref, k_gain, 0, 2 * PAIR)).astype(BF16)
    v = kv[:, PAIR:].astype(BF16)
    low = lax.broadcasted_iota(jnp.int32, (1, PAIR), 1) < HD
    first, second = kn[:, :PAIR], jnp.where(low, kn[:, PAIR:], v[:, PAIR:])
    values = v[:, :PAIR]
    q_ref[...] = qn
    kv_ref[...] = side(first, values, second)
    q_hat_ref[...] = q_hat.astype(BF16)
    k_hat_ref[...] = k_hat.astype(BF16)
    q_scale_ref[...] = q_scale.astype(BF16)
    k_scale_ref[...] = k_scale.astype(BF16)
    hook(1)
    values_t, second_t = values.T, second.T
    mixed = []
    for head in range(3):
        if head:
            hook(head + 1)
        keys = (first, first, second)[head]
        query = only(qn[:, PAIR * (head // 2) : PAIR * (head // 2 + 1)] * HD ** (-0.5), head % 2).astype(BF16)
        scores = nt(keys, query) + mask_ref[...]
        weights = jnp.exp(scores - jnp.max(scores, axis=0, keepdims=True))
        total = jnp.sum(weights, axis=0, keepdims=True)
        probs = (weights * (1.0 / total)).astype(BF16)
        p_ref[head] = probs
        mixed.append(nn((values_t[:HD], values_t[HD:], second_t[HD:])[head], probs))
    o = jnp.concatenate([jnp.zeros_like(mixed[2]), mixed[2], mixed[0], mixed[1]], axis=0).T.astype(BF16)
    o_ref[...] = o
    acc_ref[:, :half] += nt(o, near_ref[:, 4 * PAIR :])
    acc_ref[:, half:] += nt(o, far_ref[:, 4 * PAIR :])

    @pl.when(closing)
    def _():
        mid = x_ref[...] + (acc_ref[...] + line(feats_ref, OUT_BIAS))
        mid_ref[...] = mid
        hat, _ = row_norm(mid)
        m_ref[...] = (hat * line(feats_ref, LN_GAIN[1]) + line(feats_ref, LN_BIAS[1])).astype(BF16)


def mlp_work(
    m_ref, mid_ref, near_ref, far_ref, up_shift, feats_ref, act_ref, slope_ref, x2_ref, acc_ref, opening, closing, hook,
):
    half = near_ref.shape[0]
    wide = act_ref.shape[1]

    @pl.when(opening)
    def _():
        acc_ref[...] = jnp.zeros_like(acc_ref)

    near, distant = halves(m_ref[...])
    hidden = nn(near, near_ref[:, :wide]) + nn(distant, far_ref[:, :wide]) + up_shift
    hook(1)
    phi = 0.5 * (1.0 + lax.erf(hidden * ROOT_HALF))
    act = (hidden * phi).astype(BF16)
    act_ref[...] = act
    slope_ref[...] = (phi + hidden * jnp.exp(-0.5 * hidden * hidden) * INV_ROOT_TWO_PI).astype(BF16)
    acc_ref[:, :half] += nt(act, near_ref[:, wide:])
    acc_ref[:, half:] += nt(act, far_ref[:, wide:])

    @pl.when(closing)
    def _():
        x2_ref[...] = mid_ref[...] + (acc_ref[...] + line(feats_ref, LAST_BIAS))


def norm_rows(x, feats_ref):
    hat, _ = row_norm(x)
    return (hat * line(feats_ref, LN_GAIN[0]) + line(feats_ref, LN_BIAS[0])).astype(BF16)


def quiet(slot):
    pass


def attend_kernel(
    a_ref, near_ref, far_ref, heads_ref, feats_ref, x_ref, seg_k_ref, seg_q_ref, *rest
):
    step = pl.program_id(0)
    mask_ref = rest[-2]

    @pl.when(step == 0)
    def _():
        mask_ref[...] = jnp.where(seg_k_ref[...] == seg_q_ref[...], 0.0, FILL)

    attend_work(
        a_ref, near_ref, far_ref, heads_ref, feats_ref, x_ref, *rest, step == 0, step == pl.num_programs(0) - 1, quiet
    )


def attend_shapes(rows, window):
    return [
        (rows, 2 * PAIR), (window, 3 * PAIR), (rows, 2 * PAIR), (window, 2 * PAIR), (rows, 2 * PAIR), (window, 2 * PAIR),
    ]


def attend(a_win, near, far, heads, feats, x, seg_k, seg_q, layer):
    window, width = a_win.shape
    rows = x.shape[0]
    half = width // 2
    pieces = near.shape[1]
    outs = attend_shapes(rows, window)
    return pl.pallas_call(
        attend_kernel,
        grid=(pieces,),
        in_specs=[
            whole((window, width)), piece_of(0, half, 6 * PAIR), piece_of(0, half, 6 * PAIR), heads_of(layer), sheet(layer, FEATS, width),
            whole((rows, width)), whole((window, 1)), whole((1, rows)),
        ],
        out_specs=[column(*shape) for shape in outs]
        + [pl.BlockSpec((3, window, rows), lambda step: (step, 0, 0)), column(rows, 2 * PAIR)] + [whole((rows, width))] * 2,
        out_shape=[shaped((height, pieces * wide)) for height, wide in outs]
        + [shaped((3 * pieces, window, rows)), shaped((rows, pieces * 2 * PAIR)), shaped((rows, width), F32), shaped((rows, width))],
        scratch_shapes=[pltpu.VMEM((window, rows), F32), pltpu.VMEM((rows, width), F32)],
        name="attend",
    )(a_win, near, far, heads, feats, x, seg_k, seg_q)


def mlp_kernel(m_ref, mid_ref, near_ref, far_ref, up_shift_ref, feats_ref, *rest):
    step = pl.program_id(0)
    mlp_work(
        m_ref, mid_ref, near_ref, far_ref, up_shift_ref[...], feats_ref, *rest, step == 0, step == pl.num_programs(0) - 1, quiet
    )


def mlp(m, mid, near, far, up_shift, feats, layer):
    rows, width = mid.shape
    half = width // 2
    _, pieces, _, wide = up_shift.shape
    hidden = pieces * wide
    full = whole((rows, width))
    return pl.pallas_call(
        mlp_kernel,
        grid=(pieces,),
        in_specs=[
            full, full, piece_of(0, half, 2 * wide), piece_of(0, half, 2 * wide), piece_of(layer, 1, wide), sheet(layer, FEATS, width),
        ],
        out_specs=[column(rows, wide), column(rows, wide), full],
        out_shape=[shaped((rows, hidden)), shaped((rows, hidden)), shaped((rows, width), F32)],
        scratch_shapes=[pltpu.VMEM((rows, width), F32)],
        name="mlp",
    )(m, mid, near, far, up_shift, feats)


class Share:
    def __init__(self, peers, mine, landed, chunks, send, recv):
        self.peers, self.mine, self.landed, self.chunks, self.send, self.recv = peers, mine, landed, chunks, send, recv
        self.pieces, self.lines = landed.shape[0], mine.shape[0]

    def copy(self, index, source, target, device):
        return pltpu.make_async_remote_copy(
            src_ref=source, dst_ref=target, send_sem=self.send.at[index], recv_sem=self.recv.at[index], device_id=device,
            device_id_type=MESH,
        )

    def along(self):
        place = self.landed.at[self.peers.tp]
        return [self.copy(d - 1, self.mine, place, self.peers.along(d)) for d in range(1, self.pieces)]

    def across(self, stage):
        count = 1 << stage
        device = (self.peers.x, self.peers.y, self.peers.core)[stage]
        source, target = self.chunks.at[pl.ds(0, count)], self.chunks.at[pl.ds(count, count)]
        return self.copy(self.pieces - 1 + stage, source, target, device)

    def begin(self):
        for copy in self.along():
            copy.start()
        self.landed[self.peers.tp] = self.mine[...]

    def meet(self, fine):
        for copy in self.along():
            copy.wait_recv()
        row, col = (lax.broadcasted_iota(jnp.int32, (PAIR, PAIR), axis) for axis in range(2))
        total = 0.0
        for place in range(self.pieces):
            spread = jnp.logical_and(row < fine, col == row + place * fine)
            total += nn(self.landed[place], spread.astype(F32).astype(BF16))
        self.chunks[0] = total.astype(BF16)
        self.across(0).start()

    def spread(self, stage):
        self.across(stage - 1).wait_recv()
        self.across(stage).start()

    def end(self):
        self.across(2).wait_recv()
        for copy in self.along() + [self.across(stage) for stage in range(3)]:
            copy.wait_send()

    def chunk_of(self, fsdp):
        away = jnp.bitwise_xor(lax.axis_index("fsdp"), fsdp)
        return lax.rem(away, 2) * (self.chunks.shape[0] // 2) + away // 2

    def features(self, lines, width):
        chunk = width // self.chunks.shape[0]
        row, col = (lax.broadcasted_iota(jnp.int32, (2 * PAIR, width), axis) for axis in range(2))
        total = 0.0
        for place in range(0, self.chunks.shape[0], 2):
            lane = lax.rem(row, PAIR)
            spread = jnp.logical_and(lane < chunk, col == (place + row // PAIR) * chunk + lane)
            both = side(self.chunks[place, :lines, :], self.chunks[place + 1, :lines, :])
            total += nn(both, spread.astype(F32).astype(BF16))
        return total

    def owner(self, place):
        return lax.rem(self.peers.tp + self.pieces - place, self.pieces)

    def heads(self, place, start, chunk):
        owner = self.owner(place)
        rows = pl.ds(start, 16)
        both = side(self.chunks[self.chunk_of(2 * owner), rows, :], self.chunks[self.chunk_of(2 * owner + 1), rows, :])
        row, col = (lax.broadcasted_iota(jnp.int32, (2 * PAIR, 3 * PAIR), axis) for axis in range(2))
        lane = lax.rem(row, PAIR)
        feature = row // PAIR * chunk + lane
        last = jnp.logical_and(feature >= PAIR, col == feature + 3 * HD)
        spread = jnp.logical_and(lane < chunk, jnp.logical_or(col == feature, last))
        return nn(both, spread.astype(F32).astype(BF16))

    def hidden(self, start, layers, parts, fine):
        rows = pl.ds(start, 16)
        block = jnp.concatenate(
            [self.chunks[self.chunk_of(2 * self.owner(i // 2) + i % 2), rows, :] for i in range(2 * self.pieces)], axis=0
        )
        wide = self.pieces * parts * fine
        row, col = (lax.broadcasted_iota(jnp.int32, (PAIR, wide), axis) for axis in range(2))
        line_of = lax.broadcasted_iota(jnp.int32, (block.shape[0], 1), 0)
        total = 0.0
        for part in range(parts):
            target = row // fine * (parts * fine) + part * fine + lax.rem(row, fine)
            spread = jnp.logical_and(row < self.pieces * fine, col == target)
            here = nn(block, spread.astype(F32).astype(BF16))
            total += jnp.where(lax.rem(line_of, parts) == part, here, 0.0)
        row, col = (lax.broadcasted_iota(jnp.int32, (2 * self.pieces * layers, block.shape[0]), axis) for axis in range(2))
        group = jnp.logical_and(row // layers == col // 16, lax.rem(row, layers) == lax.rem(col, 16) // parts)
        return nn(group.astype(F32).astype(BF16), total.astype(BF16))


def forward_kernel(
    token_ref, hot_ref, share_ref, seg_k_ref, seg_q_ref, attn_shard_ref, mlp_shard_ref,
    q_ref, kv_ref, q_hat_ref, k_hat_ref, q_scale_ref, k_scale_ref, p_ref, o_ref, act_ref, slope_ref, mid_ref, m_ref, x2_ref,
    x0_ref, feats_ref, heads_ref, a_win_out, attn_near_out, attn_far_out, mlp_near_out, mlp_far_out,
    mask_ref, acc_ref, now_ref, a_win_ref, kept, attn_near, attn_far, mlp_near, mlp_far, send, recv, local, stored, halo_send, halo_recv,
    up_shift_ref, landed, chunks, share_send, share_recv,
):
    layers, pieces, (rows, width) = attn_near.shape[0], attn_near.shape[1], token_ref.shape
    chunk = width // chunks.shape[0]
    fine, parts, tables = chunk // pieces, act_ref.shape[1] * pieces // width, hot_ref.shape[1]
    step = pl.program_id(0)
    peers = Neighbours()
    halo = lambda layer: Halo(a_win_ref.at[layer], rows, halo_send.at[layer], halo_recv.at[layer])
    keep_window = lambda layer: pltpu.make_async_copy(a_win_ref.at[layer], a_win_out.at[layer], kept.at[layer])

    def relay(layer):
        halo(layer).relay()

    def window(layer):
        halo(layer).end()
        keep_window(layer).start()

    gathers = []
    for layer in range(layers):
        for which, (shard, near, far, near_out, far_out) in enumerate((
            (attn_shard_ref, attn_near, attn_far, attn_near_out, attn_far_out),
            (mlp_shard_ref, mlp_near, mlp_far, mlp_near_out, mlp_far_out),
        )):
            index = 2 * layer + which
            gathers.append(
                Gather(
                    peers, shard.at[layer], near.at[layer], far.at[layer], send.at[index], recv.at[index], local.at[index],
                    near_out.at[layer], far_out.at[layer], stored.at[index],
                )
            )

    share = Share(peers, share_ref, landed, chunks, share_send, share_recv)

    def open_up(_):
        share.end()
        lines = tables + 16
        found = share.features(lines, width)
        for layer in range(layers):
            feats_ref[layer] = found[tables + layer * FEATS : tables + (layer + 1) * FEATS]
        x0 = token_ref[...] + nn(hot_ref[...], found[:tables].astype(BF16))
        x0_ref[...] = x0
        now_ref[...] = x0
        a_win_ref[0, REACH : REACH + rows, :] = norm_rows(x0, feats_ref.at[0])
        halo(0).begin()
        for piece in range(pieces):
            found = share.heads(piece, lines, chunk)
            for layer in range(layers):
                heads_ref[piece, layer] = found[layer * HEADS : (layer + 1) * HEADS]
        found = share.hidden(lines + 16, layers, parts, fine)
        half = pieces * parts * fine
        for index in range(2 * pieces):
            for layer in range(layers):
                at = index * layers + layer
                up_shift_ref[layer, index // 2, :, index % 2 * half : (index % 2 + 1) * half] = found[at : at + 1]

    plan = Plan(1.0)
    for index, gather in enumerate(gathers):
        gather.jobs(plan, index)
    share_size = share_ref.shape[0] * PAIR * 2
    plan.spend(2.5)
    plan.carry([("z", pieces * share_size)], ("share", 0))
    plan.wait(("share", 0), (share.meet, fine), 0, 0)
    plan.carry([("x", share_size)], ("share", 1))
    plan.wait(("share", 1), (share.spread, 1), 0, 0)
    plan.carry([("y", 2 * share_size)], ("share", 2))
    plan.wait(("share", 2), (share.spread, 2), 0, 0)
    plan.carry([("core", 4 * share_size)], ("share", 3))
    plan.wait(("share", 3), (open_up, 0), 0, 0)
    for layer in range(layers):
        plan.carry([("z", width * 2 * rows)], ("near", layer))
        first = 1 + 2 * layer * pieces
        if layer == 0:
            plan.spend(5.0)
        at = (first, 0) if layer else (0, 0)
        plan.wait(("near", layer), (relay, layer), *at)
        plan.carry([("z", width * 2 * (REACH - rows))], ("halo", layer))
        plan.wait(("halo", layer), (window, layer), *at)
        for index in range(pieces):
            piece = turn(index, pieces)
            plan.wait(("core", 2 * layer, piece), (gathers[2 * layer].need, piece), first + index, 0)
            for slot, time in enumerate((2.0, 1.4, 1.4)):
                plan.spend(time)
                plan.slot(first + index, slot + 1)
            plan.spend(1.4)
        first += pieces
        for index in range(pieces):
            piece = turn(index, pieces)
            plan.wait(("core", 2 * layer + 1, piece), (gathers[2 * layer + 1].need, piece), first + index, 0)
            plan.spend(1.0)
            plan.slot(first + index, 1)
            plan.spend(1.5)
    table = plan.table

    def run(at, slot):
        if (at, slot) in table:

            @pl.when(step == at)
            def _():
                for work, piece in table[at, slot]:
                    work(piece)

    @pl.when(step == 0)
    def _():
        peers.greet()
        mask_ref[...] = jnp.where(seg_k_ref[...] == seg_q_ref[...], 0.0, FILL)
        share.begin()
        for gather in gathers:
            gather.own().start()
        for gather in gathers:
            gather.own().wait()

    run(0, 0)

    count = jnp.maximum(step - 1, 0)
    layer = count // (2 * pieces)
    inner = lax.rem(count, 2 * pieces)
    index = lax.rem(inner, pieces)
    piece = turn(index, pieces)
    steps_of = lambda which: [
        1 + (2 * layer + which) * pieces + index for layer in range(layers) for index in range(pieces)
    ]

    @pl.when(jnp.logical_and(step > 0, inner < pieces))
    def _():
        def hook(slot):
            for at in steps_of(0):
                run(at, slot)

        hook(0)
        attend_work(
            a_win_ref.at[layer], attn_near.at[layer, piece], attn_far.at[layer, piece], heads_ref.at[piece, layer],
            feats_ref.at[layer], now_ref,
            q_ref, kv_ref, q_hat_ref, k_hat_ref, q_scale_ref, k_scale_ref, p_ref, o_ref, mid_ref.at[layer], m_ref.at[layer],
            mask_ref, acc_ref, index == 0, index == pieces - 1, hook,
        )

    @pl.when(inner >= pieces)
    def _():
        def hook(slot):
            for at in steps_of(1):
                run(at, slot)

        hook(0)
        mlp_work(
            m_ref.at[layer], mid_ref.at[layer], mlp_near.at[layer, piece], mlp_far.at[layer, piece],
            up_shift_ref[layer, piece], feats_ref.at[layer], act_ref, slope_ref, now_ref, acc_ref, index == 0,
            index == pieces - 1, hook,
        )

        @pl.when(index == pieces - 1)
        def _():
            x2_ref[layer] = now_ref[...]

            @pl.when(layer + 1 < layers)
            def _():
                a_win_ref[layer + 1, REACH : REACH + rows, :] = norm_rows(now_ref[...], feats_ref.at[layer + 1])
                halo(layer + 1).begin()

    @pl.when(step == pl.num_programs(0) - 1)
    def _():
        for gather in gathers:
            gather.end()
        for layer in range(layers):
            keep_window(layer).wait()


def forward(tokens, hot, share, seg_k, seg_q, attn_shards, mlp_shards):
    rows, width = tokens.shape
    layers, chunk, wide = mlp_shards.shape
    half = width // 2
    window = rows + 2 * REACH
    pieces, chunks, part = lax.axis_size("tp"), lax.axis_size("fsdp"), wide // 2
    hidden = pieces * part

    def attend_at(step):
        count = jnp.maximum(step - 1, 0)
        layer, inner = count // (2 * pieces), lax.rem(count, 2 * pieces)
        return layer, turn(jnp.minimum(inner, pieces - 1), pieces)

    def mlp_at(step):
        count = jnp.maximum(step - 1, 0)
        layer, inner = count // (2 * pieces), lax.rem(count, 2 * pieces)
        done = jnp.where(inner >= pieces, layer * pieces + inner - pieces, jnp.maximum(layer * pieces - 1, 0))
        return done // pieces, turn(lax.rem(done, pieces), pieces)

    def attend_block(height, wide):
        return pl.BlockSpec((None, height, wide), lambda step: (attend_at(step)[0], 0, attend_at(step)[1]))

    mlp_block = pl.BlockSpec((None, rows, part), lambda step: (mlp_at(step)[0], 0, mlp_at(step)[1]))
    heads_at = lambda step: attend_at(step)[0] * pieces + attend_at(step)[1]
    once = lambda shape: pl.BlockSpec(shape, lambda step: (0,) * len(shape), pipeline_mode=pl.Buffered(1))
    outs = attend_shapes(rows, window) + [(rows, 2 * PAIR)]
    specs = [attend_block(*shape) for shape in outs]
    shapes = [shaped((layers, height, pieces * wide)) for height, wide in outs]
    specs.insert(6, pl.BlockSpec((3, window, rows), lambda step: (heads_at(step), 0, 0)))
    shapes.insert(6, shaped((3 * layers * pieces, window, rows)))
    held = [((layers, rows, width), F32), ((layers, rows, width), BF16), ((layers, rows, width), F32)]
    weights = [(layers, pieces, half, 6 * PAIR)] * 2 + [(layers, pieces, half, wide)] * 2
    semaphores = pltpu.SemaphoreType.DMA((2 * layers, pieces, Gather.KINDS))
    held += [((rows, width), F32), ((layers, FEATS, width), F32), ((pieces, layers, HEADS, 3 * PAIR), F32)]
    inputs = (tokens, hot, share, seg_k, seg_q, attn_shards, mlp_shards)
    return pl.pallas_call(
        forward_kernel,
        grid=(1 + 2 * layers * pieces,),
        in_specs=[once(item.shape) for item in inputs],
        out_specs=specs + [mlp_block] * 2 + [once(shape) for shape, _ in held] + [ANY] * 5,
        out_shape=shapes + [shaped((layers, rows, hidden))] * 2 + [shaped(*item) for item in held]
        + [shaped(shape) for shape in [(layers, window, width)] + weights],
        scratch_shapes=[
            pltpu.VMEM((window, rows), F32), pltpu.VMEM((rows, width), F32), pltpu.VMEM((rows, width), F32),
            pltpu.VMEM((layers, window, width), BF16), pltpu.SemaphoreType.DMA((layers,)),
            *[pltpu.VMEM(shape, BF16) for shape in weights], semaphores, semaphores, pltpu.SemaphoreType.DMA((2 * layers,)),
            pltpu.SemaphoreType.DMA((2 * layers, pieces, 2)), pltpu.SemaphoreType.DMA((layers, 4)),
            pltpu.SemaphoreType.DMA((layers, 4)), pltpu.VMEM((layers, pieces, 1, part), F32),
            pltpu.VMEM((pieces, *share.shape), BF16), pltpu.VMEM((chunks, *share.shape), BF16),
            pltpu.SemaphoreType.DMA((pieces + 2,)), pltpu.SemaphoreType.DMA((pieces + 2,)),
        ],
        compiler_params=params(20, VMEM),
        name="forward",
    )(*inputs)


def mlp_back_kernel(*refs):
    step = pl.program_id(0)
    mlp_back_work(*refs, step == 0, step == pl.num_programs(0) - 1, quiet)


def mlp_back_work(
    g_ref, down_near_ref, down_far_ref, slope_ref, up_near_ref, up_far_ref, mid_ref, feats_ref,
    gz_ref, gh_ref, up_shift_grad_ref, g1_ref, gr_ref, small_ref, acc_ref, opening, closing, hook,
):
    half = up_near_ref.shape[0]

    @pl.when(opening)
    def _():
        gz_ref[...] = g_ref[...].astype(BF16)
        acc_ref[...] = jnp.zeros_like(acc_ref)

    near, distant = halves(gz_ref[...])
    gh = ((nn(near, down_near_ref[...]) + nn(distant, down_far_ref[...])) * slope_ref[...].astype(F32)).astype(BF16)
    gh_ref[...] = gh
    hook(1)
    up_shift_grad_ref[...] = jnp.sum(gh.astype(F32), axis=0, keepdims=True)
    acc_ref[:, :half] += nt(gh, up_near_ref[...])
    acc_ref[:, half:] += nt(gh, up_far_ref[...])

    @pl.when(closing)
    def _():
        gm = acc_ref[...]
        hat, scale = row_norm(mid_ref[...])
        g1 = g_ref[...] + row_norm_back(gm * line(feats_ref, LN_GAIN[1]), hat, scale)
        gr = g1.astype(BF16)
        g1_ref[...] = g1
        gr_ref[...] = gr
        small_ref[...] = jnp.zeros_like(small_ref)
        small_ref[0:1, :] = jnp.sum(gz_ref[...].astype(F32), axis=0, keepdims=True)
        small_ref[1:2, :] = jnp.sum(gr.astype(F32), axis=0, keepdims=True)
        small_ref[2:3, :] = jnp.sum(gm * hat, axis=0, keepdims=True)
        small_ref[3:4, :] = jnp.sum(gm, axis=0, keepdims=True)


def mlp_back(grad, near, far, slope, mid, feats, layer, index):
    rows, width = grad.shape
    half = width // 2
    hidden = slope.shape[2]
    pieces = near.shape[1]
    wide = hidden // pieces
    full = whole((rows, width))
    return pl.pallas_call(
        mlp_back_kernel,
        grid=(pieces,),
        in_specs=[
            full, piece_of(index, half, wide, 1), piece_of(index, half, wide, 1), slab(index, rows, wide),
            piece_of(index, half, wide), piece_of(index, half, wide), sheet(index, rows, width), sheet(layer, FEATS, width),
        ],
        out_specs=[full, column(rows, wide), column(1, wide), full, full, whole((8, width))],
        out_shape=[
            shaped((rows, width)), shaped((rows, hidden)), shaped((1, hidden), F32), shaped((rows, width), F32),
            shaped((rows, width)), shaped((8, width), F32),
        ],
        scratch_shapes=[pltpu.VMEM((rows, width), F32)],
        cost_estimate=pl.CostEstimate(
            flops=4 * rows * width * hidden, bytes_accessed=4 * width * hidden, transcendentals=0
        ),
        name="mlp_back",
    )(grad, near, far, slope, near, far, mid, feats)


def attend_back_kernel(*refs):
    *ins, gq_ref, gkv_ref, mine_ref, left_ref, right_ref, small_ref, acc_ref = refs
    rows = gq_ref.shape[0]
    step = pl.program_id(0)

    @pl.when(step == 0)
    def _():
        acc_ref[...] = jnp.zeros_like(acc_ref)

    attend_back_work(*ins, gq_ref, gkv_ref, small_ref, acc_ref, quiet)

    @pl.when(step == pl.num_programs(0) - 1)
    def _():
        left_ref[...] = acc_ref[:REACH, :].astype(BF16)
        mine_ref[...] = acc_ref[REACH : REACH + rows, :]
        right_ref[...] = acc_ref[REACH + rows :, :].astype(BF16)


def attend_back_work(
    gr_ref, q_ref, kv_ref, q_hat_ref, k_hat_ref, q_scale_ref, k_scale_ref, p_ref, near_ref, far_ref, heads_ref,
    gq_ref, gkv_ref, small_ref, acc_ref, hook,
):
    rows = gr_ref.shape[0]
    half = near_ref.shape[0]
    near, distant = halves(gr_ref[...])
    go = (nn(near, near_ref[:, 4 * PAIR :]) + nn(distant, far_ref[:, 4 * PAIR :])).astype(BF16)
    qn, kv = q_ref[...], kv_ref[...]
    first, values, second = kv[:, :PAIR], kv[:, PAIR : 2 * PAIR], kv[:, 2 * PAIR :]
    first_t, second_t = first.T, second.T
    grad_q, grad_k, grad_v = [], [], []
    for head in range(3):
        if head:
            hook(head)
        go_head = only(go[:, PAIR:], head) if head < 2 else only(go[:, :PAIR], 1)
        query = only(qn[:, PAIR * (head // 2) : PAIR * (head // 2 + 1)] * HD ** (-0.5), head % 2).astype(BF16)
        stored = p_ref[head]
        probs = stored.astype(F32)
        grad_probs = nt((values, values, second)[head], go_head)
        delta = jnp.sum(probs * grad_probs, axis=0, keepdims=True)
        grad_scores = (probs * (grad_probs - delta)).astype(BF16)
        grad_v.append(nn(stored, go_head))
        grad_k.append(nn(grad_scores, query))
        grad_q.append(nn((first_t[:HD], first_t[HD:], second_t[:HD])[head], grad_scores))
    hook(3)
    zero = jnp.zeros_like(grad_q[2])
    grad_q = (jnp.concatenate(grad_q + [zero], axis=0) * HD ** (-0.5)).T
    grad_k = side(grad_k[0] + grad_k[1], grad_k[2])
    pair_v, last_v = grad_v[0] + grad_v[1], grad_v[2]
    q_hat = q_hat_ref[...].astype(F32)
    k_hat = k_hat_ref[...].astype(F32)
    gain = lambda which: line(heads_ref, HEAD_GAIN[which], 0, 2 * PAIR)
    gq = head_norm_back(grad_q * gain(0), q_hat, q_scale_ref[...].astype(F32)).astype(BF16)
    gk = head_norm_back(grad_k * gain(1), k_hat, k_scale_ref[...].astype(F32)).astype(BF16)
    gkv = side(gk[:, :PAIR], pair_v.astype(BF16), gk[:, PAIR:] + last_v.astype(BF16))
    gq_ref[...] = gq
    gkv_ref[...] = gkv
    total = lambda value: jnp.sum(value.astype(F32), axis=0, keepdims=True)
    small_ref[...] = jnp.zeros_like(small_ref)
    small_ref[0:1, : 2 * PAIR] = total(grad_q * q_hat)
    small_ref[1:2, : 2 * PAIR] = total(grad_k * k_hat)
    small_ref[2:3, : 2 * PAIR] = total(grad_q)
    small_ref[3:4, : 2 * PAIR] = total(gq)
    small_ref[4:5, : 2 * PAIR] = total(gk)
    small_ref[5:6, :PAIR] = total(pair_v.astype(BF16))
    small_ref[5:6, 2 * PAIR :] = total(last_v.astype(BF16))
    acc_ref[:, :half] += nt(gkv, near_ref[:, PAIR : 4 * PAIR])
    acc_ref[:, half:] += nt(gkv, far_ref[:, PAIR : 4 * PAIR])
    own = slice(REACH, REACH + rows)
    for ref, cols in ((near_ref, slice(0, half)), (far_ref, slice(half, 2 * half))):
        acc_ref[own, cols] += nt(gq[:, :PAIR], ref[:, :PAIR]) + nt(gq[:, PAIR:], ref[:, 4 * PAIR : 5 * PAIR])


def attend_back_specs(rows, width, pieces, layer, index):
    half = width // 2
    window = rows + 2 * REACH
    full = whole((rows, width))
    in_specs = [
        full, *[slab(index, *shape) for shape in attend_shapes(rows, window)],
        pl.BlockSpec((3, window, rows), lambda step: (index * pieces + step, 0, 0)), piece_of(index, half, 6 * PAIR),
        piece_of(index, half, 6 * PAIR), heads_of(layer),
    ]
    out_specs = [
        column(rows, 2 * PAIR), column(window, 3 * PAIR), full, whole((REACH, width)), whole((REACH, width)), column(8, 3 * PAIR),
    ]
    out_shape = [
        shaped((rows, pieces * 2 * PAIR)), shaped((window, pieces * 3 * PAIR)), shaped((rows, width), F32),
        shaped((REACH, width)), shaped((REACH, width)), shaped((8, pieces * 3 * PAIR), F32),
    ]
    cost = pl.CostEstimate(
        flops=2 * window * width * width * 2 + 20 * window * rows * width * 2,
        bytes_accessed=20 * window * width,
        transcendentals=0,
    )
    return in_specs, out_specs, out_shape, [pltpu.VMEM((window, width), F32)], cost


def attend_back(gr, stored, near, far, heads, layer, index):
    rows, width = gr.shape
    pieces = near.shape[1]
    in_specs, out_specs, out_shape, scratch, cost = attend_back_specs(rows, width, pieces, layer, index)
    return pl.pallas_call(
        attend_back_kernel,
        grid=(pieces,),
        in_specs=in_specs,
        out_specs=out_specs,
        out_shape=out_shape,
        scratch_shapes=scratch,
        cost_estimate=cost,
        name="attend_back",
    )(gr, *stored, near, far, heads)


def attn_weight_kernel(a_ref, gq_ref, gkv_ref, gr_ref, o_ref, keep_ref, send_ref, a_t_ref, gr_t_ref):
    rows = gq_ref.shape[0]
    half = keep_ref.shape[0]

    @pl.when(pl.program_id(0) == 0)
    def _():
        a_t_ref[...] = a_ref[...].T
        gr_t_ref[...] = gr_ref[...].T

    for part, ref in ((slice(0, half), keep_ref), (slice(half, 2 * half), send_ref)):
        from_q = nn(a_t_ref[part, REACH : REACH + rows], gq_ref[...])
        from_o = nn(gr_t_ref[part, :], o_ref[...])
        ref[:, :PAIR] = from_q[:, :PAIR].astype(BF16)
        ref[:, PAIR : 4 * PAIR] = nn(a_t_ref[part, :], gkv_ref[...]).astype(BF16)
        ref[:, 4 * PAIR : 5 * PAIR] = (from_q[:, PAIR:] + from_o[:, :PAIR]).astype(BF16)
        ref[:, 5 * PAIR :] = from_o[:, PAIR:].astype(BF16)


def attn_weight_grads(a_win, gq, gkv, gr, o):
    _, window, width = a_win.shape
    rows = gr.shape[0]
    half = width // 2
    pieces = gq.shape[1] // (2 * PAIR)
    out = column(half, 6 * PAIR)
    return pl.pallas_call(
        attn_weight_kernel,
        grid=(pieces,),
        in_specs=[
            sheet(0, window, width), column(rows, 2 * PAIR), column(window, 3 * PAIR), whole((rows, width)),
            slab(0, rows, 2 * PAIR),
        ],
        out_specs=[out, out],
        out_shape=[shaped((half, pieces * 6 * PAIR))] * 2,
        scratch_shapes=[pltpu.VMEM((width, window), BF16), pltpu.VMEM((width, rows), BF16)],
        cost_estimate=pl.CostEstimate(
            flops=2 * width * width * (2 * window + 2 * rows), bytes_accessed=8 * width * width, transcendentals=0
        ),
        name="attn_weight_grads",
    )(a_win, gq, gkv, gr, o)


def mlp_weight_kernel(m_ref, gh_ref, gz_ref, act_ref, keep_ref, send_ref, m_t_ref, gz_t_ref):
    half = keep_ref.shape[0]
    wide = gh_ref.shape[1]

    @pl.when(pl.program_id(0) == 0)
    def _():
        m_t_ref[...] = m_ref[...].T
        gz_t_ref[...] = gz_ref[...].T

    for part, ref in ((slice(0, half), keep_ref), (slice(half, 2 * half), send_ref)):
        ref[:, :wide] = nn(m_t_ref[part, :], gh_ref[...]).astype(BF16)
        ref[:, wide:] = nn(gz_t_ref[part, :], act_ref[...]).astype(BF16)


def mlp_weight_grads(m, gh, gz, act):
    _, rows, width = m.shape
    half = width // 2
    hidden = gh.shape[1]
    pieces = lax.axis_size("tp")
    wide = hidden // pieces
    out = column(half, 2 * wide)
    return pl.pallas_call(
        mlp_weight_kernel,
        grid=(pieces,),
        in_specs=[sheet(0, rows, width), column(rows, wide), whole((rows, width)), slab(0, rows, wide)],
        out_specs=[out, out],
        out_shape=[shaped((half, 2 * hidden))] * 2,
        scratch_shapes=[pltpu.VMEM((width, rows), BF16), pltpu.VMEM((width, rows), BF16)],
        cost_estimate=pl.CostEstimate(
            flops=4 * width * hidden * rows, bytes_accessed=4 * width * hidden, transcendentals=0
        ),
        name="mlp_weight_grads",
    )(m, gh, gz, act)


class Scatter:
    KINDS = 7

    def __init__(self, peers, out, away, keep, core, first, second, given, send, recv):
        self.peers, self.out, self.away, self.keep, self.core_in = peers, out, away, keep, core
        self.first_in, self.second_in, self.given, self.send, self.recv = first, second, given, send, recv
        self.chunk, self.wide = out.shape
        self.half = self.wide // 2
        self.pieces = keep.shape[0]

    def copy(self, piece, kind, source, target, device):
        return pltpu.make_async_remote_copy(
            src_ref=source, dst_ref=target, send_sem=self.send.at[piece, kind], recv_sem=self.recv.at[piece, kind],
            device_id=device, device_id_type=MESH,
        )

    def copies(self, piece, stage):
        c, left, right = self.chunk, pl.ds(0, self.half), pl.ds(self.half, self.half)
        rows = lambda start, count=1: pl.ds(start * c, count * c)
        if stage == "core":
            return [self.copy(piece, 0, self.away.at[self.slot(piece)], self.core_in.at[piece], self.peers.core)]
        if stage == "first":
            source, target = self.keep.at[piece], self.first_in.at[piece]
            return [
                self.copy(piece, 1, source.at[rows(2, 2), left], target.at[:, left], self.peers.y),
                self.copy(piece, 2, source.at[rows(1), right], target.at[rows(0), right], self.peers.x),
                self.copy(piece, 3, source.at[rows(3), right], target.at[rows(1), right], self.peers.x),
            ]
        if stage == "second":
            source, target = self.keep.at[piece], self.second_in.at[piece]
            return [
                self.copy(piece, 4, source.at[rows(1), left], target.at[:, left], self.peers.x),
                self.copy(piece, 5, source.at[rows(2), right], target.at[:, right], self.peers.y),
            ]
        target = self.given.at[(piece - 1) % self.pieces]
        return [self.copy(piece, 6, self.keep.at[piece, rows(0), :], target, self.peers.along(1))]

    def start(self, piece, stage):
        for copy in self.copies(piece, stage):
            copy.start()

    def arrived(self, piece, stage):
        for copy in self.copies(piece, stage):
            copy.wait_recv()

    def add(self, piece, start, count, cols, source):
        step = 32

        @pl.loop(0, count * self.chunk // step)
        def _(index):
            row = pl.multiple_of(index * step, step)
            into = (piece, pl.ds(start * self.chunk + row, step), cols)
            self.keep[into] = self.keep[into] + source[pl.ds(row, step), cols]

    def slot(self, piece):
        return (piece + self.pieces - 1) % self.pieces % 2

    def room(self, index, piece):
        @pl.when(index > 1)
        def _():
            for copy in self.copies(lax.rem(piece + self.pieces - 2, self.pieces), "core"):
                copy.wait_send()

    def first(self, piece):
        self.arrived(piece, "core")
        self.add(piece, 0, 4, pl.ds(0, self.wide), self.core_in.at[piece])
        self.start(piece, "first")

    def second(self, piece):
        left, right = pl.ds(0, self.half), pl.ds(self.half, self.half)
        self.arrived(piece, "first")
        source = self.first_in.at[piece]
        self.add(piece, 0, 2, left, source)
        self.add(piece, 0, 1, right, source)
        self.add(piece, 2, 1, right, source.at[pl.ds(self.chunk, self.chunk)])
        self.start(piece, "second")

    def last(self, piece):
        self.arrived(piece, "second")
        kept = pl.ds(0, self.chunk)
        total = self.keep[piece, kept, :].astype(F32) + self.second_in[piece].astype(F32)
        if piece != 1:
            self.arrived((piece - 1) % self.pieces, "give")
            total += self.given[(piece - 2) % self.pieces].astype(F32)
        if piece:
            self.keep[piece, kept, :] = total.astype(BF16)
            self.start(piece, "give")
        else:
            self.out[...] = total

    def done(self):
        for piece in range(self.pieces):
            for stage in ("core", "first", "second", "give"):
                if (stage != "give" or piece) and (stage != "core" or piece in (0, self.pieces - 1)):
                    for copy in self.copies(piece, stage):
                        copy.wait_send()

    def made(self, plan, index, piece):
        size = self.chunk * self.wide * 2
        both = lambda count: [("x", count * size), ("y", count * size)]
        key = (index, piece)
        rank = index * self.pieces + (piece - 1) % self.pieces
        plan.carry([("core", 4 * size)], ("core", *key))
        plan.add(rank, (self.first, piece), [("core", *key)], both(1), ("first", *key), index)
        plan.add(rank, (self.second, piece), [("first", *key)], both(0.5), ("second", *key), index)
        needs = [("second", *key)] + ([("give", index, (piece - 1) % self.pieces)] if piece != 1 else [])
        plan.add(rank, (self.last, piece), needs, [("z", size)] if piece else [], ("give", *key), index)


class Return:
    def __init__(self, edges, landed, rows, send, recv):
        self.edges, self.landed, self.send, self.recv = edges, landed, send, recv
        self.place, self.size = lax.axis_index("tp"), lax.axis_size("tp")
        self.rows, self.spill = rows, REACH - rows
        spill = self.spill
        self.moves = [
            (1, 2, REACH + rows, spill, 2 * rows),
            (-1, 2, 0, spill, 2 * rows + spill),
            (1, 1, REACH, rows, 0),
            (-1, 1, spill, rows, rows),
        ]

    def inside(self, distance):
        other = self.place + distance
        return jnp.logical_and(other >= 0, other < self.size)

    def sends(self, index):
        direction, far, *_ = self.moves[index]
        return self.inside(direction * far)

    def takes(self, index):
        direction, far, *_ = self.moves[index]
        return jnp.logical_and(self.inside(-direction), self.inside(direction * (far - 1)))

    def copy(self, index):
        direction, _, start, count, target = self.moves[index]
        return pltpu.make_async_remote_copy(
            src_ref=self.edges.at[pl.ds(start, count), pl.ds(0, self.landed.shape[1])],
            dst_ref=self.landed.at[pl.ds(target, count), :], send_sem=self.send.at[index], recv_sem=self.recv.at[index],
            device_id={"tp": self.place + direction}, device_id_type=MESH,
        )

    def start(self, index):
        @pl.when(self.sends(index))
        def _():
            self.copy(index).start()

    def begin(self):
        for index in range(2):
            self.start(index)

    def relay(self):
        wide = self.landed.shape[1]
        for index, into in ((0, REACH), (1, REACH - self.spill)):
            target = self.moves[index][4]

            @pl.when(self.takes(index))
            def _():
                self.copy(index).wait_recv()
                rows = slice(into, into + self.spill)
                self.edges[rows, :wide] = self.edges[rows, :wide] + self.landed[target : target + self.spill, :]

            self.start(index + 2)

    def end(self, total_ref):
        for index in range(4):

            @pl.when(self.sends(index))
            def _():
                self.copy(index).wait_send()

        for index in (2, 3):
            target = self.moves[index][4]

            @pl.when(self.takes(index))
            def _():
                self.copy(index).wait_recv()
                total_ref[...] += self.landed[target : target + self.rows, :].astype(F32)


def split_dot(left, right):
    if left.dtype == F32:
        high = left.astype(BF16)
        return nn(high, right) + nn((left - high.astype(F32)).astype(BF16), right)
    high = right.astype(BF16)
    return nn(left, high) + nn(left, (right - high.astype(F32)).astype(BF16))


def picked(mask):
    return mask.astype(F32).astype(BF16)


class Tally:
    def __init__(self, peers, chunks, inbox, send, recv, pieces):
        self.peers, self.chunks, self.inbox, self.send, self.recv, self.pieces = peers, chunks, inbox, send, recv, pieces
        self.share = Share(peers, chunks.at[0], inbox.at[pl.ds(0, pieces)], chunks, send, recv)

    def across(self, stage):
        count = 4 >> stage
        device = (self.peers.core, self.peers.y, self.peers.x)[stage]
        source, target = self.chunks.at[pl.ds(count, count)], self.inbox.at[pl.ds(8 - 2 * count, count)]
        return self.share.copy(stage, source, target, device)

    def along(self):
        place = self.inbox.at[7 + self.peers.tp]
        return [self.share.copy(2 + d, self.chunks.at[0], place, self.peers.along(d)) for d in range(1, self.pieces)]

    def build(self, tables, lines_ref, work_ref, norm_sums, mlp_sums, head_sums, up_grad):
        layers, width = norm_sums.shape[0], lines_ref.shape[1]
        count = self.chunks.shape[0]
        chunk, first = width // count, tables.shape[0]
        fine, parts = chunk // self.pieces, up_grad.shape[3] * self.pieces // width
        lines_ref[:first, :] = tables
        lines_ref[first : first + 16, :] = jnp.zeros((16, width), F32)
        for layer in range(layers):
            sums = [(norm_sums, 0), (mlp_sums, 2), (norm_sums, 1), (mlp_sums, 3), (mlp_sums, 1), (mlp_sums, 0)]
            for index, (ref, row) in enumerate(sums):
                at = first + layer * FEATS + index
                lines_ref[at : at + 1, :] = ref[layer, row : row + 1, :]
        lines = lines_ref[: first + 16, :]
        row, col = (lax.broadcasted_iota(jnp.int32, (width, PAIR), axis) for axis in range(2))
        for place in range(count):
            spread = picked(jnp.logical_and(col < chunk, row == place * chunk + col))
            self.chunks[place, : first + 16, :] = split_dot(lines, spread).astype(BF16)
        row, col = (lax.broadcasted_iota(jnp.int32, (3 * PAIR, 2 * PAIR), axis) for axis in range(2))
        lane = lax.rem(col, PAIR)
        feature = col // PAIR * chunk + lane
        last = jnp.logical_and(feature >= PAIR, row == feature + 3 * HD)
        spread = picked(jnp.logical_and(lane < chunk, jnp.logical_or(row == feature, last)))
        work_ref[:32, :] = jnp.zeros((32, width), F32)
        for piece in range(self.pieces):
            for layer in range(layers):
                for index, line_at in enumerate((3, 4, 5, 0, 1, 2)):
                    at = layer * HEADS + index
                    work_ref[at : at + 1, : 3 * PAIR] = head_sums[layer, piece, line_at : line_at + 1, :]
            both = split_dot(work_ref[:16, : 3 * PAIR], spread).astype(BF16)
            owner = self.share.owner(piece)
            for index in range(2):
                target = self.chunks.at[self.share.chunk_of(2 * owner + index)]
                target[first + 16 : first + 32, :] = both[:, index * PAIR : (index + 1) * PAIR]
        wide = self.pieces * parts * fine
        for index in range(2 * self.pieces):
            for layer in range(layers):
                at = 16 + index * layers + layer
                half = slice(index % 2 * wide, (index % 2 + 1) * wide)
                work_ref[at : at + 1, :wide] = up_grad[layer, index // 2, :, half]
        biases = work_ref[16 : 16 + 2 * self.pieces * layers, :wide]
        row, col = (lax.broadcasted_iota(jnp.int32, (wide, PAIR), axis) for axis in range(2))
        shape = (2 * self.pieces * 16, 2 * self.pieces * layers)
        line_of, from_of = (lax.broadcasted_iota(jnp.int32, shape, axis) for axis in range(2))
        total = 0.0
        for part in range(parts):
            source = col // fine * (parts * fine) + part * fine + lax.rem(col, fine)
            here = split_dot(biases, picked(jnp.logical_and(col < chunk, row == source)))
            group = jnp.logical_and(line_of // 16 == from_of // layers, lax.rem(line_of, 16) == lax.rem(from_of, layers) * parts + part)
            total += split_dot(picked(group), here)
        for index in range(2 * self.pieces):
            target = self.chunks.at[self.share.chunk_of(2 * self.share.owner(index // 2) + index % 2)]
            target[first + 32 : first + 48, :] = total[index * 16 : (index + 1) * 16].astype(BF16)
        self.across(0).start()

    def fold(self, stage):
        count = 4 >> stage
        self.across(stage).wait_recv()
        mine, found = self.chunks[:count], self.inbox[8 - 2 * count : 8 - count]
        self.chunks[:count] = (mine.astype(F32) + found.astype(F32)).astype(BF16)
        if stage < 2:
            self.across(stage + 1).start()
        else:
            for copy in self.along():
                copy.start()

    def total(self, out_ref):
        total = self.chunks[0].astype(F32)
        for copy in self.along():
            copy.wait_recv()
        for distance in range(1, self.pieces):
            total += self.inbox[7 + lax.rem(self.peers.tp + distance, self.pieces)].astype(F32)
        out_ref[...] = total
        for copy in self.along() + [self.across(stage) for stage in range(3)]:
            copy.wait_send()


def backward_kernel(
    cot_ref, hot_ref, feats_ref, m_ref, mid_ref, a_win_ref, x0_ref, x2_ref,
    mlp_near_ref, mlp_far_ref, slope_ref, act_ref,
    q_ref, kv_ref, q_hat_ref, k_hat_ref, q_scale_ref, k_scale_ref, p_ref, attn_near_ref, attn_far_ref, heads_ref, o_ref,
    g_ref, up_grad_ref, head_sums_ref, mlp_sums_ref, norm_sums_ref, tally_ref, mlp_out, attn_out,
    gz_ref, gh_ref, g1_ref, gr_ref, acc_ref, window_ref, gq_ref, gkv_ref, turned_ref, a_t_ref,
    landed_ref, halo_send, halo_recv, free, fetched, chunks, inbox, tally_send, tally_recv, *buffers,
):
    layers, pieces, rows = up_grad_ref.shape[0], up_grad_ref.shape[1], g_ref.shape[0]
    half = g_ref.shape[1] // 2
    wide = slope_ref.shape[1]
    own = slice(REACH, REACH + rows)
    total_ref = window_ref.at[own]
    step = pl.program_id(0)
    peers = Neighbours()
    scatter_of = lambda layer, which: Scatter(
        peers, (mlp_out, attn_out)[which].at[layer], *buffers[8 * which : 8 * which + 6],
        *[item.at[layer] for item in buffers[8 * which + 6 : 8 * which + 8]],
    )
    back = lambda layer: Return(a_t_ref, landed_ref.at[layer], rows, halo_send.at[layer], halo_recv.at[layer])

    def fetch(source, target):
        copy = pltpu.make_async_copy(source, target, fetched)
        copy.start()
        copy.wait()

    def pass_on(layer):
        back(layer).relay()

    def halo_back(layer):
        back(layer).end(total_ref)

    def made_free(item):
        layer, which = item
        scatter_of(layer + 1, which).done()
        for target in peers.all():
            pl.semaphore_signal(free.at[layer, which], inc=1, device_id=target, device_id_type=MESH)
        pl.semaphore_wait(free.at[layer, which], len(peers.all()))

    plan = Plan(3.0)
    plan.spend(2.5)

    def whole_return(layer, *at):
        plan.wait(("far", layer), (pass_on, layer), *at)
        plan.carry([("z", 4 * half * rows)], ("halo", layer))
        plan.wait(("halo", layer), (halo_back, layer), *at)

    order = [(index + 1) % pieces for index in range(pieces)]
    for layer in reversed(range(layers)):
        for which in range(2):
            for index, piece in enumerate(order):
                at = (2 * (layers - 1 - layer) + which) * pieces + index
                if index == 0 and layer + 1 < layers:
                    if which == 0:
                        whole_return(layer + 1, at, 0)
                    plan.finish(2 * (layers - 2 - layer) + which, at, 0)
                    plan.table.setdefault((at, 0), []).append((made_free, (layer, which)))
                plan.slot(at, 0)
                for slot, time in enumerate(((1.5,), (2.2, 1.3, 1.3))[which]):
                    plan.spend(time)
                    plan.slot(at, slot + 1)
                plan.spend((2.6, 3.0)[which])
                scatter_of(layer, which).made(plan, 2 * (layers - 1 - layer) + which, piece)
        plan.carry([("z", 4 * half * (REACH - rows))], ("far", layer))
    ending = 2 * layers * pieces
    whole_return(0, ending, 0)
    plan.spend(8.0)
    tally = Tally(peers, chunks, inbox, tally_send, tally_recv, pieces)
    size = chunks.shape[1] * PAIR * 2
    for stage, (link, count) in enumerate((("core", 4), ("y", 2), ("x", 1), ("z", pieces))):
        plan.carry([(link, count * size)], ("tally", stage))
        work = (tally.fold, stage) if stage < 3 else (tally.total, tally_ref)
        plan.wait(("tally", stage), work, ending, 1)
    plan.finish(None, ending, 1)
    table = plan.table

    def run(at, slot):
        if (at, slot) in table:

            @pl.when(step == at)
            def _():
                for work, item in table[at, slot]:
                    work(item)

    phase = step // pieces
    layer = jnp.maximum(layers - 1 - phase // 2, 0)
    index = lax.rem(step, pieces)
    piece = lax.rem(index + 1, pieces)
    in_mlp, in_attend = lax.rem(phase, 2) == 0, lax.rem(phase, 2) == 1
    is_ending = step == ending

    @pl.when(step == 0)
    def _():
        peers.greet()
        fetch(cot_ref, g_ref)

    run(ending, 0)
    for at in range(2 * pieces, ending, 2 * pieces):
        run(at, 0)

    def through_norm(layer, x):
        fetch(x, acc_ref)
        total = total_ref[...]
        hat, scale = row_norm(acc_ref[...])
        g_ref[...] = g1_ref[...] + row_norm_back(total * line(feats_ref.at[layer], LN_GAIN[0]), hat, scale)
        norm_sums_ref[layer] = jnp.zeros(norm_sums_ref.shape[1:], F32)
        norm_sums_ref[layer, 0:1, :] = jnp.sum(total * hat, axis=0, keepdims=True)
        norm_sums_ref[layer, 1:2, :] = jnp.sum(total, axis=0, keepdims=True)

    for above in range(1, layers):

        @pl.when(step == 2 * (layers - above) * pieces)
        def _():
            through_norm(above, x2_ref.at[above - 1])

    @pl.when(is_ending)
    def _():
        through_norm(0, x0_ref)
        tables = split_dot(hot_ref[...].T, g_ref[...])
        tally.build(tables, total_ref, acc_ref, norm_sums_ref, mlp_sums_ref, head_sums_ref, up_grad_ref)

    @pl.when(jnp.logical_and(in_mlp, step < ending))
    def _():
        def hook(slot):
            for at in range(ending):
                if at // pieces % 2 == 0 and not (slot == 0 and at % (2 * pieces) == 0 and at):
                    run(at, slot)

        hook(0)
        up, down = pl.ds(0, wide), pl.ds(wide, wide)
        mlp_back_work(
            g_ref, mlp_near_ref.at[:, down], mlp_far_ref.at[:, down], slope_ref, mlp_near_ref.at[:, up], mlp_far_ref.at[:, up],
            mid_ref, feats_ref.at[layer], gz_ref, gh_ref, up_grad_ref.at[layer, piece], g1_ref, gr_ref,
            mlp_sums_ref.at[layer], acc_ref, index == 0, index == pieces - 1, hook,
        )

        @pl.when(index == 0)
        def _():
            turned_ref[0] = m_ref[...].T
            turned_ref[1] = gz_ref[...].T

        away, keep = buffers[0], buffers[1]
        scatter = scatter_of(layer, 0)
        scatter.room(index, piece)
        for part, ref in ((slice(0, half), keep.at[piece]), (slice(half, 2 * half), away.at[scatter.slot(piece)])):
            ref[:, :wide] = nn(turned_ref[0, part, :], gh_ref[...]).astype(BF16)
            ref[:, wide:] = nn(turned_ref[1, part, :], act_ref[...]).astype(BF16)
        scatter.start(piece, "core")

    @pl.when(in_attend)
    def _():
        def hook(slot):
            for at in range(ending):
                if at // pieces % 2 == 1:
                    run(at, slot)

        hook(0)

        @pl.when(index == 0)
        def _():
            window_ref[...] = jnp.zeros_like(window_ref)
            a_t_ref[...] = a_win_ref[...].T
            turned_ref[0] = gr_ref[...].T

        attend_back_work(
            gr_ref, q_ref, kv_ref, q_hat_ref, k_hat_ref, q_scale_ref, k_scale_ref, p_ref, attn_near_ref, attn_far_ref,
            heads_ref, gq_ref, gkv_ref, head_sums_ref.at[layer, piece], window_ref, hook,
        )
        away, keep = buffers[8], buffers[9]
        scatter = scatter_of(layer, 1)
        scatter.room(index, piece)
        for part, ref in ((slice(0, half), keep.at[piece]), (slice(half, 2 * half), away.at[scatter.slot(piece)])):
            from_q = nn(a_t_ref[part, own], gq_ref[...])
            from_o = nn(turned_ref[0, part, :], o_ref[...])
            ref[:, :PAIR] = from_q[:, :PAIR].astype(BF16)
            ref[:, PAIR : 4 * PAIR] = nn(a_t_ref[part, :], gkv_ref[...]).astype(BF16)
            ref[:, 4 * PAIR : 5 * PAIR] = (from_q[:, PAIR:] + from_o[:, :PAIR]).astype(BF16)
            ref[:, 5 * PAIR :] = from_o[:, PAIR:].astype(BF16)
        scatter.start(piece, "core")

        @pl.when(index == pieces - 1)
        def _():
            a_t_ref[:REACH, : 2 * half] = window_ref[:REACH, :].astype(BF16)
            a_t_ref[REACH : 2 * REACH, : 2 * half] = window_ref[REACH + rows :, :].astype(BF16)
            back(layer).begin()

    run(ending, 1)

    @pl.when(is_ending)
    def _():
        for which in range(2):
            scatter_of(0, which).done()


def scatter_buffers(layers, pieces, chunk, wide):
    buffer = lambda rows: pltpu.VMEM((pieces, rows * chunk, wide), BF16)
    semaphores = pltpu.SemaphoreType.DMA((layers, pieces, Scatter.KINDS))
    away = pltpu.VMEM((2, 4 * chunk, wide), BF16)
    given = pltpu.VMEM((pieces - 1, chunk, wide), BF16)
    return [away, buffer(4), buffer(4), buffer(2), buffer(1), given, semaphores, semaphores]


def backward(cotangent, hot, lines, feats, heads, start, saved):
    *stored, o, act, slope, mid, m, x2, a_win, attn_near, attn_far, mlp_near, mlp_far = saved
    layers, window, width = a_win.shape
    rows, half, pieces = m.shape[1], width // 2, attn_near.shape[1]
    hidden = act.shape[2]
    wide, chunk = hidden // pieces, half // 4

    def mlp_at(step):
        phase = jnp.minimum(step // pieces, 2 * layers - 1)
        index = jnp.where(lax.rem(phase, 2) == 0, lax.rem(step, pieces), pieces - 1)
        return layers - 1 - phase // 2, lax.rem(index + 1, pieces)

    def attend_at(step):
        phase = jnp.minimum(step // pieces, 2 * layers - 1)
        index = jnp.where(lax.rem(phase, 2) == 1, lax.rem(step, pieces), 0)
        index = jnp.where(step == 2 * layers * pieces, pieces - 1, index)
        return layers - 1 - phase // 2, lax.rem(index + 1, pieces)

    once = lambda shape: pl.BlockSpec(shape, lambda step: (0,) * len(shape), pipeline_mode=pl.Buffered(1))
    weight = lambda at, wide: pl.BlockSpec((None, None, half, wide), lambda step: (*at(step), 0, 0))
    cols = lambda at, height, wide: pl.BlockSpec((None, height, wide), lambda step: (at(step)[0], 0, at(step)[1]))
    by_heads = pl.BlockSpec((3, window, rows), lambda step: (attend_at(step)[0] * pieces + attend_at(step)[1], 0, 0))
    layer_heads = pl.BlockSpec((None, None, HEADS, 3 * PAIR), lambda step: (attend_at(step)[1], attend_at(step)[0], 0, 0))
    layer_sheet = lambda at, height: pl.BlockSpec(
        (None, height, width), lambda step: (at(step)[0], 0, 0), pipeline_mode=pl.Buffered(1)
    )
    outs = [
        (rows, width), (layers, pieces, 1, wide), (layers, pieces, 8, 3 * PAIR), (layers, 8, width), (layers, 8, width),
        (lines, PAIR), (layers, chunk, 2 * wide), (layers, chunk, 6 * PAIR),
    ]
    vmem = lambda shape, kind=BF16: pltpu.VMEM(shape, kind)
    inputs = (cotangent, hot, feats, m, mid, a_win, start, x2, mlp_near, mlp_far, slope, act, *stored, attn_near, attn_far, heads, o)
    return pl.pallas_call(
        backward_kernel,
        grid=(2 * layers * pieces + 1,),
        in_specs=[
            ANY, once(hot.shape), once(feats.shape), layer_sheet(mlp_at, rows), layer_sheet(mlp_at, rows), layer_sheet(attend_at, window), ANY, ANY,
            weight(mlp_at, 2 * wide), weight(mlp_at, 2 * wide), cols(mlp_at, rows, wide),
            cols(mlp_at, rows, wide), *[cols(attend_at, *shape) for shape in attend_shapes(rows, window)], by_heads,
            weight(attend_at, 6 * PAIR), weight(attend_at, 6 * PAIR), layer_heads, cols(attend_at, rows, 2 * PAIR),
        ],
        out_specs=[once(shape) for shape in outs],
        out_shape=[shaped(shape, F32) for shape in outs],
        scratch_shapes=[
            vmem((rows, width)), vmem((rows, wide)), vmem((rows, width), F32), vmem((rows, width)),
            vmem((rows, width), F32), vmem((window, width), F32), vmem((rows, 2 * PAIR)), vmem((window, 3 * PAIR)),
            vmem((2, width, rows)), vmem((width, window)),
            vmem((layers, 2 * REACH, width)), pltpu.SemaphoreType.DMA((layers, 4)), pltpu.SemaphoreType.DMA((layers, 4)),
            pltpu.SemaphoreType.REGULAR((layers, 2)), pltpu.SemaphoreType.DMA, vmem((8, lines, PAIR)),
            vmem((7 + pieces, lines, PAIR)), pltpu.SemaphoreType.DMA((pieces + 2,)), pltpu.SemaphoreType.DMA((pieces + 2,)), *scatter_buffers(layers, pieces, chunk, 2 * wide),
            *scatter_buffers(layers, pieces, chunk, 6 * PAIR),
        ],
        compiler_params=params(40, VMEM),
        name="backward",
    )(*inputs)


def flip(array, bit, axis="fsdp"):
    size = lax.axis_size(axis)
    return lax.ppermute(array, axis, [(i, i ^ (1 << bit)) for i in range(size)])


def ring(array):
    size = lax.axis_size("tp")
    return lax.ppermute(array, "tp", [(i, (i + 1) % size) for i in range(size)])


def hop(array, distance):
    size = lax.axis_size("tp")
    return lax.ppermute(array, "tp", [(i, i + distance) for i in range(size) if 0 <= i + distance < size])


def bits_of(size):
    return size.bit_length() - 1


def row_bits(first_top):
    count = bits_of(lax.axis_size("fsdp"))
    tops = [count - 1, count - 2] if first_top else [count - 2, count - 1]
    return list(range(1, count - 2)), tops


def gather_by_permutes(block, first_top):
    pieces = [block]
    for _ in range(lax.axis_size("tp") - 1):
        pieces.append(ring(pieces[-1]))
    block = jnp.concatenate(pieces, axis=1)
    low, tops = row_bits(first_top)
    have = []
    for bit in low + tops:
        axis = sum(other > bit for other in have)
        block = jnp.stack([block, flip(block, bit)], axis=axis)
        have.append(bit)
    block = block.reshape((-1, len(pieces), pieces[0].shape[1])).transpose(1, 0, 2)[None]
    return block, flip(block, 0)


def add(left, right, kind=BF16):
    return (left.astype(F32) + right.astype(F32)).astype(kind)


def reduce_by_permutes(keep, send, first_top):
    low, tops = row_bits(first_top)
    block = add(keep, flip(send, 0))
    order = tops + low[::-1]
    have = sorted(order, reverse=True)
    block = block.reshape((2,) * len(have) + (-1, block.shape[-1]))
    for bit in order:
        axis = have.index(bit)
        mine = lax.index_in_dim(block, 0, axis, keepdims=False)
        other = lax.index_in_dim(block, 1, axis, keepdims=False)
        block = add(mine, flip(other, bit))
        have.remove(bit)
    pieces = jnp.split(block, lax.axis_size("tp"), axis=1)
    total = pieces[1]
    for piece in pieces[2:]:
        total = add(ring(total), piece)
    return add(ring(total), pieces[0], F32)


def attn_shard(w_qkv, w_out):
    q, k, v = (w_qkv[:, which] for which in range(3))
    o = w_out.T
    return side(q[:, :PAIR], k[:, :PAIR], v[:, :PAIR], k[:, PAIR:], v[:, PAIR:], q[:, PAIR:], o[:, PAIR:], o[:, :PAIR])


def attn_unshard(block):
    tile = lambda start, wide=PAIR: block[:, start : start + wide]
    q = side(tile(0), tile(4 * PAIR, HD))
    k = side(tile(PAIR), tile(3 * PAIR, HD))
    v = side(tile(2 * PAIR), tile(3 * PAIR + HD, HD))
    o = side(tile(5 * PAIR), tile(4 * PAIR + HD, HD))
    return jnp.stack([q, k, v], axis=1), o.T


def body(
    tokens, segment_ids, patch_pos, row_table, col_table, ln_gain, ln_bias, qkv_bias, qk_gain, query_bias, out_bias,
    fc1_bias, fc2_bias, w_qkv, w_out, w_fc1, w_fc2, cotangent,
):
    layers = w_qkv.shape[0]
    rows, width = tokens.shape
    half = width // 2
    fsdp, tp = lax.axis_size("fsdp"), lax.axis_size("tp")
    f_index, t_index = lax.axis_index("fsdp"), lax.axis_index("tp")
    hidden = fc1_bias.shape[1] * fsdp * tp
    grid = row_table.shape[0]
    fine = width // (fsdp * tp)
    parts = hidden // width
    in_kernel = fsdp == 8

    place = jnp.arange(width, dtype=jnp.int32)
    chunk = width // fsdp
    slot = place // chunk
    away = (slot % (fsdp // 2)) * 2 + slot // (fsdp // 2)
    feature_at = (f_index ^ away) * chunk + place % chunk
    head_cols = width // tp
    spot = jnp.arange(tp * 3 * PAIR, dtype=jnp.int32)
    tile, part = spot % (3 * PAIR) // PAIR, spot % PAIR // HD
    head = jnp.where(tile == 0, part, jnp.where(tile == part + 1, 2, -fsdp * tp))
    head_at = ((t_index - spot // (3 * PAIR)) % tp) * head_cols + head * HD + spot % HD
    to_feature = (place[:, None] == feature_at[None, :]).astype(BF16)
    to_head = (place[:, None] == head_at[None, :]).astype(BF16)
    device = jnp.arange(fsdp * tp, dtype=jnp.int32)
    wanted = ((t_index - device // fsdp) % tp) * fsdp + device % fsdp
    to_hidden = (wanted[:, None] == device[None, :]).astype(BF16)

    by_layer = lambda *items: jnp.concatenate([item.reshape(layers, -1, fine) for item in items], axis=1).reshape(-1, fine)
    shares = [
        row_table, col_table, by_layer(ln_gain, ln_bias, out_bias, fc2_bias), by_layer(qkv_bias, qk_gain, query_bias),
        fc1_bias.reshape(layers * parts, fine),
    ]
    count = sum(item.shape[0] for item in shares)
    attn_shards = jnp.stack([attn_shard(w_qkv[layer], w_out[layer]) for layer in range(layers)])
    mlp_shards = jnp.concatenate([w_fc1, w_fc2.transpose(0, 2, 1)], axis=2)
    grid_ids = jnp.arange(grid, dtype=jnp.int32)
    row_hot = patch_pos[0][:, None] == grid_ids[None, :]
    col_hot = patch_pos[1][:, None] == grid_ids[None, :]
    hot = side(row_hot, col_hot).astype(BF16)
    tokens = jnp.dot(tokens, to_feature, preferred_element_type=F32)
    segments = segment_ids[0]
    padded = jnp.pad(segments, (REACH, REACH), constant_values=-1)
    seg_k = lax.dynamic_slice_in_dim(padded, t_index * rows, rows + 2 * REACH).reshape(-1, 1)
    seg_q = lax.dynamic_slice_in_dim(segments, t_index * rows, rows).reshape(1, -1)
    spill = REACH - rows

    if in_kernel:
        share = jnp.concatenate([jnp.pad(item, ((0, -item.shape[0] % 16), (0, PAIR - fine))) for item in shares], axis=0)
        *kept, start, feats, heads, a_win, attn_near, attn_far, mlp_near, mlp_far = forward(
            tokens, hot, share, seg_k, seg_q, attn_shards, mlp_shards
        )
        residual = kept[-1][layers - 1]
        kept += [a_win, attn_near, attn_far, mlp_near, mlp_far]
    else:
        small = jnp.concatenate(shares, axis=0)
        flat = small.reshape(1, -1)
        for bit in range(bits_of(tp)):
            flat = jnp.concatenate([flat, flip(flat, bit, "tp")], axis=0)
        for bit in range(bits_of(fsdp)):
            flat = jnp.concatenate([flat, flip(flat, bit)], axis=0)
        flat = flat[jnp.arange(fsdp * tp) ^ (f_index * tp + t_index)]
        gathered = flat.reshape(fsdp * tp, count, fine)
        lined = gathered.transpose(1, 0, 2).reshape(count, width)
        wide = 2 * grid + 6 * layers
        feats = jnp.dot(lined[:wide], to_feature, preferred_element_type=F32)
        heads = jnp.dot(lined[wide : wide + 6 * layers], to_head, preferred_element_type=F32)
        up_shift = jnp.einsum(
            "or,rlsi->losi",
            to_hidden,
            gathered[:, wide + 6 * layers :].reshape(fsdp * tp, layers, parts, fine),
            preferred_element_type=F32,
        ).reshape(layers, tp, 1, hidden // tp)
        tables = feats[: 2 * grid].astype(BF16)
        feats = feats[2 * grid :].reshape(layers, FEATS, width)

        heads = heads.reshape(layers, HEADS, tp, 3 * PAIR).transpose(2, 0, 1, 3)
        residual = tokens + jnp.dot(hot, tables, preferred_element_type=F32)
        hat, _ = row_norm(residual)
        a_own = (hat * feats[0, LN_GAIN[0]] + feats[0, LN_BIAS[0]]).astype(BF16)
        saved = []
        for layer in range(layers):
            a_win = jnp.concatenate(
                [hop(a_own[rows - spill :], 2), hop(a_own, 1), a_own, hop(a_own, -1), hop(a_own[:spill], -2)], axis=0
            )
            attn_near, attn_far = gather_by_permutes(attn_shards[layer], layer % 2 == 0)
            *stored, probs, o, mid, m = attend(
                a_win, attn_near, attn_far, heads, feats, residual, seg_k, seg_q, layer
            )
            mlp_near, mlp_far = gather_by_permutes(mlp_shards[layer], layer % 2 == 1)
            act, slope, x2 = mlp(m, mid, mlp_near, mlp_far, up_shift, feats, layer)
            stored = [item[None] for item in stored] + [probs]
            kept = [item[None] for item in (o, mid, m, act, slope)]
            saved.append((residual, a_win[None], stored, *kept, attn_near, attn_far, mlp_near, mlp_far))
            residual = x2
            if layer + 1 < layers:
                hat, _ = row_norm(residual)
                a_own = (
                    hat * feats[layer + 1, LN_GAIN[0]] + feats[layer + 1, LN_BIAS[0]]
                ).astype(BF16)

    restore = functools.partial(
        lax.dot_general, dimension_numbers=(((1,), (1,)), ((), ())), precision=HIGHEST, preferred_element_type=F32
    )
    exact = to_feature.astype(F32)
    activations = restore(residual, exact)
    cotangent_here = jnp.dot(cotangent, exact, precision=HIGHEST, preferred_element_type=F32)
    kept_sums = [None] * layers
    if in_kernel:
        grad, _, _, _, _, tally, mlp_blocks, attn_blocks = backward(
            cotangent_here, hot, share.shape[0], feats, heads, start, kept
        )
    else:
        grad, mlp_blocks, attn_blocks = cotangent_here, [None] * layers, [None] * layers
        for layer in reversed(range(layers)):
            x, a_win, stored, o, mid, m, act, slope, attn_near, attn_far, mlp_near, mlp_far = saved[layer]
            gz, gh, up_grad, g1, gr, mlp_small = mlp_back(grad, mlp_near, mlp_far, slope, mid, feats, layer, 0)
            mlp_blocks[layer] = reduce_by_permutes(*mlp_weight_grads(m, gh, gz, act), layer % 2 == 0)
            gq, gkv, mine, left, right, attn_small = attend_back(gr, stored, attn_near, attn_far, heads, layer, 0)
            attn_blocks[layer] = reduce_by_permutes(*attn_weight_grads(a_win, gq, gkv, gr, o), layer % 2 == 1)
            ends = jnp.concatenate([hop(right[rows:], 2), hop(left[:spill], -2)], axis=0).astype(F32)
            attn_grad = mine + hop(right[:rows], 1).astype(F32) + hop(left[spill:], -1).astype(F32) + ends
            hat, scale = row_norm(x)
            grad = g1 + row_norm_back(attn_grad * feats[layer, LN_GAIN[0]], hat, scale)
            kept_sums[layer] = (
                jnp.sum(attn_grad * hat, axis=0), jnp.sum(attn_grad, axis=0), mlp_small, attn_small,
                up_grad.reshape(parts, width),
            )
    middle = mlp_blocks[0].shape[1] // 2
    w_fc1_grad = [block[:, :middle] for block in mlp_blocks]
    w_fc2_grad = [block[:, middle:].T for block in mlp_blocks]
    w_qkv_grad, w_out_grad = zip(*[attn_unshard(block) for block in attn_blocks])

    token_grad = restore(grad, exact)
    if in_kernel:
        found = lax.dynamic_slice_in_dim(tally, t_index * fine, fine, axis=1)
        rows_g, cols_g, rest = found[:grid], found[grid : 2 * grid], found[2 * grid :]
        by_feature = rest[: layers * FEATS].reshape(layers, FEATS, fine)
        by_head = rest[16 : 16 + layers * HEADS].reshape(layers, HEADS, fine)
        up_g = rest[32 : 32 + layers * parts].reshape(layers, parts * fine)
    else:
        row_grad = jnp.einsum("tg,td->gd", row_hot.astype(F32), grad, precision=HIGHEST)
        col_grad = jnp.einsum("tg,td->gd", col_hot.astype(F32), grad, precision=HIGHEST)
        featured = [row_grad, col_grad]
        headed = []
        for a_gain, a_shift, sums, head_sums, _ in kept_sums:
            featured.append(jnp.stack([a_gain, sums[2], a_shift, sums[3], sums[1], sums[0]]))
            headed += [head_sums[3:6], head_sums[0:2], head_sums[2:3]]
        headed = jnp.concatenate(headed)
        spread = jnp.concatenate(
            [restore(jnp.concatenate(featured), to_feature.astype(F32)), restore(headed, to_head.astype(F32))]
        )
        spread = spread.reshape(-1, fsdp * tp, fine).transpose(1, 0, 2)
        up_all = jnp.stack([item[4] for item in kept_sums]).reshape(layers, fsdp * tp, parts * fine)
        up_all = jnp.einsum("or,lok->rlk", to_hidden.astype(F32), up_all, precision=HIGHEST)
        flat = jnp.concatenate([spread.reshape(fsdp * tp, -1), up_all.reshape(fsdp * tp, -1)], axis=1)
        flat = flat[jnp.arange(fsdp * tp) ^ (f_index * tp + t_index)]
        for bit in reversed(range(bits_of(fsdp))):
            middle = flat.shape[0] // 2
            flat = flat[:middle] + flip(flat[middle:], bit)
        for bit in reversed(range(bits_of(tp))):
            middle = flat.shape[0] // 2
            flat = flat[:middle] + flip(flat[middle:], bit, "tp")
        found = flat.reshape(-1, fine)
        rows_g, cols_g, rest = found[:grid], found[grid : 2 * grid], found[2 * grid :]
        by_feature = rest[: layers * FEATS].reshape(layers, FEATS, fine)
        by_head = rest[layers * FEATS : layers * (FEATS + HEADS)].reshape(layers, HEADS, fine)
        up_g = rest[layers * (FEATS + HEADS) :].reshape(layers, parts * fine)
    gain_g, shift_g, out_g, last_g = by_feature[:, :2], by_feature[:, 2:4], by_feature[:, OUT_BIAS], by_feature[:, LAST_BIAS]
    proj_g, head_gain_g, head_shift_g = by_head[:, :3], by_head[:, 3:5], by_head[:, HEAD_BIAS]
    return (
        activations, token_grad, rows_g, cols_g, gain_g, shift_g, proj_g, head_gain_g, head_shift_g, out_g, up_g, last_g,
        jnp.stack(w_qkv_grad), jnp.stack(w_out_grad), jnp.stack(w_fc1_grad), jnp.stack(w_fc2_grad),
    )


def solution(mesh):
    both = ("fsdp", "tp")
    in_specs = (
        P(both, None), P("fsdp", None), P(None, both), P(None, both), P(None, both), P(None, None, both),
        P(None, None, both), P(None, None, both), P(None, None, both), P(None, both), P(None, both), P(None, both),
        P(None, both), P(None, "fsdp", None, "tp"), P(None, "tp", "fsdp"), P(None, "fsdp", "tp"), P(None, "tp", "fsdp"),
        P(both, None),
    )
    out_specs = (
        P(both, None), P(both, None), P(None, both), P(None, both), P(None, None, both), P(None, None, both),
        P(None, None, both), P(None, None, both), P(None, both), P(None, both), P(None, both), P(None, both),
        P(None, "fsdp", None, "tp"), P(None, "tp", "fsdp"), P(None, "fsdp", "tp"), P(None, "tp", "fsdp"),
    )
    return jax.shard_map(body, mesh=mesh, in_specs=in_specs, out_specs=out_specs, check_vma=False)
```

```python
import functools

import jax
import jax.numpy as jnp
from jax import lax
from jax.experimental import pallas as pl
from jax.experimental.pallas import tpu as pltpu
from jax.sharding import PartitionSpec as P

HD = 64
PAIR = 128
REACH = 384
EPS = 1e-06
FILL = -1e30
ROOT_HALF = 0.7071067811865476
INV_ROOT_TWO_PI = 0.3989422804014327
HIGHEST = lax.Precision.HIGHEST
F32 = jnp.float32
BF16 = jnp.bfloat16
MESH = pl.DeviceIdType.MESH
VMEM = 67043328
ANY = pl.BlockSpec(memory_space=pl.ANY)


def nn(left, right):
    return lax.dot_general(left, right, (((1,), (0,)), ((), ())), preferred_element_type=F32)


def nt(left, right):
    return lax.dot_general(left, right, (((1,), (1,)), ((), ())), preferred_element_type=F32)


def halves(array):
    middle = array.shape[1] // 2
    return array[:, :middle], array[:, middle:]


def row_norm(value):
    centered = value - jnp.mean(value, axis=-1, keepdims=True)
    scale = lax.rsqrt(jnp.mean(centered * centered, axis=-1, keepdims=True) + EPS)
    return centered * scale, scale


def row_norm_back(grad_hat, normed, scale):
    return scale * (
        grad_hat
        - jnp.mean(grad_hat, axis=-1, keepdims=True)
        - normed * jnp.mean(grad_hat * normed, axis=-1, keepdims=True)
    )


def head_mean(value, exact=False):
    wide = value.shape[1]
    rows = lax.broadcasted_iota(jnp.int32, (wide, wide), 0) // HD
    cols = lax.broadcasted_iota(jnp.int32, (wide, wide), 1) // HD
    spread = jnp.where(rows == cols, 1.0 / HD, 0.0).astype(BF16)
    high = value.astype(BF16)
    mean = nn(high, spread)
    if exact:
        mean += nn((value - high.astype(F32)).astype(BF16), spread)
    return mean


def head_norm(value):
    centered = value - head_mean(value, exact=True)
    scale = lax.rsqrt(head_mean(centered * centered) + EPS)
    return centered * scale, scale


def head_norm_back(grad_hat, normed, scale):
    return scale * (grad_hat - head_mean(grad_hat) - normed * head_mean(grad_hat * normed))


def only(array, part):
    return jnp.where(lax.broadcasted_iota(jnp.int32, (1, PAIR), 1) // HD == part, array, jnp.zeros_like(array))


def side(*parts):
    return jnp.concatenate(parts, axis=1)


def whole(shape):
    return pl.BlockSpec(shape, lambda step: (0,) * len(shape))


def column(height, wide, every=1, first=0):
    return pl.BlockSpec((height, wide), lambda step: (0, step * every + first))


def piece_of(layer, height, wide, first=0):
    return pl.BlockSpec((None, None, height, wide), lambda step: (layer, step, 0, first))


def slab(layer, height, wide):
    return pl.BlockSpec((None, height, wide), lambda step: (layer, 0, step))


def heads_of(layer):
    return pl.BlockSpec((None, None, HEADS, 3 * PAIR), lambda step: (step, layer, 0, 0))


def sheet(layer, height, wide):
    return pl.BlockSpec((None, height, wide), lambda step: (layer, 0, 0))


def shaped(shape, kind=BF16):
    return jax.ShapeDtypeStruct(shape, kind)


class Neighbours:
    def __init__(self):
        fsdp, tp = lax.axis_index("fsdp"), lax.axis_index("tp")
        self.size = lax.axis_size("tp")
        self.tp = tp
        self.x, self.y, self.core = ({"fsdp": jnp.bitwise_xor(fsdp, bit)} for bit in (2, 4, 1))

    def along(self, distance):
        return {"tp": lax.rem(self.tp + distance, self.size)}

    def all(self):
        return [self.x, self.y, self.core] + [self.along(distance) for distance in range(1, self.size)]

    def greet(self):
        targets = self.all()
        barrier = pltpu.get_barrier_semaphore()
        for target in targets:
            pl.semaphore_signal(barrier, inc=1, device_id=target, device_id_type=MESH)
        pl.semaphore_wait(barrier, len(targets))


class Plan:
    LINKS = {"x": (43.5e3, 2.0), "y": (43.5e3, 2.0), "z": (43.5e3, 3.5), "core": (600e3, 1.0)}

    def __init__(self, depth):
        self.depth, self.clock = {"x": 3.0, "y": 3.0, "z": depth, "core": 20.0}, 0.0
        self.free, self.here, self.jobs, self.table = dict.fromkeys(self.LINKS, 0.0), {}, [], {}

    def add(self, rank, work, needs, copies, gives, group):
        self.jobs.append((rank, len(self.jobs), work, needs, copies, gives, group))
        self.jobs.sort(key=lambda job: job[:2])

    def carry(self, copies, gives):
        end = self.clock
        for link, size in copies:
            rate, latency = self.LINKS[link]
            self.free[link] = max(self.free[link], self.clock) + size / rate
            end = max(end, self.free[link] + latency)
        self.here[gives] = end

    def slot(self, *at):
        found = True
        while found:
            found = False
            for job in self.jobs:
                _, _, work, needs, copies, gives, _ = job
                ready = all(self.here.get(need, float("inf")) <= self.clock for need in needs)
                if ready and all(self.free[link] - self.clock < self.depth[link] for link, _ in copies):
                    self.carry(copies, gives)
                    self.table.setdefault(at, []).append(work)
                    self.jobs.remove(job)
                    found = True
                    break

    def wait(self, key, work, *at):
        self.slot(*at)
        while self.here.get(key, float("inf")) > self.clock:
            self.clock += 0.25
            self.slot(*at)
        self.table.setdefault(at, []).append(work)

    def finish(self, group, *at):
        self.slot(*at)
        while any(group in (None, job[-1]) for job in self.jobs):
            self.clock += 0.25
            self.slot(*at)

    def spend(self, time):
        self.clock += time


def turn(index, pieces):
    if isinstance(index, int):
        return (index + 1) // 2 if index % 2 else (pieces - index // 2) % pieces
    return jnp.where(lax.rem(index, 2) == 1, (index + 1) // 2, lax.rem(pieces - index // 2, pieces))


class Gather:
    KINDS = 7

    def __init__(self, peers, shard, near, far, send, recv, local, near_out, far_out, stored):
        self.peers, self.shard, self.near, self.far = peers, shard, near, far
        self.send, self.recv, self.local = send, recv, local
        self.outs, self.stored = (near_out, far_out), stored
        self.chunk, self.wide = shard.shape
        self.pieces = near.shape[0]

    def at(self, piece, start, count, half=None):
        first, wide = (0, self.wide) if half is None else (half * (self.wide // 2), self.wide // 2)
        return self.near.at[piece, pl.ds(start * self.chunk, count * self.chunk), pl.ds(first, wide)]

    def copy(self, piece, kind, source, target, device):
        return pltpu.make_async_remote_copy(
            src_ref=source, dst_ref=target, send_sem=self.send.at[piece, kind], recv_sem=self.recv.at[piece, kind],
            device_id=device, device_id_type=MESH,
        )

    def copies(self, piece, stage):
        if stage == "z":
            return [self.copy(piece, 0, self.shard, self.at(piece, 0, 1), self.peers.along(piece))] if piece else []
        if stage == "first":
            half = self.wide // 2
            left = self.shard.at[:, pl.ds(0, half)] if piece == 0 else self.at(piece, 0, 1, 0)
            right = self.shard.at[:, pl.ds(half, half)] if piece == 0 else self.at(piece, 0, 1, 1)
            return [
                self.copy(piece, 1, left, self.at(piece, 1, 1, 0), self.peers.x),
                self.copy(piece, 2, right, self.at(piece, 2, 1, 1), self.peers.y),
            ]
        if stage == "second":
            return [
                self.copy(piece, 3, self.at(piece, 0, 2, 0), self.at(piece, 2, 2, 0), self.peers.y),
                self.copy(piece, 4, self.at(piece, 0, 1, 1), self.at(piece, 1, 1, 1), self.peers.x),
                self.copy(piece, 5, self.at(piece, 2, 1, 1), self.at(piece, 3, 1, 1), self.peers.x),
            ]
        return [self.copy(piece, 6, self.near.at[piece], self.far.at[piece], self.peers.core)]

    def start(self, piece, stage):
        for copy in self.copies(piece, stage):
            copy.start()

    def arrived(self, piece, stage):
        for copy in self.copies(piece, stage):
            copy.wait_recv()

    def store(self, piece):
        return [
            pltpu.make_async_copy(source.at[piece], target.at[piece], self.stored.at[piece, which])
            for which, (source, target) in enumerate(zip((self.near, self.far), self.outs))
        ]

    def own(self):
        return pltpu.make_async_copy(self.shard, self.at(0, 0, 1), self.local)

    def sent(self, piece):
        self.start(piece, "z")

    def landed(self, piece):
        self.arrived(piece, "z")
        self.start(piece, "first")

    def crossed(self, piece):
        self.arrived(piece, "first")
        self.start(piece, "second")

    def shared(self, piece):
        self.arrived(piece, "second")
        self.start(piece, "core")

    def need(self, piece):
        self.arrived(piece, "core")
        for copy in self.store(piece):
            copy.start()

    def jobs(self, plan, index):
        size = self.chunk * self.wide * 2
        for place in range(self.pieces):
            piece = turn(place, self.pieces)
            key = (index, piece)
            rank = index * self.pieces + place
            if piece:
                plan.add(rank, (self.sent, piece), [], [("z", size * self.pieces / (self.pieces - 1))], ("z", *key), index)
            both = lambda count: [("x", count * size), ("y", count * size)]
            plan.add(rank, (self.landed, piece), [("z", *key)] if piece else [], both(0.5), ("first", *key), index)
            plan.add(rank, (self.crossed, piece), [("first", *key)], both(1), ("second", *key), index)
            plan.add(rank, (self.shared, piece), [("second", *key)], [("core", 4 * size)], ("core", *key), index)

    def end(self):
        for piece in range(self.pieces):
            for stage in ("z", "first", "second", "core"):
                for copy in self.copies(piece, stage):
                    copy.wait_send()
            for copy in self.store(piece):
                copy.wait()


class Halo:
    def __init__(self, ref, rows, send, recv):
        self.ref, self.send, self.recv = ref, send, recv
        self.place, self.size = lax.axis_index("tp"), lax.axis_size("tp")
        spill = REACH - rows
        self.moves = [
            (1, 1, pl.ds(REACH, rows), pl.ds(spill, rows)),
            (-1, 1, pl.ds(REACH, rows), pl.ds(REACH + rows, rows)),
            (1, 2, pl.ds(REACH - spill, spill), pl.ds(0, spill)),
            (-1, 2, pl.ds(REACH + rows, spill), pl.ds(REACH + 2 * rows, spill)),
        ]

    def inside(self, distance):
        other = self.place + distance
        return jnp.logical_and(other >= 0, other < self.size)

    def sends(self, index):
        direction, far, *_ = self.moves[index]
        return jnp.logical_and(self.inside(direction), self.inside(direction * (1 - far)))

    def takes(self, index):
        direction, far, *_ = self.moves[index]
        return self.inside(-direction * far)

    def copy(self, index):
        direction, _, source, target = self.moves[index]
        return pltpu.make_async_remote_copy(
            src_ref=self.ref.at[source, :], dst_ref=self.ref.at[target, :], send_sem=self.send.at[index],
            recv_sem=self.recv.at[index], device_id={"tp": self.place + direction}, device_id_type=MESH,
        )

    def start(self, index):
        @pl.when(self.sends(index))
        def _():
            self.copy(index).start()

    def arrived(self, index):
        @pl.when(self.takes(index))
        def _():
            self.copy(index).wait_recv()

    def begin(self):
        for index in range(2):
            self.start(index)
        for index, (*_, target) in enumerate(self.moves):

            @pl.when(jnp.logical_not(self.takes(index)))
            def _():
                self.ref[target, :] = jnp.zeros((target.size, self.ref.shape[1]), BF16)

    def relay(self):
        for index in range(2):
            self.arrived(index)
            self.start(index + 2)

    def end(self):
        for index in range(4):
            if index > 1:
                self.arrived(index)

            @pl.when(self.sends(index))
            def _():
                self.copy(index).wait_send()


def params(collective, memory=None):
    return pltpu.CompilerParams(collective_id=collective, has_side_effects=True, vmem_limit_bytes=memory)


LN_GAIN, LN_BIAS, OUT_BIAS, LAST_BIAS, FEATS = (0, 1), (2, 3), 4, 5, 6
PROJ_BIAS, HEAD_GAIN, HEAD_BIAS, HEADS = (0, 1, 2), (3, 4), 5, 6


def line(ref, row, start=0, wide=None):
    return ref[pl.ds(row, 1), pl.ds(start, wide or ref.shape[1] - start)]


def attend_work(
    a_ref, near_ref, far_ref, heads_ref, feats_ref, x_ref, q_ref, kv_ref, q_hat_ref, k_hat_ref, q_scale_ref, k_scale_ref,
    p_ref, o_ref, mid_ref, m_ref, mask_ref, acc_ref, opening, closing, hook,
):
    rows = q_ref.shape[0]
    half = near_ref.shape[0]

    @pl.when(opening)
    def _():
        acc_ref[...] = jnp.zeros_like(acc_ref)

    tile = lambda row, which: line(heads_ref, row, which * PAIR, PAIR)
    bias, (q_gain, k_gain), q_shift = PROJ_BIAS, HEAD_GAIN, HEAD_BIAS
    near, distant = halves(a_ref[...])
    own, own_far = halves(a_ref[REACH : REACH + rows, :])
    kv = nn(near, near_ref[:, PAIR : 4 * PAIR]) + nn(distant, far_ref[:, PAIR : 4 * PAIR])
    kv += side(tile(bias[1], 0), tile(bias[2], 0), tile(bias[1], 1) + tile(bias[2], 2))
    q = side(
        nn(own, near_ref[:, :PAIR]) + nn(own_far, far_ref[:, :PAIR]),
        nn(own, near_ref[:, 4 * PAIR : 5 * PAIR]) + nn(own_far, far_ref[:, 4 * PAIR : 5 * PAIR]),
    ) + line(heads_ref, bias[0], 0, 2 * PAIR)
    q_hat, q_scale = head_norm(q)
    k_hat, k_scale = head_norm(side(kv[:, :PAIR], kv[:, 2 * PAIR :]))
    qn = (q_hat * line(heads_ref, q_gain, 0, 2 * PAIR) + line(heads_ref, q_shift, 0, 2 * PAIR)).astype(BF16)
    qn = side(qn[:, :PAIR], only(qn[:, PAIR:], 0))
    kn = (k_hat * line(heads_ref, k_gain, 0, 2 * PAIR)).astype(BF16)
    v = kv[:, PAIR:].astype(BF16)
    low = lax.broadcasted_iota(jnp.int32, (1, PAIR), 1) < HD
    first, second = kn[:, :PAIR], jnp.where(low, kn[:, PAIR:], v[:, PAIR:])
    values = v[:, :PAIR]
    q_ref[...] = qn
    kv_ref[...] = side(first, values, second)
    q_hat_ref[...] = q_hat.astype(BF16)
    k_hat_ref[...] = k_hat.astype(BF16)
    q_scale_ref[...] = q_scale.astype(BF16)
    k_scale_ref[...] = k_scale.astype(BF16)
    hook(1)
    values_t, second_t = values.T, second.T
    mixed = []
    for head in range(3):
        if head:
            hook(head + 1)
        keys = (first, first, second)[head]
        query = only(qn[:, PAIR * (head // 2) : PAIR * (head // 2 + 1)] * HD ** (-0.5), head % 2).astype(BF16)
        scores = nt(keys, query) + mask_ref[...]
        weights = jnp.exp(scores - jnp.max(scores, axis=0, keepdims=True))
        total = jnp.sum(weights, axis=0, keepdims=True)
        probs = (weights * (1.0 / total)).astype(BF16)
        p_ref[head] = probs
        mixed.append(nn((values_t[:HD], values_t[HD:], second_t[HD:])[head], probs))
    o = jnp.concatenate([jnp.zeros_like(mixed[2]), mixed[2], mixed[0], mixed[1]], axis=0).T.astype(BF16)
    o_ref[...] = o
    acc_ref[:, :half] += nt(o, near_ref[:, 4 * PAIR :])
    acc_ref[:, half:] += nt(o, far_ref[:, 4 * PAIR :])

    @pl.when(closing)
    def _():
        mid = x_ref[...] + (acc_ref[...] + line(feats_ref, OUT_BIAS))
        mid_ref[...] = mid
        hat, _ = row_norm(mid)
        m_ref[...] = (hat * line(feats_ref, LN_GAIN[1]) + line(feats_ref, LN_BIAS[1])).astype(BF16)


def mlp_work(
    m_ref, mid_ref, near_ref, far_ref, up_shift, feats_ref, act_ref, slope_ref, x2_ref, acc_ref, opening, closing, hook,
):
    half = near_ref.shape[0]
    wide = act_ref.shape[1]

    @pl.when(opening)
    def _():
        acc_ref[...] = jnp.zeros_like(acc_ref)

    near, distant = halves(m_ref[...])
    hidden = nn(near, near_ref[:, :wide]) + nn(distant, far_ref[:, :wide]) + up_shift
    hook(1)
    phi = 0.5 * (1.0 + lax.erf(hidden * ROOT_HALF))
    act = (hidden * phi).astype(BF16)
    act_ref[...] = act
    slope_ref[...] = (phi + hidden * jnp.exp(-0.5 * hidden * hidden) * INV_ROOT_TWO_PI).astype(BF16)
    acc_ref[:, :half] += nt(act, near_ref[:, wide:])
    acc_ref[:, half:] += nt(act, far_ref[:, wide:])

    @pl.when(closing)
    def _():
        x2_ref[...] = mid_ref[...] + (acc_ref[...] + line(feats_ref, LAST_BIAS))


def norm_rows(x, feats_ref):
    hat, _ = row_norm(x)
    return (hat * line(feats_ref, LN_GAIN[0]) + line(feats_ref, LN_BIAS[0])).astype(BF16)


def quiet(slot):
    pass


def attend_kernel(
    a_ref, near_ref, far_ref, heads_ref, feats_ref, x_ref, seg_k_ref, seg_q_ref, *rest
):
    step = pl.program_id(0)
    mask_ref = rest[-2]

    @pl.when(step == 0)
    def _():
        mask_ref[...] = jnp.where(seg_k_ref[...] == seg_q_ref[...], 0.0, FILL)

    attend_work(
        a_ref, near_ref, far_ref, heads_ref, feats_ref, x_ref, *rest, step == 0, step == pl.num_programs(0) - 1, quiet
    )


def attend_shapes(rows, window):
    return [
        (rows, 2 * PAIR), (window, 3 * PAIR), (rows, 2 * PAIR), (window, 2 * PAIR), (rows, 2 * PAIR), (window, 2 * PAIR),
    ]


def attend(a_win, near, far, heads, feats, x, seg_k, seg_q, layer):
    window, width = a_win.shape
    rows = x.shape[0]
    half = width // 2
    pieces = near.shape[1]
    outs = attend_shapes(rows, window)
    return pl.pallas_call(
        attend_kernel,
        grid=(pieces,),
        in_specs=[
            whole((window, width)), piece_of(0, half, 6 * PAIR), piece_of(0, half, 6 * PAIR), heads_of(layer), sheet(layer, FEATS, width),
            whole((rows, width)), whole((window, 1)), whole((1, rows)),
        ],
        out_specs=[column(*shape) for shape in outs]
        + [pl.BlockSpec((3, window, rows), lambda step: (step, 0, 0)), column(rows, 2 * PAIR)] + [whole((rows, width))] * 2,
        out_shape=[shaped((height, pieces * wide)) for height, wide in outs]
        + [shaped((3 * pieces, window, rows)), shaped((rows, pieces * 2 * PAIR)), shaped((rows, width), F32), shaped((rows, width))],
        scratch_shapes=[pltpu.VMEM((window, rows), F32), pltpu.VMEM((rows, width), F32)],
        name="attend",
    )(a_win, near, far, heads, feats, x, seg_k, seg_q)


def mlp_kernel(m_ref, mid_ref, near_ref, far_ref, up_shift_ref, feats_ref, *rest):
    step = pl.program_id(0)
    mlp_work(
        m_ref, mid_ref, near_ref, far_ref, up_shift_ref[...], feats_ref, *rest, step == 0, step == pl.num_programs(0) - 1, quiet
    )


def mlp(m, mid, near, far, up_shift, feats, layer):
    rows, width = mid.shape
    half = width // 2
    _, pieces, _, wide = up_shift.shape
    hidden = pieces * wide
    full = whole((rows, width))
    return pl.pallas_call(
        mlp_kernel,
        grid=(pieces,),
        in_specs=[
            full, full, piece_of(0, half, 2 * wide), piece_of(0, half, 2 * wide), piece_of(layer, 1, wide), sheet(layer, FEATS, width),
        ],
        out_specs=[column(rows, wide), column(rows, wide), full],
        out_shape=[shaped((rows, hidden)), shaped((rows, hidden)), shaped((rows, width), F32)],
        scratch_shapes=[pltpu.VMEM((rows, width), F32)],
        name="mlp",
    )(m, mid, near, far, up_shift, feats)


class Share:
    def __init__(self, peers, mine, landed, chunks, send, recv):
        self.peers, self.mine, self.landed, self.chunks, self.send, self.recv = peers, mine, landed, chunks, send, recv
        self.pieces, self.lines = landed.shape[0], mine.shape[0]

    def copy(self, index, source, target, device):
        return pltpu.make_async_remote_copy(
            src_ref=source, dst_ref=target, send_sem=self.send.at[index], recv_sem=self.recv.at[index], device_id=device,
            device_id_type=MESH,
        )

    def along(self):
        place = self.landed.at[self.peers.tp]
        return [self.copy(d - 1, self.mine, place, self.peers.along(d)) for d in range(1, self.pieces)]

    def across(self, stage):
        count = 1 << stage
        device = (self.peers.x, self.peers.y, self.peers.core)[stage]
        source, target = self.chunks.at[pl.ds(0, count)], self.chunks.at[pl.ds(count, count)]
        return self.copy(self.pieces - 1 + stage, source, target, device)

    def begin(self):
        for copy in self.along():
            copy.start()
        self.landed[self.peers.tp] = self.mine[...]

    def meet(self, fine):
        for copy in self.along():
            copy.wait_recv()
        row, col = (lax.broadcasted_iota(jnp.int32, (PAIR, PAIR), axis) for axis in range(2))
        total = 0.0
        for place in range(self.pieces):
            spread = jnp.logical_and(row < fine, col == row + place * fine)
            total += nn(self.landed[place], spread.astype(F32).astype(BF16))
        self.chunks[0] = total.astype(BF16)
        self.across(0).start()

    def spread(self, stage):
        self.across(stage - 1).wait_recv()
        self.across(stage).start()

    def end(self):
        self.across(2).wait_recv()
        for copy in self.along() + [self.across(stage) for stage in range(3)]:
            copy.wait_send()

    def chunk_of(self, fsdp):
        away = jnp.bitwise_xor(lax.axis_index("fsdp"), fsdp)
        return lax.rem(away, 2) * (self.chunks.shape[0] // 2) + away // 2

    def features(self, lines, width):
        chunk = width // self.chunks.shape[0]
        row, col = (lax.broadcasted_iota(jnp.int32, (2 * PAIR, width), axis) for axis in range(2))
        total = 0.0
        for place in range(0, self.chunks.shape[0], 2):
            lane = lax.rem(row, PAIR)
            spread = jnp.logical_and(lane < chunk, col == (place + row // PAIR) * chunk + lane)
            both = side(self.chunks[place, :lines, :], self.chunks[place + 1, :lines, :])
            total += nn(both, spread.astype(F32).astype(BF16))
        return total

    def owner(self, place):
        return lax.rem(self.peers.tp + self.pieces - place, self.pieces)

    def heads(self, place, start, chunk):
        owner = self.owner(place)
        rows = pl.ds(start, 16)
        both = side(self.chunks[self.chunk_of(2 * owner), rows, :], self.chunks[self.chunk_of(2 * owner + 1), rows, :])
        row, col = (lax.broadcasted_iota(jnp.int32, (2 * PAIR, 3 * PAIR), axis) for axis in range(2))
        lane = lax.rem(row, PAIR)
        feature = row // PAIR * chunk + lane
        last = jnp.logical_and(feature >= PAIR, col == feature + 3 * HD)
        spread = jnp.logical_and(lane < chunk, jnp.logical_or(col == feature, last))
        return nn(both, spread.astype(F32).astype(BF16))

    def hidden(self, start, layers, parts, fine):
        rows = pl.ds(start, 16)
        block = jnp.concatenate(
            [self.chunks[self.chunk_of(2 * self.owner(i // 2) + i % 2), rows, :] for i in range(2 * self.pieces)], axis=0
        )
        wide = self.pieces * parts * fine
        row, col = (lax.broadcasted_iota(jnp.int32, (PAIR, wide), axis) for axis in range(2))
        line_of = lax.broadcasted_iota(jnp.int32, (block.shape[0], 1), 0)
        total = 0.0
        for part in range(parts):
            target = row // fine * (parts * fine) + part * fine + lax.rem(row, fine)
            spread = jnp.logical_and(row < self.pieces * fine, col == target)
            here = nn(block, spread.astype(F32).astype(BF16))
            total += jnp.where(lax.rem(line_of, parts) == part, here, 0.0)
        row, col = (lax.broadcasted_iota(jnp.int32, (2 * self.pieces * layers, block.shape[0]), axis) for axis in range(2))
        group = jnp.logical_and(row // layers == col // 16, lax.rem(row, layers) == lax.rem(col, 16) // parts)
        return nn(group.astype(F32).astype(BF16), total.astype(BF16))


def forward_kernel(
    token_ref, hot_ref, share_ref, seg_k_ref, seg_q_ref, attn_shard_ref, mlp_shard_ref,
    q_ref, kv_ref, q_hat_ref, k_hat_ref, q_scale_ref, k_scale_ref, p_ref, o_ref, act_ref, slope_ref, mid_ref, m_ref, x2_ref,
    x0_ref, feats_ref, heads_ref, a_win_out, attn_near_out, attn_far_out, mlp_near_out, mlp_far_out,
    mask_ref, acc_ref, now_ref, a_win_ref, kept, attn_near, attn_far, mlp_near, mlp_far, send, recv, local, stored, halo_send, halo_recv,
    up_shift_ref, landed, chunks, share_send, share_recv,
):
    layers, pieces, (rows, width) = attn_near.shape[0], attn_near.shape[1], token_ref.shape
    chunk = width // chunks.shape[0]
    fine, parts, tables = chunk // pieces, act_ref.shape[1] * pieces // width, hot_ref.shape[1]
    step = pl.program_id(0)
    peers = Neighbours()
    halo = lambda layer: Halo(a_win_ref.at[layer], rows, halo_send.at[layer], halo_recv.at[layer])
    keep_window = lambda layer: pltpu.make_async_copy(a_win_ref.at[layer], a_win_out.at[layer], kept.at[layer])

    def relay(layer):
        halo(layer).relay()

    def window(layer):
        halo(layer).end()
        keep_window(layer).start()

    gathers = []
    for layer in range(layers):
        for which, (shard, near, far, near_out, far_out) in enumerate((
            (attn_shard_ref, attn_near, attn_far, attn_near_out, attn_far_out),
            (mlp_shard_ref, mlp_near, mlp_far, mlp_near_out, mlp_far_out),
        )):
            index = 2 * layer + which
            gathers.append(
                Gather(
                    peers, shard.at[layer], near.at[layer], far.at[layer], send.at[index], recv.at[index], local.at[index],
                    near_out.at[layer], far_out.at[layer], stored.at[index],
                )
            )

    share = Share(peers, share_ref, landed, chunks, share_send, share_recv)

    def open_up(_):
        share.end()
        lines = tables + 16
        found = share.features(lines, width)
        for layer in range(layers):
            feats_ref[layer] = found[tables + layer * FEATS : tables + (layer + 1) * FEATS]
        x0 = token_ref[...] + nn(hot_ref[...], found[:tables].astype(BF16))
        x0_ref[...] = x0
        now_ref[...] = x0
        a_win_ref[0, REACH : REACH + rows, :] = norm_rows(x0, feats_ref.at[0])
        halo(0).begin()
        for piece in range(pieces):
            found = share.heads(piece, lines, chunk)
            for layer in range(layers):
                heads_ref[piece, layer] = found[layer * HEADS : (layer + 1) * HEADS]
        found = share.hidden(lines + 16, layers, parts, fine)
        half = pieces * parts * fine
        for index in range(2 * pieces):
            for layer in range(layers):
                at = index * layers + layer
                up_shift_ref[layer, index // 2, :, index % 2 * half : (index % 2 + 1) * half] = found[at : at + 1]

    plan = Plan(1.0)
    for index, gather in enumerate(gathers):
        gather.jobs(plan, index)
    share_size = share_ref.shape[0] * PAIR * 2
    plan.spend(2.5)
    plan.carry([("z", pieces * share_size)], ("share", 0))
    plan.wait(("share", 0), (share.meet, fine), 0, 0)
    plan.carry([("x", share_size)], ("share", 1))
    plan.wait(("share", 1), (share.spread, 1), 0, 0)
    plan.carry([("y", 2 * share_size)], ("share", 2))
    plan.wait(("share", 2), (share.spread, 2), 0, 0)
    plan.carry([("core", 4 * share_size)], ("share", 3))
    plan.wait(("share", 3), (open_up, 0), 0, 0)
    for layer in range(layers):
        plan.carry([("z", width * 2 * rows)], ("near", layer))
        first = 1 + 2 * layer * pieces
        if layer == 0:
            plan.spend(5.0)
        at = (first, 0) if layer else (0, 0)
        plan.wait(("near", layer), (relay, layer), *at)
        plan.carry([("z", width * 2 * (REACH - rows))], ("halo", layer))
        plan.wait(("halo", layer), (window, layer), *at)
        for index in range(pieces):
            piece = turn(index, pieces)
            plan.wait(("core", 2 * layer, piece), (gathers[2 * layer].need, piece), first + index, 0)
            for slot, time in enumerate((2.0, 1.4, 1.4)):
                plan.spend(time)
                plan.slot(first + index, slot + 1)
            plan.spend(1.4)
        first += pieces
        for index in range(pieces):
            piece = turn(index, pieces)
            plan.wait(("core", 2 * layer + 1, piece), (gathers[2 * layer + 1].need, piece), first + index, 0)
            plan.spend(1.0)
            plan.slot(first + index, 1)
            plan.spend(1.5)
    table = plan.table

    def run(at, slot):
        if (at, slot) in table:

            @pl.when(step == at)
            def _():
                for work, piece in table[at, slot]:
                    work(piece)

    @pl.when(step == 0)
    def _():
        peers.greet()
        mask_ref[...] = jnp.where(seg_k_ref[...] == seg_q_ref[...], 0.0, FILL)
        share.begin()
        for gather in gathers:
            gather.own().start()
        for gather in gathers:
            gather.own().wait()

    run(0, 0)

    count = jnp.maximum(step - 1, 0)
    layer = count // (2 * pieces)
    inner = lax.rem(count, 2 * pieces)
    index = lax.rem(inner, pieces)
    piece = turn(index, pieces)
    steps_of = lambda which: [
        1 + (2 * layer + which) * pieces + index for layer in range(layers) for index in range(pieces)
    ]

    @pl.when(jnp.logical_and(step > 0, inner < pieces))
    def _():
        def hook(slot):
            for at in steps_of(0):
                run(at, slot)

        hook(0)
        attend_work(
            a_win_ref.at[layer], attn_near.at[layer, piece], attn_far.at[layer, piece], heads_ref.at[piece, layer],
            feats_ref.at[layer], now_ref,
            q_ref, kv_ref, q_hat_ref, k_hat_ref, q_scale_ref, k_scale_ref, p_ref, o_ref, mid_ref.at[layer], m_ref.at[layer],
            mask_ref, acc_ref, index == 0, index == pieces - 1, hook,
        )

    @pl.when(inner >= pieces)
    def _():
        def hook(slot):
            for at in steps_of(1):
                run(at, slot)

        hook(0)
        mlp_work(
            m_ref.at[layer], mid_ref.at[layer], mlp_near.at[layer, piece], mlp_far.at[layer, piece],
            up_shift_ref[layer, piece], feats_ref.at[layer], act_ref, slope_ref, now_ref, acc_ref, index == 0,
            index == pieces - 1, hook,
        )

        @pl.when(index == pieces - 1)
        def _():
            x2_ref[layer] = now_ref[...]

            @pl.when(layer + 1 < layers)
            def _():
                a_win_ref[layer + 1, REACH : REACH + rows, :] = norm_rows(now_ref[...], feats_ref.at[layer + 1])
                halo(layer + 1).begin()

    @pl.when(step == pl.num_programs(0) - 1)
    def _():
        for gather in gathers:
            gather.end()
        for layer in range(layers):
            keep_window(layer).wait()


def forward(tokens, hot, share, seg_k, seg_q, attn_shards, mlp_shards):
    rows, width = tokens.shape
    layers, chunk, wide = mlp_shards.shape
    half = width // 2
    window = rows + 2 * REACH
    pieces, chunks, part = lax.axis_size("tp"), lax.axis_size("fsdp"), wide // 2
    hidden = pieces * part

    def attend_at(step):
        count = jnp.maximum(step - 1, 0)
        layer, inner = count // (2 * pieces), lax.rem(count, 2 * pieces)
        return layer, turn(jnp.minimum(inner, pieces - 1), pieces)

    def mlp_at(step):
        count = jnp.maximum(step - 1, 0)
        layer, inner = count // (2 * pieces), lax.rem(count, 2 * pieces)
        done = jnp.where(inner >= pieces, layer * pieces + inner - pieces, jnp.maximum(layer * pieces - 1, 0))
        return done // pieces, turn(lax.rem(done, pieces), pieces)

    def attend_block(height, wide):
        return pl.BlockSpec((None, height, wide), lambda step: (attend_at(step)[0], 0, attend_at(step)[1]))

    mlp_block = pl.BlockSpec((None, rows, part), lambda step: (mlp_at(step)[0], 0, mlp_at(step)[1]))
    heads_at = lambda step: attend_at(step)[0] * pieces + attend_at(step)[1]
    once = lambda shape: pl.BlockSpec(shape, lambda step: (0,) * len(shape), pipeline_mode=pl.Buffered(1))
    outs = attend_shapes(rows, window) + [(rows, 2 * PAIR)]
    specs = [attend_block(*shape) for shape in outs]
    shapes = [shaped((layers, height, pieces * wide)) for height, wide in outs]
    specs.insert(6, pl.BlockSpec((3, window, rows), lambda step: (heads_at(step), 0, 0)))
    shapes.insert(6, shaped((3 * layers * pieces, window, rows)))
    held = [((layers, rows, width), F32), ((layers, rows, width), BF16), ((layers, rows, width), F32)]
    weights = [(layers, pieces, half, 6 * PAIR)] * 2 + [(layers, pieces, half, wide)] * 2
    semaphores = pltpu.SemaphoreType.DMA((2 * layers, pieces, Gather.KINDS))
    held += [((rows, width), F32), ((layers, FEATS, width), F32), ((pieces, layers, HEADS, 3 * PAIR), F32)]
    inputs = (tokens, hot, share, seg_k, seg_q, attn_shards, mlp_shards)
    return pl.pallas_call(
        forward_kernel,
        grid=(1 + 2 * layers * pieces,),
        in_specs=[once(item.shape) for item in inputs],
        out_specs=specs + [mlp_block] * 2 + [once(shape) for shape, _ in held] + [ANY] * 5,
        out_shape=shapes + [shaped((layers, rows, hidden))] * 2 + [shaped(*item) for item in held]
        + [shaped(shape) for shape in [(layers, window, width)] + weights],
        scratch_shapes=[
            pltpu.VMEM((window, rows), F32), pltpu.VMEM((rows, width), F32), pltpu.VMEM((rows, width), F32),
            pltpu.VMEM((layers, window, width), BF16), pltpu.SemaphoreType.DMA((layers,)),
            *[pltpu.VMEM(shape, BF16) for shape in weights], semaphores, semaphores, pltpu.SemaphoreType.DMA((2 * layers,)),
            pltpu.SemaphoreType.DMA((2 * layers, pieces, 2)), pltpu.SemaphoreType.DMA((layers, 4)),
            pltpu.SemaphoreType.DMA((layers, 4)), pltpu.VMEM((layers, pieces, 1, part), F32),
            pltpu.VMEM((pieces, *share.shape), BF16), pltpu.VMEM((chunks, *share.shape), BF16),
            pltpu.SemaphoreType.DMA((pieces + 2,)), pltpu.SemaphoreType.DMA((pieces + 2,)),
        ],
        compiler_params=params(20, VMEM),
        name="forward",
    )(*inputs)


def mlp_back_kernel(*refs):
    step = pl.program_id(0)
    mlp_back_work(*refs, step == 0, step == pl.num_programs(0) - 1, quiet)


def mlp_back_work(
    g_ref, down_near_ref, down_far_ref, slope_ref, up_near_ref, up_far_ref, mid_ref, feats_ref,
    gz_ref, gh_ref, up_shift_grad_ref, g1_ref, gr_ref, small_ref, acc_ref, opening, closing, hook,
):
    half = up_near_ref.shape[0]

    @pl.when(opening)
    def _():
        gz_ref[...] = g_ref[...].astype(BF16)
        acc_ref[...] = jnp.zeros_like(acc_ref)

    near, distant = halves(gz_ref[...])
    gh = ((nn(near, down_near_ref[...]) + nn(distant, down_far_ref[...])) * slope_ref[...].astype(F32)).astype(BF16)
    gh_ref[...] = gh
    hook(1)
    up_shift_grad_ref[...] = jnp.sum(gh.astype(F32), axis=0, keepdims=True)
    acc_ref[:, :half] += nt(gh, up_near_ref[...])
    acc_ref[:, half:] += nt(gh, up_far_ref[...])

    @pl.when(closing)
    def _():
        gm = acc_ref[...]
        hat, scale = row_norm(mid_ref[...])
        g1 = g_ref[...] + row_norm_back(gm * line(feats_ref, LN_GAIN[1]), hat, scale)
        gr = g1.astype(BF16)
        g1_ref[...] = g1
        gr_ref[...] = gr
        small_ref[...] = jnp.zeros_like(small_ref)
        small_ref[0:1, :] = jnp.sum(gz_ref[...].astype(F32), axis=0, keepdims=True)
        small_ref[1:2, :] = jnp.sum(gr.astype(F32), axis=0, keepdims=True)
        small_ref[2:3, :] = jnp.sum(gm * hat, axis=0, keepdims=True)
        small_ref[3:4, :] = jnp.sum(gm, axis=0, keepdims=True)


def mlp_back(grad, near, far, slope, mid, feats, layer, index):
    rows, width = grad.shape
    half = width // 2
    hidden = slope.shape[2]
    pieces = near.shape[1]
    wide = hidden // pieces
    full = whole((rows, width))
    return pl.pallas_call(
        mlp_back_kernel,
        grid=(pieces,),
        in_specs=[
            full, piece_of(index, half, wide, 1), piece_of(index, half, wide, 1), slab(index, rows, wide),
            piece_of(index, half, wide), piece_of(index, half, wide), sheet(index, rows, width), sheet(layer, FEATS, width),
        ],
        out_specs=[full, column(rows, wide), column(1, wide), full, full, whole((8, width))],
        out_shape=[
            shaped((rows, width)), shaped((rows, hidden)), shaped((1, hidden), F32), shaped((rows, width), F32),
            shaped((rows, width)), shaped((8, width), F32),
        ],
        scratch_shapes=[pltpu.VMEM((rows, width), F32)],
        cost_estimate=pl.CostEstimate(
            flops=4 * rows * width * hidden, bytes_accessed=4 * width * hidden, transcendentals=0
        ),
        name="mlp_back",
    )(grad, near, far, slope, near, far, mid, feats)


def attend_back_kernel(*refs):
    *ins, gq_ref, gkv_ref, mine_ref, left_ref, right_ref, small_ref, acc_ref = refs
    rows = gq_ref.shape[0]
    step = pl.program_id(0)

    @pl.when(step == 0)
    def _():
        acc_ref[...] = jnp.zeros_like(acc_ref)

    attend_back_work(*ins, gq_ref, gkv_ref, small_ref, acc_ref, quiet)

    @pl.when(step == pl.num_programs(0) - 1)
    def _():
        left_ref[...] = acc_ref[:REACH, :].astype(BF16)
        mine_ref[...] = acc_ref[REACH : REACH + rows, :]
        right_ref[...] = acc_ref[REACH + rows :, :].astype(BF16)


def attend_back_work(
    gr_ref, q_ref, kv_ref, q_hat_ref, k_hat_ref, q_scale_ref, k_scale_ref, p_ref, near_ref, far_ref, heads_ref,
    gq_ref, gkv_ref, small_ref, acc_ref, hook,
):
    rows = gr_ref.shape[0]
    half = near_ref.shape[0]
    near, distant = halves(gr_ref[...])
    go = (nn(near, near_ref[:, 4 * PAIR :]) + nn(distant, far_ref[:, 4 * PAIR :])).astype(BF16)
    qn, kv = q_ref[...], kv_ref[...]
    first, values, second = kv[:, :PAIR], kv[:, PAIR : 2 * PAIR], kv[:, 2 * PAIR :]
    first_t, second_t = first.T, second.T
    grad_q, grad_k, grad_v = [], [], []
    for head in range(3):
        if head:
            hook(head)
        go_head = only(go[:, PAIR:], head) if head < 2 else only(go[:, :PAIR], 1)
        query = only(qn[:, PAIR * (head // 2) : PAIR * (head // 2 + 1)] * HD ** (-0.5), head % 2).astype(BF16)
        stored = p_ref[head]
        probs = stored.astype(F32)
        grad_probs = nt((values, values, second)[head], go_head)
        delta = jnp.sum(probs * grad_probs, axis=0, keepdims=True)
        grad_scores = (probs * (grad_probs - delta)).astype(BF16)
        grad_v.append(nn(stored, go_head))
        grad_k.append(nn(grad_scores, query))
        grad_q.append(nn((first_t[:HD], first_t[HD:], second_t[:HD])[head], grad_scores))
    hook(3)
    zero = jnp.zeros_like(grad_q[2])
    grad_q = (jnp.concatenate(grad_q + [zero], axis=0) * HD ** (-0.5)).T
    grad_k = side(grad_k[0] + grad_k[1], grad_k[2])
    pair_v, last_v = grad_v[0] + grad_v[1], grad_v[2]
    q_hat = q_hat_ref[...].astype(F32)
    k_hat = k_hat_ref[...].astype(F32)
    gain = lambda which: line(heads_ref, HEAD_GAIN[which], 0, 2 * PAIR)
    gq = head_norm_back(grad_q * gain(0), q_hat, q_scale_ref[...].astype(F32)).astype(BF16)
    gk = head_norm_back(grad_k * gain(1), k_hat, k_scale_ref[...].astype(F32)).astype(BF16)
    gkv = side(gk[:, :PAIR], pair_v.astype(BF16), gk[:, PAIR:] + last_v.astype(BF16))
    gq_ref[...] = gq
    gkv_ref[...] = gkv
    total = lambda value: jnp.sum(value.astype(F32), axis=0, keepdims=True)
    small_ref[...] = jnp.zeros_like(small_ref)
    small_ref[0:1, : 2 * PAIR] = total(grad_q * q_hat)
    small_ref[1:2, : 2 * PAIR] = total(grad_k * k_hat)
    small_ref[2:3, : 2 * PAIR] = total(grad_q)
    small_ref[3:4, : 2 * PAIR] = total(gq)
    small_ref[4:5, : 2 * PAIR] = total(gk)
    small_ref[5:6, :PAIR] = total(pair_v.astype(BF16))
    small_ref[5:6, 2 * PAIR :] = total(last_v.astype(BF16))
    acc_ref[:, :half] += nt(gkv, near_ref[:, PAIR : 4 * PAIR])
    acc_ref[:, half:] += nt(gkv, far_ref[:, PAIR : 4 * PAIR])
    own = slice(REACH, REACH + rows)
    for ref, cols in ((near_ref, slice(0, half)), (far_ref, slice(half, 2 * half))):
        acc_ref[own, cols] += nt(gq[:, :PAIR], ref[:, :PAIR]) + nt(gq[:, PAIR:], ref[:, 4 * PAIR : 5 * PAIR])


def attend_back_specs(rows, width, pieces, layer, index):
    half = width // 2
    window = rows + 2 * REACH
    full = whole((rows, width))
    in_specs = [
        full, *[slab(index, *shape) for shape in attend_shapes(rows, window)],
        pl.BlockSpec((3, window, rows), lambda step: (index * pieces + step, 0, 0)), piece_of(index, half, 6 * PAIR),
        piece_of(index, half, 6 * PAIR), heads_of(layer),
    ]
    out_specs = [
        column(rows, 2 * PAIR), column(window, 3 * PAIR), full, whole((REACH, width)), whole((REACH, width)), column(8, 3 * PAIR),
    ]
    out_shape = [
        shaped((rows, pieces * 2 * PAIR)), shaped((window, pieces * 3 * PAIR)), shaped((rows, width), F32),
        shaped((REACH, width)), shaped((REACH, width)), shaped((8, pieces * 3 * PAIR), F32),
    ]
    cost = pl.CostEstimate(
        flops=2 * window * width * width * 2 + 20 * window * rows * width * 2,
        bytes_accessed=20 * window * width,
        transcendentals=0,
    )
    return in_specs, out_specs, out_shape, [pltpu.VMEM((window, width), F32)], cost


def attend_back(gr, stored, near, far, heads, layer, index):
    rows, width = gr.shape
    pieces = near.shape[1]
    in_specs, out_specs, out_shape, scratch, cost = attend_back_specs(rows, width, pieces, layer, index)
    return pl.pallas_call(
        attend_back_kernel,
        grid=(pieces,),
        in_specs=in_specs,
        out_specs=out_specs,
        out_shape=out_shape,
        scratch_shapes=scratch,
        cost_estimate=cost,
        name="attend_back",
    )(gr, *stored, near, far, heads)


def attn_weight_kernel(a_ref, gq_ref, gkv_ref, gr_ref, o_ref, keep_ref, send_ref, a_t_ref, gr_t_ref):
    rows = gq_ref.shape[0]
    half = keep_ref.shape[0]

    @pl.when(pl.program_id(0) == 0)
    def _():
        a_t_ref[...] = a_ref[...].T
        gr_t_ref[...] = gr_ref[...].T

    for part, ref in ((slice(0, half), keep_ref), (slice(half, 2 * half), send_ref)):
        from_q = nn(a_t_ref[part, REACH : REACH + rows], gq_ref[...])
        from_o = nn(gr_t_ref[part, :], o_ref[...])
        ref[:, :PAIR] = from_q[:, :PAIR].astype(BF16)
        ref[:, PAIR : 4 * PAIR] = nn(a_t_ref[part, :], gkv_ref[...]).astype(BF16)
        ref[:, 4 * PAIR : 5 * PAIR] = (from_q[:, PAIR:] + from_o[:, :PAIR]).astype(BF16)
        ref[:, 5 * PAIR :] = from_o[:, PAIR:].astype(BF16)


def attn_weight_grads(a_win, gq, gkv, gr, o):
    _, window, width = a_win.shape
    rows = gr.shape[0]
    half = width // 2
    pieces = gq.shape[1] // (2 * PAIR)
    out = column(half, 6 * PAIR)
    return pl.pallas_call(
        attn_weight_kernel,
        grid=(pieces,),
        in_specs=[
            sheet(0, window, width), column(rows, 2 * PAIR), column(window, 3 * PAIR), whole((rows, width)),
            slab(0, rows, 2 * PAIR),
        ],
        out_specs=[out, out],
        out_shape=[shaped((half, pieces * 6 * PAIR))] * 2,
        scratch_shapes=[pltpu.VMEM((width, window), BF16), pltpu.VMEM((width, rows), BF16)],
        cost_estimate=pl.CostEstimate(
            flops=2 * width * width * (2 * window + 2 * rows), bytes_accessed=8 * width * width, transcendentals=0
        ),
        name="attn_weight_grads",
    )(a_win, gq, gkv, gr, o)


def mlp_weight_kernel(m_ref, gh_ref, gz_ref, act_ref, keep_ref, send_ref, m_t_ref, gz_t_ref):
    half = keep_ref.shape[0]
    wide = gh_ref.shape[1]

    @pl.when(pl.program_id(0) == 0)
    def _():
        m_t_ref[...] = m_ref[...].T
        gz_t_ref[...] = gz_ref[...].T

    for part, ref in ((slice(0, half), keep_ref), (slice(half, 2 * half), send_ref)):
        ref[:, :wide] = nn(m_t_ref[part, :], gh_ref[...]).astype(BF16)
        ref[:, wide:] = nn(gz_t_ref[part, :], act_ref[...]).astype(BF16)


def mlp_weight_grads(m, gh, gz, act):
    _, rows, width = m.shape
    half = width // 2
    hidden = gh.shape[1]
    pieces = lax.axis_size("tp")
    wide = hidden // pieces
    out = column(half, 2 * wide)
    return pl.pallas_call(
        mlp_weight_kernel,
        grid=(pieces,),
        in_specs=[sheet(0, rows, width), column(rows, wide), whole((rows, width)), slab(0, rows, wide)],
        out_specs=[out, out],
        out_shape=[shaped((half, 2 * hidden))] * 2,
        scratch_shapes=[pltpu.VMEM((width, rows), BF16), pltpu.VMEM((width, rows), BF16)],
        cost_estimate=pl.CostEstimate(
            flops=4 * width * hidden * rows, bytes_accessed=4 * width * hidden, transcendentals=0
        ),
        name="mlp_weight_grads",
    )(m, gh, gz, act)


class Scatter:
    KINDS = 7

    def __init__(self, peers, out, away, keep, core, first, second, given, send, recv):
        self.peers, self.out, self.away, self.keep, self.core_in = peers, out, away, keep, core
        self.first_in, self.second_in, self.given, self.send, self.recv = first, second, given, send, recv
        self.chunk, self.wide = out.shape
        self.half = self.wide // 2
        self.pieces = keep.shape[0]

    def copy(self, piece, kind, source, target, device):
        return pltpu.make_async_remote_copy(
            src_ref=source, dst_ref=target, send_sem=self.send.at[piece, kind], recv_sem=self.recv.at[piece, kind],
            device_id=device, device_id_type=MESH,
        )

    def copies(self, piece, stage):
        c, left, right = self.chunk, pl.ds(0, self.half), pl.ds(self.half, self.half)
        rows = lambda start, count=1: pl.ds(start * c, count * c)
        if stage == "core":
            return [self.copy(piece, 0, self.away.at[self.slot(piece)], self.core_in.at[piece], self.peers.core)]
        if stage == "first":
            source, target = self.keep.at[piece], self.first_in.at[piece]
            return [
                self.copy(piece, 1, source.at[rows(2, 2), left], target.at[:, left], self.peers.y),
                self.copy(piece, 2, source.at[rows(1), right], target.at[rows(0), right], self.peers.x),
                self.copy(piece, 3, source.at[rows(3), right], target.at[rows(1), right], self.peers.x),
            ]
        if stage == "second":
            source, target = self.keep.at[piece], self.second_in.at[piece]
            return [
                self.copy(piece, 4, source.at[rows(1), left], target.at[:, left], self.peers.x),
                self.copy(piece, 5, source.at[rows(2), right], target.at[:, right], self.peers.y),
            ]
        target = self.given.at[(piece - 1) % self.pieces]
        return [self.copy(piece, 6, self.keep.at[piece, rows(0), :], target, self.peers.along(1))]

    def start(self, piece, stage):
        for copy in self.copies(piece, stage):
            copy.start()

    def arrived(self, piece, stage):
        for copy in self.copies(piece, stage):
            copy.wait_recv()

    def add(self, piece, start, count, cols, source):
        step = 32

        @pl.loop(0, count * self.chunk // step)
        def _(index):
            row = pl.multiple_of(index * step, step)
            into = (piece, pl.ds(start * self.chunk + row, step), cols)
            self.keep[into] = self.keep[into] + source[pl.ds(row, step), cols]

    def slot(self, piece):
        return (piece + self.pieces - 1) % self.pieces % 2

    def room(self, index, piece):
        @pl.when(index > 1)
        def _():
            for copy in self.copies(lax.rem(piece + self.pieces - 2, self.pieces), "core"):
                copy.wait_send()

    def first(self, piece):
        self.arrived(piece, "core")
        self.add(piece, 0, 4, pl.ds(0, self.wide), self.core_in.at[piece])
        self.start(piece, "first")

    def second(self, piece):
        left, right = pl.ds(0, self.half), pl.ds(self.half, self.half)
        self.arrived(piece, "first")
        source = self.first_in.at[piece]
        self.add(piece, 0, 2, left, source)
        self.add(piece, 0, 1, right, source)
        self.add(piece, 2, 1, right, source.at[pl.ds(self.chunk, self.chunk)])
        self.start(piece, "second")

    def last(self, piece):
        self.arrived(piece, "second")
        kept = pl.ds(0, self.chunk)
        total = self.keep[piece, kept, :].astype(F32) + self.second_in[piece].astype(F32)
        if piece != 1:
            self.arrived((piece - 1) % self.pieces, "give")
            total += self.given[(piece - 2) % self.pieces].astype(F32)
        if piece:
            self.keep[piece, kept, :] = total.astype(BF16)
            self.start(piece, "give")
        else:
            self.out[...] = total

    def done(self):
        for piece in range(self.pieces):
            for stage in ("core", "first", "second", "give"):
                if (stage != "give" or piece) and (stage != "core" or piece in (0, self.pieces - 1)):
                    for copy in self.copies(piece, stage):
                        copy.wait_send()

    def made(self, plan, index, piece):
        size = self.chunk * self.wide * 2
        both = lambda count: [("x", count * size), ("y", count * size)]
        key = (index, piece)
        rank = index * self.pieces + (piece - 1) % self.pieces
        plan.carry([("core", 4 * size)], ("core", *key))
        plan.add(rank, (self.first, piece), [("core", *key)], both(1), ("first", *key), index)
        plan.add(rank, (self.second, piece), [("first", *key)], both(0.5), ("second", *key), index)
        needs = [("second", *key)] + ([("give", index, (piece - 1) % self.pieces)] if piece != 1 else [])
        plan.add(rank, (self.last, piece), needs, [("z", size)] if piece else [], ("give", *key), index)


class Return:
    def __init__(self, edges, landed, rows, send, recv):
        self.edges, self.landed, self.send, self.recv = edges, landed, send, recv
        self.place, self.size = lax.axis_index("tp"), lax.axis_size("tp")
        self.rows, self.spill = rows, REACH - rows
        spill = self.spill
        self.moves = [
            (1, 2, REACH + rows, spill, 2 * rows),
            (-1, 2, 0, spill, 2 * rows + spill),
            (1, 1, REACH, rows, 0),
            (-1, 1, spill, rows, rows),
        ]

    def inside(self, distance):
        other = self.place + distance
        return jnp.logical_and(other >= 0, other < self.size)

    def sends(self, index):
        direction, far, *_ = self.moves[index]
        return self.inside(direction * far)

    def takes(self, index):
        direction, far, *_ = self.moves[index]
        return jnp.logical_and(self.inside(-direction), self.inside(direction * (far - 1)))

    def copy(self, index):
        direction, _, start, count, target = self.moves[index]
        return pltpu.make_async_remote_copy(
            src_ref=self.edges.at[pl.ds(start, count), pl.ds(0, self.landed.shape[1])],
            dst_ref=self.landed.at[pl.ds(target, count), :], send_sem=self.send.at[index], recv_sem=self.recv.at[index],
            device_id={"tp": self.place + direction}, device_id_type=MESH,
        )

    def start(self, index):
        @pl.when(self.sends(index))
        def _():
            self.copy(index).start()

    def begin(self):
        for index in range(2):
            self.start(index)

    def relay(self):
        wide = self.landed.shape[1]
        for index, into in ((0, REACH), (1, REACH - self.spill)):
            target = self.moves[index][4]

            @pl.when(self.takes(index))
            def _():
                self.copy(index).wait_recv()
                rows = slice(into, into + self.spill)
                self.edges[rows, :wide] = self.edges[rows, :wide] + self.landed[target : target + self.spill, :]

            self.start(index + 2)

    def end(self, total_ref):
        for index in range(4):

            @pl.when(self.sends(index))
            def _():
                self.copy(index).wait_send()

        for index in (2, 3):
            target = self.moves[index][4]

            @pl.when(self.takes(index))
            def _():
                self.copy(index).wait_recv()
                total_ref[...] += self.landed[target : target + self.rows, :].astype(F32)


def split_dot(left, right):
    if left.dtype == F32:
        high = left.astype(BF16)
        return nn(high, right) + nn((left - high.astype(F32)).astype(BF16), right)
    high = right.astype(BF16)
    return nn(left, high) + nn(left, (right - high.astype(F32)).astype(BF16))


def picked(mask):
    return mask.astype(F32).astype(BF16)


class Tally:
    def __init__(self, peers, chunks, inbox, send, recv, pieces):
        self.peers, self.chunks, self.inbox, self.send, self.recv, self.pieces = peers, chunks, inbox, send, recv, pieces
        self.share = Share(peers, chunks.at[0], inbox.at[pl.ds(0, pieces)], chunks, send, recv)

    def across(self, stage):
        count = 4 >> stage
        device = (self.peers.core, self.peers.y, self.peers.x)[stage]
        source, target = self.chunks.at[pl.ds(count, count)], self.inbox.at[pl.ds(8 - 2 * count, count)]
        return self.share.copy(stage, source, target, device)

    def along(self):
        place = self.inbox.at[7 + self.peers.tp]
        return [self.share.copy(2 + d, self.chunks.at[0], place, self.peers.along(d)) for d in range(1, self.pieces)]

    def build(self, tables, lines_ref, work_ref, norm_sums, mlp_sums, head_sums, up_grad):
        layers, width = norm_sums.shape[0], lines_ref.shape[1]
        count = self.chunks.shape[0]
        chunk, first = width // count, tables.shape[0]
        fine, parts = chunk // self.pieces, up_grad.shape[3] * self.pieces // width
        lines_ref[:first, :] = tables
        lines_ref[first : first + 16, :] = jnp.zeros((16, width), F32)
        for layer in range(layers):
            sums = [(norm_sums, 0), (mlp_sums, 2), (norm_sums, 1), (mlp_sums, 3), (mlp_sums, 1), (mlp_sums, 0)]
            for index, (ref, row) in enumerate(sums):
                at = first + layer * FEATS + index
                lines_ref[at : at + 1, :] = ref[layer, row : row + 1, :]
        lines = lines_ref[: first + 16, :]
        row, col = (lax.broadcasted_iota(jnp.int32, (width, PAIR), axis) for axis in range(2))
        for place in range(count):
            spread = picked(jnp.logical_and(col < chunk, row == place * chunk + col))
            self.chunks[place, : first + 16, :] = split_dot(lines, spread).astype(BF16)
        row, col = (lax.broadcasted_iota(jnp.int32, (3 * PAIR, 2 * PAIR), axis) for axis in range(2))
        lane = lax.rem(col, PAIR)
        feature = col // PAIR * chunk + lane
        last = jnp.logical_and(feature >= PAIR, row == feature + 3 * HD)
        spread = picked(jnp.logical_and(lane < chunk, jnp.logical_or(row == feature, last)))
        work_ref[:32, :] = jnp.zeros((32, width), F32)
        for piece in range(self.pieces):
            for layer in range(layers):
                for index, line_at in enumerate((3, 4, 5, 0, 1, 2)):
                    at = layer * HEADS + index
                    work_ref[at : at + 1, : 3 * PAIR] = head_sums[layer, piece, line_at : line_at + 1, :]
            both = split_dot(work_ref[:16, : 3 * PAIR], spread).astype(BF16)
            owner = self.share.owner(piece)
            for index in range(2):
                target = self.chunks.at[self.share.chunk_of(2 * owner + index)]
                target[first + 16 : first + 32, :] = both[:, index * PAIR : (index + 1) * PAIR]
        wide = self.pieces * parts * fine
        for index in range(2 * self.pieces):
            for layer in range(layers):
                at = 16 + index * layers + layer
                half = slice(index % 2 * wide, (index % 2 + 1) * wide)
                work_ref[at : at + 1, :wide] = up_grad[layer, index // 2, :, half]
        biases = work_ref[16 : 16 + 2 * self.pieces * layers, :wide]
        row, col = (lax.broadcasted_iota(jnp.int32, (wide, PAIR), axis) for axis in range(2))
        shape = (2 * self.pieces * 16, 2 * self.pieces * layers)
        line_of, from_of = (lax.broadcasted_iota(jnp.int32, shape, axis) for axis in range(2))
        total = 0.0
        for part in range(parts):
            source = col // fine * (parts * fine) + part * fine + lax.rem(col, fine)
            here = split_dot(biases, picked(jnp.logical_and(col < chunk, row == source)))
            group = jnp.logical_and(line_of // 16 == from_of // layers, lax.rem(line_of, 16) == lax.rem(from_of, layers) * parts + part)
            total += split_dot(picked(group), here)
        for index in range(2 * self.pieces):
            target = self.chunks.at[self.share.chunk_of(2 * self.share.owner(index // 2) + index % 2)]
            target[first + 32 : first + 48, :] = total[index * 16 : (index + 1) * 16].astype(BF16)
        self.across(0).start()

    def fold(self, stage):
        count = 4 >> stage
        self.across(stage).wait_recv()
        mine, found = self.chunks[:count], self.inbox[8 - 2 * count : 8 - count]
        self.chunks[:count] = (mine.astype(F32) + found.astype(F32)).astype(BF16)
        if stage < 2:
            self.across(stage + 1).start()
        else:
            for copy in self.along():
                copy.start()

    def total(self, out_ref):
        total = self.chunks[0].astype(F32)
        for copy in self.along():
            copy.wait_recv()
        for distance in range(1, self.pieces):
            total += self.inbox[7 + lax.rem(self.peers.tp + distance, self.pieces)].astype(F32)
        out_ref[...] = total
        for copy in self.along() + [self.across(stage) for stage in range(3)]:
            copy.wait_send()


def backward_kernel(
    cot_ref, hot_ref, feats_ref, m_ref, mid_ref, a_win_ref, x0_ref, x2_ref,
    mlp_near_ref, mlp_far_ref, slope_ref, act_ref,
    q_ref, kv_ref, q_hat_ref, k_hat_ref, q_scale_ref, k_scale_ref, p_ref, attn_near_ref, attn_far_ref, heads_ref, o_ref,
    g_ref, up_grad_ref, head_sums_ref, mlp_sums_ref, norm_sums_ref, tally_ref, mlp_out, attn_out,
    gz_ref, gh_ref, g1_ref, gr_ref, acc_ref, window_ref, gq_ref, gkv_ref, turned_ref, a_t_ref,
    landed_ref, halo_send, halo_recv, free, fetched, chunks, inbox, tally_send, tally_recv, *buffers,
):
    layers, pieces, rows = up_grad_ref.shape[0], up_grad_ref.shape[1], g_ref.shape[0]
    half = g_ref.shape[1] // 2
    wide = slope_ref.shape[1]
    own = slice(REACH, REACH + rows)
    total_ref = window_ref.at[own]
    step = pl.program_id(0)
    peers = Neighbours()
    scatter_of = lambda layer, which: Scatter(
        peers, (mlp_out, attn_out)[which].at[layer], *buffers[8 * which : 8 * which + 6],
        *[item.at[layer] for item in buffers[8 * which + 6 : 8 * which + 8]],
    )
    back = lambda layer: Return(a_t_ref, landed_ref.at[layer], rows, halo_send.at[layer], halo_recv.at[layer])

    def fetch(source, target):
        copy = pltpu.make_async_copy(source, target, fetched)
        copy.start()
        copy.wait()

    def pass_on(layer):
        back(layer).relay()

    def halo_back(layer):
        back(layer).end(total_ref)

    def made_free(item):
        layer, which = item
        scatter_of(layer + 1, which).done()
        for target in peers.all():
            pl.semaphore_signal(free.at[layer, which], inc=1, device_id=target, device_id_type=MESH)
        pl.semaphore_wait(free.at[layer, which], len(peers.all()))

    plan = Plan(3.0)
    plan.spend(2.5)

    def whole_return(layer, *at):
        plan.wait(("far", layer), (pass_on, layer), *at)
        plan.carry([("z", 4 * half * rows)], ("halo", layer))
        plan.wait(("halo", layer), (halo_back, layer), *at)

    order = [(index + 1) % pieces for index in range(pieces)]
    for layer in reversed(range(layers)):
        for which in range(2):
            for index, piece in enumerate(order):
                at = (2 * (layers - 1 - layer) + which) * pieces + index
                if index == 0 and layer + 1 < layers:
                    if which == 0:
                        whole_return(layer + 1, at, 0)
                    plan.finish(2 * (layers - 2 - layer) + which, at, 0)
                    plan.table.setdefault((at, 0), []).append((made_free, (layer, which)))
                plan.slot(at, 0)
                for slot, time in enumerate(((1.5,), (2.2, 1.3, 1.3))[which]):
                    plan.spend(time)
                    plan.slot(at, slot + 1)
                plan.spend((2.6, 3.0)[which])
                scatter_of(layer, which).made(plan, 2 * (layers - 1 - layer) + which, piece)
        plan.carry([("z", 4 * half * (REACH - rows))], ("far", layer))
    ending = 2 * layers * pieces
    whole_return(0, ending, 0)
    plan.spend(8.0)
    tally = Tally(peers, chunks, inbox, tally_send, tally_recv, pieces)
    size = chunks.shape[1] * PAIR * 2
    for stage, (link, count) in enumerate((("core", 4), ("y", 2), ("x", 1), ("z", pieces))):
        plan.carry([(link, count * size)], ("tally", stage))
        work = (tally.fold, stage) if stage < 3 else (tally.total, tally_ref)
        plan.wait(("tally", stage), work, ending, 1)
    plan.finish(None, ending, 1)
    table = plan.table

    def run(at, slot):
        if (at, slot) in table:

            @pl.when(step == at)
            def _():
                for work, item in table[at, slot]:
                    work(item)

    phase = step // pieces
    layer = jnp.maximum(layers - 1 - phase // 2, 0)
    index = lax.rem(step, pieces)
    piece = lax.rem(index + 1, pieces)
    in_mlp, in_attend = lax.rem(phase, 2) == 0, lax.rem(phase, 2) == 1
    is_ending = step == ending

    @pl.when(step == 0)
    def _():
        peers.greet()
        fetch(cot_ref, g_ref)

    run(ending, 0)
    for at in range(2 * pieces, ending, 2 * pieces):
        run(at, 0)

    def through_norm(layer, x):
        fetch(x, acc_ref)
        total = total_ref[...]
        hat, scale = row_norm(acc_ref[...])
        g_ref[...] = g1_ref[...] + row_norm_back(total * line(feats_ref.at[layer], LN_GAIN[0]), hat, scale)
        norm_sums_ref[layer] = jnp.zeros(norm_sums_ref.shape[1:], F32)
        norm_sums_ref[layer, 0:1, :] = jnp.sum(total * hat, axis=0, keepdims=True)
        norm_sums_ref[layer, 1:2, :] = jnp.sum(total, axis=0, keepdims=True)

    for above in range(1, layers):

        @pl.when(step == 2 * (layers - above) * pieces)
        def _():
            through_norm(above, x2_ref.at[above - 1])

    @pl.when(is_ending)
    def _():
        through_norm(0, x0_ref)
        tables = split_dot(hot_ref[...].T, g_ref[...])
        tally.build(tables, total_ref, acc_ref, norm_sums_ref, mlp_sums_ref, head_sums_ref, up_grad_ref)

    @pl.when(jnp.logical_and(in_mlp, step < ending))
    def _():
        def hook(slot):
            for at in range(ending):
                if at // pieces % 2 == 0 and not (slot == 0 and at % (2 * pieces) == 0 and at):
                    run(at, slot)

        hook(0)
        up, down = pl.ds(0, wide), pl.ds(wide, wide)
        mlp_back_work(
            g_ref, mlp_near_ref.at[:, down], mlp_far_ref.at[:, down], slope_ref, mlp_near_ref.at[:, up], mlp_far_ref.at[:, up],
            mid_ref, feats_ref.at[layer], gz_ref, gh_ref, up_grad_ref.at[layer, piece], g1_ref, gr_ref,
            mlp_sums_ref.at[layer], acc_ref, index == 0, index == pieces - 1, hook,
        )

        @pl.when(index == 0)
        def _():
            turned_ref[0] = m_ref[...].T
            turned_ref[1] = gz_ref[...].T

        away, keep = buffers[0], buffers[1]
        scatter = scatter_of(layer, 0)
        scatter.room(index, piece)
        for part, ref in ((slice(0, half), keep.at[piece]), (slice(half, 2 * half), away.at[scatter.slot(piece)])):
            ref[:, :wide] = nn(turned_ref[0, part, :], gh_ref[...]).astype(BF16)
            ref[:, wide:] = nn(turned_ref[1, part, :], act_ref[...]).astype(BF16)
        scatter.start(piece, "core")

    @pl.when(in_attend)
    def _():
        def hook(slot):
            for at in range(ending):
                if at // pieces % 2 == 1:
                    run(at, slot)

        hook(0)

        @pl.when(index == 0)
        def _():
            window_ref[...] = jnp.zeros_like(window_ref)
            a_t_ref[...] = a_win_ref[...].T
            turned_ref[0] = gr_ref[...].T

        attend_back_work(
            gr_ref, q_ref, kv_ref, q_hat_ref, k_hat_ref, q_scale_ref, k_scale_ref, p_ref, attn_near_ref, attn_far_ref,
            heads_ref, gq_ref, gkv_ref, head_sums_ref.at[layer, piece], window_ref, hook,
        )
        away, keep = buffers[8], buffers[9]
        scatter = scatter_of(layer, 1)
        scatter.room(index, piece)
        for part, ref in ((slice(0, half), keep.at[piece]), (slice(half, 2 * half), away.at[scatter.slot(piece)])):
            from_q = nn(a_t_ref[part, own], gq_ref[...])
            from_o = nn(turned_ref[0, part, :], o_ref[...])
            ref[:, :PAIR] = from_q[:, :PAIR].astype(BF16)
            ref[:, PAIR : 4 * PAIR] = nn(a_t_ref[part, :], gkv_ref[...]).astype(BF16)
            ref[:, 4 * PAIR : 5 * PAIR] = (from_q[:, PAIR:] + from_o[:, :PAIR]).astype(BF16)
            ref[:, 5 * PAIR :] = from_o[:, PAIR:].astype(BF16)
        scatter.start(piece, "core")

        @pl.when(index == pieces - 1)
        def _():
            a_t_ref[:REACH, : 2 * half] = window_ref[:REACH, :].astype(BF16)
            a_t_ref[REACH : 2 * REACH, : 2 * half] = window_ref[REACH + rows :, :].astype(BF16)
            back(layer).begin()

    run(ending, 1)

    @pl.when(is_ending)
    def _():
        for which in range(2):
            scatter_of(0, which).done()


def scatter_buffers(layers, pieces, chunk, wide):
    buffer = lambda rows: pltpu.VMEM((pieces, rows * chunk, wide), BF16)
    semaphores = pltpu.SemaphoreType.DMA((layers, pieces, Scatter.KINDS))
    away = pltpu.VMEM((2, 4 * chunk, wide), BF16)
    given = pltpu.VMEM((pieces - 1, chunk, wide), BF16)
    return [away, buffer(4), buffer(4), buffer(2), buffer(1), given, semaphores, semaphores]


def backward(cotangent, hot, lines, feats, heads, start, saved):
    *stored, o, act, slope, mid, m, x2, a_win, attn_near, attn_far, mlp_near, mlp_far = saved
    layers, window, width = a_win.shape
    rows, half, pieces = m.shape[1], width // 2, attn_near.shape[1]
    hidden = act.shape[2]
    wide, chunk = hidden // pieces, half // 4

    def mlp_at(step):
        phase = jnp.minimum(step // pieces, 2 * layers - 1)
        index = jnp.where(lax.rem(phase, 2) == 0, lax.rem(step, pieces), pieces - 1)
        return layers - 1 - phase // 2, lax.rem(index + 1, pieces)

    def attend_at(step):
        phase = jnp.minimum(step // pieces, 2 * layers - 1)
        index = jnp.where(lax.rem(phase, 2) == 1, lax.rem(step, pieces), 0)
        index = jnp.where(step == 2 * layers * pieces, pieces - 1, index)
        return layers - 1 - phase // 2, lax.rem(index + 1, pieces)

    once = lambda shape: pl.BlockSpec(shape, lambda step: (0,) * len(shape), pipeline_mode=pl.Buffered(1))
    weight = lambda at, wide: pl.BlockSpec((None, None, half, wide), lambda step: (*at(step), 0, 0))
    cols = lambda at, height, wide: pl.BlockSpec((None, height, wide), lambda step: (at(step)[0], 0, at(step)[1]))
    by_heads = pl.BlockSpec((3, window, rows), lambda step: (attend_at(step)[0] * pieces + attend_at(step)[1], 0, 0))
    layer_heads = pl.BlockSpec((None, None, HEADS, 3 * PAIR), lambda step: (attend_at(step)[1], attend_at(step)[0], 0, 0))
    layer_sheet = lambda at, height: pl.BlockSpec(
        (None, height, width), lambda step: (at(step)[0], 0, 0), pipeline_mode=pl.Buffered(1)
    )
    outs = [
        (rows, width), (layers, pieces, 1, wide), (layers, pieces, 8, 3 * PAIR), (layers, 8, width), (layers, 8, width),
        (lines, PAIR), (layers, chunk, 2 * wide), (layers, chunk, 6 * PAIR),
    ]
    vmem = lambda shape, kind=BF16: pltpu.VMEM(shape, kind)
    inputs = (cotangent, hot, feats, m, mid, a_win, start, x2, mlp_near, mlp_far, slope, act, *stored, attn_near, attn_far, heads, o)
    return pl.pallas_call(
        backward_kernel,
        grid=(2 * layers * pieces + 1,),
        in_specs=[
            ANY, once(hot.shape), once(feats.shape), layer_sheet(mlp_at, rows), layer_sheet(mlp_at, rows), layer_sheet(attend_at, window), ANY, ANY,
            weight(mlp_at, 2 * wide), weight(mlp_at, 2 * wide), cols(mlp_at, rows, wide),
            cols(mlp_at, rows, wide), *[cols(attend_at, *shape) for shape in attend_shapes(rows, window)], by_heads,
            weight(attend_at, 6 * PAIR), weight(attend_at, 6 * PAIR), layer_heads, cols(attend_at, rows, 2 * PAIR),
        ],
        out_specs=[once(shape) for shape in outs],
        out_shape=[shaped(shape, F32) for shape in outs],
        scratch_shapes=[
            vmem((rows, width)), vmem((rows, wide)), vmem((rows, width), F32), vmem((rows, width)),
            vmem((rows, width), F32), vmem((window, width), F32), vmem((rows, 2 * PAIR)), vmem((window, 3 * PAIR)),
            vmem((2, width, rows)), vmem((width, window)),
            vmem((layers, 2 * REACH, width)), pltpu.SemaphoreType.DMA((layers, 4)), pltpu.SemaphoreType.DMA((layers, 4)),
            pltpu.SemaphoreType.REGULAR((layers, 2)), pltpu.SemaphoreType.DMA, vmem((8, lines, PAIR)),
            vmem((7 + pieces, lines, PAIR)), pltpu.SemaphoreType.DMA((pieces + 2,)), pltpu.SemaphoreType.DMA((pieces + 2,)), *scatter_buffers(layers, pieces, chunk, 2 * wide),
            *scatter_buffers(layers, pieces, chunk, 6 * PAIR),
        ],
        compiler_params=params(40, VMEM),
        name="backward",
    )(*inputs)


def flip(array, bit, axis="fsdp"):
    size = lax.axis_size(axis)
    return lax.ppermute(array, axis, [(i, i ^ (1 << bit)) for i in range(size)])


def ring(array):
    size = lax.axis_size("tp")
    return lax.ppermute(array, "tp", [(i, (i + 1) % size) for i in range(size)])


def hop(array, distance):
    size = lax.axis_size("tp")
    return lax.ppermute(array, "tp", [(i, i + distance) for i in range(size) if 0 <= i + distance < size])


def bits_of(size):
    return size.bit_length() - 1


def row_bits(first_top):
    count = bits_of(lax.axis_size("fsdp"))
    tops = [count - 1, count - 2] if first_top else [count - 2, count - 1]
    return list(range(1, count - 2)), tops


def gather_by_permutes(block, first_top):
    pieces = [block]
    for _ in range(lax.axis_size("tp") - 1):
        pieces.append(ring(pieces[-1]))
    block = jnp.concatenate(pieces, axis=1)
    low, tops = row_bits(first_top)
    have = []
    for bit in low + tops:
        axis = sum(other > bit for other in have)
        block = jnp.stack([block, flip(block, bit)], axis=axis)
        have.append(bit)
    block = block.reshape((-1, len(pieces), pieces[0].shape[1])).transpose(1, 0, 2)[None]
    return block, flip(block, 0)


def add(left, right, kind=BF16):
    return (left.astype(F32) + right.astype(F32)).astype(kind)


def reduce_by_permutes(keep, send, first_top):
    low, tops = row_bits(first_top)
    block = add(keep, flip(send, 0))
    order = tops + low[::-1]
    have = sorted(order, reverse=True)
    block = block.reshape((2,) * len(have) + (-1, block.shape[-1]))
    for bit in order:
        axis = have.index(bit)
        mine = lax.index_in_dim(block, 0, axis, keepdims=False)
        other = lax.index_in_dim(block, 1, axis, keepdims=False)
        block = add(mine, flip(other, bit))
        have.remove(bit)
    pieces = jnp.split(block, lax.axis_size("tp"), axis=1)
    total = pieces[1]
    for piece in pieces[2:]:
        total = add(ring(total), piece)
    return add(ring(total), pieces[0], F32)


def attn_shard(w_qkv, w_out):
    q, k, v = (w_qkv[:, which] for which in range(3))
    o = w_out.T
    return side(q[:, :PAIR], k[:, :PAIR], v[:, :PAIR], k[:, PAIR:], v[:, PAIR:], q[:, PAIR:], o[:, PAIR:], o[:, :PAIR])


def attn_unshard(block):
    tile = lambda start, wide=PAIR: block[:, start : start + wide]
    q = side(tile(0), tile(4 * PAIR, HD))
    k = side(tile(PAIR), tile(3 * PAIR, HD))
    v = side(tile(2 * PAIR), tile(3 * PAIR + HD, HD))
    o = side(tile(5 * PAIR), tile(4 * PAIR + HD, HD))
    return jnp.stack([q, k, v], axis=1), o.T


def body(
    tokens, segment_ids, patch_pos, row_table, col_table, ln_gain, ln_bias, qkv_bias, qk_gain, query_bias, out_bias,
    fc1_bias, fc2_bias, w_qkv, w_out, w_fc1, w_fc2, cotangent,
):
    layers = w_qkv.shape[0]
    rows, width = tokens.shape
    half = width // 2
    fsdp, tp = lax.axis_size("fsdp"), lax.axis_size("tp")
    f_index, t_index = lax.axis_index("fsdp"), lax.axis_index("tp")
    hidden = fc1_bias.shape[1] * fsdp * tp
    grid = row_table.shape[0]
    fine = width // (fsdp * tp)
    parts = hidden // width
    in_kernel = fsdp == 8

    place = jnp.arange(width, dtype=jnp.int32)
    chunk = width // fsdp
    slot = place // chunk
    away = (slot % (fsdp // 2)) * 2 + slot // (fsdp // 2)
    feature_at = (f_index ^ away) * chunk + place % chunk
    head_cols = width // tp
    spot = jnp.arange(tp * 3 * PAIR, dtype=jnp.int32)
    tile, part = spot % (3 * PAIR) // PAIR, spot % PAIR // HD
    head = jnp.where(tile == 0, part, jnp.where(tile == part + 1, 2, -fsdp * tp))
    head_at = ((t_index - spot // (3 * PAIR)) % tp) * head_cols + head * HD + spot % HD
    to_feature = (place[:, None] == feature_at[None, :]).astype(BF16)
    to_head = (place[:, None] == head_at[None, :]).astype(BF16)
    device = jnp.arange(fsdp * tp, dtype=jnp.int32)
    wanted = ((t_index - device // fsdp) % tp) * fsdp + device % fsdp
    to_hidden = (wanted[:, None] == device[None, :]).astype(BF16)

    by_layer = lambda *items: jnp.concatenate([item.reshape(layers, -1, fine) for item in items], axis=1).reshape(-1, fine)
    shares = [
        row_table, col_table, by_layer(ln_gain, ln_bias, out_bias, fc2_bias), by_layer(qkv_bias, qk_gain, query_bias),
        fc1_bias.reshape(layers * parts, fine),
    ]
    count = sum(item.shape[0] for item in shares)
    attn_shards = jnp.stack([attn_shard(w_qkv[layer], w_out[layer]) for layer in range(layers)])
    mlp_shards = jnp.concatenate([w_fc1, w_fc2.transpose(0, 2, 1)], axis=2)
    grid_ids = jnp.arange(grid, dtype=jnp.int32)
    row_hot = patch_pos[0][:, None] == grid_ids[None, :]
    col_hot = patch_pos[1][:, None] == grid_ids[None, :]
    hot = side(row_hot, col_hot).astype(BF16)
    tokens = jnp.dot(tokens, to_feature, preferred_element_type=F32)
    segments = segment_ids[0]
    padded = jnp.pad(segments, (REACH, REACH), constant_values=-1)
    seg_k = lax.dynamic_slice_in_dim(padded, t_index * rows, rows + 2 * REACH).reshape(-1, 1)
    seg_q = lax.dynamic_slice_in_dim(segments, t_index * rows, rows).reshape(1, -1)
    spill = REACH - rows

    if in_kernel:
        share = jnp.concatenate([jnp.pad(item, ((0, -item.shape[0] % 16), (0, PAIR - fine))) for item in shares], axis=0)
        *kept, start, feats, heads, a_win, attn_near, attn_far, mlp_near, mlp_far = forward(
            tokens, hot, share, seg_k, seg_q, attn_shards, mlp_shards
        )
        residual = kept[-1][layers - 1]
        kept += [a_win, attn_near, attn_far, mlp_near, mlp_far]
    else:
        small = jnp.concatenate(shares, axis=0)
        flat = small.reshape(1, -1)
        for bit in range(bits_of(tp)):
            flat = jnp.concatenate([flat, flip(flat, bit, "tp")], axis=0)
        for bit in range(bits_of(fsdp)):
            flat = jnp.concatenate([flat, flip(flat, bit)], axis=0)
        flat = flat[jnp.arange(fsdp * tp) ^ (f_index * tp + t_index)]
        gathered = flat.reshape(fsdp * tp, count, fine)
        lined = gathered.transpose(1, 0, 2).reshape(count, width)
        wide = 2 * grid + 6 * layers
        feats = jnp.dot(lined[:wide], to_feature, preferred_element_type=F32)
        heads = jnp.dot(lined[wide : wide + 6 * layers], to_head, preferred_element_type=F32)
        up_shift = jnp.einsum(
            "or,rlsi->losi",
            to_hidden,
            gathered[:, wide + 6 * layers :].reshape(fsdp * tp, layers, parts, fine),
            preferred_element_type=F32,
        ).reshape(layers, tp, 1, hidden // tp)
        tables = feats[: 2 * grid].astype(BF16)
        feats = feats[2 * grid :].reshape(layers, FEATS, width)

        heads = heads.reshape(layers, HEADS, tp, 3 * PAIR).transpose(2, 0, 1, 3)
        residual = tokens + jnp.dot(hot, tables, preferred_element_type=F32)
        hat, _ = row_norm(residual)
        a_own = (hat * feats[0, LN_GAIN[0]] + feats[0, LN_BIAS[0]]).astype(BF16)
        saved = []
        for layer in range(layers):
            a_win = jnp.concatenate(
                [hop(a_own[rows - spill :], 2), hop(a_own, 1), a_own, hop(a_own, -1), hop(a_own[:spill], -2)], axis=0
            )
            attn_near, attn_far = gather_by_permutes(attn_shards[layer], layer % 2 == 0)
            *stored, probs, o, mid, m = attend(
                a_win, attn_near, attn_far, heads, feats, residual, seg_k, seg_q, layer
            )
            mlp_near, mlp_far = gather_by_permutes(mlp_shards[layer], layer % 2 == 1)
            act, slope, x2 = mlp(m, mid, mlp_near, mlp_far, up_shift, feats, layer)
            stored = [item[None] for item in stored] + [probs]
            kept = [item[None] for item in (o, mid, m, act, slope)]
            saved.append((residual, a_win[None], stored, *kept, attn_near, attn_far, mlp_near, mlp_far))
            residual = x2
            if layer + 1 < layers:
                hat, _ = row_norm(residual)
                a_own = (
                    hat * feats[layer + 1, LN_GAIN[0]] + feats[layer + 1, LN_BIAS[0]]
                ).astype(BF16)

    restore = functools.partial(
        lax.dot_general, dimension_numbers=(((1,), (1,)), ((), ())), precision=lax.Precision.HIGH, preferred_element_type=F32
    )
    exact = to_feature.astype(F32)
    activations = restore(residual, exact)
    cotangent_here = jnp.dot(cotangent, exact, precision=lax.Precision.HIGH, preferred_element_type=F32)
    kept_sums = [None] * layers
    if in_kernel:
        grad, _, _, _, _, tally, mlp_blocks, attn_blocks = backward(
            cotangent_here, hot, share.shape[0], feats, heads, start, kept
        )
    else:
        grad, mlp_blocks, attn_blocks = cotangent_here, [None] * layers, [None] * layers
        for layer in reversed(range(layers)):
            x, a_win, stored, o, mid, m, act, slope, attn_near, attn_far, mlp_near, mlp_far = saved[layer]
            gz, gh, up_grad, g1, gr, mlp_small = mlp_back(grad, mlp_near, mlp_far, slope, mid, feats, layer, 0)
            mlp_blocks[layer] = reduce_by_permutes(*mlp_weight_grads(m, gh, gz, act), layer % 2 == 0)
            gq, gkv, mine, left, right, attn_small = attend_back(gr, stored, attn_near, attn_far, heads, layer, 0)
            attn_blocks[layer] = reduce_by_permutes(*attn_weight_grads(a_win, gq, gkv, gr, o), layer % 2 == 1)
            ends = jnp.concatenate([hop(right[rows:], 2), hop(left[:spill], -2)], axis=0).astype(F32)
            attn_grad = mine + hop(right[:rows], 1).astype(F32) + hop(left[spill:], -1).astype(F32) + ends
            hat, scale = row_norm(x)
            grad = g1 + row_norm_back(attn_grad * feats[layer, LN_GAIN[0]], hat, scale)
            kept_sums[layer] = (
                jnp.sum(attn_grad * hat, axis=0), jnp.sum(attn_grad, axis=0), mlp_small, attn_small,
                up_grad.reshape(parts, width),
            )
    middle = mlp_blocks[0].shape[1] // 2
    w_fc1_grad = [block[:, :middle] for block in mlp_blocks]
    w_fc2_grad = [block[:, middle:].T for block in mlp_blocks]
    w_qkv_grad, w_out_grad = zip(*[attn_unshard(block) for block in attn_blocks])

    token_grad = restore(grad, exact)
    if in_kernel:
        found = lax.dynamic_slice_in_dim(tally, t_index * fine, fine, axis=1)
        rows_g, cols_g, rest = found[:grid], found[grid : 2 * grid], found[2 * grid :]
        by_feature = rest[: layers * FEATS].reshape(layers, FEATS, fine)
        by_head = rest[16 : 16 + layers * HEADS].reshape(layers, HEADS, fine)
        up_g = rest[32 : 32 + layers * parts].reshape(layers, parts * fine)
    else:
        row_grad = jnp.einsum("tg,td->gd", row_hot.astype(F32), grad, precision=HIGHEST)
        col_grad = jnp.einsum("tg,td->gd", col_hot.astype(F32), grad, precision=HIGHEST)
        featured = [row_grad, col_grad]
        headed = []
        for a_gain, a_shift, sums, head_sums, _ in kept_sums:
            featured.append(jnp.stack([a_gain, sums[2], a_shift, sums[3], sums[1], sums[0]]))
            headed += [head_sums[3:6], head_sums[0:2], head_sums[2:3]]
        headed = jnp.concatenate(headed)
        spread = jnp.concatenate(
            [restore(jnp.concatenate(featured), to_feature.astype(F32)), restore(headed, to_head.astype(F32))]
        )
        spread = spread.reshape(-1, fsdp * tp, fine).transpose(1, 0, 2)
        up_all = jnp.stack([item[4] for item in kept_sums]).reshape(layers, fsdp * tp, parts * fine)
        up_all = jnp.einsum("or,lok->rlk", to_hidden.astype(F32), up_all, precision=HIGHEST)
        flat = jnp.concatenate([spread.reshape(fsdp * tp, -1), up_all.reshape(fsdp * tp, -1)], axis=1)
        flat = flat[jnp.arange(fsdp * tp) ^ (f_index * tp + t_index)]
        for bit in reversed(range(bits_of(fsdp))):
            middle = flat.shape[0] // 2
            flat = flat[:middle] + flip(flat[middle:], bit)
        for bit in reversed(range(bits_of(tp))):
            middle = flat.shape[0] // 2
            flat = flat[:middle] + flip(flat[middle:], bit, "tp")
        found = flat.reshape(-1, fine)
        rows_g, cols_g, rest = found[:grid], found[grid : 2 * grid], found[2 * grid :]
        by_feature = rest[: layers * FEATS].reshape(layers, FEATS, fine)
        by_head = rest[layers * FEATS : layers * (FEATS + HEADS)].reshape(layers, HEADS, fine)
        up_g = rest[layers * (FEATS + HEADS) :].reshape(layers, parts * fine)
    gain_g, shift_g, out_g, last_g = by_feature[:, :2], by_feature[:, 2:4], by_feature[:, OUT_BIAS], by_feature[:, LAST_BIAS]
    proj_g, head_gain_g, head_shift_g = by_head[:, :3], by_head[:, 3:5], by_head[:, HEAD_BIAS]
    return (
        activations, token_grad, rows_g, cols_g, gain_g, shift_g, proj_g, head_gain_g, head_shift_g, out_g, up_g, last_g,
        jnp.stack(w_qkv_grad), jnp.stack(w_out_grad), jnp.stack(w_fc1_grad), jnp.stack(w_fc2_grad),
    )


def solution(mesh):
    both = ("fsdp", "tp")
    in_specs = (
        P(both, None), P("fsdp", None), P(None, both), P(None, both), P(None, both), P(None, None, both),
        P(None, None, both), P(None, None, both), P(None, None, both), P(None, both), P(None, both), P(None, both),
        P(None, both), P(None, "fsdp", None, "tp"), P(None, "tp", "fsdp"), P(None, "fsdp", "tp"), P(None, "tp", "fsdp"),
        P(both, None),
    )
    out_specs = (
        P(both, None), P(both, None), P(None, both), P(None, both), P(None, None, both), P(None, None, both),
        P(None, None, both), P(None, None, both), P(None, both), P(None, both), P(None, both), P(None, both),
        P(None, "fsdp", None, "tp"), P(None, "tp", "fsdp"), P(None, "fsdp", "tp"), P(None, "tp", "fsdp"),
    )
    return jax.shard_map(body, mesh=mesh, in_specs=in_specs, out_specs=out_specs, check_vma=False)
```
